512 devices in a mesh: seq: 32 (over y, x), head: 16 (over z, core).
Axes of the slice: x: 4, y: 8, z: 8, core: 2. Of those that a mesh axis runs over, the one named last changes fastest.
Arguments:
- x_input: bfloat16 [4096, 16384], P('seq', 'head'), may hold values from -6 to 6
- z_input: bfloat16 [4096, 16384], P('seq', 'head'), may hold values from -52 to 52
- bc_input: bfloat16 [2, 4096, 128], P(None, 'seq'), may hold values from -2.09375 to 2.09375
- dt_raw: float32 [128, 4096], P('head', 'seq'), may hold values from -1.5 to 4.5
- dt_bias: float32 [128], P('head'), may hold values from -4.2 to 0.3
- a_log: float32 [128], P('head')
- d_skip: float32 [128], P('head'), may hold values from 0.5 to 1.5
- conv_x: float32 [4, 16384], P(None, 'head'), may hold values from -3 to 3
- convolution_bc_taps: float32 [2, 4, 128], replicated, may hold values from -3 to 3
- rescale_factor: float32 [16384], P('head'), may hold values from 0.5 to 1.5
- grad_out: bfloat16 [4096, 16384], P('seq', 'head'), may hold values from -40 to 40
Outputs:
- grad_x: bfloat16 [4096, 16384], P('seq', 'head')
- grad_z: bfloat16 [4096, 16384], P('seq', 'head')
- grad_bc: bfloat16 [2, 4096, 128], P(None, ('seq', 'head'))
- grad_dt: float32 [128, 4096], P('head', 'seq')
The draws below stay inside these ranges and needn't reach their ends.
All inputs are finite; a program needn't handle non-finite values.
Results may differ from the reference program's by a relative error of at most 0.0086.
Values may be sent and summed in bfloat16 or wider, within the bound.
A program may use at most 64 MiB of HBM per device.

```python
import math
import jax
import jax.numpy as jnp
from jax import lax

HEADS = 128
HEAD_DIM = 128
NSTATE = 128
KCONV = 4
TOK_DEV = 128
STREAM_LENGTH = 4096
INNER = 16384
N_SEQ = 32


def head_kinds(key):
    slow_share = 0.5
    return jax.random.uniform(jax.random.fold_in(key, 101), (HEADS,)) < slow_share


def draw_a_log(key, part):
    slow_heads = head_kinds(key)
    slow_log = math.log(1.0 / (0.0215 * STREAM_LENGTH)) + jax.random.uniform(jax.random.fold_in(key, 102), (HEADS,), minval=math.log(0.3), maxval=math.log(1.5))
    fast_log = jax.random.uniform(jax.random.fold_in(key, 103), (HEADS,), minval=math.log(0.028), maxval=math.log(0.05))
    return jnp.where(slow_heads, slow_log, fast_log).astype(jnp.float32)


def draw_dt_bias(key, part):
    slow_heads = head_kinds(key)
    slow_bias = jax.random.uniform(jax.random.fold_in(key, 104), (HEADS,), minval=-4.2, maxval=-3.8)
    fast_bias = jax.random.uniform(jax.random.fold_in(key, 105), (HEADS,), minval=-0.3, maxval=0.3)
    return jnp.where(slow_heads, slow_bias, fast_bias).astype(jnp.float32)


def draw_dt_raw(key, part):
    spread = 1.0
    equal_fraction = jax.random.uniform(jax.random.fold_in(key, 110), (HEADS, STREAM_LENGTH), minval=-spread, maxval=spread)
    position_cells = jax.random.randint(jax.random.fold_in(key, 111), (4,), 0, STREAM_LENGTH)
    device_batches = jnp.any(jnp.arange(STREAM_LENGTH)[None, :] == position_cells[:, None], axis=0)
    return (equal_fraction + 3.0 * device_batches[None, :].astype(jnp.float32)).astype(jnp.float32)


def scaled_sample(key, base, column_range):
    column_scale = 10.0 ** (column_range * jnp.arange(INNER, dtype=jnp.float32) / INNER)
    row_scale = 10.0 ** (jax.random.uniform(jax.random.fold_in(key, 121), (STREAM_LENGTH, 1)) - 0.5)
    sample = jnp.clip(jax.random.normal(jax.random.fold_in(key, 123), (STREAM_LENGTH, INNER)), -4.0, 4.0)
    return base * sample * column_scale[None, :] * row_scale


def draw_z_input(key, part):
    column_range = 1.0
    return scaled_sample(jax.random.fold_in(key, 130), 0.4, column_range).astype(jnp.bfloat16)


def draw_grad_out(key, part):
    column_range = 0.5
    return scaled_sample(jax.random.fold_in(key, 140), 0.7, column_range).astype(jnp.bfloat16)


def steps_of(key, shape, pieces, low, top_value):
    def one(dim, shards_of):
        draws = jax.random.uniform(jax.random.fold_in(jax.random.fold_in(key, 6), dim), (shards_of,), jnp.float32, low / len(pieces), top_value / len(pieces))
        return jnp.repeat(jnp.exp(draws), shape[dim] // shards_of).reshape((-1,) + (1,) * (len(shape) - dim - 1))

    gain = one(*pieces[0])
    for cut in pieces[1:]:
        gain = gain * one(*cut)
    return gain


def scatter_about(key, dims, deviation, most, split=(), kind=jnp.bfloat16):
    drawn = jax.random.normal(key, dims, jnp.float32) * deviation
    if len(split) > 0:
        drawn = steps_of(key, dims, split, -0.22, 0.18) * drawn
    return jnp.clip(drawn, min=-most, max=most).astype(kind)


def setup_inputs(seed: int = 0) -> dict:
    splits = jax.random.split(jax.random.key(seed), 12)
    x_input = scatter_about(splits[0], (STREAM_LENGTH, INNER), 1.0, 6.0, ((0, 32), (1, 16)))
    z_input = draw_z_input(jax.random.fold_in(splits[11], 71), 0)
    bc_input = scatter_about(splits[2], (2, STREAM_LENGTH, NSTATE), 0.35, 2.09375, ((1, 32),))
    dt_raw = draw_dt_raw(jax.random.fold_in(splits[11], 71), 0)
    dt_bias = draw_dt_bias(jax.random.fold_in(splits[11], 71), 0)
    a_log = draw_a_log(jax.random.fold_in(splits[11], 71), 0)
    d_skip = jnp.clip(0.5 + 1.0 * jax.random.uniform(splits[6], (HEADS,), jnp.float32) ** steps_of(splits[6], (HEADS,), ((0, 16),), -0.2, 0.2), 0.5, 1.5)
    conv_x = scatter_about(splits[7], (KCONV, INNER), KCONV ** -0.5, 3.0, ((1, 16),), jnp.float32)
    convolution_bc_taps = scatter_about(splits[8], (2, KCONV, NSTATE), KCONV ** -0.5, 3.0, (), jnp.float32)
    rescale_factor = jnp.clip(1.0 + 0.1 * jax.random.normal(splits[9], (INNER,), jnp.float32), 0.5, 1.5)
    grad_out = draw_grad_out(jax.random.fold_in(splits[11], 71), 0)
    return dict(x_input=x_input, z_input=z_input, bc_input=bc_input, dt_raw=dt_raw, dt_bias=dt_bias, a_log=a_log, d_skip=d_skip, conv_x=conv_x, convolution_bc_taps=convolution_bc_taps, rescale_factor=rescale_factor, grad_out=grad_out)


EPS = 1e-05

def silu_grad(value):
    sigma = jax.nn.sigmoid(value)
    return sigma * (1.0 + value * (1.0 - sigma))

def conv_rows(extended, weight_matrix):
    length = extended.shape[-2] - 3
    summed = weight_matrix[..., 0, :][..., None, :] * extended[..., 0:length, :]
    for offset in range(1, 4):
        summed = summed + weight_matrix[..., offset, :][..., None, :] * extended[..., offset:offset + length, :]
    return summed

def conv_back(extended, weight_matrix):
    length = extended.shape[-2] - 3
    summed = weight_matrix[..., 0, :][..., None, :] * extended[..., 3:3 + length, :]
    for offset in range(1, 4):
        summed = summed + weight_matrix[..., offset, :][..., None, :] * extended[..., 3 - offset:3 - offset + length, :]
    return summed

def decay_of(cumul, causal):
    between = cumul[:, None] - cumul[None, :]
    return jnp.where(causal, jnp.exp(jnp.minimum(between, 0.0)), 0.0)

def weighted_rows(trailing_decay, step_size, b_rows):
    return ((trailing_decay * step_size)[:, None] * b_rows.astype(jnp.float32)).astype(jnp.bfloat16)

def head_forward(cumul, step_size, gram_matrix, x_head, state_low, c_rows, skip_gain, causal):
    decay_matrix = decay_of(cumul, causal)
    mixer_low = (gram_matrix * decay_matrix * step_size[None, :]).astype(jnp.bfloat16)
    intra_out = jnp.dot(mixer_low, x_head, preferred_element_type=jnp.float32)
    handed_forward = jnp.dot(c_rows, state_low, preferred_element_type=jnp.float32)
    return intra_out + jnp.exp(cumul)[:, None] * handed_forward + skip_gain * x_head.astype(jnp.float32)

def head_backward(cumul, step_size, gram_matrix, x_head, grad_head, state_low, state_exact, out_low, out_exact, b_rows, c_rows, skip_gain, decay_rate, causal):
    decay_matrix = decay_of(cumul, causal)
    mixer_low = (gram_matrix * decay_matrix * step_size[None, :]).astype(jnp.bfloat16)
    grad_mix = jnp.dot(grad_head, x_head.T, preferred_element_type=jnp.float32)
    decayed_grad = grad_mix * decay_matrix
    weighted_grad = decayed_grad * step_size[None, :]
    gram_grad = weighted_grad * gram_matrix
    lifted = jnp.exp(cumul)
    handed_forward = jnp.dot(c_rows, state_low, preferred_element_type=jnp.float32)
    reached = jnp.dot(x_head, out_low.T, preferred_element_type=jnp.float32)
    trailing_decay = jnp.exp(cumul[-1] - cumul)
    inner_b = lax.optimization_barrier(jnp.sum(b_rows.astype(jnp.float32) * reached, axis=1))
    state_term = trailing_decay * step_size * inner_b
    grad_cumul = lax.optimization_barrier(jnp.sum(gram_grad, axis=1)) - lax.optimization_barrier(jnp.sum(gram_grad, axis=0))
    grad_cumul = grad_cumul + lifted * lax.optimization_barrier(jnp.sum(grad_head.astype(jnp.float32) * handed_forward, axis=1)) - state_term
    end_grad = jnp.sum(state_term) + jnp.exp(cumul[-1]) * jnp.sum(out_exact * state_exact)
    grad_cumul = grad_cumul.at[-1].add(end_grad)
    grad_log = jnp.cumsum(grad_cumul[::-1])[::-1]
    grad_step = lax.optimization_barrier(jnp.sum(decayed_grad * gram_matrix, axis=0)) + trailing_decay * inner_b + decay_rate * grad_log
    weighted_b = weighted_rows(trailing_decay, step_size, b_rows)
    grad_x = jnp.dot(mixer_low.T, grad_head, preferred_element_type=jnp.float32)
    grad_x = grad_x + skip_gain * grad_head.astype(jnp.float32) + jnp.dot(weighted_b, out_low, preferred_element_type=jnp.float32)
    grad_c = lifted[:, None] * jnp.dot(grad_head, state_low.T, preferred_element_type=jnp.float32)
    grad_b = (trailing_decay * step_size)[:, None] * reached
    return (grad_x, grad_step, grad_c, grad_b, weighted_grad)

def block_prep(x_rows, b_rows, step_size, decay_rate):
    length = x_rows.shape[0]
    head_count = step_size.shape[0]
    cumul = jnp.cumsum(decay_rate[:, None] * step_size, axis=1)
    trailing_decay = jnp.exp(cumul[:, -1:] - cumul)
    x_heads = jnp.moveaxis(x_rows.reshape(length, head_count, -1), 1, 0)

    def one_head(head_items):
        weighted_b = weighted_rows(head_items[0], head_items[1], b_rows)
        return jnp.dot(weighted_b.T, head_items[2], preferred_element_type=jnp.float32)
    local_state = lax.map(one_head, (trailing_decay, step_size, x_heads))
    return (cumul, x_heads, local_state)

def block_mix(cumul, step_size, gram_matrix, x_heads, state_low, c_rows, skip_gain, causal):

    def one_head(head_items):
        return head_forward(head_items[0], head_items[1], gram_matrix, head_items[2], head_items[3], c_rows, head_items[4], causal)
    outputs = lax.map(one_head, (cumul, step_size, x_heads, state_low, skip_gain))
    return jnp.moveaxis(outputs, 0, 1).reshape(outputs.shape[1], -1)

def carry_grad(cumul, c_rows, grad_heads):

    def one_head(head_items):
        lifted_c = (jnp.exp(head_items[0])[:, None] * c_rows.astype(jnp.float32)).astype(jnp.bfloat16)
        return jnp.dot(lifted_c.T, head_items[1], preferred_element_type=jnp.float32)
    return lax.map(one_head, (cumul, grad_heads))

def block_back(cumul, step_size, gram_matrix, x_heads, grad_heads, state_exact, out_exact, b_rows, c_rows, skip_gain, decay_rate, causal):
    length = b_rows.shape[0]
    nstate = b_rows.shape[1]
    state_low = state_exact.astype(jnp.bfloat16)
    out_low = out_exact.astype(jnp.bfloat16)

    def one_head(running, head_items):
        cumulative_head, step_head, x_head, grad_head, low_in, exact_in, low_out, exact_out, skip_head, rate_head = head_items
        grad_x, grad_step, grad_c, grad_b, weighted_grad = head_backward(cumulative_head, step_head, gram_matrix, x_head, grad_head, low_in, exact_in, low_out, exact_out, b_rows, c_rows, skip_head, rate_head, causal)
        return ((running[0] + weighted_grad, running[1] + grad_c, running[2] + grad_b), (grad_x, grad_step))
    initial = (jnp.zeros((length, length), jnp.float32), jnp.zeros((length, nstate), jnp.float32), jnp.zeros((length, nstate), jnp.float32))
    (grad_sum, c_sum, b_sum), (grad_xs, grad_steps) = lax.scan(one_head, initial, (cumul, step_size, x_heads, grad_heads, state_low, state_exact, out_low, out_exact, skip_gain, decay_rate))
    grad_c = c_sum + jnp.dot(grad_sum, b_rows.astype(jnp.float32), precision=lax.Precision.HIGHEST)
    grad_b = b_sum + jnp.dot(grad_sum.T, c_rows.astype(jnp.float32), precision=lax.Precision.HIGHEST)
    grad_x = jnp.moveaxis(grad_xs, 0, 1).reshape(length, -1)
    return (grad_x, jnp.stack([grad_b, grad_c]), grad_steps)

def reference(x_input, z_input, bc_input, dt_raw, dt_bias, a_log, d_skip, conv_x, convolution_bc_taps, rescale_factor, grad_out):
    length = TOK_DEV
    channels = x_input.shape[1]
    head_count = dt_raw.shape[0]
    nstate = bc_input.shape[2]
    decay_rate = -jnp.exp(a_log)
    step_all = jax.nn.softplus(dt_raw + dt_bias[:, None])
    input_extended_left = jnp.concatenate([jnp.zeros((3, channels), jnp.bfloat16), x_input], axis=0)
    bc_padded = jnp.concatenate([jnp.zeros((2, 3, nstate), jnp.bfloat16), bc_input], axis=1)
    causal = jnp.tril(jnp.ones((length, length), dtype=bool))

    def prepare(block_index):
        first_row = (block_index * length).astype(jnp.int32)
        x_ext = lax.dynamic_slice_in_dim(input_extended_left, first_row, length + 3, 0)
        bc_ext = lax.dynamic_slice_in_dim(bc_padded, first_row, length + 3, 1)
        step_size = lax.dynamic_slice_in_dim(step_all, first_row, length, 1)
        x_pre = conv_rows(x_ext.astype(jnp.float32), conv_x)
        bc_pre = conv_rows(bc_ext.astype(jnp.float32), convolution_bc_taps)
        x_rows = jax.nn.silu(x_pre).astype(jnp.bfloat16)
        bc_rows = jax.nn.silu(bc_pre).astype(jnp.bfloat16)
        gram_matrix = jnp.dot(bc_rows[1], bc_rows[0].T, preferred_element_type=jnp.float32)
        cumul, x_heads, local_state = block_prep(x_rows, bc_rows[0], step_size, decay_rate)
        return (first_row, x_pre, bc_pre, bc_rows, step_size, gram_matrix, cumul, x_heads, local_state)

    def forward_block(state_exact, block_index):
        first_row, x_pre, bc_pre, bc_rows, step_size, gram_matrix, cumul, x_heads, local_state = prepare(block_index)
        z_rows = lax.dynamic_slice_in_dim(z_input, first_row, length, 0).astype(jnp.float32)
        grad_rows = lax.dynamic_slice_in_dim(grad_out, first_row, length, 0).astype(jnp.float32)
        mixed_out = block_mix(cumul, step_size, gram_matrix, x_heads, state_exact.astype(jnp.bfloat16), bc_rows[1], d_skip, causal)
        gate_value = jax.nn.silu(z_rows)
        gated = mixed_out * gate_value
        inv_rms = lax.rsqrt(lax.optimization_barrier(jnp.sum(gated * gated, axis=1)) / INNER + EPS)
        normed = gated * inv_rms[:, None]
        scaled = grad_rows * rescale_factor
        mean_dot = lax.optimization_barrier(jnp.sum(scaled * normed, axis=1)) / INNER
        grad_gated = inv_rms[:, None] * (scaled - normed * mean_dot[:, None])
        grad_z = (grad_gated * mixed_out * silu_grad(z_rows)).astype(jnp.bfloat16)
        grad_mixed = (grad_gated * gate_value).astype(jnp.bfloat16)
        grad_heads = jnp.moveaxis(grad_mixed.reshape(length, head_count, -1), 1, 0)
        state_grad = carry_grad(cumul, bc_rows[1], grad_heads)
        totals = cumul[:, -1]
        state_next = jnp.exp(totals)[:, None, None] * state_exact + local_state
        return (state_next, (state_exact, state_grad, grad_z, grad_heads))
    zero_state = jnp.zeros((head_count, nstate, HEAD_DIM), jnp.float32)
    block_ids = jnp.arange(N_SEQ, dtype=jnp.int32)
    final_state, (states_in, state_grads, grad_z_blocks, grad_head_blocks) = lax.scan(forward_block, zero_state, block_ids)

    def backward_block(running, block_items):
        out_exact, rim_x, rim_bc = running
        block_index, state_exact, state_grad, grad_heads = block_items
        first_row, x_pre, bc_pre, bc_rows, step_size, gram_matrix, cumul, x_heads, unused_state = prepare(block_index)
        grad_x_rows, grad_bc_rows, grad_steps = block_back(cumul, step_size, gram_matrix, x_heads, grad_heads, state_exact, out_exact, bc_rows[0], bc_rows[1], d_skip, decay_rate, causal)
        grad_x_pre = grad_x_rows * silu_grad(x_pre)
        grad_bc_pre = grad_bc_rows * silu_grad(bc_pre)
        grad_x_block = conv_back(jnp.concatenate([grad_x_pre, rim_x], axis=0), conv_x).astype(jnp.bfloat16)
        grad_bc_block = conv_back(jnp.concatenate([grad_bc_pre, rim_bc], axis=1), convolution_bc_taps).astype(jnp.bfloat16)
        raw_rows = lax.dynamic_slice_in_dim(dt_raw, first_row, length, 1)
        grad_dt_block = grad_steps * jax.nn.sigmoid(raw_rows + dt_bias[:, None])
        totals = cumul[:, -1]
        out_prior = state_grad + jnp.exp(totals)[:, None, None] * out_exact
        return ((out_prior, grad_x_pre[:3], grad_bc_pre[:, :3]), (grad_x_block, grad_bc_block, grad_dt_block))
    initial = (zero_state, jnp.zeros((3, channels), jnp.float32), jnp.zeros((2, 3, nstate), jnp.float32))
    final_back, (input_slope_parts, grad_bc_blocks, grad_dt_blocks) = lax.scan(backward_block, initial, (block_ids, states_in, state_grads, grad_head_blocks), reverse=True)
    grad_x = input_slope_parts.reshape(STREAM_LENGTH, channels)
    grad_z = grad_z_blocks.reshape(STREAM_LENGTH, channels)
    grad_bc = jnp.moveaxis(grad_bc_blocks, 0, 1).reshape(2, STREAM_LENGTH, nstate)
    grad_dt = jnp.moveaxis(grad_dt_blocks, 0, 1).reshape(head_count, STREAM_LENGTH)
    return (grad_x, grad_z, grad_bc, grad_dt)
```

```python
import jax
import jax.numpy as jnp
from jax import lax
from jax.sharding import PartitionSpec as P

INNER = 16384


EPS = 1e-05
HIGH = lax.Precision.HIGHEST


def passed_along(block, axis, distance):
    devices = range(lax.axis_size(axis))
    route = [(i - distance, i) for i in devices if i - distance in devices]
    return lax.ppermute(block, axis, route)


def silu_grad(value):
    sigma = jax.nn.sigmoid(value)
    return sigma * (1.0 + value * (1.0 - sigma))


def conv_rows(extended, weight_matrix):
    length = extended.shape[-2] - 3
    summed = weight_matrix[..., 0, :][..., None, :] * extended[..., 0:length, :]
    for offset in range(1, 4):
        summed = (
            summed
            + weight_matrix[..., offset, :][..., None, :]
            * extended[..., offset : offset + length, :]
        )
    return summed


def conv_back(extended, weight_matrix):
    length = extended.shape[-2] - 3
    summed = weight_matrix[..., 0, :][..., None, :] * extended[..., 3 : 3 + length, :]
    for offset in range(1, 4):
        summed = (
            summed
            + weight_matrix[..., offset, :][..., None, :]
            * extended[..., 3 - offset : 3 - offset + length, :]
        )
    return summed


def to_pieces(state, count):
    heads, nstate, width = state.shape
    rows = nstate // count
    return jnp.moveaxis(state.reshape(heads, count, rows, width), 1, 0)


def from_pieces(pieces):
    count, heads, rows, width = pieces.shape
    return jnp.moveaxis(pieces, 0, 1).reshape(heads, count * rows, width)


def scan_forward(totals, local_state):
    count = lax.axis_size("seq")
    heads, nstate, width = local_state.shape
    pieces = to_pieces(local_state, count)
    rows = pieces.shape[2]
    tot_row = jnp.zeros((count, heads, 1, width), jnp.float32)
    tot_row = tot_row.at[:, :, 0, 0].set(jnp.broadcast_to(totals, (count, heads)))
    sent = jnp.concatenate([pieces, tot_row], axis=2)
    got = lax.all_to_all(sent, "seq", 0, 0, tiled=True)
    block_totals = got[:, :, rows, 0]
    running = jnp.cumsum(block_totals, axis=0)
    before = running - block_totals
    later = jnp.arange(count)[:, None] > jnp.arange(count)[None, :]
    gap = before.T[:, :, None] - running.T[:, None, :]
    weight = jnp.where(later[None], jnp.exp(jnp.minimum(gap, 0.0)), 0.0)
    data = got[:, :, :rows, :].reshape(count, heads, rows * width)
    scanned = jnp.einsum("hkj,jhx->khx", weight, data, precision=HIGH)
    back = lax.all_to_all(scanned.reshape(count, heads, rows, width), "seq", 0, 0, tiled=True)
    return from_pieces(back), weight


def scan_backward(weight, state_grad):
    count = lax.axis_size("seq")
    heads, nstate, width = state_grad.shape
    pieces = to_pieces(state_grad, count)
    rows = pieces.shape[2]
    got = lax.all_to_all(pieces, "seq", 0, 0, tiled=True)
    data = got.reshape(count, heads, rows * width)
    scanned = jnp.einsum("hjk,jhx->khx", weight, data, precision=HIGH)
    back = lax.all_to_all(scanned.reshape(count, heads, rows, width), "seq", 0, 0, tiled=True)
    return from_pieces(back)


def shards(
    x_input,
    z_input,
    bc_input,
    dt_raw,
    dt_bias,
    a_log,
    d_skip,
    conv_x,
    convolution_bc_taps,
    rescale_factor,
    grad_out,
):
    length = x_input.shape[0]
    channels = x_input.shape[1]
    head_count = dt_raw.shape[0]
    width = channels // head_count
    f32 = jnp.float32
    bf16 = jnp.bfloat16
    decay_rate = -jnp.exp(a_log)
    step_size = jax.nn.softplus(dt_raw + dt_bias[:, None])
    causal = jnp.tril(jnp.ones((length, length), dtype=bool))
    rows_prior = passed_along((x_input[length - 3 :], bc_input[:, length - 3 :]), "seq", 1)
    x_ext = jnp.concatenate([rows_prior[0], x_input], axis=0)
    bc_ext = jnp.concatenate([rows_prior[1], bc_input], axis=1)
    x_pre = conv_rows(x_ext.astype(f32), conv_x)
    bc_pre = conv_rows(bc_ext.astype(f32), convolution_bc_taps)
    x_rows = jax.nn.silu(x_pre).astype(bf16)
    bc_rows = jax.nn.silu(bc_pre).astype(bf16)
    b_rows = bc_rows[0]
    c_rows = bc_rows[1]
    gram = jnp.dot(c_rows, b_rows.T, preferred_element_type=f32)
    x_heads = x_rows.reshape(length, head_count, width)

    cumul = jnp.cumsum(decay_rate[:, None] * step_size, axis=1)
    totals = cumul[:, -1]
    trailing = jnp.exp(cumul[:, -1:] - cumul)
    tail_step = trailing * step_size
    weighted_b = (tail_step[:, :, None] * b_rows.astype(f32)[None]).astype(bf16)
    local_state = jnp.einsum("hsn,shp->hnp", weighted_b, x_heads, preferred_element_type=f32)

    state_exact, weight = scan_forward(totals, local_state)
    state_low = state_exact.astype(bf16)

    between = cumul[:, :, None] - cumul[:, None, :]
    decay = jnp.where(causal[None], jnp.exp(jnp.minimum(between, 0.0)), 0.0)
    mixer_low = (gram[None] * decay * step_size[:, None, :]).astype(bf16)
    intra = jnp.einsum("hts,shp->thp", mixer_low, x_heads, preferred_element_type=f32)
    handed = jnp.einsum("tn,hnp->thp", c_rows, state_low, preferred_element_type=f32)
    lifted = jnp.exp(cumul)
    mixed_heads = (
        intra + lifted.T[:, :, None] * handed + d_skip[None, :, None] * x_heads.astype(f32)
    )
    mixed_out = mixed_heads.reshape(length, channels)

    z_rows = z_input.astype(f32)
    gate_value = jax.nn.silu(z_rows)
    gated = mixed_out * gate_value
    scaled = grad_out.astype(f32) * rescale_factor
    sums = lax.psum(
        jnp.stack([jnp.sum(gated * gated, axis=1), jnp.sum(scaled * gated, axis=1)]), "head"
    )
    inv_rms = lax.rsqrt(sums[0] / INNER + EPS)
    normed = gated * inv_rms[:, None]
    mean_dot = inv_rms * sums[1] / INNER
    grad_gated = inv_rms[:, None] * (scaled - normed * mean_dot[:, None])
    grad_z = (grad_gated * mixed_out * silu_grad(z_rows)).astype(bf16)
    grad_mixed = (grad_gated * gate_value).astype(bf16)
    grad_heads = grad_mixed.reshape(length, head_count, width)

    lifted_c = (lifted[:, :, None] * c_rows.astype(f32)[None]).astype(bf16)
    state_grad = jnp.einsum("htn,thp->hnp", lifted_c, grad_heads, preferred_element_type=f32)
    out_exact = scan_backward(weight, state_grad)
    out_low = out_exact.astype(bf16)

    grad_mix = jnp.einsum("thp,shp->hts", grad_heads, x_heads, preferred_element_type=f32)
    decayed = grad_mix * decay
    zterm = decayed * step_size[:, None, :]
    gram_grad = zterm * gram[None]
    reached = jnp.einsum("shp,hnp->hsn", x_heads, out_low, preferred_element_type=f32)
    inner_b = jnp.sum(b_rows.astype(f32)[None] * reached, axis=2)
    state_term = tail_step * inner_b
    grad_cumul = jnp.sum(gram_grad, axis=2) - jnp.sum(gram_grad, axis=1)
    carried_dot = jnp.sum(grad_heads.astype(f32) * handed, axis=2).T
    grad_cumul = grad_cumul + lifted * carried_dot - state_term
    end_grad = jnp.sum(state_term, axis=1) + jnp.exp(totals) * jnp.sum(
        out_exact * state_exact, axis=(1, 2)
    )
    grad_cumul = grad_cumul.at[:, -1].add(end_grad)
    grad_log = jnp.cumsum(grad_cumul[:, ::-1], axis=1)[:, ::-1]
    grad_steps = (
        jnp.sum(decayed * gram[None], axis=1)
        + trailing * inner_b
        + decay_rate[:, None] * grad_log
    )
    grad_x_heads = jnp.einsum("hts,thp->shp", mixer_low, grad_heads, preferred_element_type=f32)
    grad_x_heads = (
        grad_x_heads
        + d_skip[None, :, None] * grad_heads.astype(f32)
        + jnp.einsum("hsn,hnp->shp", weighted_b, out_low, preferred_element_type=f32)
    )
    grad_c_heads = lifted[:, :, None] * jnp.einsum(
        "thp,hnp->htn", grad_heads, state_low, preferred_element_type=f32
    )
    grad_b_heads = tail_step[:, :, None] * reached
    grad_sum = jnp.sum(zterm, axis=0)
    grad_c = jnp.sum(grad_c_heads, axis=0) + jnp.dot(grad_sum, b_rows.astype(f32), precision=HIGH)
    grad_b = jnp.sum(grad_b_heads, axis=0) + jnp.dot(
        grad_sum.T, c_rows.astype(f32), precision=HIGH
    )
    grad_bc_rows = jnp.stack([grad_b, grad_c])
    grad_x_rows = grad_x_heads.reshape(length, channels)

    grad_x_pre = grad_x_rows * silu_grad(x_pre)
    row_share = length // lax.axis_size("head")
    first_row = lax.axis_index("head") * row_share
    grad_bc_all = lax.psum(grad_bc_rows, "head")
    grad_bc_pre = grad_bc_all * silu_grad(bc_pre)
    rows_next = passed_along((grad_x_pre[:3], grad_bc_pre[:, :3]), "seq", -1)
    grad_x = conv_back(jnp.concatenate([grad_x_pre, rows_next[0]], axis=0), conv_x).astype(bf16)
    grad_bc_full = conv_back(
        jnp.concatenate([grad_bc_pre, rows_next[1]], axis=1), convolution_bc_taps
    )
    grad_bc = lax.dynamic_slice_in_dim(grad_bc_full, first_row, row_share, 1).astype(bf16)
    grad_dt = grad_steps * jax.nn.sigmoid(dt_raw + dt_bias[:, None])
    return (grad_x, grad_z, grad_bc, grad_dt)


def solution(mesh):
    return jax.shard_map(
        shards,
        mesh=mesh,
        in_specs=(
            P("seq", "head"),
            P("seq", "head"),
            P(None, "seq", None),
            P("head", "seq"),
            P("head"),
            P("head"),
            P("head"),
            P(None, "head"),
            P(),
            P("head"),
            P("seq", "head"),
        ),
        out_specs=(
            P("seq", "head"),
            P("seq", "head"),
            P(None, ("seq", "head"), None),
            P("head", "seq"),
        ),
        check_vma=False,
    )
```

```python
import jax
import jax.numpy as jnp
from jax import lax
from jax.experimental import pallas as pl
from jax.experimental.pallas import tpu as pltpu
from jax.sharding import PartitionSpec as P
import functools

MESH = pl.DeviceIdType.MESH
AXES = ("seq", "head")


def exchange_kernel(axis, n, in_ref, out_ref, land, send_sem, recv_sem):
    me = lax.axis_index(axis)
    coords = {a: lax.axis_index(a) for a in AXES}

    def dev(k):
        return tuple(k if a == axis else coords[a] for a in AXES)

    barrier = pltpu.get_barrier_semaphore()
    for i in range(1, n):
        pl.semaphore_signal(barrier, inc=1, device_id=dev(lax.rem(me + i, n)), device_id_type=MESH)
    pl.semaphore_wait(barrier, n - 1)
    copies = []
    for i in range(1, n):
        peer = lax.rem(me + i, n)
        copy = pltpu.make_async_remote_copy(
            src_ref=in_ref.at[peer],
            dst_ref=land.at[me],
            send_sem=send_sem.at[i],
            recv_sem=recv_sem.at[i],
            device_id=dev(peer),
            device_id_type=MESH,
        )
        copy.start()
        copies.append(copy)
    land[me] = in_ref[me]
    for i in range(1, n):
        copies[i - 1].wait_send()
        src = lax.rem(me + (n - i), n)
        incoming = pltpu.make_async_remote_copy(
            src_ref=in_ref.at[src],
            dst_ref=land.at[src],
            send_sem=send_sem.at[i],
            recv_sem=recv_sem.at[i],
            device_id=dev(src),
            device_id_type=MESH,
        )
        incoming.wait_recv()
    out_ref[...] = land[...]


def exchange(x, axis, cid):
    n = lax.axis_size(axis)
    return pl.pallas_call(
        functools.partial(exchange_kernel, axis, n),
        out_shape=jax.ShapeDtypeStruct(x.shape, x.dtype),
        in_specs=[pl.BlockSpec(memory_space=pltpu.VMEM)],
        out_specs=pl.BlockSpec(memory_space=pltpu.VMEM),
        scratch_shapes=[
            pltpu.VMEM(x.shape, x.dtype),
            pltpu.SemaphoreType.DMA((n,)),
            pltpu.SemaphoreType.DMA((n,)),
        ],
        compiler_params=pltpu.CompilerParams(collective_id=cid, has_side_effects=True),
    )(x)

INNER = 16384


EPS = 1e-05
HIGH = lax.Precision.HIGHEST


def passed_along(block, axis, distance):
    devices = range(lax.axis_size(axis))
    route = [(i - distance, i) for i in devices if i - distance in devices]
    return lax.ppermute(block, axis, route)


def silu_grad(value):
    sigma = jax.nn.sigmoid(value)
    return sigma * (1.0 + value * (1.0 - sigma))


def conv_rows(extended, weight_matrix):
    length = extended.shape[-2] - 3
    summed = weight_matrix[..., 0, :][..., None, :] * extended[..., 0:length, :]
    for offset in range(1, 4):
        summed = (
            summed
            + weight_matrix[..., offset, :][..., None, :]
            * extended[..., offset : offset + length, :]
        )
    return summed


def conv_back(extended, weight_matrix):
    length = extended.shape[-2] - 3
    summed = weight_matrix[..., 0, :][..., None, :] * extended[..., 3 : 3 + length, :]
    for offset in range(1, 4):
        summed = (
            summed
            + weight_matrix[..., offset, :][..., None, :]
            * extended[..., 3 - offset : 3 - offset + length, :]
        )
    return summed


def to_pieces(state, count):
    heads, nstate, width = state.shape
    rows = nstate // count
    return jnp.moveaxis(state.reshape(heads, count, rows, width), 1, 0)


def from_pieces(pieces):
    count, heads, rows, width = pieces.shape
    return jnp.moveaxis(pieces, 0, 1).reshape(heads, count * rows, width)


def scan_forward(totals, local_state):
    count = lax.axis_size("seq")
    heads, nstate, width = local_state.shape
    rows = nstate // count
    pieces = to_pieces(local_state, count).reshape(count, heads * rows, width)
    tot_row = jnp.zeros((count, 8, width), jnp.float32)
    tot_row = tot_row.at[:, 0, :heads].set(jnp.broadcast_to(totals, (count, heads)))
    sent = jnp.concatenate([pieces, tot_row], axis=1)
    got = exchange(sent, "seq", 0)
    block_totals = got[:, heads * rows, :heads]
    running = jnp.cumsum(block_totals, axis=0)
    before = running - block_totals
    later = jnp.arange(count)[:, None] > jnp.arange(count)[None, :]
    gap = before.T[:, :, None] - running.T[:, None, :]
    weight = jnp.where(later[None], jnp.exp(jnp.minimum(gap, 0.0)), 0.0)
    data = got[:, : heads * rows, :].reshape(count, heads, rows * width)
    scanned = jnp.einsum("hkj,jhx->khx", weight, data, precision=HIGH)
    back = exchange(scanned.reshape(count, heads * rows, width), "seq", 1)
    return from_pieces(back.reshape(count, heads, rows, width)), weight


def scan_backward(weight, state_grad):
    count = lax.axis_size("seq")
    heads, nstate, width = state_grad.shape
    rows = nstate // count
    pieces = to_pieces(state_grad, count).reshape(count, heads * rows, width)
    got = exchange(pieces, "seq", 1)
    data = got.reshape(count, heads, rows * width)
    scanned = jnp.einsum("hjk,jhx->khx", weight, data, precision=HIGH)
    back = exchange(scanned.reshape(count, heads * rows, width), "seq", 1)
    return from_pieces(back.reshape(count, heads, rows, width))


def shards(
    x_input,
    z_input,
    bc_input,
    dt_raw,
    dt_bias,
    a_log,
    d_skip,
    conv_x,
    convolution_bc_taps,
    rescale_factor,
    grad_out,
):
    length = x_input.shape[0]
    channels = x_input.shape[1]
    head_count = dt_raw.shape[0]
    width = channels // head_count
    f32 = jnp.float32
    bf16 = jnp.bfloat16
    decay_rate = -jnp.exp(a_log)
    step_size = jax.nn.softplus(dt_raw + dt_bias[:, None])
    causal = jnp.tril(jnp.ones((length, length), dtype=bool))
    rows_prior = passed_along((x_input[length - 3 :], bc_input[:, length - 3 :]), "seq", 1)
    x_ext = jnp.concatenate([rows_prior[0], x_input], axis=0)
    bc_ext = jnp.concatenate([rows_prior[1], bc_input], axis=1)
    x_pre = conv_rows(x_ext.astype(f32), conv_x)
    bc_pre = conv_rows(bc_ext.astype(f32), convolution_bc_taps)
    x_rows = jax.nn.silu(x_pre).astype(bf16)
    bc_rows = jax.nn.silu(bc_pre).astype(bf16)
    b_rows = bc_rows[0]
    c_rows = bc_rows[1]
    gram = jnp.dot(c_rows, b_rows.T, preferred_element_type=f32)
    x_heads = x_rows.reshape(length, head_count, width)

    cumul = jnp.cumsum(decay_rate[:, None] * step_size, axis=1)
    totals = cumul[:, -1]
    trailing = jnp.exp(cumul[:, -1:] - cumul)
    tail_step = trailing * step_size
    weighted_b = (tail_step[:, :, None] * b_rows.astype(f32)[None]).astype(bf16)
    local_state = jnp.einsum("hsn,shp->hnp", weighted_b, x_heads, preferred_element_type=f32)

    state_exact, weight = scan_forward(totals, local_state)
    state_low = state_exact.astype(bf16)

    between = cumul[:, :, None] - cumul[:, None, :]
    decay = jnp.where(causal[None], jnp.exp(jnp.minimum(between, 0.0)), 0.0)
    mixer_low = (gram[None] * decay * step_size[:, None, :]).astype(bf16)
    intra = jnp.einsum("hts,shp->thp", mixer_low, x_heads, preferred_element_type=f32)
    handed = jnp.einsum("tn,hnp->thp", c_rows, state_low, preferred_element_type=f32)
    lifted = jnp.exp(cumul)
    mixed_heads = (
        intra + lifted.T[:, :, None] * handed + d_skip[None, :, None] * x_heads.astype(f32)
    )
    mixed_out = mixed_heads.reshape(length, channels)

    z_rows = z_input.astype(f32)
    gate_value = jax.nn.silu(z_rows)
    gated = mixed_out * gate_value
    scaled = grad_out.astype(f32) * rescale_factor
    hcount = lax.axis_size("head")
    own_sums = jnp.stack([jnp.sum(gated * gated, axis=1), jnp.sum(scaled * gated, axis=1)])
    own_sums = jnp.concatenate([own_sums, jnp.zeros((6, length), f32)], axis=0)
    sums = jnp.sum(exchange(jnp.broadcast_to(own_sums, (hcount,) + own_sums.shape), "head", 3), axis=0)
    inv_rms = lax.rsqrt(sums[0] / INNER + EPS)
    normed = gated * inv_rms[:, None]
    mean_dot = inv_rms * sums[1] / INNER
    grad_gated = inv_rms[:, None] * (scaled - normed * mean_dot[:, None])
    grad_z = (grad_gated * mixed_out * silu_grad(z_rows)).astype(bf16)
    grad_mixed = (grad_gated * gate_value).astype(bf16)
    grad_heads = grad_mixed.reshape(length, head_count, width)

    lifted_c = (lifted[:, :, None] * c_rows.astype(f32)[None]).astype(bf16)
    state_grad = jnp.einsum("htn,thp->hnp", lifted_c, grad_heads, preferred_element_type=f32)
    out_exact = scan_backward(weight, state_grad)
    out_low = out_exact.astype(bf16)

    grad_mix = jnp.einsum("thp,shp->hts", grad_heads, x_heads, preferred_element_type=f32)
    decayed = grad_mix * decay
    zterm = decayed * step_size[:, None, :]
    gram_grad = zterm * gram[None]
    reached = jnp.einsum("shp,hnp->hsn", x_heads, out_low, preferred_element_type=f32)
    inner_b = jnp.sum(b_rows.astype(f32)[None] * reached, axis=2)
    state_term = tail_step * inner_b
    grad_cumul = jnp.sum(gram_grad, axis=2) - jnp.sum(gram_grad, axis=1)
    carried_dot = jnp.sum(grad_heads.astype(f32) * handed, axis=2).T
    grad_cumul = grad_cumul + lifted * carried_dot - state_term
    end_grad = jnp.sum(state_term, axis=1) + jnp.exp(totals) * jnp.sum(
        out_exact * state_exact, axis=(1, 2)
    )
    grad_cumul = grad_cumul.at[:, -1].add(end_grad)
    grad_log = jnp.cumsum(grad_cumul[:, ::-1], axis=1)[:, ::-1]
    grad_steps = (
        jnp.sum(decayed * gram[None], axis=1)
        + trailing * inner_b
        + decay_rate[:, None] * grad_log
    )
    grad_x_heads = jnp.einsum("hts,thp->shp", mixer_low, grad_heads, preferred_element_type=f32)
    grad_x_heads = (
        grad_x_heads
        + d_skip[None, :, None] * grad_heads.astype(f32)
        + jnp.einsum("hsn,hnp->shp", weighted_b, out_low, preferred_element_type=f32)
    )
    grad_c_heads = lifted[:, :, None] * jnp.einsum(
        "thp,hnp->htn", grad_heads, state_low, preferred_element_type=f32
    )
    grad_b_heads = tail_step[:, :, None] * reached
    grad_sum = jnp.sum(zterm, axis=0)
    grad_c = jnp.sum(grad_c_heads, axis=0) + jnp.dot(grad_sum, b_rows.astype(f32), precision=HIGH)
    grad_b = jnp.sum(grad_b_heads, axis=0) + jnp.dot(
        grad_sum.T, c_rows.astype(f32), precision=HIGH
    )
    grad_bc_rows = jnp.stack([grad_b, grad_c])
    grad_x_rows = grad_x_heads.reshape(length, channels)

    grad_x_pre = grad_x_rows * silu_grad(x_pre)
    hcount = lax.axis_size("head")
    row_share = length // hcount
    first_row = lax.axis_index("head") * row_share
    bc_pieces = jnp.moveaxis(grad_bc_rows.reshape(2, hcount, row_share, -1), 1, 0)
    bc_got = exchange(bc_pieces.reshape(hcount, 2 * row_share, -1), "head", 2)
    grad_bc_mine = jnp.sum(bc_got, axis=0).reshape(2, row_share, -1)
    bc_pre_mine = lax.dynamic_slice_in_dim(bc_pre, first_row, row_share, 1)
    grad_bc_pre = grad_bc_mine * silu_grad(bc_pre_mine)
    total_dev = lax.axis_size("seq") * hcount
    rim_bc = lax.ppermute(
        grad_bc_pre[:, :3], ("seq", "head"), [(i + 1, i) for i in range(total_dev - 1)]
    )
    rim_x = passed_along(grad_x_pre[:3], "seq", -1)
    grad_x = conv_back(jnp.concatenate([grad_x_pre, rim_x], axis=0), conv_x).astype(bf16)
    grad_bc = conv_back(
        jnp.concatenate([grad_bc_pre, rim_bc], axis=1), convolution_bc_taps
    ).astype(bf16)
    grad_dt = grad_steps * jax.nn.sigmoid(dt_raw + dt_bias[:, None])
    return (grad_x, grad_z, grad_bc, grad_dt)


def solution(mesh):
    return jax.shard_map(
        shards,
        mesh=mesh,
        in_specs=(
            P("seq", "head"),
            P("seq", "head"),
            P(None, "seq", None),
            P("head", "seq"),
            P("head"),
            P("head"),
            P("head"),
            P(None, "head"),
            P(),
            P("head"),
            P("seq", "head"),
        ),
        out_specs=(
            P("seq", "head"),
            P("seq", "head"),
            P(None, ("seq", "head"), None),
            P("head", "seq"),
        ),
        check_vma=False,
    )
```

```python
import jax
import jax.numpy as jnp
from jax import lax
from jax.experimental import pallas as pl
from jax.experimental.pallas import tpu as pltpu
from jax.sharding import PartitionSpec as P
import functools

MESH = pl.DeviceIdType.MESH
AXES = ("seq", "head")


def exchange_kernel(axis, n, in_ref, out_ref, land, send_sem, recv_sem):
    me = lax.axis_index(axis)
    coords = {a: lax.axis_index(a) for a in AXES}

    def dev(k):
        return tuple(k if a == axis else coords[a] for a in AXES)

    barrier = pltpu.get_barrier_semaphore()
    for i in range(1, n):
        pl.semaphore_signal(barrier, inc=1, device_id=dev(lax.rem(me + i, n)), device_id_type=MESH)
    pl.semaphore_wait(barrier, n - 1)
    copies = []
    for i in range(1, n):
        peer = lax.rem(me + i, n)
        copy = pltpu.make_async_remote_copy(
            src_ref=in_ref.at[peer],
            dst_ref=land.at[me],
            send_sem=send_sem.at[i],
            recv_sem=recv_sem.at[i],
            device_id=dev(peer),
            device_id_type=MESH,
        )
        copy.start()
        copies.append(copy)
    land[me] = in_ref[me]
    for i in range(1, n):
        copies[i - 1].wait_send()
        src = lax.rem(me + (n - i), n)
        incoming = pltpu.make_async_remote_copy(
            src_ref=in_ref.at[src],
            dst_ref=land.at[src],
            send_sem=send_sem.at[i],
            recv_sem=recv_sem.at[i],
            device_id=dev(src),
            device_id_type=MESH,
        )
        incoming.wait_recv()
    out_ref[...] = land[...]


def exchange(x, axis, cid):
    n = lax.axis_size(axis)
    return pl.pallas_call(
        functools.partial(exchange_kernel, axis, n),
        out_shape=jax.ShapeDtypeStruct(x.shape, x.dtype),
        in_specs=[pl.BlockSpec(memory_space=pltpu.VMEM)],
        out_specs=pl.BlockSpec(memory_space=pltpu.VMEM),
        scratch_shapes=[
            pltpu.VMEM(x.shape, x.dtype),
            pltpu.SemaphoreType.DMA((n,)),
            pltpu.SemaphoreType.DMA((n,)),
        ],
        compiler_params=pltpu.CompilerParams(collective_id=cid, has_side_effects=True),
    )(x)

INNER = 16384


EPS = 1e-05
HIGH = lax.Precision.HIGHEST


def passed_along(block, axis, distance):
    devices = range(lax.axis_size(axis))
    route = [(i - distance, i) for i in devices if i - distance in devices]
    return lax.ppermute(block, axis, route)


def silu_grad(value):
    sigma = jax.nn.sigmoid(value)
    return sigma * (1.0 + value * (1.0 - sigma))


def conv_rows(extended, weight_matrix):
    length = extended.shape[-2] - 3
    summed = weight_matrix[..., 0, :][..., None, :] * extended[..., 0:length, :]
    for offset in range(1, 4):
        summed = (
            summed
            + weight_matrix[..., offset, :][..., None, :]
            * extended[..., offset : offset + length, :]
        )
    return summed


def conv_back(extended, weight_matrix):
    length = extended.shape[-2] - 3
    summed = weight_matrix[..., 0, :][..., None, :] * extended[..., 3 : 3 + length, :]
    for offset in range(1, 4):
        summed = (
            summed
            + weight_matrix[..., offset, :][..., None, :]
            * extended[..., 3 - offset : 3 - offset + length, :]
        )
    return summed


def to_pieces(state, count):
    heads, nstate, width = state.shape
    rows = nstate // count
    return jnp.moveaxis(state.reshape(heads, count, rows, width), 1, 0)


def from_pieces(pieces):
    count, heads, rows, width = pieces.shape
    return jnp.moveaxis(pieces, 0, 1).reshape(heads, count * rows, width)


def scan_forward(totals, local_state):
    count = lax.axis_size("seq")
    heads, nstate, width = local_state.shape
    rows = nstate // count
    pieces = to_pieces(local_state, count).reshape(count, heads * rows, width)
    tot_row = jnp.zeros((count, 8, width), jnp.float32)
    tot_row = tot_row.at[:, 0, :heads].set(jnp.broadcast_to(totals, (count, heads)))
    sent = jnp.concatenate([pieces, tot_row], axis=1)
    got = exchange(sent, "seq", 0)
    block_totals = got[:, heads * rows, :heads]
    running = jnp.cumsum(block_totals, axis=0)
    before = running - block_totals
    later = jnp.arange(count)[:, None] > jnp.arange(count)[None, :]
    gap = before.T[:, :, None] - running.T[:, None, :]
    weight = jnp.where(later[None], jnp.exp(jnp.minimum(gap, 0.0)), 0.0)
    data = got[:, : heads * rows, :].reshape(count, heads, rows * width)
    scanned = jnp.einsum("hkj,jhx->khx", weight, data, precision=HIGH)
    back = exchange(scanned.reshape(count, heads * rows, width), "seq", 1)
    return from_pieces(back.reshape(count, heads, rows, width)), weight


def scan_backward(weight, state_grad):
    count = lax.axis_size("seq")
    heads, nstate, width = state_grad.shape
    rows = nstate // count
    pieces = to_pieces(state_grad, count).reshape(count, heads * rows, width)
    got = exchange(pieces, "seq", 1)
    data = got.reshape(count, heads, rows * width)
    scanned = jnp.einsum("hjk,jhx->khx", weight, data, precision=HIGH)
    back = exchange(scanned.reshape(count, heads * rows, width), "seq", 1)
    return from_pieces(back.reshape(count, heads, rows, width))


def shards(
    x_input,
    z_input,
    bc_input,
    dt_raw,
    dt_bias,
    a_log,
    d_skip,
    conv_x,
    convolution_bc_taps,
    rescale_factor,
    grad_out,
):
    length = x_input.shape[0]
    channels = x_input.shape[1]
    head_count = dt_raw.shape[0]
    width = channels // head_count
    f32 = jnp.float32
    bf16 = jnp.bfloat16
    decay_rate = -jnp.exp(a_log)
    step_size = jax.nn.softplus(dt_raw + dt_bias[:, None])
    causal = jnp.tril(jnp.ones((length, length), dtype=bool))
    nstate = bc_input.shape[2]
    rows_last = jnp.concatenate(
        [x_input[length - 3 :], jnp.moveaxis(bc_input[:, length - 3 :], 0, 1).reshape(3, 2 * nstate)],
        axis=1,
    )
    rows_prior = passed_along(rows_last, "seq", 1)
    x_ext = jnp.concatenate([rows_prior[:, :channels], x_input], axis=0)
    bc_prior = jnp.moveaxis(rows_prior[:, channels:].reshape(3, 2, nstate), 0, 1)
    bc_ext = jnp.concatenate([bc_prior, bc_input], axis=1)
    x_pre = conv_rows(x_ext.astype(f32), conv_x)
    bc_pre = conv_rows(bc_ext.astype(f32), convolution_bc_taps)
    x_rows = jax.nn.silu(x_pre).astype(bf16)
    bc_rows = jax.nn.silu(bc_pre).astype(bf16)
    b_rows = bc_rows[0]
    c_rows = bc_rows[1]
    gram = jnp.dot(c_rows, b_rows.T, preferred_element_type=f32)
    x_heads = x_rows.reshape(length, head_count, width)

    cumul = jnp.cumsum(decay_rate[:, None] * step_size, axis=1)
    totals = cumul[:, -1]
    trailing = jnp.exp(cumul[:, -1:] - cumul)
    tail_step = trailing * step_size
    weighted_b = (tail_step[:, :, None] * b_rows.astype(f32)[None]).astype(bf16)
    local_state = jnp.einsum("hsn,shp->hnp", weighted_b, x_heads, preferred_element_type=f32)

    state_exact, weight = scan_forward(totals, local_state)
    state_low = state_exact.astype(bf16)

    between = cumul[:, :, None] - cumul[:, None, :]
    decay = jnp.where(causal[None], jnp.exp(jnp.minimum(between, 0.0)), 0.0)
    mixer_low = (gram[None] * decay * step_size[:, None, :]).astype(bf16)
    intra = jnp.einsum("hts,shp->thp", mixer_low, x_heads, preferred_element_type=f32)
    handed = jnp.einsum("tn,hnp->thp", c_rows, state_low, preferred_element_type=f32)
    lifted = jnp.exp(cumul)
    mixed_heads = (
        intra + lifted.T[:, :, None] * handed + d_skip[None, :, None] * x_heads.astype(f32)
    )
    mixed_out = mixed_heads.reshape(length, channels)

    z_rows = z_input.astype(f32)
    gate_value = jax.nn.silu(z_rows)
    gated = mixed_out * gate_value
    scaled = grad_out.astype(f32) * rescale_factor
    hcount = lax.axis_size("head")
    own_sums = jnp.stack([jnp.sum(gated * gated, axis=1), jnp.sum(scaled * gated, axis=1)])
    own_sums = jnp.concatenate([own_sums, jnp.zeros((6, length), f32)], axis=0)
    sums = jnp.sum(exchange(jnp.broadcast_to(own_sums, (hcount,) + own_sums.shape), "head", 3), axis=0)
    inv_rms = lax.rsqrt(sums[0] / INNER + EPS)
    normed = gated * inv_rms[:, None]
    mean_dot = inv_rms * sums[1] / INNER
    grad_gated = inv_rms[:, None] * (scaled - normed * mean_dot[:, None])
    grad_z = (grad_gated * mixed_out * silu_grad(z_rows)).astype(bf16)
    grad_mixed = (grad_gated * gate_value).astype(bf16)
    grad_heads = grad_mixed.reshape(length, head_count, width)

    lifted_c = (lifted[:, :, None] * c_rows.astype(f32)[None]).astype(bf16)
    state_grad = jnp.einsum("htn,thp->hnp", lifted_c, grad_heads, preferred_element_type=f32)
    out_exact = scan_backward(weight, state_grad)
    out_low = out_exact.astype(bf16)

    grad_mix = jnp.einsum("thp,shp->hts", grad_heads, x_heads, preferred_element_type=f32)
    decayed = grad_mix * decay
    zterm = decayed * step_size[:, None, :]
    gram_grad = zterm * gram[None]
    reached = jnp.einsum("shp,hnp->hsn", x_heads, out_low, preferred_element_type=f32)
    inner_b = jnp.sum(b_rows.astype(f32)[None] * reached, axis=2)
    state_term = tail_step * inner_b
    grad_cumul = jnp.sum(gram_grad, axis=2) - jnp.sum(gram_grad, axis=1)
    carried_dot = jnp.sum(grad_heads.astype(f32) * handed, axis=2).T
    grad_cumul = grad_cumul + lifted * carried_dot - state_term
    end_grad = jnp.sum(state_term, axis=1) + jnp.exp(totals) * jnp.sum(
        out_exact * state_exact, axis=(1, 2)
    )
    grad_cumul = grad_cumul.at[:, -1].add(end_grad)
    grad_log = jnp.cumsum(grad_cumul[:, ::-1], axis=1)[:, ::-1]
    grad_steps = (
        jnp.sum(decayed * gram[None], axis=1)
        + trailing * inner_b
        + decay_rate[:, None] * grad_log
    )
    grad_x_heads = jnp.einsum("hts,thp->shp", mixer_low, grad_heads, preferred_element_type=f32)
    grad_x_heads = (
        grad_x_heads
        + d_skip[None, :, None] * grad_heads.astype(f32)
        + jnp.einsum("hsn,hnp->shp", weighted_b, out_low, preferred_element_type=f32)
    )
    grad_c_heads = lifted[:, :, None] * jnp.einsum(
        "thp,hnp->htn", grad_heads, state_low, preferred_element_type=f32
    )
    grad_b_heads = tail_step[:, :, None] * reached
    grad_sum = jnp.sum(zterm, axis=0)
    grad_c = jnp.sum(grad_c_heads, axis=0) + jnp.dot(grad_sum, b_rows.astype(f32), precision=HIGH)
    grad_b = jnp.sum(grad_b_heads, axis=0) + jnp.dot(
        grad_sum.T, c_rows.astype(f32), precision=HIGH
    )
    grad_bc_rows = jnp.stack([grad_b, grad_c])
    grad_x_rows = grad_x_heads.reshape(length, channels)

    grad_x_pre = grad_x_rows * silu_grad(x_pre)
    hcount = lax.axis_size("head")
    row_share = length // hcount
    hidx = lax.axis_index("head")
    first_row = hidx * row_share
    picks = []
    for h in range(hcount):
        own = [h * row_share + i for i in range(row_share + 3)]
        own = [r if r < length else 0 for r in own]
        picks.append(own + [0, 1, 2] + [0] * (16 - row_share - 6))
    picks = jnp.array(picks, jnp.int32)
    piece_rows = picks.shape[1]
    bc_pieces = jnp.moveaxis(jnp.take(grad_bc_rows, picks.reshape(-1), axis=1).reshape(2, hcount, piece_rows, -1), 1, 0)
    bc_got = exchange(bc_pieces.reshape(hcount, 2 * piece_rows, -1), "head", 2)
    grad_bc_mine = jnp.sum(bc_got, axis=0).reshape(2, piece_rows, -1)
    bc_pre_pad = jnp.concatenate([bc_pre, jnp.zeros((2, 3, nstate), f32)], axis=1)
    bc_pre_mine = lax.dynamic_slice_in_dim(bc_pre_pad, first_row, row_share + 3, 1)
    grad_bc_pre = grad_bc_mine[:, : row_share + 3] * silu_grad(bc_pre_mine)
    grad_bc_top = grad_bc_mine[:, row_share + 3 : row_share + 6] * silu_grad(bc_pre[:, :3])
    rows_first = jnp.concatenate(
        [grad_x_pre[:3], jnp.moveaxis(grad_bc_top, 0, 1).reshape(3, 2 * nstate)], axis=1
    )
    rows_next = passed_along(rows_first, "seq", -1)
    rim_x = rows_next[:, :channels]
    rim_bc = jnp.moveaxis(rows_next[:, channels:].reshape(3, 2, nstate), 0, 1)
    grad_bc_ext = jnp.where(
        hidx == hcount - 1,
        jnp.concatenate([grad_bc_pre[:, :row_share], rim_bc], axis=1),
        grad_bc_pre,
    )
    grad_x = conv_back(jnp.concatenate([grad_x_pre, rim_x], axis=0), conv_x).astype(bf16)
    grad_bc = conv_back(grad_bc_ext, convolution_bc_taps).astype(bf16)
    grad_dt = grad_steps * jax.nn.sigmoid(dt_raw + dt_bias[:, None])
    return (grad_x, grad_z, grad_bc, grad_dt)


def solution(mesh):
    return jax.shard_map(
        shards,
        mesh=mesh,
        in_specs=(
            P("seq", "head"),
            P("seq", "head"),
            P(None, "seq", None),
            P("head", "seq"),
            P("head"),
            P("head"),
            P("head"),
            P(None, "head"),
            P(),
            P("head"),
            P("seq", "head"),
        ),
        out_specs=(
            P("seq", "head"),
            P("seq", "head"),
            P(None, ("seq", "head"), None),
            P("head", "seq"),
        ),
        check_vma=False,
    )
```

```python
import jax
import jax.numpy as jnp
from jax import lax
from jax.experimental import pallas as pl
from jax.experimental.pallas import tpu as pltpu
from jax.sharding import PartitionSpec as P
import functools

MESH = pl.DeviceIdType.MESH
AXES = ("seq", "head")


def exchange_kernel(axis, n, in_ref, out_ref, land, send_sem, recv_sem):
    me = lax.axis_index(axis)
    coords = {a: lax.axis_index(a) for a in AXES}

    def dev(k):
        return tuple(k if a == axis else coords[a] for a in AXES)

    barrier = pltpu.get_barrier_semaphore()
    for i in range(1, n):
        pl.semaphore_signal(barrier, inc=1, device_id=dev(lax.rem(me + i, n)), device_id_type=MESH)
    pl.semaphore_wait(barrier, n - 1)
    copies = []
    for i in range(1, n):
        peer = lax.rem(me + i, n)
        copy = pltpu.make_async_remote_copy(
            src_ref=in_ref.at[peer],
            dst_ref=land.at[me],
            send_sem=send_sem.at[i],
            recv_sem=recv_sem.at[i],
            device_id=dev(peer),
            device_id_type=MESH,
        )
        copy.start()
        copies.append(copy)
    land[me] = in_ref[me]
    for i in range(1, n):
        copies[i - 1].wait_send()
        src = lax.rem(me + (n - i), n)
        incoming = pltpu.make_async_remote_copy(
            src_ref=in_ref.at[src],
            dst_ref=land.at[src],
            send_sem=send_sem.at[i],
            recv_sem=recv_sem.at[i],
            device_id=dev(src),
            device_id_type=MESH,
        )
        incoming.wait_recv()
    out_ref[...] = land[...]


def exchange(x, axis, cid):
    n = lax.axis_size(axis)
    return pl.pallas_call(
        functools.partial(exchange_kernel, axis, n),
        out_shape=jax.ShapeDtypeStruct(x.shape, x.dtype),
        in_specs=[pl.BlockSpec(memory_space=pltpu.VMEM)],
        out_specs=pl.BlockSpec(memory_space=pltpu.VMEM),
        scratch_shapes=[
            pltpu.VMEM(x.shape, x.dtype),
            pltpu.SemaphoreType.DMA((n,)),
            pltpu.SemaphoreType.DMA((n,)),
        ],
        compiler_params=pltpu.CompilerParams(collective_id=cid, has_side_effects=True),
    )(x)

def _peer_copies(axis, n, src_of, dst, send_sem, recv_sem):
    me = lax.axis_index(axis)
    coords = {a: lax.axis_index(a) for a in AXES}

    def dev(k):
        return tuple(k if a == axis else coords[a] for a in AXES)

    copies = []
    for i in range(1, n):
        peer = lax.rem(me + i, n)
        copy = pltpu.make_async_remote_copy(
            src_ref=src_of(peer),
            dst_ref=dst.at[me],
            send_sem=send_sem.at[i],
            recv_sem=recv_sem.at[i],
            device_id=dev(peer),
            device_id_type=MESH,
        )
        copy.start()
        copies.append(copy)
    return copies


def _peer_waits(axis, n, copies, src_of, dst, send_sem, recv_sem):
    me = lax.axis_index(axis)
    coords = {a: lax.axis_index(a) for a in AXES}

    def dev(k):
        return tuple(k if a == axis else coords[a] for a in AXES)

    for i in range(1, n):
        copies[i - 1].wait_send()
        src = lax.rem(me + (n - i), n)
        incoming = pltpu.make_async_remote_copy(
            src_ref=src_of(src),
            dst_ref=dst.at[src],
            send_sem=send_sem.at[i],
            recv_sem=recv_sem.at[i],
            device_id=dev(src),
            device_id_type=MESH,
        )
        incoming.wait_recv()


def _barrier(axis, n):
    me = lax.axis_index(axis)
    coords = {a: lax.axis_index(a) for a in AXES}
    barrier = pltpu.get_barrier_semaphore()
    for i in range(1, n):
        peer = lax.rem(me + i, n)
        dev = tuple(peer if a == axis else coords[a] for a in AXES)
        pl.semaphore_signal(barrier, inc=1, device_id=dev, device_id_type=MESH)
    pl.semaphore_wait(barrier, n - 1)


def scan_kernel(forward, axis, n, heads, *refs):
    if forward:
        in_ref, out_ref, scale_out, land, res, land2, s1, r1, s2, r2 = refs
    else:
        in_ref, scale_in, out_ref, land, res, land2, s1, r1, s2, r2 = refs
    me = lax.axis_index(axis)
    rows = res.shape[1]
    _barrier(axis, n)
    copies = _peer_copies(axis, n, lambda p: in_ref.at[p], land, s1, r1)
    land[me] = in_ref[me]
    _peer_waits(axis, n, copies, lambda p: in_ref.at[p], land, s1, r1)
    if forward:
        per = rows // heads
        lane = lax.broadcasted_iota(jnp.int32, (rows, 128), 1)
        row = lax.broadcasted_iota(jnp.int32, (rows, 128), 0)
        pick = lane == row // per
        for k in range(n):
            grow = jnp.exp(land[k, rows : rows + 1, :])
            factor = jnp.sum(jnp.where(pick, grow, 0.0), axis=1, keepdims=True)
            scale_out[k] = jnp.broadcast_to(factor, (rows, 128))
        acc = jnp.zeros((rows, 128), jnp.float32)
        for k in range(n):
            res[k] = acc
            acc = scale_out[k] * acc + land[k, :rows, :]
    else:
        acc = jnp.zeros((rows, 128), jnp.float32)
        for k in reversed(range(n)):
            res[k] = acc
            acc = land[k] + scale_in[k] * acc
    copies = _peer_copies(axis, n, lambda p: res.at[p], land2, s2, r2)
    land2[me] = res[me]
    _peer_waits(axis, n, copies, lambda p: res.at[p], land2, s2, r2)
    out_ref[...] = land2[...]


def scan_pieces(x, axis, heads, cid, scales=None):
    n = lax.axis_size(axis)
    forward = scales is None
    rows = x.shape[1] - 8 if forward else x.shape[1]
    piece = (n, rows, 128)
    vm = pl.BlockSpec(memory_space=pltpu.VMEM)
    scratch = [
        pltpu.VMEM(x.shape, jnp.float32),
        pltpu.VMEM(piece, jnp.float32),
        pltpu.VMEM(piece, jnp.float32),
        pltpu.SemaphoreType.DMA((n,)),
        pltpu.SemaphoreType.DMA((n,)),
        pltpu.SemaphoreType.DMA((n,)),
        pltpu.SemaphoreType.DMA((n,)),
    ]
    params = pltpu.CompilerParams(collective_id=cid, has_side_effects=True)
    kern = functools.partial(scan_kernel, forward, axis, n, heads)
    if forward:
        return pl.pallas_call(
            kern,
            out_shape=(jax.ShapeDtypeStruct(piece, jnp.float32), jax.ShapeDtypeStruct(piece, jnp.float32)),
            in_specs=[vm],
            out_specs=(vm, vm),
            scratch_shapes=scratch,
            compiler_params=params,
        )(x)
    return pl.pallas_call(
        kern,
        out_shape=jax.ShapeDtypeStruct(piece, jnp.float32),
        in_specs=[vm, vm],
        out_specs=vm,
        scratch_shapes=scratch,
        compiler_params=params,
    )(x, scales)


INNER = 16384


EPS = 1e-05
HIGH = lax.Precision.HIGHEST


def passed_along(block, axis, distance):
    devices = range(lax.axis_size(axis))
    route = [(i - distance, i) for i in devices if i - distance in devices]
    return lax.ppermute(block, axis, route)


def silu_grad(value):
    sigma = jax.nn.sigmoid(value)
    return sigma * (1.0 + value * (1.0 - sigma))


def conv_rows(extended, weight_matrix):
    length = extended.shape[-2] - 3
    summed = weight_matrix[..., 0, :][..., None, :] * extended[..., 0:length, :]
    for offset in range(1, 4):
        summed = (
            summed
            + weight_matrix[..., offset, :][..., None, :]
            * extended[..., offset : offset + length, :]
        )
    return summed


def conv_back(extended, weight_matrix):
    length = extended.shape[-2] - 3
    summed = weight_matrix[..., 0, :][..., None, :] * extended[..., 3 : 3 + length, :]
    for offset in range(1, 4):
        summed = (
            summed
            + weight_matrix[..., offset, :][..., None, :]
            * extended[..., 3 - offset : 3 - offset + length, :]
        )
    return summed


def to_pieces(state, count):
    heads, nstate, width = state.shape
    rows = nstate // count
    return jnp.moveaxis(state.reshape(heads, count, rows, width), 1, 0)


def from_pieces(pieces):
    count, heads, rows, width = pieces.shape
    return jnp.moveaxis(pieces, 0, 1).reshape(heads, count * rows, width)


def scan_forward(totals, local_state):
    count = lax.axis_size("seq")
    heads, nstate, width = local_state.shape
    rows = nstate // count
    pieces = to_pieces(local_state, count).reshape(count, heads * rows, width)
    tot_row = jnp.zeros((count, 8, width), jnp.float32)
    tot_row = tot_row.at[:, 0, :heads].set(jnp.broadcast_to(totals, (count, heads)))
    sent = jnp.concatenate([pieces, tot_row], axis=1)
    back, scales = scan_pieces(sent, "seq", heads, 0)
    return from_pieces(back.reshape(count, heads, rows, width)), scales


def scan_backward(scales, state_grad):
    count = lax.axis_size("seq")
    heads, nstate, width = state_grad.shape
    rows = nstate // count
    pieces = to_pieces(state_grad, count).reshape(count, heads * rows, width)
    back = scan_pieces(pieces, "seq", heads, 1, scales)
    return from_pieces(back.reshape(count, heads, rows, width))


def shards(
    x_input,
    z_input,
    bc_input,
    dt_raw,
    dt_bias,
    a_log,
    d_skip,
    conv_x,
    convolution_bc_taps,
    rescale_factor,
    grad_out,
):
    length = x_input.shape[0]
    channels = x_input.shape[1]
    head_count = dt_raw.shape[0]
    width = channels // head_count
    f32 = jnp.float32
    bf16 = jnp.bfloat16
    decay_rate = -jnp.exp(a_log)
    step_size = jax.nn.softplus(dt_raw + dt_bias[:, None])
    causal = jnp.tril(jnp.ones((length, length), dtype=bool))
    nstate = bc_input.shape[2]
    rows_last = jnp.concatenate(
        [x_input[length - 3 :], jnp.moveaxis(bc_input[:, length - 3 :], 0, 1).reshape(3, 2 * nstate)],
        axis=1,
    )
    rows_prior = passed_along(rows_last, "seq", 1)
    x_ext = jnp.concatenate([rows_prior[:, :channels], x_input], axis=0)
    bc_prior = jnp.moveaxis(rows_prior[:, channels:].reshape(3, 2, nstate), 0, 1)
    bc_ext = jnp.concatenate([bc_prior, bc_input], axis=1)
    x_pre = conv_rows(x_ext.astype(f32), conv_x)
    bc_pre = conv_rows(bc_ext.astype(f32), convolution_bc_taps)
    x_rows = jax.nn.silu(x_pre).astype(bf16)
    bc_rows = jax.nn.silu(bc_pre).astype(bf16)
    b_rows = bc_rows[0]
    c_rows = bc_rows[1]
    gram = jnp.dot(c_rows, b_rows.T, preferred_element_type=f32)
    x_heads = x_rows.reshape(length, head_count, width)

    cumul = jnp.cumsum(decay_rate[:, None] * step_size, axis=1)
    totals = cumul[:, -1]
    trailing = jnp.exp(cumul[:, -1:] - cumul)
    tail_step = trailing * step_size
    weighted_b = (tail_step[:, :, None] * b_rows.astype(f32)[None]).astype(bf16)
    local_state = jnp.einsum("hsn,shp->hnp", weighted_b, x_heads, preferred_element_type=f32)

    state_exact, weight = scan_forward(totals, local_state)
    state_low = state_exact.astype(bf16)

    between = cumul[:, :, None] - cumul[:, None, :]
    decay = jnp.where(causal[None], jnp.exp(jnp.minimum(between, 0.0)), 0.0)
    mixer_low = (gram[None] * decay * step_size[:, None, :]).astype(bf16)
    intra = jnp.einsum("hts,shp->thp", mixer_low, x_heads, preferred_element_type=f32)
    handed = jnp.einsum("tn,hnp->thp", c_rows, state_low, preferred_element_type=f32)
    lifted = jnp.exp(cumul)
    mixed_heads = (
        intra + lifted.T[:, :, None] * handed + d_skip[None, :, None] * x_heads.astype(f32)
    )
    mixed_out = mixed_heads.reshape(length, channels)

    z_rows = z_input.astype(f32)
    gate_value = jax.nn.silu(z_rows)
    gated = mixed_out * gate_value
    scaled = grad_out.astype(f32) * rescale_factor
    hcount = lax.axis_size("head")
    own_sums = jnp.stack([jnp.sum(gated * gated, axis=1), jnp.sum(scaled * gated, axis=1)])
    own_sums = jnp.concatenate([own_sums, jnp.zeros((6, length), f32)], axis=0)
    sums = jnp.sum(exchange(jnp.broadcast_to(own_sums, (hcount,) + own_sums.shape), "head", 3), axis=0)
    inv_rms = lax.rsqrt(sums[0] / INNER + EPS)
    normed = gated * inv_rms[:, None]
    mean_dot = inv_rms * sums[1] / INNER
    grad_gated = inv_rms[:, None] * (scaled - normed * mean_dot[:, None])
    grad_z = (grad_gated * mixed_out * silu_grad(z_rows)).astype(bf16)
    grad_mixed = (grad_gated * gate_value).astype(bf16)
    grad_heads = grad_mixed.reshape(length, head_count, width)

    lifted_c = (lifted[:, :, None] * c_rows.astype(f32)[None]).astype(bf16)
    state_grad = jnp.einsum("htn,thp->hnp", lifted_c, grad_heads, preferred_element_type=f32)
    out_exact = scan_backward(weight, state_grad)
    out_low = out_exact.astype(bf16)

    grad_mix = jnp.einsum("thp,shp->hts", grad_heads, x_heads, preferred_element_type=f32)
    decayed = grad_mix * decay
    zterm = decayed * step_size[:, None, :]
    gram_grad = zterm * gram[None]
    reached = jnp.einsum("shp,hnp->hsn", x_heads, out_low, preferred_element_type=f32)
    inner_b = jnp.sum(b_rows.astype(f32)[None] * reached, axis=2)
    state_term = tail_step * inner_b
    grad_cumul = jnp.sum(gram_grad, axis=2) - jnp.sum(gram_grad, axis=1)
    carried_dot = jnp.sum(grad_heads.astype(f32) * handed, axis=2).T
    grad_cumul = grad_cumul + lifted * carried_dot - state_term
    end_grad = jnp.sum(state_term, axis=1) + jnp.exp(totals) * jnp.sum(
        out_exact * state_exact, axis=(1, 2)
    )
    grad_cumul = grad_cumul.at[:, -1].add(end_grad)
    grad_log = jnp.cumsum(grad_cumul[:, ::-1], axis=1)[:, ::-1]
    grad_steps = (
        jnp.sum(decayed * gram[None], axis=1)
        + trailing * inner_b
        + decay_rate[:, None] * grad_log
    )
    grad_x_heads = jnp.einsum("hts,thp->shp", mixer_low, grad_heads, preferred_element_type=f32)
    grad_x_heads = (
        grad_x_heads
        + d_skip[None, :, None] * grad_heads.astype(f32)
        + jnp.einsum("hsn,hnp->shp", weighted_b, out_low, preferred_element_type=f32)
    )
    grad_c_heads = lifted[:, :, None] * jnp.einsum(
        "thp,hnp->htn", grad_heads, state_low, preferred_element_type=f32
    )
    grad_b_heads = tail_step[:, :, None] * reached
    grad_sum = jnp.sum(zterm, axis=0)
    grad_c = jnp.sum(grad_c_heads, axis=0) + jnp.dot(grad_sum, b_rows.astype(f32), precision=HIGH)
    grad_b = jnp.sum(grad_b_heads, axis=0) + jnp.dot(
        grad_sum.T, c_rows.astype(f32), precision=HIGH
    )
    grad_bc_rows = jnp.stack([grad_b, grad_c])
    grad_x_rows = grad_x_heads.reshape(length, channels)

    grad_x_pre = grad_x_rows * silu_grad(x_pre)
    hcount = lax.axis_size("head")
    row_share = length // hcount
    hidx = lax.axis_index("head")
    first_row = hidx * row_share
    picks = []
    for h in range(hcount):
        own = [h * row_share + i for i in range(row_share + 3)]
        own = [r if r < length else 0 for r in own]
        picks.append(own + [0, 1, 2] + [0] * (16 - row_share - 6))
    picks = jnp.array(picks, jnp.int32)
    piece_rows = picks.shape[1]
    bc_pieces = jnp.moveaxis(jnp.take(grad_bc_rows, picks.reshape(-1), axis=1).reshape(2, hcount, piece_rows, -1), 1, 0)
    bc_got = exchange(bc_pieces.reshape(hcount, 2 * piece_rows, -1), "head", 2)
    grad_bc_mine = jnp.sum(bc_got, axis=0).reshape(2, piece_rows, -1)
    bc_pre_pad = jnp.concatenate([bc_pre, jnp.zeros((2, 3, nstate), f32)], axis=1)
    bc_pre_mine = lax.dynamic_slice_in_dim(bc_pre_pad, first_row, row_share + 3, 1)
    grad_bc_pre = grad_bc_mine[:, : row_share + 3] * silu_grad(bc_pre_mine)
    grad_bc_top = grad_bc_mine[:, row_share + 3 : row_share + 6] * silu_grad(bc_pre[:, :3])
    rows_first = jnp.concatenate(
        [grad_x_pre[:3], jnp.moveaxis(grad_bc_top, 0, 1).reshape(3, 2 * nstate)], axis=1
    )
    rows_next = passed_along(rows_first, "seq", -1)
    rim_x = rows_next[:, :channels]
    rim_bc = jnp.moveaxis(rows_next[:, channels:].reshape(3, 2, nstate), 0, 1)
    grad_bc_ext = jnp.where(
        hidx == hcount - 1,
        jnp.concatenate([grad_bc_pre[:, :row_share], rim_bc], axis=1),
        grad_bc_pre,
    )
    grad_x = conv_back(jnp.concatenate([grad_x_pre, rim_x], axis=0), conv_x).astype(bf16)
    grad_bc = conv_back(grad_bc_ext, convolution_bc_taps).astype(bf16)
    grad_dt = grad_steps * jax.nn.sigmoid(dt_raw + dt_bias[:, None])
    return (grad_x, grad_z, grad_bc, grad_dt)


def solution(mesh):
    return jax.shard_map(
        shards,
        mesh=mesh,
        in_specs=(
            P("seq", "head"),
            P("seq", "head"),
            P(None, "seq", None),
            P("head", "seq"),
            P("head"),
            P("head"),
            P("head"),
            P(None, "head"),
            P(),
            P("head"),
            P("seq", "head"),
        ),
        out_specs=(
            P("seq", "head"),
            P("seq", "head"),
            P(None, ("seq", "head"), None),
            P("head", "seq"),
        ),
        check_vma=False,
    )
```

```python
import jax
import jax.numpy as jnp
from jax import lax
from jax.experimental import pallas as pl
from jax.experimental.pallas import tpu as pltpu
from jax.sharding import PartitionSpec as P
import functools

MESH = pl.DeviceIdType.MESH
AXES = ("seq", "head")


def exchange_kernel(axis, n, in_ref, out_ref, land, send_sem, recv_sem):
    me = lax.axis_index(axis)
    coords = {a: lax.axis_index(a) for a in AXES}

    def dev(k):
        return tuple(k if a == axis else coords[a] for a in AXES)

    barrier = pltpu.get_barrier_semaphore()
    for i in range(1, n):
        pl.semaphore_signal(barrier, inc=1, device_id=dev(lax.rem(me + i, n)), device_id_type=MESH)
    pl.semaphore_wait(barrier, n - 1)
    copies = []
    for i in range(1, n):
        peer = lax.rem(me + i, n)
        copy = pltpu.make_async_remote_copy(
            src_ref=in_ref.at[peer],
            dst_ref=land.at[me],
            send_sem=send_sem.at[i],
            recv_sem=recv_sem.at[i],
            device_id=dev(peer),
            device_id_type=MESH,
        )
        copy.start()
        copies.append(copy)
    land[me] = in_ref[me]
    for i in range(1, n):
        copies[i - 1].wait_send()
        src = lax.rem(me + (n - i), n)
        incoming = pltpu.make_async_remote_copy(
            src_ref=in_ref.at[src],
            dst_ref=land.at[src],
            send_sem=send_sem.at[i],
            recv_sem=recv_sem.at[i],
            device_id=dev(src),
            device_id_type=MESH,
        )
        incoming.wait_recv()
    out_ref[...] = land[...]


def exchange(x, axis, cid):
    n = lax.axis_size(axis)
    return pl.pallas_call(
        functools.partial(exchange_kernel, axis, n),
        out_shape=jax.ShapeDtypeStruct(x.shape, x.dtype),
        in_specs=[pl.BlockSpec(memory_space=pltpu.VMEM)],
        out_specs=pl.BlockSpec(memory_space=pltpu.VMEM),
        scratch_shapes=[
            pltpu.VMEM(x.shape, x.dtype),
            pltpu.SemaphoreType.DMA((n,)),
            pltpu.SemaphoreType.DMA((n,)),
        ],
        compiler_params=pltpu.CompilerParams(collective_id=cid, has_side_effects=True),
    )(x)

def _peer_copies(axis, n, src_of, dst, send_sem, recv_sem):
    me = lax.axis_index(axis)
    coords = {a: lax.axis_index(a) for a in AXES}

    def dev(k):
        return tuple(k if a == axis else coords[a] for a in AXES)

    copies = []
    for i in range(1, n):
        peer = lax.rem(me + i, n)
        copy = pltpu.make_async_remote_copy(
            src_ref=src_of(peer),
            dst_ref=dst.at[me],
            send_sem=send_sem.at[i],
            recv_sem=recv_sem.at[i],
            device_id=dev(peer),
            device_id_type=MESH,
        )
        copy.start()
        copies.append(copy)
    return copies


def _peer_waits(axis, n, copies, src_of, dst, send_sem, recv_sem):
    me = lax.axis_index(axis)
    coords = {a: lax.axis_index(a) for a in AXES}

    def dev(k):
        return tuple(k if a == axis else coords[a] for a in AXES)

    for i in range(1, n):
        copies[i - 1].wait_send()
        src = lax.rem(me + (n - i), n)
        incoming = pltpu.make_async_remote_copy(
            src_ref=src_of(src),
            dst_ref=dst.at[src],
            send_sem=send_sem.at[i],
            recv_sem=recv_sem.at[i],
            device_id=dev(src),
            device_id_type=MESH,
        )
        incoming.wait_recv()


def _barrier(axis, n):
    me = lax.axis_index(axis)
    coords = {a: lax.axis_index(a) for a in AXES}
    barrier = pltpu.get_barrier_semaphore()
    for i in range(1, n):
        peer = lax.rem(me + i, n)
        dev = tuple(peer if a == axis else coords[a] for a in AXES)
        pl.semaphore_signal(barrier, inc=1, device_id=dev, device_id_type=MESH)
    pl.semaphore_wait(barrier, n - 1)


def scan_kernel(forward, axis, n, heads, *refs):
    if forward:
        in_ref, out_ref, scale_out, land, res, land2, s1, r1, s2, r2 = refs
    else:
        in_ref, scale_in, out_ref, land, res, land2, s1, r1, s2, r2 = refs
    me = lax.axis_index(axis)
    rows = res.shape[1]
    _barrier(axis, n)
    copies = _peer_copies(axis, n, lambda p: in_ref.at[p], land, s1, r1)
    land[me] = in_ref[me]
    _peer_waits(axis, n, copies, lambda p: in_ref.at[p], land, s1, r1)
    if forward:
        per = rows // heads
        lane = lax.broadcasted_iota(jnp.int32, (rows, 128), 1)
        row = lax.broadcasted_iota(jnp.int32, (rows, 128), 0)
        pick = lane == row // per
        for k in range(n):
            parts = land[k, rows : rows + 3, :].astype(jnp.float32)
            grow = jnp.exp(parts[0:1] + parts[1:2] + parts[2:3])
            factor = jnp.sum(jnp.where(pick, grow, 0.0), axis=1, keepdims=True)
            scale_out[k] = jnp.broadcast_to(factor, (rows, 128))
        acc = jnp.zeros((rows, 128), jnp.float32)
        for k in range(n):
            res[k] = acc.astype(res.dtype)
            acc = scale_out[k] * acc + land[k, :rows, :].astype(jnp.float32)
    else:
        acc = jnp.zeros((rows, 128), jnp.float32)
        for k in reversed(range(n)):
            res[k] = acc.astype(res.dtype)
            acc = land[k].astype(jnp.float32) + scale_in[k] * acc
    copies = _peer_copies(axis, n, lambda p: res.at[p], land2, s2, r2)
    land2[me] = res[me]
    _peer_waits(axis, n, copies, lambda p: res.at[p], land2, s2, r2)
    out_ref[...] = land2[...]


def scan_pieces(x, axis, heads, cid, scales=None):
    n = lax.axis_size(axis)
    forward = scales is None
    rows = x.shape[1] - 16 if forward else x.shape[1]
    piece = (n, rows, 128)
    low = x.dtype
    vm = pl.BlockSpec(memory_space=pltpu.VMEM)
    scratch = [
        pltpu.VMEM(x.shape, low),
        pltpu.VMEM(piece, low),
        pltpu.VMEM(piece, low),
        pltpu.SemaphoreType.DMA((n,)),
        pltpu.SemaphoreType.DMA((n,)),
        pltpu.SemaphoreType.DMA((n,)),
        pltpu.SemaphoreType.DMA((n,)),
    ]
    params = pltpu.CompilerParams(collective_id=cid, has_side_effects=True)
    kern = functools.partial(scan_kernel, forward, axis, n, heads)
    if forward:
        return pl.pallas_call(
            kern,
            out_shape=(jax.ShapeDtypeStruct(piece, low), jax.ShapeDtypeStruct(piece, jnp.float32)),
            in_specs=[vm],
            out_specs=(vm, vm),
            scratch_shapes=scratch,
            compiler_params=params,
        )(x)
    return pl.pallas_call(
        kern,
        out_shape=jax.ShapeDtypeStruct(piece, low),
        in_specs=[vm, vm],
        out_specs=vm,
        scratch_shapes=scratch,
        compiler_params=params,
    )(x, scales)


INNER = 16384


EPS = 1e-05
HIGH = lax.Precision.HIGHEST


def passed_along(block, axis, distance):
    devices = range(lax.axis_size(axis))
    route = [(i - distance, i) for i in devices if i - distance in devices]
    return lax.ppermute(block, axis, route)


def silu_grad(value):
    sigma = jax.nn.sigmoid(value)
    return sigma * (1.0 + value * (1.0 - sigma))


def conv_rows(extended, weight_matrix):
    length = extended.shape[-2] - 3
    summed = weight_matrix[..., 0, :][..., None, :] * extended[..., 0:length, :]
    for offset in range(1, 4):
        summed = (
            summed
            + weight_matrix[..., offset, :][..., None, :]
            * extended[..., offset : offset + length, :]
        )
    return summed


def conv_back(extended, weight_matrix):
    length = extended.shape[-2] - 3
    summed = weight_matrix[..., 0, :][..., None, :] * extended[..., 3 : 3 + length, :]
    for offset in range(1, 4):
        summed = (
            summed
            + weight_matrix[..., offset, :][..., None, :]
            * extended[..., 3 - offset : 3 - offset + length, :]
        )
    return summed


def to_pieces(state, count):
    heads, nstate, width = state.shape
    rows = nstate // count
    return jnp.moveaxis(state.reshape(heads, count, rows, width), 1, 0)


def from_pieces(pieces):
    count, heads, rows, width = pieces.shape
    return jnp.moveaxis(pieces, 0, 1).reshape(heads, count * rows, width)


def scan_forward(totals, local_state):
    count = lax.axis_size("seq")
    heads, nstate, width = local_state.shape
    rows = nstate // count
    pieces = to_pieces(local_state, count).reshape(count, heads * rows, width)
    high = lax.reduce_precision(totals, exponent_bits=8, mantissa_bits=7)
    rest = totals - high
    middle = lax.reduce_precision(rest, exponent_bits=8, mantissa_bits=7)
    parts = jnp.stack([high, middle, rest - middle])
    tot_row = jnp.zeros((count, 16, width), jnp.float32)
    tot_row = tot_row.at[:, 0:3, :heads].set(jnp.broadcast_to(parts, (count, 3, heads)))
    sent = jnp.concatenate([pieces, tot_row], axis=1).astype(jnp.bfloat16)
    back, scales = scan_pieces(sent, "seq", heads, 0)
    return from_pieces(back.reshape(count, heads, rows, width)).astype(jnp.float32), scales


def scan_backward(scales, state_grad):
    count = lax.axis_size("seq")
    heads, nstate, width = state_grad.shape
    rows = nstate // count
    pieces = to_pieces(state_grad, count).reshape(count, heads * rows, width).astype(jnp.bfloat16)
    back = scan_pieces(pieces, "seq", heads, 1, scales)
    return from_pieces(back.reshape(count, heads, rows, width)).astype(jnp.float32)


def shards(
    x_input,
    z_input,
    bc_input,
    dt_raw,
    dt_bias,
    a_log,
    d_skip,
    conv_x,
    convolution_bc_taps,
    rescale_factor,
    grad_out,
):
    length = x_input.shape[0]
    channels = x_input.shape[1]
    head_count = dt_raw.shape[0]
    width = channels // head_count
    f32 = jnp.float32
    bf16 = jnp.bfloat16
    decay_rate = -jnp.exp(a_log)
    step_size = jax.nn.softplus(dt_raw + dt_bias[:, None])
    causal = jnp.tril(jnp.ones((length, length), dtype=bool))
    nstate = bc_input.shape[2]
    rows_last = jnp.concatenate(
        [x_input[length - 3 :], jnp.moveaxis(bc_input[:, length - 3 :], 0, 1).reshape(3, 2 * nstate)],
        axis=1,
    )
    rows_prior = passed_along(rows_last, "seq", 1)
    x_ext = jnp.concatenate([rows_prior[:, :channels], x_input], axis=0)
    bc_prior = jnp.moveaxis(rows_prior[:, channels:].reshape(3, 2, nstate), 0, 1)
    bc_ext = jnp.concatenate([bc_prior, bc_input], axis=1)
    x_pre = conv_rows(x_ext.astype(f32), conv_x)
    bc_pre = conv_rows(bc_ext.astype(f32), convolution_bc_taps)
    x_rows = jax.nn.silu(x_pre).astype(bf16)
    bc_rows = jax.nn.silu(bc_pre).astype(bf16)
    b_rows = bc_rows[0]
    c_rows = bc_rows[1]
    gram = jnp.dot(c_rows, b_rows.T, preferred_element_type=f32)
    x_heads = x_rows.reshape(length, head_count, width)

    cumul = jnp.cumsum(decay_rate[:, None] * step_size, axis=1)
    totals = cumul[:, -1]
    trailing = jnp.exp(cumul[:, -1:] - cumul)
    tail_step = trailing * step_size
    weighted_b = (tail_step[:, :, None] * b_rows.astype(f32)[None]).astype(bf16)
    local_state = jnp.einsum("hsn,shp->hnp", weighted_b, x_heads, preferred_element_type=f32)

    state_exact, weight = scan_forward(totals, local_state)
    state_low = state_exact.astype(bf16)

    between = cumul[:, :, None] - cumul[:, None, :]
    decay = jnp.where(causal[None], jnp.exp(jnp.minimum(between, 0.0)), 0.0)
    mixer_low = (gram[None] * decay * step_size[:, None, :]).astype(bf16)
    intra = jnp.einsum("hts,shp->thp", mixer_low, x_heads, preferred_element_type=f32)
    handed = jnp.einsum("tn,hnp->thp", c_rows, state_low, preferred_element_type=f32)
    lifted = jnp.exp(cumul)
    mixed_heads = (
        intra + lifted.T[:, :, None] * handed + d_skip[None, :, None] * x_heads.astype(f32)
    )
    mixed_out = mixed_heads.reshape(length, channels)

    z_rows = z_input.astype(f32)
    gate_value = jax.nn.silu(z_rows)
    gated = mixed_out * gate_value
    scaled = grad_out.astype(f32) * rescale_factor
    hcount = lax.axis_size("head")
    own_sums = jnp.stack([jnp.sum(gated * gated, axis=1), jnp.sum(scaled * gated, axis=1)])
    own_sums = jnp.concatenate([own_sums, jnp.zeros((6, length), f32)], axis=0)
    sums = jnp.sum(exchange(jnp.broadcast_to(own_sums, (hcount,) + own_sums.shape), "head", 3), axis=0)
    inv_rms = lax.rsqrt(sums[0] / INNER + EPS)
    normed = gated * inv_rms[:, None]
    mean_dot = inv_rms * sums[1] / INNER
    grad_gated = inv_rms[:, None] * (scaled - normed * mean_dot[:, None])
    grad_z = (grad_gated * mixed_out * silu_grad(z_rows)).astype(bf16)
    grad_mixed = (grad_gated * gate_value).astype(bf16)
    grad_heads = grad_mixed.reshape(length, head_count, width)

    lifted_c = (lifted[:, :, None] * c_rows.astype(f32)[None]).astype(bf16)
    state_grad = jnp.einsum("htn,thp->hnp", lifted_c, grad_heads, preferred_element_type=f32)
    out_exact = scan_backward(weight, state_grad)
    out_low = out_exact.astype(bf16)

    grad_mix = jnp.einsum("thp,shp->hts", grad_heads, x_heads, preferred_element_type=f32)
    decayed = grad_mix * decay
    zterm = decayed * step_size[:, None, :]
    gram_grad = zterm * gram[None]
    reached = jnp.einsum("shp,hnp->hsn", x_heads, out_low, preferred_element_type=f32)
    inner_b = jnp.sum(b_rows.astype(f32)[None] * reached, axis=2)
    state_term = tail_step * inner_b
    grad_cumul = jnp.sum(gram_grad, axis=2) - jnp.sum(gram_grad, axis=1)
    carried_dot = jnp.sum(grad_heads.astype(f32) * handed, axis=2).T
    grad_cumul = grad_cumul + lifted * carried_dot - state_term
    end_grad = jnp.sum(state_term, axis=1) + jnp.exp(totals) * jnp.sum(
        out_exact * state_exact, axis=(1, 2)
    )
    grad_cumul = grad_cumul.at[:, -1].add(end_grad)
    grad_log = jnp.cumsum(grad_cumul[:, ::-1], axis=1)[:, ::-1]
    grad_steps = (
        jnp.sum(decayed * gram[None], axis=1)
        + trailing * inner_b
        + decay_rate[:, None] * grad_log
    )
    grad_x_heads = jnp.einsum("hts,thp->shp", mixer_low, grad_heads, preferred_element_type=f32)
    grad_x_heads = (
        grad_x_heads
        + d_skip[None, :, None] * grad_heads.astype(f32)
        + jnp.einsum("hsn,hnp->shp", weighted_b, out_low, preferred_element_type=f32)
    )
    grad_c_heads = lifted[:, :, None] * jnp.einsum(
        "thp,hnp->htn", grad_heads, state_low, preferred_element_type=f32
    )
    grad_b_heads = tail_step[:, :, None] * reached
    grad_sum = jnp.sum(zterm, axis=0)
    grad_c = jnp.sum(grad_c_heads, axis=0) + jnp.dot(grad_sum, b_rows.astype(f32), precision=HIGH)
    grad_b = jnp.sum(grad_b_heads, axis=0) + jnp.dot(
        grad_sum.T, c_rows.astype(f32), precision=HIGH
    )
    grad_bc_rows = jnp.stack([grad_b, grad_c])
    grad_x_rows = grad_x_heads.reshape(length, channels)

    grad_x_pre = grad_x_rows * silu_grad(x_pre)
    hcount = lax.axis_size("head")
    row_share = length // hcount
    hidx = lax.axis_index("head")
    first_row = hidx * row_share
    picks = []
    for h in range(hcount):
        own = [h * row_share + i for i in range(row_share + 3)]
        own = [r if r < length else 0 for r in own]
        picks.append(own + [0, 1, 2] + [0] * (16 - row_share - 6))
    picks = jnp.array(picks, jnp.int32)
    piece_rows = picks.shape[1]
    bc_pieces = jnp.moveaxis(jnp.take(grad_bc_rows, picks.reshape(-1), axis=1).reshape(2, hcount, piece_rows, -1), 1, 0)
    bc_got = exchange(bc_pieces.reshape(hcount, 2 * piece_rows, -1), "head", 2)
    grad_bc_mine = jnp.sum(bc_got, axis=0).reshape(2, piece_rows, -1)
    bc_pre_pad = jnp.concatenate([bc_pre, jnp.zeros((2, 3, nstate), f32)], axis=1)
    bc_pre_mine = lax.dynamic_slice_in_dim(bc_pre_pad, first_row, row_share + 3, 1)
    grad_bc_pre = grad_bc_mine[:, : row_share + 3] * silu_grad(bc_pre_mine)
    grad_bc_top = grad_bc_mine[:, row_share + 3 : row_share + 6] * silu_grad(bc_pre[:, :3])
    rows_first = jnp.concatenate(
        [grad_x_pre[:3], jnp.moveaxis(grad_bc_top, 0, 1).reshape(3, 2 * nstate)], axis=1
    )
    rows_next = passed_along(rows_first, "seq", -1)
    rim_x = rows_next[:, :channels]
    rim_bc = jnp.moveaxis(rows_next[:, channels:].reshape(3, 2, nstate), 0, 1)
    grad_bc_ext = jnp.where(
        hidx == hcount - 1,
        jnp.concatenate([grad_bc_pre[:, :row_share], rim_bc], axis=1),
        grad_bc_pre,
    )
    grad_x = conv_back(jnp.concatenate([grad_x_pre, rim_x], axis=0), conv_x).astype(bf16)
    grad_bc = conv_back(grad_bc_ext, convolution_bc_taps).astype(bf16)
    grad_dt = grad_steps * jax.nn.sigmoid(dt_raw + dt_bias[:, None])
    return (grad_x, grad_z, grad_bc, grad_dt)


def solution(mesh):
    return jax.shard_map(
        shards,
        mesh=mesh,
        in_specs=(
            P("seq", "head"),
            P("seq", "head"),
            P(None, "seq", None),
            P("head", "seq"),
            P("head"),
            P("head"),
            P("head"),
            P(None, "head"),
            P(),
            P("head"),
            P("seq", "head"),
        ),
        out_specs=(
            P("seq", "head"),
            P("seq", "head"),
            P(None, ("seq", "head"), None),
            P("head", "seq"),
        ),
        check_vma=False,
    )
```

```python
import jax
import jax.numpy as jnp
from jax import lax
from jax.experimental import pallas as pl
from jax.experimental.pallas import tpu as pltpu
from jax.sharding import PartitionSpec as P
import functools

MESH = pl.DeviceIdType.MESH
AXES = ("seq", "head")


def exchange_kernel(axis, n, in_ref, out_ref, land, send_sem, recv_sem):
    me = lax.axis_index(axis)
    coords = {a: lax.axis_index(a) for a in AXES}

    def dev(k):
        return tuple(k if a == axis else coords[a] for a in AXES)

    barrier = pltpu.get_barrier_semaphore()
    for i in range(1, n):
        pl.semaphore_signal(barrier, inc=1, device_id=dev(lax.rem(me + i, n)), device_id_type=MESH)
    pl.semaphore_wait(barrier, n - 1)
    copies = []
    for i in range(1, n):
        peer = lax.rem(me + i, n)
        copy = pltpu.make_async_remote_copy(
            src_ref=in_ref.at[peer],
            dst_ref=land.at[me],
            send_sem=send_sem.at[i],
            recv_sem=recv_sem.at[i],
            device_id=dev(peer),
            device_id_type=MESH,
        )
        copy.start()
        copies.append(copy)
    land[me] = in_ref[me]
    for i in range(1, n):
        copies[i - 1].wait_send()
        src = lax.rem(me + (n - i), n)
        incoming = pltpu.make_async_remote_copy(
            src_ref=in_ref.at[src],
            dst_ref=land.at[src],
            send_sem=send_sem.at[i],
            recv_sem=recv_sem.at[i],
            device_id=dev(src),
            device_id_type=MESH,
        )
        incoming.wait_recv()
    out_ref[...] = land[...]


def exchange(x, axis, cid):
    n = lax.axis_size(axis)
    return pl.pallas_call(
        functools.partial(exchange_kernel, axis, n),
        out_shape=jax.ShapeDtypeStruct(x.shape, x.dtype),
        in_specs=[pl.BlockSpec(memory_space=pltpu.VMEM)],
        out_specs=pl.BlockSpec(memory_space=pltpu.VMEM),
        scratch_shapes=[
            pltpu.VMEM(x.shape, x.dtype),
            pltpu.SemaphoreType.DMA((n,)),
            pltpu.SemaphoreType.DMA((n,)),
        ],
        compiler_params=pltpu.CompilerParams(collective_id=cid, has_side_effects=True),
    )(x)

def _peer_copies(axis, n, src_of, dst, send_sem, recv_sem):
    me = lax.axis_index(axis)
    coords = {a: lax.axis_index(a) for a in AXES}

    def dev(k):
        return tuple(k if a == axis else coords[a] for a in AXES)

    copies = []
    for i in range(1, n):
        peer = lax.rem(me + i, n)
        copy = pltpu.make_async_remote_copy(
            src_ref=src_of(peer),
            dst_ref=dst.at[me],
            send_sem=send_sem.at[i],
            recv_sem=recv_sem.at[i],
            device_id=dev(peer),
            device_id_type=MESH,
        )
        copy.start()
        copies.append(copy)
    return copies


def _peer_waits(axis, n, copies, src_of, dst, send_sem, recv_sem):
    me = lax.axis_index(axis)
    coords = {a: lax.axis_index(a) for a in AXES}

    def dev(k):
        return tuple(k if a == axis else coords[a] for a in AXES)

    for i in range(1, n):
        copies[i - 1].wait_send()
        src = lax.rem(me + (n - i), n)
        incoming = pltpu.make_async_remote_copy(
            src_ref=src_of(src),
            dst_ref=dst.at[src],
            send_sem=send_sem.at[i],
            recv_sem=recv_sem.at[i],
            device_id=dev(src),
            device_id_type=MESH,
        )
        incoming.wait_recv()


def _barrier(axis, n):
    me = lax.axis_index(axis)
    coords = {a: lax.axis_index(a) for a in AXES}
    barrier = pltpu.get_barrier_semaphore()
    for i in range(1, n):
        peer = lax.rem(me + i, n)
        dev = tuple(peer if a == axis else coords[a] for a in AXES)
        pl.semaphore_signal(barrier, inc=1, device_id=dev, device_id_type=MESH)
    pl.semaphore_wait(barrier, n - 1)


def scan_kernel(forward, axis, n, heads, *refs):
    if forward:
        in_ref, out_ref, scale_out, land, res, land2, s1, r1, s2, r2 = refs
    else:
        in_ref, scale_in, out_ref, land, res, land2, s1, r1, s2, r2 = refs
    me = lax.axis_index(axis)
    rows = res.shape[1]
    _barrier(axis, n)
    copies = _peer_copies(axis, n, lambda p: in_ref.at[p], land, s1, r1)
    land[me] = in_ref[me]
    _peer_waits(axis, n, copies, lambda p: in_ref.at[p], land, s1, r1)
    if forward:
        lane = lax.broadcasted_iota(jnp.int32, (1, 128), 1)
        pick = lane == me // (n // heads)
        for k in range(n):
            parts = land[k, rows : rows + 3, :].astype(jnp.float32)
            grow = jnp.exp(parts[0:1] + parts[1:2] + parts[2:3])
            factor = jnp.sum(jnp.where(pick, grow, 0.0), axis=1, keepdims=True)
            scale_out[k] = jnp.broadcast_to(factor, (rows, 128))
        acc = jnp.zeros((rows, 128), jnp.float32)
        for k in range(n):
            res[k] = acc.astype(res.dtype)
            acc = scale_out[k] * acc + land[k, :rows, :].astype(jnp.float32)
    else:
        acc = jnp.zeros((rows, 128), jnp.float32)
        for k in reversed(range(n)):
            res[k] = acc.astype(res.dtype)
            acc = land[k].astype(jnp.float32) + scale_in[k] * acc
    copies = _peer_copies(axis, n, lambda p: res.at[p], land2, s2, r2)
    land2[me] = res[me]
    _peer_waits(axis, n, copies, lambda p: res.at[p], land2, s2, r2)
    out_ref[...] = land2[...]


def scan_pieces(x, axis, heads, cid, scales=None):
    n = lax.axis_size(axis)
    forward = scales is None
    rows = x.shape[1] - 16 if forward else x.shape[1]
    piece = (n, rows, 128)
    low = x.dtype
    vm = pl.BlockSpec(memory_space=pltpu.VMEM)
    scratch = [
        pltpu.VMEM(x.shape, low),
        pltpu.VMEM(piece, low),
        pltpu.VMEM(piece, low),
        pltpu.SemaphoreType.DMA((n,)),
        pltpu.SemaphoreType.DMA((n,)),
        pltpu.SemaphoreType.DMA((n,)),
        pltpu.SemaphoreType.DMA((n,)),
    ]
    params = pltpu.CompilerParams(collective_id=cid, has_side_effects=True)
    kern = functools.partial(scan_kernel, forward, axis, n, heads)
    if forward:
        return pl.pallas_call(
            kern,
            out_shape=(jax.ShapeDtypeStruct(piece, low), jax.ShapeDtypeStruct(piece, jnp.float32)),
            in_specs=[vm],
            out_specs=(vm, vm),
            scratch_shapes=scratch,
            compiler_params=params,
        )(x)
    return pl.pallas_call(
        kern,
        out_shape=jax.ShapeDtypeStruct(piece, low),
        in_specs=[vm, vm],
        out_specs=vm,
        scratch_shapes=scratch,
        compiler_params=params,
    )(x, scales)


INNER = 16384


EPS = 1e-05
HIGH = lax.Precision.HIGHEST


def passed_along(block, axis, distance):
    devices = range(lax.axis_size(axis))
    route = [(i - distance, i) for i in devices if i - distance in devices]
    return lax.ppermute(block, axis, route)


def silu_grad(value):
    sigma = jax.nn.sigmoid(value)
    return sigma * (1.0 + value * (1.0 - sigma))


def conv_rows(extended, weight_matrix):
    length = extended.shape[-2] - 3
    summed = weight_matrix[..., 0, :][..., None, :] * extended[..., 0:length, :]
    for offset in range(1, 4):
        summed = (
            summed
            + weight_matrix[..., offset, :][..., None, :]
            * extended[..., offset : offset + length, :]
        )
    return summed


def conv_back(extended, weight_matrix):
    length = extended.shape[-2] - 3
    summed = weight_matrix[..., 0, :][..., None, :] * extended[..., 3 : 3 + length, :]
    for offset in range(1, 4):
        summed = (
            summed
            + weight_matrix[..., offset, :][..., None, :]
            * extended[..., 3 - offset : 3 - offset + length, :]
        )
    return summed


def to_pieces(state, count):
    heads, nstate, width = state.shape
    return state.reshape(count, heads * nstate // count, width)


def from_pieces(pieces, heads):
    count, rows, width = pieces.shape
    return pieces.reshape(heads, count * rows // heads, width)


def scan_forward(totals, local_state):
    count = lax.axis_size("seq")
    heads, nstate, width = local_state.shape
    pieces = to_pieces(local_state, count)
    high = lax.reduce_precision(totals, exponent_bits=8, mantissa_bits=7)
    rest = totals - high
    middle = lax.reduce_precision(rest, exponent_bits=8, mantissa_bits=7)
    parts = jnp.stack([high, middle, rest - middle])
    tot_row = jnp.zeros((count, 16, width), jnp.float32)
    tot_row = tot_row.at[:, 0:3, :heads].set(jnp.broadcast_to(parts, (count, 3, heads)))
    sent = jnp.concatenate([pieces, tot_row], axis=1).astype(jnp.bfloat16)
    back, scales = scan_pieces(sent, "seq", heads, 0)
    return from_pieces(back, heads).astype(jnp.float32), scales


def scan_backward(scales, state_grad):
    count = lax.axis_size("seq")
    heads = state_grad.shape[0]
    pieces = to_pieces(state_grad, count).astype(jnp.bfloat16)
    back = scan_pieces(pieces, "seq", heads, 1, scales)
    return from_pieces(back, heads).astype(jnp.float32)


def shards(
    x_input,
    z_input,
    bc_input,
    dt_raw,
    dt_bias,
    a_log,
    d_skip,
    conv_x,
    convolution_bc_taps,
    rescale_factor,
    grad_out,
):
    length = x_input.shape[0]
    channels = x_input.shape[1]
    head_count = dt_raw.shape[0]
    width = channels // head_count
    f32 = jnp.float32
    bf16 = jnp.bfloat16
    decay_rate = -jnp.exp(a_log)
    step_size = jax.nn.softplus(dt_raw + dt_bias[:, None])
    causal = jnp.tril(jnp.ones((length, length), dtype=bool))
    nstate = bc_input.shape[2]
    rows_last = jnp.concatenate(
        [x_input[length - 3 :], jnp.moveaxis(bc_input[:, length - 3 :], 0, 1).reshape(3, 2 * nstate)],
        axis=1,
    )
    rows_prior = passed_along(rows_last, "seq", 1)
    x_ext = jnp.concatenate([rows_prior[:, :channels], x_input], axis=0)
    bc_prior = jnp.moveaxis(rows_prior[:, channels:].reshape(3, 2, nstate), 0, 1)
    bc_ext = jnp.concatenate([bc_prior, bc_input], axis=1)
    x_pre = conv_rows(x_ext.astype(f32), conv_x)
    bc_pre = conv_rows(bc_ext.astype(f32), convolution_bc_taps)
    x_rows = jax.nn.silu(x_pre).astype(bf16)
    bc_rows = jax.nn.silu(bc_pre).astype(bf16)
    b_rows = bc_rows[0]
    c_rows = bc_rows[1]
    gram = jnp.dot(c_rows, b_rows.T, preferred_element_type=f32)
    x_heads = x_rows.reshape(length, head_count, width)

    cumul = jnp.cumsum(decay_rate[:, None] * step_size, axis=1)
    totals = cumul[:, -1]
    trailing = jnp.exp(cumul[:, -1:] - cumul)
    tail_step = trailing * step_size
    weighted_b = (tail_step[:, :, None] * b_rows.astype(f32)[None]).astype(bf16)
    local_state = jnp.einsum("hsn,shp->hnp", weighted_b, x_heads, preferred_element_type=f32)

    state_exact, weight = scan_forward(totals, local_state)
    state_low = state_exact.astype(bf16)

    between = cumul[:, :, None] - cumul[:, None, :]
    decay = jnp.where(causal[None], jnp.exp(jnp.minimum(between, 0.0)), 0.0)
    mixer_low = (gram[None] * decay * step_size[:, None, :]).astype(bf16)
    intra = jnp.einsum("hts,shp->thp", mixer_low, x_heads, preferred_element_type=f32)
    handed = jnp.einsum("tn,hnp->thp", c_rows, state_low, preferred_element_type=f32)
    lifted = jnp.exp(cumul)
    mixed_heads = (
        intra + lifted.T[:, :, None] * handed + d_skip[None, :, None] * x_heads.astype(f32)
    )
    mixed_out = mixed_heads.reshape(length, channels)

    z_rows = z_input.astype(f32)
    gate_value = jax.nn.silu(z_rows)
    gated = mixed_out * gate_value
    scaled = grad_out.astype(f32) * rescale_factor
    hcount = lax.axis_size("head")
    own_sums = jnp.stack([jnp.sum(gated * gated, axis=1), jnp.sum(scaled * gated, axis=1)])
    own_sums = jnp.concatenate([own_sums, jnp.zeros((6, length), f32)], axis=0)
    sums = jnp.sum(exchange(jnp.broadcast_to(own_sums, (hcount,) + own_sums.shape), "head", 3), axis=0)
    inv_rms = lax.rsqrt(sums[0] / INNER + EPS)
    normed = gated * inv_rms[:, None]
    mean_dot = inv_rms * sums[1] / INNER
    grad_gated = inv_rms[:, None] * (scaled - normed * mean_dot[:, None])
    grad_z = (grad_gated * mixed_out * silu_grad(z_rows)).astype(bf16)
    grad_mixed = (grad_gated * gate_value).astype(bf16)
    grad_heads = grad_mixed.reshape(length, head_count, width)

    lifted_c = (lifted[:, :, None] * c_rows.astype(f32)[None]).astype(bf16)
    state_grad = jnp.einsum("htn,thp->hnp", lifted_c, grad_heads, preferred_element_type=f32)
    out_exact = scan_backward(weight, state_grad)
    out_low = out_exact.astype(bf16)

    grad_mix = jnp.einsum("thp,shp->hts", grad_heads, x_heads, preferred_element_type=f32)
    decayed = grad_mix * decay
    zterm = decayed * step_size[:, None, :]
    gram_grad = zterm * gram[None]
    reached = jnp.einsum("shp,hnp->hsn", x_heads, out_low, preferred_element_type=f32)
    inner_b = jnp.sum(b_rows.astype(f32)[None] * reached, axis=2)
    state_term = tail_step * inner_b
    grad_cumul = jnp.sum(gram_grad, axis=2) - jnp.sum(gram_grad, axis=1)
    carried_dot = jnp.sum(grad_heads.astype(f32) * handed, axis=2).T
    grad_cumul = grad_cumul + lifted * carried_dot - state_term
    end_grad = jnp.sum(state_term, axis=1) + jnp.exp(totals) * jnp.sum(
        out_exact * state_exact, axis=(1, 2)
    )
    grad_cumul = grad_cumul.at[:, -1].add(end_grad)
    grad_log = jnp.cumsum(grad_cumul[:, ::-1], axis=1)[:, ::-1]
    grad_steps = (
        jnp.sum(decayed * gram[None], axis=1)
        + trailing * inner_b
        + decay_rate[:, None] * grad_log
    )
    grad_x_heads = jnp.einsum("hts,thp->shp", mixer_low, grad_heads, preferred_element_type=f32)
    grad_x_heads = (
        grad_x_heads
        + d_skip[None, :, None] * grad_heads.astype(f32)
        + jnp.einsum("hsn,hnp->shp", weighted_b, out_low, preferred_element_type=f32)
    )
    grad_c_heads = lifted[:, :, None] * jnp.einsum(
        "thp,hnp->htn", grad_heads, state_low, preferred_element_type=f32
    )
    grad_b_heads = tail_step[:, :, None] * reached
    grad_sum = jnp.sum(zterm, axis=0)
    grad_c = jnp.sum(grad_c_heads, axis=0) + jnp.dot(grad_sum, b_rows.astype(f32), precision=HIGH)
    grad_b = jnp.sum(grad_b_heads, axis=0) + jnp.dot(
        grad_sum.T, c_rows.astype(f32), precision=HIGH
    )
    grad_bc_rows = jnp.stack([grad_b, grad_c])
    grad_x_rows = grad_x_heads.reshape(length, channels)

    grad_x_pre = grad_x_rows * silu_grad(x_pre)
    hcount = lax.axis_size("head")
    row_share = length // hcount
    hidx = lax.axis_index("head")
    first_row = hidx * row_share
    picks = []
    for h in range(hcount):
        own = [h * row_share + i for i in range(row_share + 3)]
        own = [r if r < length else 0 for r in own]
        picks.append(own + [0, 1, 2] + [0] * (16 - row_share - 6))
    picks = jnp.array(picks, jnp.int32)
    piece_rows = picks.shape[1]
    bc_pieces = jnp.moveaxis(jnp.take(grad_bc_rows, picks.reshape(-1), axis=1).reshape(2, hcount, piece_rows, -1), 1, 0)
    bc_got = exchange(bc_pieces.reshape(hcount, 2 * piece_rows, -1), "head", 2)
    grad_bc_mine = jnp.sum(bc_got, axis=0).reshape(2, piece_rows, -1)
    bc_pre_pad = jnp.concatenate([bc_pre, jnp.zeros((2, 3, nstate), f32)], axis=1)
    bc_pre_mine = lax.dynamic_slice_in_dim(bc_pre_pad, first_row, row_share + 3, 1)
    grad_bc_pre = grad_bc_mine[:, : row_share + 3] * silu_grad(bc_pre_mine)
    grad_bc_top = grad_bc_mine[:, row_share + 3 : row_share + 6] * silu_grad(bc_pre[:, :3])
    rows_first = jnp.concatenate(
        [grad_x_pre[:3], jnp.moveaxis(grad_bc_top, 0, 1).reshape(3, 2 * nstate)], axis=1
    )
    rows_next = passed_along(rows_first, "seq", -1)
    rim_x = rows_next[:, :channels]
    rim_bc = jnp.moveaxis(rows_next[:, channels:].reshape(3, 2, nstate), 0, 1)
    grad_bc_ext = jnp.where(
        hidx == hcount - 1,
        jnp.concatenate([grad_bc_pre[:, :row_share], rim_bc], axis=1),
        grad_bc_pre,
    )
    grad_x = conv_back(jnp.concatenate([grad_x_pre, rim_x], axis=0), conv_x).astype(bf16)
    grad_bc = conv_back(grad_bc_ext, convolution_bc_taps).astype(bf16)
    grad_dt = grad_steps * jax.nn.sigmoid(dt_raw + dt_bias[:, None])
    return (grad_x, grad_z, grad_bc, grad_dt)


def solution(mesh):
    return jax.shard_map(
        shards,
        mesh=mesh,
        in_specs=(
            P("seq", "head"),
            P("seq", "head"),
            P(None, "seq", None),
            P("head", "seq"),
            P("head"),
            P("head"),
            P("head"),
            P(None, "head"),
            P(),
            P("head"),
            P("seq", "head"),
        ),
        out_specs=(
            P("seq", "head"),
            P("seq", "head"),
            P(None, ("seq", "head"), None),
            P("head", "seq"),
        ),
        check_vma=False,
    )
```

```python
import jax
import jax.numpy as jnp
from jax import lax
from jax.experimental import pallas as pl
from jax.experimental.pallas import tpu as pltpu
from jax.sharding import PartitionSpec as P
import functools

MESH = pl.DeviceIdType.MESH
AXES = ("seq", "head")


def exchange_kernel(axis, n, in_ref, out_ref, land, send_sem, recv_sem):
    me = lax.axis_index(axis)
    coords = {a: lax.axis_index(a) for a in AXES}

    def dev(k):
        return tuple(k if a == axis else coords[a] for a in AXES)

    barrier = pltpu.get_barrier_semaphore()
    for i in range(1, n):
        pl.semaphore_signal(barrier, inc=1, device_id=dev(lax.rem(me + i, n)), device_id_type=MESH)
    pl.semaphore_wait(barrier, n - 1)
    copies = []
    for i in range(1, n):
        peer = lax.rem(me + i, n)
        copy = pltpu.make_async_remote_copy(
            src_ref=in_ref.at[peer],
            dst_ref=land.at[me],
            send_sem=send_sem.at[i],
            recv_sem=recv_sem.at[i],
            device_id=dev(peer),
            device_id_type=MESH,
        )
        copy.start()
        copies.append(copy)
    land[me] = in_ref[me]
    for i in range(1, n):
        copies[i - 1].wait_send()
        src = lax.rem(me + (n - i), n)
        incoming = pltpu.make_async_remote_copy(
            src_ref=in_ref.at[src],
            dst_ref=land.at[src],
            send_sem=send_sem.at[i],
            recv_sem=recv_sem.at[i],
            device_id=dev(src),
            device_id_type=MESH,
        )
        incoming.wait_recv()
    out_ref[...] = land[...]


def exchange(x, axis, cid):
    n = lax.axis_size(axis)
    return pl.pallas_call(
        functools.partial(exchange_kernel, axis, n),
        out_shape=jax.ShapeDtypeStruct(x.shape, x.dtype),
        in_specs=[pl.BlockSpec(memory_space=pltpu.VMEM)],
        out_specs=pl.BlockSpec(memory_space=pltpu.VMEM),
        scratch_shapes=[
            pltpu.VMEM(x.shape, x.dtype),
            pltpu.SemaphoreType.DMA((n,)),
            pltpu.SemaphoreType.DMA((n,)),
        ],
        compiler_params=pltpu.CompilerParams(collective_id=cid, has_side_effects=True),
    )(x)

def _peer_copies(axis, n, src_of, dst, send_sem, recv_sem):
    me = lax.axis_index(axis)
    coords = {a: lax.axis_index(a) for a in AXES}

    def dev(k):
        return tuple(k if a == axis else coords[a] for a in AXES)

    copies = []
    for i in range(1, n):
        peer = lax.rem(me + i, n)
        copy = pltpu.make_async_remote_copy(
            src_ref=src_of(peer),
            dst_ref=dst.at[me],
            send_sem=send_sem.at[i],
            recv_sem=recv_sem.at[i],
            device_id=dev(peer),
            device_id_type=MESH,
        )
        copy.start()
        copies.append(copy)
    return copies


def _peer_waits(axis, n, copies, src_of, dst, send_sem, recv_sem):
    me = lax.axis_index(axis)
    coords = {a: lax.axis_index(a) for a in AXES}

    def dev(k):
        return tuple(k if a == axis else coords[a] for a in AXES)

    for i in range(1, n):
        copies[i - 1].wait_send()
        src = lax.rem(me + (n - i), n)
        incoming = pltpu.make_async_remote_copy(
            src_ref=src_of(src),
            dst_ref=dst.at[src],
            send_sem=send_sem.at[i],
            recv_sem=recv_sem.at[i],
            device_id=dev(src),
            device_id_type=MESH,
        )
        incoming.wait_recv()


def _barrier(axis, n):
    me = lax.axis_index(axis)
    coords = {a: lax.axis_index(a) for a in AXES}
    barrier = pltpu.get_barrier_semaphore()
    for i in range(1, n):
        peer = lax.rem(me + i, n)
        dev = tuple(peer if a == axis else coords[a] for a in AXES)
        pl.semaphore_signal(barrier, inc=1, device_id=dev, device_id_type=MESH)
    pl.semaphore_wait(barrier, n - 1)


def scan_kernel(forward, axis, n, heads, *refs):
    if forward:
        in_ref, out_ref, scale_out, land, res, land2, s1, r1, s2, r2 = refs
    else:
        in_ref, scale_in, out_ref, land, res, land2, s1, r1, s2, r2 = refs
    me = lax.axis_index(axis)
    rows = res.shape[1]
    _barrier(axis, n)
    copies = _peer_copies(axis, n, lambda p: in_ref.at[p], land, s1, r1)
    land[me] = in_ref[me]
    _peer_waits(axis, n, copies, lambda p: in_ref.at[p], land, s1, r1)
    if forward:
        lane = lax.broadcasted_iota(jnp.int32, (1, 128), 1)
        pick = lane == me // (n // heads)
        for k in range(n):
            parts = land[k, rows : rows + 3, :].astype(jnp.float32)
            grow = jnp.exp(parts[0:1] + parts[1:2] + parts[2:3])
            factor = jnp.sum(jnp.where(pick, grow, 0.0), axis=1, keepdims=True)
            scale_out[k] = jnp.broadcast_to(factor, (rows, 128))
        acc = jnp.zeros((rows, 128), jnp.float32)
        for k in range(n):
            res[k] = acc.astype(res.dtype)
            acc = scale_out[k] * acc + land[k, :rows, :].astype(jnp.float32)
    else:
        acc = jnp.zeros((rows, 128), jnp.float32)
        for k in reversed(range(n)):
            res[k] = acc.astype(res.dtype)
            acc = land[k].astype(jnp.float32) + scale_in[k] * acc
    copies = _peer_copies(axis, n, lambda p: res.at[p], land2, s2, r2)
    land2[me] = res[me]
    _peer_waits(axis, n, copies, lambda p: res.at[p], land2, s2, r2)
    out_ref[...] = land2[...]


def scan_pieces(x, axis, heads, cid, scales=None):
    n = lax.axis_size(axis)
    forward = scales is None
    rows = x.shape[1] - 16 if forward else x.shape[1]
    piece = (n, rows, 128)
    low = x.dtype
    vm = pl.BlockSpec(memory_space=pltpu.VMEM)
    scratch = [
        pltpu.VMEM(x.shape, low),
        pltpu.VMEM(piece, low),
        pltpu.VMEM(piece, low),
        pltpu.SemaphoreType.DMA((n,)),
        pltpu.SemaphoreType.DMA((n,)),
        pltpu.SemaphoreType.DMA((n,)),
        pltpu.SemaphoreType.DMA((n,)),
    ]
    params = pltpu.CompilerParams(collective_id=cid, has_side_effects=True)
    kern = functools.partial(scan_kernel, forward, axis, n, heads)
    if forward:
        return pl.pallas_call(
            kern,
            out_shape=(jax.ShapeDtypeStruct(piece, low), jax.ShapeDtypeStruct(piece, jnp.float32)),
            in_specs=[vm],
            out_specs=(vm, vm),
            scratch_shapes=scratch,
            compiler_params=params,
        )(x)
    return pl.pallas_call(
        kern,
        out_shape=jax.ShapeDtypeStruct(piece, low),
        in_specs=[vm, vm],
        out_specs=vm,
        scratch_shapes=scratch,
        compiler_params=params,
    )(x, scales)


def forward_kernel(n, hn, heads, *refs):
    (in_ref, c_ref, base_ref, lift_ref, gate_ref, scaled_ref,
     out_ref, scale_out, mixed_out, handed_out, sums_out,
     land, res, land2, gath, s1, r1, s2, r2, s3, r3) = refs
    me = lax.axis_index("seq")
    hme = lax.axis_index("head")
    rows = res.shape[1]
    width = 128
    barrier = pltpu.get_barrier_semaphore()
    for i in range(1, n):
        pl.semaphore_signal(barrier, inc=1, device_id=(lax.rem(me + i, n), hme), device_id_type=MESH)
    for i in range(1, hn):
        pl.semaphore_signal(barrier, inc=1, device_id=(me, lax.rem(hme + i, hn)), device_id_type=MESH)
    pl.semaphore_wait(barrier, n - 1 + hn - 1)
    copies = _peer_copies("seq", n, lambda p: in_ref.at[p], land, s1, r1)
    land[me] = in_ref[me]
    _peer_waits("seq", n, copies, lambda p: in_ref.at[p], land, s1, r1)
    lane = lax.broadcasted_iota(jnp.int32, (1, width), 1)
    pick = lane == me // (n // heads)
    for k in range(n):
        parts = land[k, rows : rows + 3, :].astype(jnp.float32)
        grow = jnp.exp(parts[0:1] + parts[1:2] + parts[2:3])
        factor = jnp.sum(jnp.where(pick, grow, 0.0), axis=1, keepdims=True)
        scale_out[k] = jnp.broadcast_to(factor, (rows, width))
    acc = jnp.zeros((rows, width), jnp.float32)
    for k in range(n):
        res[k] = acc.astype(res.dtype)
        acc = scale_out[k] * acc + land[k, :rows, :].astype(jnp.float32)
    copies = _peer_copies("seq", n, lambda p: res.at[p], land2, s2, r2)
    land2[me] = res[me]
    _peer_waits("seq", n, copies, lambda p: res.at[p], land2, s2, r2)
    out_ref[...] = land2[...]
    per = n // heads
    length = c_ref.shape[0]
    sq = jnp.zeros((length, 1), jnp.float32)
    sd = jnp.zeros((length, 1), jnp.float32)
    for h in range(heads):
        state = land2[h * per : (h + 1) * per].reshape(per * rows, width)
        hand = jnp.dot(c_ref[...], state, preferred_element_type=jnp.float32)
        cols = slice(h * width, (h + 1) * width)
        handed_out[:, cols] = hand
        mix = base_ref[:, cols] + lift_ref[:, cols] * hand
        mixed_out[:, cols] = mix
        gated = mix * gate_ref[:, cols]
        sq = sq + jnp.sum(gated * gated, axis=1, keepdims=True)
        sd = sd + jnp.sum(scaled_ref[:, cols] * gated, axis=1, keepdims=True)
    sq_row = jnp.broadcast_to(sq, (length, length)).T[0:8]
    sd_row = jnp.broadcast_to(sd, (length, length)).T[0:8]
    row = lax.broadcasted_iota(jnp.int32, (8, length), 0)
    mine = jnp.where(row == 0, sq_row, jnp.where(row == 1, sd_row, 0.0))
    gath[hme] = mine
    copies = []
    for i in range(1, hn):
        peer = lax.rem(hme + i, hn)
        copy = pltpu.make_async_remote_copy(
            src_ref=gath.at[hme],
            dst_ref=gath.at[hme],
            send_sem=s3.at[i],
            recv_sem=r3.at[i],
            device_id=(me, peer),
            device_id_type=MESH,
        )
        copy.start()
        copies.append(copy)
    for i in range(1, hn):
        copies[i - 1].wait_send()
        src = lax.rem(hme + (hn - i), hn)
        incoming = pltpu.make_async_remote_copy(
            src_ref=gath.at[src],
            dst_ref=gath.at[src],
            send_sem=s3.at[i],
            recv_sem=r3.at[i],
            device_id=(me, src),
            device_id_type=MESH,
        )
        incoming.wait_recv()
    total = gath[0]
    for j in range(1, hn):
        total = total + gath[j]
    sums_out[...] = total


def forward_scan_mix(x, c_rows, base, lift, gate, scaled, heads, cid):
    n = lax.axis_size("seq")
    hn = lax.axis_size("head")
    rows = x.shape[1] - 16
    piece = (n, rows, 128)
    length, channels = base.shape
    vm = pl.BlockSpec(memory_space=pltpu.VMEM)
    f32 = jnp.float32
    return pl.pallas_call(
        functools.partial(forward_kernel, n, hn, heads),
        out_shape=(
            jax.ShapeDtypeStruct(piece, x.dtype),
            jax.ShapeDtypeStruct(piece, f32),
            jax.ShapeDtypeStruct((length, channels), f32),
            jax.ShapeDtypeStruct((length, channels), f32),
            jax.ShapeDtypeStruct((8, length), f32),
        ),
        in_specs=[vm] * 6,
        out_specs=(vm,) * 5,
        scratch_shapes=[
            pltpu.VMEM(x.shape, x.dtype),
            pltpu.VMEM(piece, x.dtype),
            pltpu.VMEM(piece, x.dtype),
            pltpu.VMEM((hn, 8, length), f32),
            pltpu.SemaphoreType.DMA((n,)),
            pltpu.SemaphoreType.DMA((n,)),
            pltpu.SemaphoreType.DMA((n,)),
            pltpu.SemaphoreType.DMA((n,)),
            pltpu.SemaphoreType.DMA((hn,)),
            pltpu.SemaphoreType.DMA((hn,)),
        ],
        compiler_params=pltpu.CompilerParams(collective_id=cid, has_side_effects=True),
    )(x, c_rows, base, lift, gate, scaled)


INNER = 16384


EPS = 1e-05
HIGH = lax.Precision.HIGHEST


def passed_along(block, axis, distance):
    devices = range(lax.axis_size(axis))
    route = [(i - distance, i) for i in devices if i - distance in devices]
    return lax.ppermute(block, axis, route)


def silu_grad(value):
    sigma = jax.nn.sigmoid(value)
    return sigma * (1.0 + value * (1.0 - sigma))


def conv_rows(extended, weight_matrix):
    length = extended.shape[-2] - 3
    summed = weight_matrix[..., 0, :][..., None, :] * extended[..., 0:length, :]
    for offset in range(1, 4):
        summed = (
            summed
            + weight_matrix[..., offset, :][..., None, :]
            * extended[..., offset : offset + length, :]
        )
    return summed


def conv_back(extended, weight_matrix):
    length = extended.shape[-2] - 3
    summed = weight_matrix[..., 0, :][..., None, :] * extended[..., 3 : 3 + length, :]
    for offset in range(1, 4):
        summed = (
            summed
            + weight_matrix[..., offset, :][..., None, :]
            * extended[..., 3 - offset : 3 - offset + length, :]
        )
    return summed


def to_pieces(state, count):
    heads, nstate, width = state.shape
    return state.reshape(count, heads * nstate // count, width)


def from_pieces(pieces, heads):
    count, rows, width = pieces.shape
    return pieces.reshape(heads, count * rows // heads, width)


def scan_forward(totals, local_state, c_rows, base, lift, gate, scaled):
    count = lax.axis_size("seq")
    heads, nstate, width = local_state.shape
    pieces = to_pieces(local_state, count)
    high = lax.reduce_precision(totals, exponent_bits=8, mantissa_bits=7)
    rest = totals - high
    middle = lax.reduce_precision(rest, exponent_bits=8, mantissa_bits=7)
    parts = jnp.stack([high, middle, rest - middle])
    tot_row = jnp.zeros((count, 16, width), jnp.float32)
    tot_row = tot_row.at[:, 0:3, :heads].set(jnp.broadcast_to(parts, (count, 3, heads)))
    sent = jnp.concatenate([pieces, tot_row], axis=1).astype(jnp.bfloat16)
    back, scales, mixed, handed, sums = forward_scan_mix(sent, c_rows, base, lift, gate, scaled, heads, 0)
    return from_pieces(back, heads).astype(jnp.float32), scales, mixed, handed, sums


def scan_backward(scales, state_grad):
    count = lax.axis_size("seq")
    heads = state_grad.shape[0]
    pieces = to_pieces(state_grad, count).astype(jnp.bfloat16)
    back = scan_pieces(pieces, "seq", heads, 1, scales)
    return from_pieces(back, heads).astype(jnp.float32)


def shards(
    x_input,
    z_input,
    bc_input,
    dt_raw,
    dt_bias,
    a_log,
    d_skip,
    conv_x,
    convolution_bc_taps,
    rescale_factor,
    grad_out,
):
    length = x_input.shape[0]
    channels = x_input.shape[1]
    head_count = dt_raw.shape[0]
    width = channels // head_count
    f32 = jnp.float32
    bf16 = jnp.bfloat16
    decay_rate = -jnp.exp(a_log)
    step_size = jax.nn.softplus(dt_raw + dt_bias[:, None])
    causal = jnp.tril(jnp.ones((length, length), dtype=bool))
    nstate = bc_input.shape[2]
    rows_last = jnp.concatenate(
        [x_input[length - 3 :], jnp.moveaxis(bc_input[:, length - 3 :], 0, 1).reshape(3, 2 * nstate)],
        axis=1,
    )
    rows_prior = passed_along(rows_last, "seq", 1)
    x_ext = jnp.concatenate([rows_prior[:, :channels], x_input], axis=0)
    bc_prior = jnp.moveaxis(rows_prior[:, channels:].reshape(3, 2, nstate), 0, 1)
    bc_ext = jnp.concatenate([bc_prior, bc_input], axis=1)
    x_pre = conv_rows(x_ext.astype(f32), conv_x)
    bc_pre = conv_rows(bc_ext.astype(f32), convolution_bc_taps)
    x_rows = jax.nn.silu(x_pre).astype(bf16)
    bc_rows = jax.nn.silu(bc_pre).astype(bf16)
    b_rows = bc_rows[0]
    c_rows = bc_rows[1]
    gram = jnp.dot(c_rows, b_rows.T, preferred_element_type=f32)
    x_heads = x_rows.reshape(length, head_count, width)

    cumul = jnp.cumsum(decay_rate[:, None] * step_size, axis=1)
    totals = cumul[:, -1]
    trailing = jnp.exp(cumul[:, -1:] - cumul)
    tail_step = trailing * step_size
    weighted_b = (tail_step[:, :, None] * b_rows.astype(f32)[None]).astype(bf16)
    local_state = jnp.einsum("hsn,shp->hnp", weighted_b, x_heads, preferred_element_type=f32)

    between = cumul[:, :, None] - cumul[:, None, :]
    decay = jnp.where(causal[None], jnp.exp(jnp.minimum(between, 0.0)), 0.0)
    mixer_low = (gram[None] * decay * step_size[:, None, :]).astype(bf16)
    intra = jnp.einsum("hts,shp->thp", mixer_low, x_heads, preferred_element_type=f32)
    lifted = jnp.exp(cumul)
    base = (intra + d_skip[None, :, None] * x_heads.astype(f32)).reshape(length, channels)
    lift_full = jnp.broadcast_to(lifted.T[:, :, None], (length, head_count, width)).reshape(length, channels)
    z_rows = z_input.astype(f32)
    gate_value = jax.nn.silu(z_rows)
    scaled = grad_out.astype(f32) * rescale_factor

    state_exact, weight, mixed_out, handed_flat, sums = scan_forward(
        totals, local_state, c_rows, base, lift_full, gate_value, scaled
    )
    state_low = state_exact.astype(bf16)
    handed = handed_flat.reshape(length, head_count, width)
    gated = mixed_out * gate_value
    inv_rms = lax.rsqrt(sums[0] / INNER + EPS)
    normed = gated * inv_rms[:, None]
    mean_dot = inv_rms * sums[1] / INNER
    grad_gated = inv_rms[:, None] * (scaled - normed * mean_dot[:, None])
    grad_z = (grad_gated * mixed_out * silu_grad(z_rows)).astype(bf16)
    grad_mixed = (grad_gated * gate_value).astype(bf16)
    grad_heads = grad_mixed.reshape(length, head_count, width)

    lifted_c = (lifted[:, :, None] * c_rows.astype(f32)[None]).astype(bf16)
    state_grad = jnp.einsum("htn,thp->hnp", lifted_c, grad_heads, preferred_element_type=f32)
    out_exact = scan_backward(weight, state_grad)
    out_low = out_exact.astype(bf16)

    grad_mix = jnp.einsum("thp,shp->hts", grad_heads, x_heads, preferred_element_type=f32)
    decayed = grad_mix * decay
    zterm = decayed * step_size[:, None, :]
    gram_grad = zterm * gram[None]
    reached = jnp.einsum("shp,hnp->hsn", x_heads, out_low, preferred_element_type=f32)
    inner_b = jnp.sum(b_rows.astype(f32)[None] * reached, axis=2)
    state_term = tail_step * inner_b
    grad_cumul = jnp.sum(gram_grad, axis=2) - jnp.sum(gram_grad, axis=1)
    carried_dot = jnp.sum(grad_heads.astype(f32) * handed, axis=2).T
    grad_cumul = grad_cumul + lifted * carried_dot - state_term
    end_grad = jnp.sum(state_term, axis=1) + jnp.exp(totals) * jnp.sum(
        out_exact * state_exact, axis=(1, 2)
    )
    grad_cumul = grad_cumul.at[:, -1].add(end_grad)
    grad_log = jnp.cumsum(grad_cumul[:, ::-1], axis=1)[:, ::-1]
    grad_steps = (
        jnp.sum(decayed * gram[None], axis=1)
        + trailing * inner_b
        + decay_rate[:, None] * grad_log
    )
    grad_x_heads = jnp.einsum("hts,thp->shp", mixer_low, grad_heads, preferred_element_type=f32)
    grad_x_heads = (
        grad_x_heads
        + d_skip[None, :, None] * grad_heads.astype(f32)
        + jnp.einsum("hsn,hnp->shp", weighted_b, out_low, preferred_element_type=f32)
    )
    grad_c_heads = lifted[:, :, None] * jnp.einsum(
        "thp,hnp->htn", grad_heads, state_low, preferred_element_type=f32
    )
    grad_b_heads = tail_step[:, :, None] * reached
    grad_sum = jnp.sum(zterm, axis=0)
    grad_c = jnp.sum(grad_c_heads, axis=0) + jnp.dot(grad_sum, b_rows.astype(f32), precision=HIGH)
    grad_b = jnp.sum(grad_b_heads, axis=0) + jnp.dot(
        grad_sum.T, c_rows.astype(f32), precision=HIGH
    )
    grad_bc_rows = jnp.stack([grad_b, grad_c])
    grad_x_rows = grad_x_heads.reshape(length, channels)

    grad_x_pre = grad_x_rows * silu_grad(x_pre)
    hcount = lax.axis_size("head")
    row_share = length // hcount
    hidx = lax.axis_index("head")
    first_row = hidx * row_share
    picks = []
    for h in range(hcount):
        own = [h * row_share + i for i in range(row_share + 3)]
        own = [r if r < length else 0 for r in own]
        picks.append(own + [0, 1, 2] + [0] * (16 - row_share - 6))
    picks = jnp.array(picks, jnp.int32)
    piece_rows = picks.shape[1]
    bc_pieces = jnp.moveaxis(jnp.take(grad_bc_rows, picks.reshape(-1), axis=1).reshape(2, hcount, piece_rows, -1), 1, 0)
    bc_got = exchange(bc_pieces.reshape(hcount, 2 * piece_rows, -1), "head", 2)
    grad_bc_mine = jnp.sum(bc_got, axis=0).reshape(2, piece_rows, -1)
    bc_pre_pad = jnp.concatenate([bc_pre, jnp.zeros((2, 3, nstate), f32)], axis=1)
    bc_pre_mine = lax.dynamic_slice_in_dim(bc_pre_pad, first_row, row_share + 3, 1)
    grad_bc_pre = grad_bc_mine[:, : row_share + 3] * silu_grad(bc_pre_mine)
    grad_bc_top = grad_bc_mine[:, row_share + 3 : row_share + 6] * silu_grad(bc_pre[:, :3])
    rows_first = jnp.concatenate(
        [grad_x_pre[:3], jnp.moveaxis(grad_bc_top, 0, 1).reshape(3, 2 * nstate)], axis=1
    )
    rows_next = passed_along(rows_first, "seq", -1)
    rim_x = rows_next[:, :channels]
    rim_bc = jnp.moveaxis(rows_next[:, channels:].reshape(3, 2, nstate), 0, 1)
    grad_bc_ext = jnp.where(
        hidx == hcount - 1,
        jnp.concatenate([grad_bc_pre[:, :row_share], rim_bc], axis=1),
        grad_bc_pre,
    )
    grad_x = conv_back(jnp.concatenate([grad_x_pre, rim_x], axis=0), conv_x).astype(bf16)
    grad_bc = conv_back(grad_bc_ext, convolution_bc_taps).astype(bf16)
    grad_dt = grad_steps * jax.nn.sigmoid(dt_raw + dt_bias[:, None])
    return (grad_x, grad_z, grad_bc, grad_dt)


def solution(mesh):
    return jax.shard_map(
        shards,
        mesh=mesh,
        in_specs=(
            P("seq", "head"),
            P("seq", "head"),
            P(None, "seq", None),
            P("head", "seq"),
            P("head"),
            P("head"),
            P("head"),
            P(None, "head"),
            P(),
            P("head"),
            P("seq", "head"),
        ),
        out_specs=(
            P("seq", "head"),
            P("seq", "head"),
            P(None, ("seq", "head"), None),
            P("head", "seq"),
        ),
        check_vma=False,
    )
```

```python
import jax
import jax.numpy as jnp
from jax import lax
from jax.experimental import pallas as pl
from jax.experimental.pallas import tpu as pltpu
from jax.sharding import PartitionSpec as P
import functools

MESH = pl.DeviceIdType.MESH
AXES = ("seq", "head")


def exchange_kernel(axis, n, in_ref, out_ref, land, send_sem, recv_sem):
    me = lax.axis_index(axis)
    coords = {a: lax.axis_index(a) for a in AXES}

    def dev(k):
        return tuple(k if a == axis else coords[a] for a in AXES)

    barrier = pltpu.get_barrier_semaphore()
    for i in range(1, n):
        pl.semaphore_signal(barrier, inc=1, device_id=dev(lax.rem(me + i, n)), device_id_type=MESH)
    pl.semaphore_wait(barrier, n - 1)
    copies = []
    for i in range(1, n):
        peer = lax.rem(me + i, n)
        copy = pltpu.make_async_remote_copy(
            src_ref=in_ref.at[peer],
            dst_ref=land.at[me],
            send_sem=send_sem.at[i],
            recv_sem=recv_sem.at[i],
            device_id=dev(peer),
            device_id_type=MESH,
        )
        copy.start()
        copies.append(copy)
    land[me] = in_ref[me]
    for i in range(1, n):
        copies[i - 1].wait_send()
        src = lax.rem(me + (n - i), n)
        incoming = pltpu.make_async_remote_copy(
            src_ref=in_ref.at[src],
            dst_ref=land.at[src],
            send_sem=send_sem.at[i],
            recv_sem=recv_sem.at[i],
            device_id=dev(src),
            device_id_type=MESH,
        )
        incoming.wait_recv()
    out_ref[...] = land[...]


def exchange(x, axis, cid):
    n = lax.axis_size(axis)
    return pl.pallas_call(
        functools.partial(exchange_kernel, axis, n),
        out_shape=jax.ShapeDtypeStruct(x.shape, x.dtype),
        in_specs=[pl.BlockSpec(memory_space=pltpu.VMEM)],
        out_specs=pl.BlockSpec(memory_space=pltpu.VMEM),
        scratch_shapes=[
            pltpu.VMEM(x.shape, x.dtype),
            pltpu.SemaphoreType.DMA((n,)),
            pltpu.SemaphoreType.DMA((n,)),
        ],
        compiler_params=pltpu.CompilerParams(collective_id=cid, has_side_effects=True),
    )(x)

def _peer_copies(axis, n, src_of, dst, send_sem, recv_sem):
    me = lax.axis_index(axis)
    coords = {a: lax.axis_index(a) for a in AXES}

    def dev(k):
        return tuple(k if a == axis else coords[a] for a in AXES)

    copies = []
    for i in range(1, n):
        peer = lax.rem(me + i, n)
        copy = pltpu.make_async_remote_copy(
            src_ref=src_of(peer),
            dst_ref=dst.at[me],
            send_sem=send_sem.at[i],
            recv_sem=recv_sem.at[i],
            device_id=dev(peer),
            device_id_type=MESH,
        )
        copy.start()
        copies.append(copy)
    return copies


def _peer_waits(axis, n, copies, src_of, dst, send_sem, recv_sem):
    me = lax.axis_index(axis)
    coords = {a: lax.axis_index(a) for a in AXES}

    def dev(k):
        return tuple(k if a == axis else coords[a] for a in AXES)

    for i in range(1, n):
        copies[i - 1].wait_send()
        src = lax.rem(me + (n - i), n)
        incoming = pltpu.make_async_remote_copy(
            src_ref=src_of(src),
            dst_ref=dst.at[src],
            send_sem=send_sem.at[i],
            recv_sem=recv_sem.at[i],
            device_id=dev(src),
            device_id_type=MESH,
        )
        incoming.wait_recv()


def _barrier(axis, n):
    me = lax.axis_index(axis)
    coords = {a: lax.axis_index(a) for a in AXES}
    barrier = pltpu.get_barrier_semaphore()
    for i in range(1, n):
        peer = lax.rem(me + i, n)
        dev = tuple(peer if a == axis else coords[a] for a in AXES)
        pl.semaphore_signal(barrier, inc=1, device_id=dev, device_id_type=MESH)
    pl.semaphore_wait(barrier, n - 1)


def scan_kernel(forward, axis, n, heads, *refs):
    if forward:
        in_ref, out_ref, scale_out, land, res, land2, s1, r1, s2, r2 = refs
    else:
        in_ref, scale_in, out_ref, land, res, land2, s1, r1, s2, r2 = refs
    me = lax.axis_index(axis)
    rows = res.shape[1]
    _barrier(axis, n)
    copies = _peer_copies(axis, n, lambda p: in_ref.at[p], land, s1, r1)
    land[me] = in_ref[me]
    _peer_waits(axis, n, copies, lambda p: in_ref.at[p], land, s1, r1)
    if forward:
        lane = lax.broadcasted_iota(jnp.int32, (1, 128), 1)
        pick = lane == me // (n // heads)
        for k in range(n):
            parts = land[k, rows : rows + 3, :].astype(jnp.float32)
            grow = jnp.exp(parts[0:1] + parts[1:2] + parts[2:3])
            factor = jnp.sum(jnp.where(pick, grow, 0.0), axis=1, keepdims=True)
            scale_out[k] = jnp.broadcast_to(factor, (rows, 128))
        acc = jnp.zeros((rows, 128), jnp.float32)
        for k in range(n):
            res[k] = acc.astype(res.dtype)
            acc = scale_out[k] * acc + land[k, :rows, :].astype(jnp.float32)
    else:
        acc = jnp.zeros((rows, 128), jnp.float32)
        for k in reversed(range(n)):
            res[k] = acc.astype(res.dtype)
            acc = land[k].astype(jnp.float32) + scale_in[k] * acc
    copies = _peer_copies(axis, n, lambda p: res.at[p], land2, s2, r2)
    land2[me] = res[me]
    _peer_waits(axis, n, copies, lambda p: res.at[p], land2, s2, r2)
    out_ref[...] = land2[...]


def scan_pieces(x, axis, heads, cid, scales=None):
    n = lax.axis_size(axis)
    forward = scales is None
    rows = x.shape[1] - 16 if forward else x.shape[1]
    piece = (n, rows, 128)
    low = x.dtype
    vm = pl.BlockSpec(memory_space=pltpu.VMEM)
    scratch = [
        pltpu.VMEM(x.shape, low),
        pltpu.VMEM(piece, low),
        pltpu.VMEM(piece, low),
        pltpu.SemaphoreType.DMA((n,)),
        pltpu.SemaphoreType.DMA((n,)),
        pltpu.SemaphoreType.DMA((n,)),
        pltpu.SemaphoreType.DMA((n,)),
    ]
    params = pltpu.CompilerParams(collective_id=cid, has_side_effects=True)
    kern = functools.partial(scan_kernel, forward, axis, n, heads)
    if forward:
        return pl.pallas_call(
            kern,
            out_shape=(jax.ShapeDtypeStruct(piece, low), jax.ShapeDtypeStruct(piece, jnp.float32)),
            in_specs=[vm],
            out_specs=(vm, vm),
            scratch_shapes=scratch,
            compiler_params=params,
        )(x)
    return pl.pallas_call(
        kern,
        out_shape=jax.ShapeDtypeStruct(piece, low),
        in_specs=[vm, vm],
        out_specs=vm,
        scratch_shapes=scratch,
        compiler_params=params,
    )(x, scales)


def tail_kernel(n, hn, in_ref, rim_ref, out_ref, rim_out, land, send, rim_land, s1, r1, s2, r2):
    me = lax.axis_index("seq")
    hme = lax.axis_index("head")
    prev = lax.rem(me + n - 1, n)
    nxt = lax.rem(me + 1, n)
    barrier = pltpu.get_barrier_semaphore()
    for i in range(1, hn):
        pl.semaphore_signal(barrier, inc=1, device_id=(me, lax.rem(hme + i, hn)), device_id_type=MESH)
    pl.semaphore_signal(barrier, inc=1, device_id=(prev, hme), device_id_type=MESH)
    pl.semaphore_signal(barrier, inc=1, device_id=(nxt, hme), device_id_type=MESH)
    pl.semaphore_wait(barrier, hn + 1)
    rim_copy = pltpu.make_async_remote_copy(
        src_ref=rim_ref, dst_ref=rim_land, send_sem=s2.at[0], recv_sem=r2.at[0],
        device_id=(prev, hme), device_id_type=MESH,
    )
    rim_copy.start()
    send[...] = in_ref[...]
    rim_copy.wait_send()
    rim_copy.wait_recv()
    keep = (1 - me // (n - 1)).astype(jnp.float32)
    rows = in_ref.shape[1] // 2
    nst = in_ref.shape[2]
    width = rim_ref.shape[1] - nst
    rim_bc = rim_land[0:8, width:] * keep
    last = hn - 1
    send[last, 8:11, :] = send[last, 8:11, :] + rim_bc[0:3]
    send[last, rows + 8 : rows + 11, :] = send[last, rows + 8 : rows + 11, :] + rim_bc[3:6]
    rim_out[...] = rim_land[0:8, 0:width] * keep
    src_of = lambda p: send.at[p]
    copies = []
    for i in range(1, hn):
        peer = lax.rem(hme + i, hn)
        copy = pltpu.make_async_remote_copy(
            src_ref=send.at[peer], dst_ref=land.at[hme], send_sem=s1.at[i], recv_sem=r1.at[i],
            device_id=(me, peer), device_id_type=MESH,
        )
        copy.start()
        copies.append(copy)
    land[hme] = send[hme]
    for i in range(1, hn):
        copies[i - 1].wait_send()
        src = lax.rem(hme + (hn - i), hn)
        incoming = pltpu.make_async_remote_copy(
            src_ref=send.at[src], dst_ref=land.at[src], send_sem=s1.at[i], recv_sem=r1.at[i],
            device_id=(me, src), device_id_type=MESH,
        )
        incoming.wait_recv()
    total = land[0]
    for j in range(1, hn):
        total = total + land[j]
    out_ref[...] = total


def tail_exchange(pieces, rim, cid):
    n = lax.axis_size("seq")
    hn = lax.axis_size("head")
    vm = pl.BlockSpec(memory_space=pltpu.VMEM)
    width = rim.shape[1] - pieces.shape[2]
    return pl.pallas_call(
        functools.partial(tail_kernel, n, hn),
        out_shape=(
            jax.ShapeDtypeStruct(pieces.shape[1:], jnp.float32),
            jax.ShapeDtypeStruct((8, width), jnp.float32),
        ),
        in_specs=[vm, vm],
        out_specs=(vm, vm),
        scratch_shapes=[
            pltpu.VMEM(pieces.shape, jnp.float32),
            pltpu.VMEM(pieces.shape, jnp.float32),
            pltpu.VMEM(rim.shape, jnp.float32),
            pltpu.SemaphoreType.DMA((hn,)),
            pltpu.SemaphoreType.DMA((hn,)),
            pltpu.SemaphoreType.DMA((1,)),
            pltpu.SemaphoreType.DMA((1,)),
        ],
        compiler_params=pltpu.CompilerParams(collective_id=cid, has_side_effects=True),
    )(pieces, rim)


INNER = 16384


EPS = 1e-05
HIGH = lax.Precision.HIGHEST


def passed_along(block, axis, distance):
    devices = range(lax.axis_size(axis))
    route = [(i - distance, i) for i in devices if i - distance in devices]
    return lax.ppermute(block, axis, route)


def silu_grad(value):
    sigma = jax.nn.sigmoid(value)
    return sigma * (1.0 + value * (1.0 - sigma))


def conv_rows(extended, weight_matrix):
    length = extended.shape[-2] - 3
    summed = weight_matrix[..., 0, :][..., None, :] * extended[..., 0:length, :]
    for offset in range(1, 4):
        summed = (
            summed
            + weight_matrix[..., offset, :][..., None, :]
            * extended[..., offset : offset + length, :]
        )
    return summed


def conv_back(extended, weight_matrix):
    length = extended.shape[-2] - 3
    summed = weight_matrix[..., 0, :][..., None, :] * extended[..., 3 : 3 + length, :]
    for offset in range(1, 4):
        summed = (
            summed
            + weight_matrix[..., offset, :][..., None, :]
            * extended[..., 3 - offset : 3 - offset + length, :]
        )
    return summed


def to_pieces(state, count):
    heads, nstate, width = state.shape
    return state.reshape(count, heads * nstate // count, width)


def from_pieces(pieces, heads):
    count, rows, width = pieces.shape
    return pieces.reshape(heads, count * rows // heads, width)


def scan_forward(totals, local_state):
    count = lax.axis_size("seq")
    heads, nstate, width = local_state.shape
    pieces = to_pieces(local_state, count)
    high = lax.reduce_precision(totals, exponent_bits=8, mantissa_bits=7)
    rest = totals - high
    middle = lax.reduce_precision(rest, exponent_bits=8, mantissa_bits=7)
    parts = jnp.stack([high, middle, rest - middle])
    tot_row = jnp.zeros((count, 16, width), jnp.float32)
    tot_row = tot_row.at[:, 0:3, :heads].set(jnp.broadcast_to(parts, (count, 3, heads)))
    sent = jnp.concatenate([pieces, tot_row], axis=1).astype(jnp.bfloat16)
    back, scales = scan_pieces(sent, "seq", heads, 0)
    return from_pieces(back, heads).astype(jnp.float32), scales


def scan_backward(scales, state_grad):
    count = lax.axis_size("seq")
    heads = state_grad.shape[0]
    pieces = to_pieces(state_grad, count).astype(jnp.bfloat16)
    back = scan_pieces(pieces, "seq", heads, 1, scales)
    return from_pieces(back, heads).astype(jnp.float32)


def shards(
    x_input,
    z_input,
    bc_input,
    dt_raw,
    dt_bias,
    a_log,
    d_skip,
    conv_x,
    convolution_bc_taps,
    rescale_factor,
    grad_out,
):
    length = x_input.shape[0]
    channels = x_input.shape[1]
    head_count = dt_raw.shape[0]
    width = channels // head_count
    f32 = jnp.float32
    bf16 = jnp.bfloat16
    decay_rate = -jnp.exp(a_log)
    step_size = jax.nn.softplus(dt_raw + dt_bias[:, None])
    causal = jnp.tril(jnp.ones((length, length), dtype=bool))
    nstate = bc_input.shape[2]
    rows_last = jnp.concatenate(
        [x_input[length - 3 :], jnp.moveaxis(bc_input[:, length - 3 :], 0, 1).reshape(3, 2 * nstate)],
        axis=1,
    )
    rows_prior = passed_along(rows_last, "seq", 1)
    x_ext = jnp.concatenate([rows_prior[:, :channels], x_input], axis=0)
    bc_prior = jnp.moveaxis(rows_prior[:, channels:].reshape(3, 2, nstate), 0, 1)
    bc_ext = jnp.concatenate([bc_prior, bc_input], axis=1)
    x_pre = conv_rows(x_ext.astype(f32), conv_x)
    bc_pre = conv_rows(bc_ext.astype(f32), convolution_bc_taps)
    x_rows = jax.nn.silu(x_pre).astype(bf16)
    bc_rows = jax.nn.silu(bc_pre).astype(bf16)
    b_rows = bc_rows[0]
    c_rows = bc_rows[1]
    gram = jnp.dot(c_rows, b_rows.T, preferred_element_type=f32)
    x_heads = x_rows.reshape(length, head_count, width)

    cumul = jnp.cumsum(decay_rate[:, None] * step_size, axis=1)
    totals = cumul[:, -1]
    trailing = jnp.exp(cumul[:, -1:] - cumul)
    tail_step = trailing * step_size
    weighted_b = (tail_step[:, :, None] * b_rows.astype(f32)[None]).astype(bf16)
    local_state = jnp.einsum("hsn,shp->hnp", weighted_b, x_heads, preferred_element_type=f32)

    state_exact, weight = scan_forward(totals, local_state)
    state_low = state_exact.astype(bf16)

    between = cumul[:, :, None] - cumul[:, None, :]
    decay = jnp.where(causal[None], jnp.exp(jnp.minimum(between, 0.0)), 0.0)
    mixer_low = (gram[None] * decay * step_size[:, None, :]).astype(bf16)
    intra = jnp.einsum("hts,shp->thp", mixer_low, x_heads, preferred_element_type=f32)
    handed = jnp.einsum("tn,hnp->thp", c_rows, state_low, preferred_element_type=f32)
    lifted = jnp.exp(cumul)
    mixed_heads = (
        intra + lifted.T[:, :, None] * handed + d_skip[None, :, None] * x_heads.astype(f32)
    )
    mixed_out = mixed_heads.reshape(length, channels)

    z_rows = z_input.astype(f32)
    gate_value = jax.nn.silu(z_rows)
    gated = mixed_out * gate_value
    scaled = grad_out.astype(f32) * rescale_factor
    hcount = lax.axis_size("head")
    own_sums = jnp.stack([jnp.sum(gated * gated, axis=1), jnp.sum(scaled * gated, axis=1)])
    own_sums = jnp.concatenate([own_sums, jnp.zeros((6, length), f32)], axis=0)
    sums = jnp.sum(exchange(jnp.broadcast_to(own_sums, (hcount,) + own_sums.shape), "head", 3), axis=0)
    inv_rms = lax.rsqrt(sums[0] / INNER + EPS)
    normed = gated * inv_rms[:, None]
    mean_dot = inv_rms * sums[1] / INNER
    grad_gated = inv_rms[:, None] * (scaled - normed * mean_dot[:, None])
    grad_z = (grad_gated * mixed_out * silu_grad(z_rows)).astype(bf16)
    grad_mixed = (grad_gated * gate_value).astype(bf16)
    grad_heads = grad_mixed.reshape(length, head_count, width)

    lifted_c = (lifted[:, :, None] * c_rows.astype(f32)[None]).astype(bf16)
    state_grad = jnp.einsum("htn,thp->hnp", lifted_c, grad_heads, preferred_element_type=f32)
    out_exact = scan_backward(weight, state_grad)
    out_low = out_exact.astype(bf16)

    grad_mix = jnp.einsum("thp,shp->hts", grad_heads, x_heads, preferred_element_type=f32)
    decayed = grad_mix * decay
    zterm = decayed * step_size[:, None, :]
    gram_grad = zterm * gram[None]
    reached = jnp.einsum("shp,hnp->hsn", x_heads, out_low, preferred_element_type=f32)
    inner_b = jnp.sum(b_rows.astype(f32)[None] * reached, axis=2)
    state_term = tail_step * inner_b
    grad_cumul = jnp.sum(gram_grad, axis=2) - jnp.sum(gram_grad, axis=1)
    carried_dot = jnp.sum(grad_heads.astype(f32) * handed, axis=2).T
    grad_cumul = grad_cumul + lifted * carried_dot - state_term
    end_grad = jnp.sum(state_term, axis=1) + jnp.exp(totals) * jnp.sum(
        out_exact * state_exact, axis=(1, 2)
    )
    grad_cumul = grad_cumul.at[:, -1].add(end_grad)
    grad_log = jnp.cumsum(grad_cumul[:, ::-1], axis=1)[:, ::-1]
    grad_steps = (
        jnp.sum(decayed * gram[None], axis=1)
        + trailing * inner_b
        + decay_rate[:, None] * grad_log
    )
    grad_x_heads = jnp.einsum("hts,thp->shp", mixer_low, grad_heads, preferred_element_type=f32)
    grad_x_heads = (
        grad_x_heads
        + d_skip[None, :, None] * grad_heads.astype(f32)
        + jnp.einsum("hsn,hnp->shp", weighted_b, out_low, preferred_element_type=f32)
    )
    grad_c_heads = lifted[:, :, None] * jnp.einsum(
        "thp,hnp->htn", grad_heads, state_low, preferred_element_type=f32
    )
    grad_b_heads = tail_step[:, :, None] * reached
    grad_sum = jnp.sum(zterm, axis=0)
    grad_c = jnp.sum(grad_c_heads, axis=0) + jnp.dot(grad_sum, b_rows.astype(f32), precision=HIGH)
    grad_b = jnp.sum(grad_b_heads, axis=0) + jnp.dot(
        grad_sum.T, c_rows.astype(f32), precision=HIGH
    )
    grad_bc_rows = jnp.stack([grad_b, grad_c])
    grad_x_rows = grad_x_heads.reshape(length, channels)

    grad_x_pre = grad_x_rows * silu_grad(x_pre)
    hcount = lax.axis_size("head")
    row_share = length // hcount
    hidx = lax.axis_index("head")
    first_row = hidx * row_share
    picks = []
    for h in range(hcount):
        own = [h * row_share + i for i in range(row_share + 3)]
        own = [r if r < length else length for r in own]
        picks.append(own + [length] * (16 - row_share - 3))
    picks = jnp.array(picks, jnp.int32)
    piece_rows = picks.shape[1]
    bc_rows_z = jnp.concatenate([grad_bc_rows, jnp.zeros((2, 1, nstate), f32)], axis=1)
    bc_pieces = jnp.moveaxis(jnp.take(bc_rows_z, picks.reshape(-1), axis=1).reshape(2, hcount, piece_rows, -1), 1, 0)
    top = (grad_bc_rows[:, :3] * silu_grad(bc_pre[:, :3])).reshape(6, nstate)
    rim_send = jnp.zeros((8, channels + nstate), f32)
    rim_send = rim_send.at[0:3, :channels].set(grad_x_pre[:3]).at[0:6, channels:].set(top)
    summed, rim_got = tail_exchange(bc_pieces.reshape(hcount, 2 * piece_rows, -1), rim_send, 2)
    grad_bc_mine = summed.reshape(2, piece_rows, -1)[:, : row_share + 3]
    bc_pre_pad = jnp.concatenate([bc_pre, jnp.zeros((2, 3, nstate), f32)], axis=1)
    bc_pre_mine = lax.dynamic_slice_in_dim(bc_pre_pad, first_row, row_share + 3, 1)
    in_rim = (hidx == hcount - 1) & (jnp.arange(row_share + 3) >= row_share)
    grad_bc_ext = grad_bc_mine * jnp.where(in_rim[None, :, None], 1.0, silu_grad(bc_pre_mine))
    rim_x = rim_got[:3]
    grad_x = conv_back(jnp.concatenate([grad_x_pre, rim_x], axis=0), conv_x).astype(bf16)
    grad_bc = conv_back(grad_bc_ext, convolution_bc_taps).astype(bf16)
    grad_dt = grad_steps * jax.nn.sigmoid(dt_raw + dt_bias[:, None])
    return (grad_x, grad_z, grad_bc, grad_dt)


def solution(mesh):
    return jax.shard_map(
        shards,
        mesh=mesh,
        in_specs=(
            P("seq", "head"),
            P("seq", "head"),
            P(None, "seq", None),
            P("head", "seq"),
            P("head"),
            P("head"),
            P("head"),
            P(None, "head"),
            P(),
            P("head"),
            P("seq", "head"),
        ),
        out_specs=(
            P("seq", "head"),
            P("seq", "head"),
            P(None, ("seq", "head"), None),
            P("head", "seq"),
        ),
        check_vma=False,
    )
```

```python
import jax
import jax.numpy as jnp
from jax import lax
from jax.experimental import pallas as pl
from jax.experimental.pallas import tpu as pltpu
from jax.sharding import PartitionSpec as P
import functools

MESH = pl.DeviceIdType.MESH
AXES = ("seq", "head")


def exchange_kernel(axis, n, in_ref, out_ref, land, send_sem, recv_sem):
    me = lax.axis_index(axis)
    coords = {a: lax.axis_index(a) for a in AXES}

    def dev(k):
        return tuple(k if a == axis else coords[a] for a in AXES)

    barrier = pltpu.get_barrier_semaphore()
    for i in range(1, n):
        pl.semaphore_signal(barrier, inc=1, device_id=dev(lax.rem(me + i, n)), device_id_type=MESH)
    pl.semaphore_wait(barrier, n - 1)
    copies = []
    for i in range(1, n):
        peer = lax.rem(me + i, n)
        copy = pltpu.make_async_remote_copy(
            src_ref=in_ref.at[peer],
            dst_ref=land.at[me],
            send_sem=send_sem.at[i],
            recv_sem=recv_sem.at[i],
            device_id=dev(peer),
            device_id_type=MESH,
        )
        copy.start()
        copies.append(copy)
    land[me] = in_ref[me]
    for i in range(1, n):
        copies[i - 1].wait_send()
        src = lax.rem(me + (n - i), n)
        incoming = pltpu.make_async_remote_copy(
            src_ref=in_ref.at[src],
            dst_ref=land.at[src],
            send_sem=send_sem.at[i],
            recv_sem=recv_sem.at[i],
            device_id=dev(src),
            device_id_type=MESH,
        )
        incoming.wait_recv()
    out_ref[...] = land[...]


def exchange(x, axis, cid):
    n = lax.axis_size(axis)
    return pl.pallas_call(
        functools.partial(exchange_kernel, axis, n),
        out_shape=jax.ShapeDtypeStruct(x.shape, x.dtype),
        in_specs=[pl.BlockSpec(memory_space=pltpu.VMEM)],
        out_specs=pl.BlockSpec(memory_space=pltpu.VMEM),
        scratch_shapes=[
            pltpu.VMEM(x.shape, x.dtype),
            pltpu.SemaphoreType.DMA((n,)),
            pltpu.SemaphoreType.DMA((n,)),
        ],
        compiler_params=pltpu.CompilerParams(collective_id=cid, has_side_effects=True),
    )(x)

def _peer_copies(axis, n, src_of, dst, send_sem, recv_sem):
    me = lax.axis_index(axis)
    coords = {a: lax.axis_index(a) for a in AXES}

    def dev(k):
        return tuple(k if a == axis else coords[a] for a in AXES)

    copies = []
    for i in range(1, n):
        peer = lax.rem(me + i, n)
        copy = pltpu.make_async_remote_copy(
            src_ref=src_of(peer),
            dst_ref=dst.at[me],
            send_sem=send_sem.at[i],
            recv_sem=recv_sem.at[i],
            device_id=dev(peer),
            device_id_type=MESH,
        )
        copy.start()
        copies.append(copy)
    return copies


def _peer_waits(axis, n, copies, src_of, dst, send_sem, recv_sem):
    me = lax.axis_index(axis)
    coords = {a: lax.axis_index(a) for a in AXES}

    def dev(k):
        return tuple(k if a == axis else coords[a] for a in AXES)

    for i in range(1, n):
        copies[i - 1].wait_send()
        src = lax.rem(me + (n - i), n)
        incoming = pltpu.make_async_remote_copy(
            src_ref=src_of(src),
            dst_ref=dst.at[src],
            send_sem=send_sem.at[i],
            recv_sem=recv_sem.at[i],
            device_id=dev(src),
            device_id_type=MESH,
        )
        incoming.wait_recv()


def _barrier(axis, n):
    me = lax.axis_index(axis)
    coords = {a: lax.axis_index(a) for a in AXES}
    barrier = pltpu.get_barrier_semaphore()
    for i in range(1, n):
        peer = lax.rem(me + i, n)
        dev = tuple(peer if a == axis else coords[a] for a in AXES)
        pl.semaphore_signal(barrier, inc=1, device_id=dev, device_id_type=MESH)
    pl.semaphore_wait(barrier, n - 1)


def scan_kernel(forward, axis, n, heads, *refs):
    if forward:
        in_ref, out_ref, scale_out, land, res, land2, s1, r1, s2, r2 = refs
    else:
        in_ref, scale_in, out_ref, land, res, land2, s1, r1, s2, r2 = refs
    me = lax.axis_index(axis)
    rows = res.shape[1]
    _barrier(axis, n)
    copies = _peer_copies(axis, n, lambda p: in_ref.at[p], land, s1, r1)
    land[me] = in_ref[me]
    _peer_waits(axis, n, copies, lambda p: in_ref.at[p], land, s1, r1)
    if forward:
        lane = lax.broadcasted_iota(jnp.int32, (1, 128), 1)
        pick = lane == me // (n // heads)
        for k in range(n):
            parts = land[k, rows : rows + 3, :].astype(jnp.float32)
            grow = jnp.exp(parts[0:1] + parts[1:2] + parts[2:3])
            factor = jnp.sum(jnp.where(pick, grow, 0.0), axis=1, keepdims=True)
            scale_out[k] = jnp.broadcast_to(factor, (rows, 128))
        acc = jnp.zeros((rows, 128), jnp.float32)
        for k in range(n):
            res[k] = acc.astype(res.dtype)
            acc = scale_out[k] * acc + land[k, :rows, :].astype(jnp.float32)
    else:
        acc = jnp.zeros((rows, 128), jnp.float32)
        for k in reversed(range(n)):
            res[k] = acc.astype(res.dtype)
            acc = land[k].astype(jnp.float32) + scale_in[k] * acc
    copies = _peer_copies(axis, n, lambda p: res.at[p], land2, s2, r2)
    land2[me] = res[me]
    _peer_waits(axis, n, copies, lambda p: res.at[p], land2, s2, r2)
    out_ref[...] = land2[...]


def scan_pieces(x, axis, heads, cid, scales=None):
    n = lax.axis_size(axis)
    forward = scales is None
    rows = x.shape[1] - 16 if forward else x.shape[1]
    piece = (n, rows, 128)
    low = x.dtype
    vm = pl.BlockSpec(memory_space=pltpu.VMEM)
    scratch = [
        pltpu.VMEM(x.shape, low),
        pltpu.VMEM(piece, low),
        pltpu.VMEM(piece, low),
        pltpu.SemaphoreType.DMA((n,)),
        pltpu.SemaphoreType.DMA((n,)),
        pltpu.SemaphoreType.DMA((n,)),
        pltpu.SemaphoreType.DMA((n,)),
    ]
    params = pltpu.CompilerParams(collective_id=cid, has_side_effects=True)
    kern = functools.partial(scan_kernel, forward, axis, n, heads)
    if forward:
        return pl.pallas_call(
            kern,
            out_shape=(jax.ShapeDtypeStruct(piece, low), jax.ShapeDtypeStruct(piece, jnp.float32)),
            in_specs=[vm],
            out_specs=(vm, vm),
            scratch_shapes=scratch,
            compiler_params=params,
        )(x)
    return pl.pallas_call(
        kern,
        out_shape=jax.ShapeDtypeStruct(piece, low),
        in_specs=[vm, vm],
        out_specs=vm,
        scratch_shapes=scratch,
        compiler_params=params,
    )(x, scales)


def tail_kernel(n, hn, in_ref, rim_ref, out_ref, rim_out, land, send, rim_land, s1, r1, s2, r2):
    me = lax.axis_index("seq")
    hme = lax.axis_index("head")
    prev = lax.rem(me + n - 1, n)
    nxt = lax.rem(me + 1, n)
    barrier = pltpu.get_barrier_semaphore()
    for i in range(1, hn):
        pl.semaphore_signal(barrier, inc=1, device_id=(me, lax.rem(hme + i, hn)), device_id_type=MESH)
    pl.semaphore_signal(barrier, inc=1, device_id=(prev, hme), device_id_type=MESH)
    pl.semaphore_signal(barrier, inc=1, device_id=(nxt, hme), device_id_type=MESH)
    pl.semaphore_wait(barrier, hn + 1)
    rim_copy = pltpu.make_async_remote_copy(
        src_ref=rim_ref, dst_ref=rim_land, send_sem=s2.at[0], recv_sem=r2.at[0],
        device_id=(prev, hme), device_id_type=MESH,
    )
    rim_copy.start()
    send[...] = in_ref[...]
    rim_copy.wait_send()
    rim_copy.wait_recv()
    keep = (1 - me // (n - 1)).astype(jnp.float32)
    rows = in_ref.shape[1] // 2
    nst = in_ref.shape[2]
    width = rim_ref.shape[1] - nst
    rim_bc = rim_land[0:8, width:] * keep
    last = hn - 1
    send[last, 8:11, :] = send[last, 8:11, :] + rim_bc[0:3]
    send[last, rows + 8 : rows + 11, :] = send[last, rows + 8 : rows + 11, :] + rim_bc[3:6]
    rim_out[...] = rim_land[0:8, 0:width] * keep
    src_of = lambda p: send.at[p]
    copies = []
    for i in range(1, hn):
        peer = lax.rem(hme + i, hn)
        copy = pltpu.make_async_remote_copy(
            src_ref=send.at[peer], dst_ref=land.at[hme], send_sem=s1.at[i], recv_sem=r1.at[i],
            device_id=(me, peer), device_id_type=MESH,
        )
        copy.start()
        copies.append(copy)
    land[hme] = send[hme]
    for i in range(1, hn):
        copies[i - 1].wait_send()
        src = lax.rem(hme + (hn - i), hn)
        incoming = pltpu.make_async_remote_copy(
            src_ref=send.at[src], dst_ref=land.at[src], send_sem=s1.at[i], recv_sem=r1.at[i],
            device_id=(me, src), device_id_type=MESH,
        )
        incoming.wait_recv()
    total = land[0]
    for j in range(1, hn):
        total = total + land[j]
    out_ref[...] = total


def tail_exchange(pieces, rim, cid):
    n = lax.axis_size("seq")
    hn = lax.axis_size("head")
    vm = pl.BlockSpec(memory_space=pltpu.VMEM)
    width = rim.shape[1] - pieces.shape[2]
    return pl.pallas_call(
        functools.partial(tail_kernel, n, hn),
        out_shape=(
            jax.ShapeDtypeStruct(pieces.shape[1:], jnp.float32),
            jax.ShapeDtypeStruct((8, width), jnp.float32),
        ),
        in_specs=[vm, vm],
        out_specs=(vm, vm),
        scratch_shapes=[
            pltpu.VMEM(pieces.shape, jnp.float32),
            pltpu.VMEM(pieces.shape, jnp.float32),
            pltpu.VMEM(rim.shape, jnp.float32),
            pltpu.SemaphoreType.DMA((hn,)),
            pltpu.SemaphoreType.DMA((hn,)),
            pltpu.SemaphoreType.DMA((1,)),
            pltpu.SemaphoreType.DMA((1,)),
        ],
        compiler_params=pltpu.CompilerParams(collective_id=cid, has_side_effects=True),
    )(pieces, rim)


INNER = 16384


EPS = 1e-05
HIGH = lax.Precision.HIGHEST


def passed_along(block, axis, distance):
    devices = range(lax.axis_size(axis))
    route = [(i - distance, i) for i in devices if i - distance in devices]
    return lax.ppermute(block, axis, route)


def silu_grad(value):
    sigma = jax.nn.sigmoid(value)
    return sigma * (1.0 + value * (1.0 - sigma))


def conv_rows(extended, weight_matrix):
    length = extended.shape[-2] - 3
    summed = weight_matrix[..., 0, :][..., None, :] * extended[..., 0:length, :]
    for offset in range(1, 4):
        summed = (
            summed
            + weight_matrix[..., offset, :][..., None, :]
            * extended[..., offset : offset + length, :]
        )
    return summed


def conv_back(extended, weight_matrix):
    length = extended.shape[-2] - 3
    summed = weight_matrix[..., 0, :][..., None, :] * extended[..., 3 : 3 + length, :]
    for offset in range(1, 4):
        summed = (
            summed
            + weight_matrix[..., offset, :][..., None, :]
            * extended[..., 3 - offset : 3 - offset + length, :]
        )
    return summed


def to_pieces(state, count):
    heads, nstate, width = state.shape
    return state.reshape(count, heads * nstate // count, width)


def from_pieces(pieces, heads):
    count, rows, width = pieces.shape
    return pieces.reshape(heads, count * rows // heads, width)


def scan_forward(totals, local_state):
    count = lax.axis_size("seq")
    heads, nstate, width = local_state.shape
    pieces = to_pieces(local_state, count)
    high = lax.reduce_precision(totals, exponent_bits=8, mantissa_bits=7)
    rest = totals - high
    middle = lax.reduce_precision(rest, exponent_bits=8, mantissa_bits=7)
    parts = jnp.stack([high, middle, rest - middle])
    tot_row = jnp.pad(parts, ((0, 13), (0, width - heads)))
    tot_row = jnp.broadcast_to(tot_row, (count, 16, width))
    sent = jnp.concatenate([pieces, tot_row], axis=1).astype(jnp.bfloat16)
    back, scales = scan_pieces(sent, "seq", heads, 0)
    return from_pieces(back, heads).astype(jnp.float32), scales


def scan_backward(scales, state_grad):
    count = lax.axis_size("seq")
    heads = state_grad.shape[0]
    pieces = to_pieces(state_grad, count).astype(jnp.bfloat16)
    back = scan_pieces(pieces, "seq", heads, 1, scales)
    return from_pieces(back, heads).astype(jnp.float32)


def shards(
    x_input,
    z_input,
    bc_input,
    dt_raw,
    dt_bias,
    a_log,
    d_skip,
    conv_x,
    convolution_bc_taps,
    rescale_factor,
    grad_out,
):
    length = x_input.shape[0]
    channels = x_input.shape[1]
    head_count = dt_raw.shape[0]
    width = channels // head_count
    f32 = jnp.float32
    bf16 = jnp.bfloat16
    decay_rate = -jnp.exp(a_log)
    step_size = jax.nn.softplus(dt_raw + dt_bias[:, None])
    causal = jnp.tril(jnp.ones((length, length), dtype=bool))
    nstate = bc_input.shape[2]
    rows_last = jnp.concatenate(
        [x_input[length - 3 :], jnp.moveaxis(bc_input[:, length - 3 :], 0, 1).reshape(3, 2 * nstate)],
        axis=1,
    )
    rows_prior = passed_along(rows_last, "seq", 1)
    x_ext = jnp.concatenate([rows_prior[:, :channels], x_input], axis=0)
    bc_prior = jnp.moveaxis(rows_prior[:, channels:].reshape(3, 2, nstate), 0, 1)
    bc_ext = jnp.concatenate([bc_prior, bc_input], axis=1)
    x_pre = conv_rows(x_ext.astype(f32), conv_x)
    bc_pre = conv_rows(bc_ext.astype(f32), convolution_bc_taps)
    x_rows = jax.nn.silu(x_pre).astype(bf16)
    bc_rows = jax.nn.silu(bc_pre).astype(bf16)
    b_rows = bc_rows[0]
    c_rows = bc_rows[1]
    gram = jnp.dot(c_rows, b_rows.T, preferred_element_type=f32)
    x_heads = x_rows.reshape(length, head_count, width)

    cumul = jnp.cumsum(decay_rate[:, None] * step_size, axis=1)
    totals = cumul[:, -1]
    trailing = jnp.exp(cumul[:, -1:] - cumul)
    tail_step = trailing * step_size
    weighted_b = (tail_step[:, :, None] * b_rows.astype(f32)[None]).astype(bf16)
    local_state = jnp.einsum("hsn,shp->hnp", weighted_b, x_heads, preferred_element_type=f32)

    state_exact, weight = scan_forward(totals, local_state)
    state_low = state_exact.astype(bf16)

    between = cumul[:, :, None] - cumul[:, None, :]
    decay = jnp.where(causal[None], jnp.exp(jnp.minimum(between, 0.0)), 0.0)
    mixer_low = (gram[None] * decay * step_size[:, None, :]).astype(bf16)
    intra = jnp.einsum("hts,shp->thp", mixer_low, x_heads, preferred_element_type=f32)
    handed = jnp.einsum("tn,hnp->thp", c_rows, state_low, preferred_element_type=f32)
    lifted = jnp.exp(cumul)
    mixed_heads = (
        intra + lifted.T[:, :, None] * handed + d_skip[None, :, None] * x_heads.astype(f32)
    )
    mixed_out = mixed_heads.reshape(length, channels)

    z_rows = z_input.astype(f32)
    gate_value = jax.nn.silu(z_rows)
    gated = mixed_out * gate_value
    scaled = grad_out.astype(f32) * rescale_factor
    hcount = lax.axis_size("head")
    own_sums = jnp.stack([jnp.sum(gated * gated, axis=1), jnp.sum(scaled * gated, axis=1)])
    own_sums = jnp.concatenate([own_sums, jnp.zeros((6, length), f32)], axis=0)
    sums = jnp.sum(exchange(jnp.broadcast_to(own_sums, (hcount,) + own_sums.shape), "head", 3), axis=0)
    inv_rms = lax.rsqrt(sums[0] / INNER + EPS)
    normed = gated * inv_rms[:, None]
    mean_dot = inv_rms * sums[1] / INNER
    grad_gated = inv_rms[:, None] * (scaled - normed * mean_dot[:, None])
    grad_z = (grad_gated * mixed_out * silu_grad(z_rows)).astype(bf16)
    grad_mixed = (grad_gated * gate_value).astype(bf16)
    grad_heads = grad_mixed.reshape(length, head_count, width)

    lifted_c = (lifted[:, :, None] * c_rows.astype(f32)[None]).astype(bf16)
    state_grad = jnp.einsum("htn,thp->hnp", lifted_c, grad_heads, preferred_element_type=f32)
    out_exact = scan_backward(weight, state_grad)
    out_low = out_exact.astype(bf16)

    grad_mix = jnp.einsum("thp,shp->hts", grad_heads, x_heads, preferred_element_type=f32)
    decayed = grad_mix * decay
    zterm = decayed * step_size[:, None, :]
    gram_grad = zterm * gram[None]
    reached = jnp.einsum("shp,hnp->hsn", x_heads, out_low, preferred_element_type=f32)
    inner_b = jnp.sum(b_rows.astype(f32)[None] * reached, axis=2)
    state_term = tail_step * inner_b
    grad_cumul = jnp.sum(gram_grad, axis=2) - jnp.sum(gram_grad, axis=1)
    carried_dot = jnp.sum(grad_heads.astype(f32) * handed, axis=2).T
    grad_cumul = grad_cumul + lifted * carried_dot - state_term
    end_grad = jnp.sum(state_term, axis=1) + jnp.exp(totals) * jnp.sum(
        out_exact * state_exact, axis=(1, 2)
    )
    grad_cumul = grad_cumul.at[:, -1].add(end_grad)
    grad_log = jnp.cumsum(grad_cumul[:, ::-1], axis=1)[:, ::-1]
    grad_steps = (
        jnp.sum(decayed * gram[None], axis=1)
        + trailing * inner_b
        + decay_rate[:, None] * grad_log
    )
    grad_x_heads = jnp.einsum("hts,thp->shp", mixer_low, grad_heads, preferred_element_type=f32)
    grad_x_heads = (
        grad_x_heads
        + d_skip[None, :, None] * grad_heads.astype(f32)
        + jnp.einsum("hsn,hnp->shp", weighted_b, out_low, preferred_element_type=f32)
    )
    grad_c_heads = lifted[:, :, None] * jnp.einsum(
        "thp,hnp->htn", grad_heads, state_low, preferred_element_type=f32
    )
    grad_b_heads = tail_step[:, :, None] * reached
    grad_sum = jnp.sum(zterm, axis=0)
    grad_c = jnp.sum(grad_c_heads, axis=0) + jnp.dot(grad_sum, b_rows.astype(f32), precision=HIGH)
    grad_b = jnp.sum(grad_b_heads, axis=0) + jnp.dot(
        grad_sum.T, c_rows.astype(f32), precision=HIGH
    )
    grad_bc_rows = jnp.stack([grad_b, grad_c])
    grad_x_rows = grad_x_heads.reshape(length, channels)

    grad_x_pre = grad_x_rows * silu_grad(x_pre)
    hcount = lax.axis_size("head")
    row_share = length // hcount
    hidx = lax.axis_index("head")
    first_row = hidx * row_share
    picks = []
    for h in range(hcount):
        own = [h * row_share + i for i in range(row_share + 3)]
        own = [r if r < length else length for r in own]
        picks.append(own + [length] * (16 - row_share - 3))
    picks = jnp.array(picks, jnp.int32)
    piece_rows = picks.shape[1]
    bc_rows_z = jnp.concatenate([grad_bc_rows, jnp.zeros((2, 1, nstate), f32)], axis=1)
    bc_pieces = jnp.moveaxis(jnp.take(bc_rows_z, picks.reshape(-1), axis=1).reshape(2, hcount, piece_rows, -1), 1, 0)
    top = (grad_bc_rows[:, :3] * silu_grad(bc_pre[:, :3])).reshape(6, nstate)
    rim_send = jnp.concatenate(
        [jnp.pad(grad_x_pre[:3], ((0, 5), (0, 0))), jnp.pad(top, ((0, 2), (0, 0)))], axis=1
    )
    summed, rim_got = tail_exchange(bc_pieces.reshape(hcount, 2 * piece_rows, -1), rim_send, 2)
    grad_bc_mine = summed.reshape(2, piece_rows, -1)[:, : row_share + 3]
    bc_pre_pad = jnp.concatenate([bc_pre, jnp.zeros((2, 3, nstate), f32)], axis=1)
    bc_pre_mine = lax.dynamic_slice_in_dim(bc_pre_pad, first_row, row_share + 3, 1)
    in_rim = (hidx == hcount - 1) & (jnp.arange(row_share + 3) >= row_share)
    grad_bc_ext = grad_bc_mine * jnp.where(in_rim[None, :, None], 1.0, silu_grad(bc_pre_mine))
    rim_x = rim_got[:3]
    grad_x = conv_back(jnp.concatenate([grad_x_pre, rim_x], axis=0), conv_x).astype(bf16)
    grad_bc = conv_back(grad_bc_ext, convolution_bc_taps).astype(bf16)
    grad_dt = grad_steps * jax.nn.sigmoid(dt_raw + dt_bias[:, None])
    return (grad_x, grad_z, grad_bc, grad_dt)


def solution(mesh):
    return jax.shard_map(
        shards,
        mesh=mesh,
        in_specs=(
            P("seq", "head"),
            P("seq", "head"),
            P(None, "seq", None),
            P("head", "seq"),
            P("head"),
            P("head"),
            P("head"),
            P(None, "head"),
            P(),
            P("head"),
            P("seq", "head"),
        ),
        out_specs=(
            P("seq", "head"),
            P("seq", "head"),
            P(None, ("seq", "head"), None),
            P("head", "seq"),
        ),
        check_vma=False,
    )
```

```python
import jax
import jax.numpy as jnp
from jax import lax
from jax.experimental import pallas as pl
from jax.experimental.pallas import tpu as pltpu
from jax.sharding import PartitionSpec as P
import functools

MESH = pl.DeviceIdType.MESH
AXES = ("seq", "head")


def exchange_kernel(axis, n, in_ref, out_ref, land, send_sem, recv_sem):
    me = lax.axis_index(axis)
    coords = {a: lax.axis_index(a) for a in AXES}

    def dev(k):
        return tuple(k if a == axis else coords[a] for a in AXES)

    barrier = pltpu.get_barrier_semaphore()
    for i in range(1, n):
        pl.semaphore_signal(barrier, inc=1, device_id=dev(lax.rem(me + i, n)), device_id_type=MESH)
    pl.semaphore_wait(barrier, n - 1)
    copies = []
    for i in range(1, n):
        peer = lax.rem(me + i, n)
        copy = pltpu.make_async_remote_copy(
            src_ref=in_ref.at[peer],
            dst_ref=land.at[me],
            send_sem=send_sem.at[i],
            recv_sem=recv_sem.at[i],
            device_id=dev(peer),
            device_id_type=MESH,
        )
        copy.start()
        copies.append(copy)
    land[me] = in_ref[me]
    for i in range(1, n):
        copies[i - 1].wait_send()
        src = lax.rem(me + (n - i), n)
        incoming = pltpu.make_async_remote_copy(
            src_ref=in_ref.at[src],
            dst_ref=land.at[src],
            send_sem=send_sem.at[i],
            recv_sem=recv_sem.at[i],
            device_id=dev(src),
            device_id_type=MESH,
        )
        incoming.wait_recv()
    out_ref[...] = land[...]


def exchange(x, axis, cid):
    n = lax.axis_size(axis)
    return pl.pallas_call(
        functools.partial(exchange_kernel, axis, n),
        out_shape=jax.ShapeDtypeStruct(x.shape, x.dtype),
        in_specs=[pl.BlockSpec(memory_space=pltpu.VMEM)],
        out_specs=pl.BlockSpec(memory_space=pltpu.VMEM),
        scratch_shapes=[
            pltpu.VMEM(x.shape, x.dtype),
            pltpu.SemaphoreType.DMA((n,)),
            pltpu.SemaphoreType.DMA((n,)),
        ],
        compiler_params=pltpu.CompilerParams(collective_id=cid, has_side_effects=True),
    )(x)

def _peer_copies(axis, n, src_of, dst, send_sem, recv_sem):
    me = lax.axis_index(axis)
    coords = {a: lax.axis_index(a) for a in AXES}

    def dev(k):
        return tuple(k if a == axis else coords[a] for a in AXES)

    copies = []
    for i in range(1, n):
        peer = lax.rem(me + i, n)
        copy = pltpu.make_async_remote_copy(
            src_ref=src_of(peer),
            dst_ref=dst.at[me],
            send_sem=send_sem.at[i],
            recv_sem=recv_sem.at[i],
            device_id=dev(peer),
            device_id_type=MESH,
        )
        copy.start()
        copies.append(copy)
    return copies


def _peer_waits(axis, n, copies, src_of, dst, send_sem, recv_sem):
    me = lax.axis_index(axis)
    coords = {a: lax.axis_index(a) for a in AXES}

    def dev(k):
        return tuple(k if a == axis else coords[a] for a in AXES)

    for i in range(1, n):
        copies[i - 1].wait_send()
        src = lax.rem(me + (n - i), n)
        incoming = pltpu.make_async_remote_copy(
            src_ref=src_of(src),
            dst_ref=dst.at[src],
            send_sem=send_sem.at[i],
            recv_sem=recv_sem.at[i],
            device_id=dev(src),
            device_id_type=MESH,
        )
        incoming.wait_recv()


def _barrier(axis, n):
    me = lax.axis_index(axis)
    coords = {a: lax.axis_index(a) for a in AXES}
    barrier = pltpu.get_barrier_semaphore()
    for i in range(1, n):
        peer = lax.rem(me + i, n)
        dev = tuple(peer if a == axis else coords[a] for a in AXES)
        pl.semaphore_signal(barrier, inc=1, device_id=dev, device_id_type=MESH)
    pl.semaphore_wait(barrier, n - 1)


def scan_kernel(forward, axis, n, heads, *refs):
    if forward:
        in_ref, out_ref, scale_out, land, res, land2, s1, r1, s2, r2 = refs
    else:
        in_ref, scale_in, out_ref, land, res, land2, s1, r1, s2, r2 = refs
    me = lax.axis_index(axis)
    rows = res.shape[1]
    _barrier(axis, n)
    copies = _peer_copies(axis, n, lambda p: in_ref.at[p], land, s1, r1)
    land[me] = in_ref[me]
    _peer_waits(axis, n, copies, lambda p: in_ref.at[p], land, s1, r1)
    if forward:
        lane = lax.broadcasted_iota(jnp.int32, (1, 128), 1)
        pick = lane == me // (n // heads)
        for k in range(n):
            parts = land[k, rows : rows + 3, :].astype(jnp.float32)
            grow = jnp.exp(parts[0:1] + parts[1:2] + parts[2:3])
            factor = jnp.sum(jnp.where(pick, grow, 0.0), axis=1, keepdims=True)
            scale_out[k] = jnp.broadcast_to(factor, (rows, 128))
        acc = jnp.zeros((rows, 128), jnp.float32)
        for k in range(n):
            res[k] = acc.astype(res.dtype)
            acc = scale_out[k] * acc + land[k, :rows, :].astype(jnp.float32)
    else:
        acc = jnp.zeros((rows, 128), jnp.float32)
        for k in reversed(range(n)):
            res[k] = acc.astype(res.dtype)
            acc = land[k].astype(jnp.float32) + scale_in[k] * acc
    copies = _peer_copies(axis, n, lambda p: res.at[p], land2, s2, r2)
    land2[me] = res[me]
    _peer_waits(axis, n, copies, lambda p: res.at[p], land2, s2, r2)
    out_ref[...] = land2[...]


def scan_pieces(x, axis, heads, cid, scales=None):
    n = lax.axis_size(axis)
    forward = scales is None
    rows = x.shape[1] - 16 if forward else x.shape[1]
    piece = (n, rows, 128)
    low = x.dtype
    vm = pl.BlockSpec(memory_space=pltpu.VMEM)
    scratch = [
        pltpu.VMEM(x.shape, low),
        pltpu.VMEM(piece, low),
        pltpu.VMEM(piece, low),
        pltpu.SemaphoreType.DMA((n,)),
        pltpu.SemaphoreType.DMA((n,)),
        pltpu.SemaphoreType.DMA((n,)),
        pltpu.SemaphoreType.DMA((n,)),
    ]
    params = pltpu.CompilerParams(collective_id=cid, has_side_effects=True)
    kern = functools.partial(scan_kernel, forward, axis, n, heads)
    if forward:
        return pl.pallas_call(
            kern,
            out_shape=(jax.ShapeDtypeStruct(piece, low), jax.ShapeDtypeStruct(piece, jnp.float32)),
            in_specs=[vm],
            out_specs=(vm, vm),
            scratch_shapes=scratch,
            compiler_params=params,
        )(x)
    return pl.pallas_call(
        kern,
        out_shape=jax.ShapeDtypeStruct(piece, low),
        in_specs=[vm, vm],
        out_specs=vm,
        scratch_shapes=scratch,
        compiler_params=params,
    )(x, scales)


def tail_kernel(n, hn, in_ref, rim_ref, out_ref, rim_out, land, send, rim_land, s1, r1, s2, r2):
    me = lax.axis_index("seq")
    hme = lax.axis_index("head")
    prev = lax.rem(me + n - 1, n)
    nxt = lax.rem(me + 1, n)
    barrier = pltpu.get_barrier_semaphore()
    for i in range(1, hn):
        pl.semaphore_signal(barrier, inc=1, device_id=(me, lax.rem(hme + i, hn)), device_id_type=MESH)
    pl.semaphore_signal(barrier, inc=1, device_id=(prev, hme), device_id_type=MESH)
    pl.semaphore_signal(barrier, inc=1, device_id=(nxt, hme), device_id_type=MESH)
    pl.semaphore_wait(barrier, hn + 1)
    rim_copy = pltpu.make_async_remote_copy(
        src_ref=rim_ref, dst_ref=rim_land, send_sem=s2.at[0], recv_sem=r2.at[0],
        device_id=(prev, hme), device_id_type=MESH,
    )
    rim_copy.start()
    send[...] = in_ref[...]
    rim_copy.wait_send()
    rim_copy.wait_recv()
    keep = (1 - me // (n - 1)).astype(jnp.float32)
    rows = in_ref.shape[1] // 2
    nst = in_ref.shape[2]
    width = rim_ref.shape[1] - nst
    rim_bc = rim_land[0:8, width:] * keep
    last = hn - 1
    send[last, 8:11, :] = send[last, 8:11, :] + rim_bc[0:3]
    send[last, rows + 8 : rows + 11, :] = send[last, rows + 8 : rows + 11, :] + rim_bc[3:6]
    rim_out[...] = rim_land[0:8, 0:width] * keep
    src_of = lambda p: send.at[p]
    copies = []
    for i in range(1, hn):
        peer = lax.rem(hme + i, hn)
        copy = pltpu.make_async_remote_copy(
            src_ref=send.at[peer], dst_ref=land.at[hme], send_sem=s1.at[i], recv_sem=r1.at[i],
            device_id=(me, peer), device_id_type=MESH,
        )
        copy.start()
        copies.append(copy)
    land[hme] = send[hme]
    for i in range(1, hn):
        copies[i - 1].wait_send()
        src = lax.rem(hme + (hn - i), hn)
        incoming = pltpu.make_async_remote_copy(
            src_ref=send.at[src], dst_ref=land.at[src], send_sem=s1.at[i], recv_sem=r1.at[i],
            device_id=(me, src), device_id_type=MESH,
        )
        incoming.wait_recv()
    total = land[0]
    for j in range(1, hn):
        total = total + land[j]
    out_ref[...] = total


def tail_exchange(pieces, rim, cid):
    n = lax.axis_size("seq")
    hn = lax.axis_size("head")
    vm = pl.BlockSpec(memory_space=pltpu.VMEM)
    width = rim.shape[1] - pieces.shape[2]
    return pl.pallas_call(
        functools.partial(tail_kernel, n, hn),
        out_shape=(
            jax.ShapeDtypeStruct(pieces.shape[1:], jnp.float32),
            jax.ShapeDtypeStruct((8, width), jnp.float32),
        ),
        in_specs=[vm, vm],
        out_specs=(vm, vm),
        scratch_shapes=[
            pltpu.VMEM(pieces.shape, jnp.float32),
            pltpu.VMEM(pieces.shape, jnp.float32),
            pltpu.VMEM(rim.shape, jnp.float32),
            pltpu.SemaphoreType.DMA((hn,)),
            pltpu.SemaphoreType.DMA((hn,)),
            pltpu.SemaphoreType.DMA((1,)),
            pltpu.SemaphoreType.DMA((1,)),
        ],
        compiler_params=pltpu.CompilerParams(collective_id=cid, has_side_effects=True),
    )(pieces, rim)


INNER = 16384


EPS = 1e-05
HIGH = lax.Precision.HIGHEST


def passed_along(block, axis, distance):
    devices = range(lax.axis_size(axis))
    route = [(i - distance, i) for i in devices if i - distance in devices]
    return lax.ppermute(block, axis, route)


def silu_grad(value):
    sigma = jax.nn.sigmoid(value)
    return sigma * (1.0 + value * (1.0 - sigma))


def conv_rows(extended, weight_matrix):
    length = extended.shape[-2] - 3
    summed = weight_matrix[..., 0, :][..., None, :] * extended[..., 0:length, :]
    for offset in range(1, 4):
        summed = (
            summed
            + weight_matrix[..., offset, :][..., None, :]
            * extended[..., offset : offset + length, :]
        )
    return summed


def conv_back(extended, weight_matrix):
    length = extended.shape[-2] - 3
    summed = weight_matrix[..., 0, :][..., None, :] * extended[..., 3 : 3 + length, :]
    for offset in range(1, 4):
        summed = (
            summed
            + weight_matrix[..., offset, :][..., None, :]
            * extended[..., 3 - offset : 3 - offset + length, :]
        )
    return summed


def to_pieces(state, count):
    heads, nstate, width = state.shape
    return state.reshape(count, heads * nstate // count, width)


def from_pieces(pieces, heads):
    count, rows, width = pieces.shape
    return pieces.reshape(heads, count * rows // heads, width)


def scan_forward(totals, local_state):
    count = lax.axis_size("seq")
    heads, nstate, width = local_state.shape
    pieces = to_pieces(local_state, count)
    high = lax.reduce_precision(totals, exponent_bits=8, mantissa_bits=7)
    rest = totals - high
    middle = lax.reduce_precision(rest, exponent_bits=8, mantissa_bits=7)
    parts = jnp.stack([high, middle, rest - middle])
    tot_row = jnp.pad(parts, ((0, 13), (0, width - heads)))
    tot_row = jnp.broadcast_to(tot_row, (count, 16, width))
    sent = jnp.concatenate([pieces, tot_row], axis=1).astype(jnp.bfloat16)
    back, scales = scan_pieces(sent, "seq", heads, 0)
    return from_pieces(back, heads).astype(jnp.float32), scales


def scan_backward(scales, state_grad):
    count = lax.axis_size("seq")
    heads = state_grad.shape[0]
    pieces = to_pieces(state_grad, count).astype(jnp.bfloat16)
    back = scan_pieces(pieces, "seq", heads, 1, scales)
    return from_pieces(back, heads).astype(jnp.float32)


def shards(
    x_input,
    z_input,
    bc_input,
    dt_raw,
    dt_bias,
    a_log,
    d_skip,
    conv_x,
    convolution_bc_taps,
    rescale_factor,
    grad_out,
):
    length = x_input.shape[0]
    channels = x_input.shape[1]
    head_count = dt_raw.shape[0]
    width = channels // head_count
    f32 = jnp.float32
    bf16 = jnp.bfloat16
    decay_rate = -jnp.exp(a_log)
    step_size = jax.nn.softplus(dt_raw + dt_bias[:, None])
    causal = jnp.tril(jnp.ones((length, length), dtype=bool))
    nstate = bc_input.shape[2]
    rows_last = jnp.concatenate(
        [x_input[length - 3 :], jnp.moveaxis(bc_input[:, length - 3 :], 0, 1).reshape(3, 2 * nstate)],
        axis=1,
    )
    rows_prior = passed_along(rows_last, "seq", 1)
    bc_prior = jnp.moveaxis(rows_prior[:, channels:].reshape(3, 2, nstate), 0, 1)
    x_in = x_input.astype(f32)
    bc_in = bc_input.astype(f32)
    x_pre_body = conv_rows(x_in, conv_x)
    bc_pre_body = conv_rows(bc_in, convolution_bc_taps)
    x_pre_head = conv_rows(jnp.concatenate([rows_prior[:, :channels].astype(f32), x_in[:3]], axis=0), conv_x)
    bc_pre_head = conv_rows(
        jnp.concatenate([bc_prior.astype(f32), bc_in[:, :3]], axis=1), convolution_bc_taps
    )
    x_body = jax.nn.silu(x_pre_body).astype(bf16)
    x_head = jax.nn.silu(x_pre_head).astype(bf16)
    bc_body = jax.nn.silu(bc_pre_body).astype(bf16)
    bc_head = jax.nn.silu(bc_pre_head).astype(bf16)
    x_pre = jnp.concatenate([x_pre_head, x_pre_body], axis=0)
    bc_pre = jnp.concatenate([bc_pre_head, bc_pre_body], axis=1)
    x_rows = jnp.concatenate([x_head, x_body], axis=0)
    bc_rows = jnp.concatenate([bc_head, bc_body], axis=1)
    b_rows = bc_rows[0]
    c_rows = bc_rows[1]
    gram = jnp.dot(c_rows, b_rows.T, preferred_element_type=f32)
    x_heads = x_rows.reshape(length, head_count, width)

    cumul = jnp.cumsum(decay_rate[:, None] * step_size, axis=1)
    totals = cumul[:, -1]
    trailing = jnp.exp(cumul[:, -1:] - cumul)
    tail_step = trailing * step_size
    weighted_b = (tail_step[:, :, None] * b_rows.astype(f32)[None]).astype(bf16)
    wb_body = (tail_step[:, 3:, None] * bc_body[0].astype(f32)[None]).astype(bf16)
    wb_head = (tail_step[:, :3, None] * bc_head[0].astype(f32)[None]).astype(bf16)
    local_state = jnp.einsum(
        "hsn,shp->hnp", wb_body, x_body.reshape(length - 3, head_count, width), preferred_element_type=f32
    ) + jnp.einsum(
        "hsn,shp->hnp", wb_head, x_head.reshape(3, head_count, width), preferred_element_type=f32
    )

    state_exact, weight = scan_forward(totals, local_state)
    state_low = state_exact.astype(bf16)

    between = cumul[:, :, None] - cumul[:, None, :]
    decay = jnp.where(causal[None], jnp.exp(jnp.minimum(between, 0.0)), 0.0)
    mixer_low = (gram[None] * decay * step_size[:, None, :]).astype(bf16)
    intra = jnp.einsum("hts,shp->thp", mixer_low, x_heads, preferred_element_type=f32)
    handed = jnp.einsum("tn,hnp->thp", c_rows, state_low, preferred_element_type=f32)
    lifted = jnp.exp(cumul)
    mixed_heads = (
        intra + lifted.T[:, :, None] * handed + d_skip[None, :, None] * x_heads.astype(f32)
    )
    mixed_out = mixed_heads.reshape(length, channels)

    z_rows = z_input.astype(f32)
    gate_value = jax.nn.silu(z_rows)
    gated = mixed_out * gate_value
    scaled = grad_out.astype(f32) * rescale_factor
    hcount = lax.axis_size("head")
    own_sums = jnp.stack([jnp.sum(gated * gated, axis=1), jnp.sum(scaled * gated, axis=1)])
    own_sums = jnp.concatenate([own_sums, jnp.zeros((6, length), f32)], axis=0)
    sums = jnp.sum(exchange(jnp.broadcast_to(own_sums, (hcount,) + own_sums.shape), "head", 3), axis=0)
    inv_rms = lax.rsqrt(sums[0] / INNER + EPS)
    normed = gated * inv_rms[:, None]
    mean_dot = inv_rms * sums[1] / INNER
    grad_gated = inv_rms[:, None] * (scaled - normed * mean_dot[:, None])
    grad_z = (grad_gated * mixed_out * silu_grad(z_rows)).astype(bf16)
    grad_mixed = (grad_gated * gate_value).astype(bf16)
    grad_heads = grad_mixed.reshape(length, head_count, width)

    lifted_c = (lifted[:, :, None] * c_rows.astype(f32)[None]).astype(bf16)
    state_grad = jnp.einsum("htn,thp->hnp", lifted_c, grad_heads, preferred_element_type=f32)
    out_exact = scan_backward(weight, state_grad)
    out_low = out_exact.astype(bf16)

    grad_mix = jnp.einsum("thp,shp->hts", grad_heads, x_heads, preferred_element_type=f32)
    decayed = grad_mix * decay
    zterm = decayed * step_size[:, None, :]
    gram_grad = zterm * gram[None]
    reached = jnp.einsum("shp,hnp->hsn", x_heads, out_low, preferred_element_type=f32)
    inner_b = jnp.sum(b_rows.astype(f32)[None] * reached, axis=2)
    state_term = tail_step * inner_b
    grad_cumul = jnp.sum(gram_grad, axis=2) - jnp.sum(gram_grad, axis=1)
    carried_dot = jnp.sum(grad_heads.astype(f32) * handed, axis=2).T
    grad_cumul = grad_cumul + lifted * carried_dot - state_term
    end_grad = jnp.sum(state_term, axis=1) + jnp.exp(totals) * jnp.sum(
        out_exact * state_exact, axis=(1, 2)
    )
    grad_cumul = grad_cumul.at[:, -1].add(end_grad)
    grad_log = jnp.cumsum(grad_cumul[:, ::-1], axis=1)[:, ::-1]
    grad_steps = (
        jnp.sum(decayed * gram[None], axis=1)
        + trailing * inner_b
        + decay_rate[:, None] * grad_log
    )
    grad_x_heads = jnp.einsum("hts,thp->shp", mixer_low, grad_heads, preferred_element_type=f32)
    grad_x_heads = (
        grad_x_heads
        + d_skip[None, :, None] * grad_heads.astype(f32)
        + jnp.einsum("hsn,hnp->shp", weighted_b, out_low, preferred_element_type=f32)
    )
    grad_c_heads = lifted[:, :, None] * jnp.einsum(
        "thp,hnp->htn", grad_heads, state_low, preferred_element_type=f32
    )
    grad_b_heads = tail_step[:, :, None] * reached
    grad_sum = jnp.sum(zterm, axis=0)
    grad_c = jnp.sum(grad_c_heads, axis=0) + jnp.dot(grad_sum, b_rows.astype(f32), precision=HIGH)
    grad_b = jnp.sum(grad_b_heads, axis=0) + jnp.dot(
        grad_sum.T, c_rows.astype(f32), precision=HIGH
    )
    grad_bc_rows = jnp.stack([grad_b, grad_c])
    grad_x_rows = grad_x_heads.reshape(length, channels)

    grad_x_pre = grad_x_rows * silu_grad(x_pre)
    hcount = lax.axis_size("head")
    row_share = length // hcount
    hidx = lax.axis_index("head")
    first_row = hidx * row_share
    picks = []
    for h in range(hcount):
        own = [h * row_share + i for i in range(row_share + 3)]
        own = [r if r < length else length for r in own]
        picks.append(own + [length] * (16 - row_share - 3))
    picks = jnp.array(picks, jnp.int32)
    piece_rows = picks.shape[1]
    bc_rows_z = jnp.concatenate([grad_bc_rows, jnp.zeros((2, 1, nstate), f32)], axis=1)
    bc_pieces = jnp.moveaxis(jnp.take(bc_rows_z, picks.reshape(-1), axis=1).reshape(2, hcount, piece_rows, -1), 1, 0)
    top = (grad_bc_rows[:, :3] * silu_grad(bc_pre[:, :3])).reshape(6, nstate)
    rim_send = jnp.concatenate(
        [jnp.pad(grad_x_pre[:3], ((0, 5), (0, 0))), jnp.pad(top, ((0, 2), (0, 0)))], axis=1
    )
    summed, rim_got = tail_exchange(bc_pieces.reshape(hcount, 2 * piece_rows, -1), rim_send, 2)
    grad_bc_mine = summed.reshape(2, piece_rows, -1)[:, : row_share + 3]
    bc_pre_pad = jnp.concatenate([bc_pre, jnp.zeros((2, 3, nstate), f32)], axis=1)
    bc_pre_mine = lax.dynamic_slice_in_dim(bc_pre_pad, first_row, row_share + 3, 1)
    in_rim = (hidx == hcount - 1) & (jnp.arange(row_share + 3) >= row_share)
    grad_bc_ext = grad_bc_mine * jnp.where(in_rim[None, :, None], 1.0, silu_grad(bc_pre_mine))
    rim_x = rim_got[:3]
    grad_x = conv_back(jnp.concatenate([grad_x_pre, rim_x], axis=0), conv_x).astype(bf16)
    grad_bc = conv_back(grad_bc_ext, convolution_bc_taps).astype(bf16)
    grad_dt = grad_steps * jax.nn.sigmoid(dt_raw + dt_bias[:, None])
    return (grad_x, grad_z, grad_bc, grad_dt)


def solution(mesh):
    return jax.shard_map(
        shards,
        mesh=mesh,
        in_specs=(
            P("seq", "head"),
            P("seq", "head"),
            P(None, "seq", None),
            P("head", "seq"),
            P("head"),
            P("head"),
            P("head"),
            P(None, "head"),
            P(),
            P("head"),
            P("seq", "head"),
        ),
        out_specs=(
            P("seq", "head"),
            P("seq", "head"),
            P(None, ("seq", "head"), None),
            P("head", "seq"),
        ),
        check_vma=False,
    )
```

```python
import jax
import jax.numpy as jnp
from jax import lax
from jax.experimental import pallas as pl
from jax.experimental.pallas import tpu as pltpu
from jax.sharding import PartitionSpec as P
import functools

MESH = pl.DeviceIdType.MESH
AXES = ("seq", "head")


def exchange_kernel(axis, n, in_ref, out_ref, land, send_sem, recv_sem):
    me = lax.axis_index(axis)
    coords = {a: lax.axis_index(a) for a in AXES}

    def dev(k):
        return tuple(k if a == axis else coords[a] for a in AXES)

    barrier = pltpu.get_barrier_semaphore()
    for i in range(1, n):
        pl.semaphore_signal(barrier, inc=1, device_id=dev(lax.rem(me + i, n)), device_id_type=MESH)
    pl.semaphore_wait(barrier, n - 1)
    copies = []
    for i in range(1, n):
        peer = lax.rem(me + i, n)
        copy = pltpu.make_async_remote_copy(
            src_ref=in_ref.at[peer],
            dst_ref=land.at[me],
            send_sem=send_sem.at[i],
            recv_sem=recv_sem.at[i],
            device_id=dev(peer),
            device_id_type=MESH,
        )
        copy.start()
        copies.append(copy)
    land[me] = in_ref[me]
    for i in range(1, n):
        copies[i - 1].wait_send()
        src = lax.rem(me + (n - i), n)
        incoming = pltpu.make_async_remote_copy(
            src_ref=in_ref.at[src],
            dst_ref=land.at[src],
            send_sem=send_sem.at[i],
            recv_sem=recv_sem.at[i],
            device_id=dev(src),
            device_id_type=MESH,
        )
        incoming.wait_recv()
    out_ref[...] = land[...]


def exchange(x, axis, cid):
    n = lax.axis_size(axis)
    return pl.pallas_call(
        functools.partial(exchange_kernel, axis, n),
        out_shape=jax.ShapeDtypeStruct(x.shape, x.dtype),
        in_specs=[pl.BlockSpec(memory_space=pltpu.VMEM)],
        out_specs=pl.BlockSpec(memory_space=pltpu.VMEM),
        scratch_shapes=[
            pltpu.VMEM(x.shape, x.dtype),
            pltpu.SemaphoreType.DMA((n,)),
            pltpu.SemaphoreType.DMA((n,)),
        ],
        compiler_params=pltpu.CompilerParams(collective_id=cid, has_side_effects=True),
    )(x)

def _peer_copies(axis, n, src_of, dst, send_sem, recv_sem):
    me = lax.axis_index(axis)
    coords = {a: lax.axis_index(a) for a in AXES}

    def dev(k):
        return tuple(k if a == axis else coords[a] for a in AXES)

    copies = []
    for i in range(1, n):
        peer = lax.rem(me + i, n)
        copy = pltpu.make_async_remote_copy(
            src_ref=src_of(peer),
            dst_ref=dst.at[me],
            send_sem=send_sem.at[i],
            recv_sem=recv_sem.at[i],
            device_id=dev(peer),
            device_id_type=MESH,
        )
        copy.start()
        copies.append(copy)
    return copies


def _peer_waits(axis, n, copies, src_of, dst, send_sem, recv_sem):
    me = lax.axis_index(axis)
    coords = {a: lax.axis_index(a) for a in AXES}

    def dev(k):
        return tuple(k if a == axis else coords[a] for a in AXES)

    for i in range(1, n):
        copies[i - 1].wait_send()
        src = lax.rem(me + (n - i), n)
        incoming = pltpu.make_async_remote_copy(
            src_ref=src_of(src),
            dst_ref=dst.at[src],
            send_sem=send_sem.at[i],
            recv_sem=recv_sem.at[i],
            device_id=dev(src),
            device_id_type=MESH,
        )
        incoming.wait_recv()


def _barrier(axis, n):
    me = lax.axis_index(axis)
    coords = {a: lax.axis_index(a) for a in AXES}
    barrier = pltpu.get_barrier_semaphore()
    for i in range(1, n):
        peer = lax.rem(me + i, n)
        dev = tuple(peer if a == axis else coords[a] for a in AXES)
        pl.semaphore_signal(barrier, inc=1, device_id=dev, device_id_type=MESH)
    pl.semaphore_wait(barrier, n - 1)


def scan_kernel(forward, axis, n, heads, *refs):
    if forward:
        in_ref, out_ref, scale_out, land, res, land2, s1, r1, s2, r2 = refs
    else:
        in_ref, scale_in, out_ref, land, res, land2, s1, r1, s2, r2 = refs
    me = lax.axis_index(axis)
    rows = res.shape[1]
    _barrier(axis, n)
    copies = _peer_copies(axis, n, lambda p: in_ref.at[p], land, s1, r1)
    land[me] = in_ref[me]
    _peer_waits(axis, n, copies, lambda p: in_ref.at[p], land, s1, r1)
    if forward:
        lane = lax.broadcasted_iota(jnp.int32, (1, 128), 1)
        pick = lane == me // (n // heads)
        for k in range(n):
            parts = land[k, rows : rows + 3, :].astype(jnp.float32)
            grow = jnp.exp(parts[0:1] + parts[1:2] + parts[2:3])
            factor = jnp.sum(jnp.where(pick, grow, 0.0), axis=1, keepdims=True)
            scale_out[k] = jnp.broadcast_to(factor, (8, 128))
        acc = jnp.zeros((rows, 128), jnp.float32)
        for k in range(n):
            res[k] = acc.astype(res.dtype)
            acc = scale_out[k][0:1, 0:1] * acc + land[k, :rows, :].astype(jnp.float32)
    else:
        acc = jnp.zeros((rows, 128), jnp.float32)
        for k in reversed(range(n)):
            res[k] = acc.astype(res.dtype)
            acc = land[k].astype(jnp.float32) + scale_in[k][0:1, 0:1] * acc
    copies = _peer_copies(axis, n, lambda p: res.at[p], land2, s2, r2)
    land2[me] = res[me]
    _peer_waits(axis, n, copies, lambda p: res.at[p], land2, s2, r2)
    out_ref[...] = land2[...]


def scan_pieces(x, axis, heads, cid, scales=None):
    n = lax.axis_size(axis)
    forward = scales is None
    rows = x.shape[1] - 16 if forward else x.shape[1]
    piece = (n, rows, 128)
    low = x.dtype
    vm = pl.BlockSpec(memory_space=pltpu.VMEM)
    scratch = [
        pltpu.VMEM(x.shape, low),
        pltpu.VMEM(piece, low),
        pltpu.VMEM(piece, low),
        pltpu.SemaphoreType.DMA((n,)),
        pltpu.SemaphoreType.DMA((n,)),
        pltpu.SemaphoreType.DMA((n,)),
        pltpu.SemaphoreType.DMA((n,)),
    ]
    params = pltpu.CompilerParams(collective_id=cid, has_side_effects=True)
    kern = functools.partial(scan_kernel, forward, axis, n, heads)
    if forward:
        return pl.pallas_call(
            kern,
            out_shape=(jax.ShapeDtypeStruct(piece, low), jax.ShapeDtypeStruct((n, 8, 128), jnp.float32)),
            in_specs=[vm],
            out_specs=(vm, vm),
            scratch_shapes=scratch,
            compiler_params=params,
        )(x)
    return pl.pallas_call(
        kern,
        out_shape=jax.ShapeDtypeStruct(piece, low),
        in_specs=[vm, vm],
        out_specs=vm,
        scratch_shapes=scratch,
        compiler_params=params,
    )(x, scales)


def tail_kernel(n, hn, in_ref, rim_ref, out_ref, rim_out, land, send, rim_land, s1, r1, s2, r2):
    me = lax.axis_index("seq")
    hme = lax.axis_index("head")
    prev = lax.rem(me + n - 1, n)
    nxt = lax.rem(me + 1, n)
    barrier = pltpu.get_barrier_semaphore()
    for i in range(1, hn):
        pl.semaphore_signal(barrier, inc=1, device_id=(me, lax.rem(hme + i, hn)), device_id_type=MESH)
    pl.semaphore_signal(barrier, inc=1, device_id=(prev, hme), device_id_type=MESH)
    pl.semaphore_signal(barrier, inc=1, device_id=(nxt, hme), device_id_type=MESH)
    pl.semaphore_wait(barrier, hn + 1)
    rim_copy = pltpu.make_async_remote_copy(
        src_ref=rim_ref, dst_ref=rim_land, send_sem=s2.at[0], recv_sem=r2.at[0],
        device_id=(prev, hme), device_id_type=MESH,
    )
    rim_copy.start()
    send[...] = in_ref[...]
    rim_copy.wait_send()
    rim_copy.wait_recv()
    keep = (1 - me // (n - 1)).astype(jnp.float32)
    rows = in_ref.shape[1] // 2
    nst = in_ref.shape[2]
    width = rim_ref.shape[1] - nst
    rim_bc = rim_land[0:8, width:] * keep
    last = hn - 1
    send[last, 8:11, :] = send[last, 8:11, :] + rim_bc[0:3]
    send[last, rows + 8 : rows + 11, :] = send[last, rows + 8 : rows + 11, :] + rim_bc[3:6]
    rim_out[...] = rim_land[0:8, 0:width] * keep
    src_of = lambda p: send.at[p]
    copies = []
    for i in range(1, hn):
        peer = lax.rem(hme + i, hn)
        copy = pltpu.make_async_remote_copy(
            src_ref=send.at[peer], dst_ref=land.at[hme], send_sem=s1.at[i], recv_sem=r1.at[i],
            device_id=(me, peer), device_id_type=MESH,
        )
        copy.start()
        copies.append(copy)
    land[hme] = send[hme]
    for i in range(1, hn):
        copies[i - 1].wait_send()
        src = lax.rem(hme + (hn - i), hn)
        incoming = pltpu.make_async_remote_copy(
            src_ref=send.at[src], dst_ref=land.at[src], send_sem=s1.at[i], recv_sem=r1.at[i],
            device_id=(me, src), device_id_type=MESH,
        )
        incoming.wait_recv()
    total = land[0]
    for j in range(1, hn):
        total = total + land[j]
    out_ref[...] = total


def tail_exchange(pieces, rim, cid):
    n = lax.axis_size("seq")
    hn = lax.axis_size("head")
    vm = pl.BlockSpec(memory_space=pltpu.VMEM)
    width = rim.shape[1] - pieces.shape[2]
    return pl.pallas_call(
        functools.partial(tail_kernel, n, hn),
        out_shape=(
            jax.ShapeDtypeStruct(pieces.shape[1:], jnp.float32),
            jax.ShapeDtypeStruct((8, width), jnp.float32),
        ),
        in_specs=[vm, vm],
        out_specs=(vm, vm),
        scratch_shapes=[
            pltpu.VMEM(pieces.shape, jnp.float32),
            pltpu.VMEM(pieces.shape, jnp.float32),
            pltpu.VMEM(rim.shape, jnp.float32),
            pltpu.SemaphoreType.DMA((hn,)),
            pltpu.SemaphoreType.DMA((hn,)),
            pltpu.SemaphoreType.DMA((1,)),
            pltpu.SemaphoreType.DMA((1,)),
        ],
        compiler_params=pltpu.CompilerParams(collective_id=cid, has_side_effects=True),
    )(pieces, rim)


INNER = 16384


EPS = 1e-05
HIGH = lax.Precision.HIGHEST


def passed_along(block, axis, distance):
    devices = range(lax.axis_size(axis))
    route = [(i - distance, i) for i in devices if i - distance in devices]
    return lax.ppermute(block, axis, route)


def silu_grad(value):
    sigma = jax.nn.sigmoid(value)
    return sigma * (1.0 + value * (1.0 - sigma))


def conv_rows(extended, weight_matrix):
    length = extended.shape[-2] - 3
    summed = weight_matrix[..., 0, :][..., None, :] * extended[..., 0:length, :]
    for offset in range(1, 4):
        summed = (
            summed
            + weight_matrix[..., offset, :][..., None, :]
            * extended[..., offset : offset + length, :]
        )
    return summed


def conv_back(extended, weight_matrix):
    length = extended.shape[-2] - 3
    summed = weight_matrix[..., 0, :][..., None, :] * extended[..., 3 : 3 + length, :]
    for offset in range(1, 4):
        summed = (
            summed
            + weight_matrix[..., offset, :][..., None, :]
            * extended[..., 3 - offset : 3 - offset + length, :]
        )
    return summed


def to_pieces(state, count):
    heads, nstate, width = state.shape
    return state.reshape(count, heads * nstate // count, width)


def from_pieces(pieces, heads):
    count, rows, width = pieces.shape
    return pieces.reshape(heads, count * rows // heads, width)


def scan_forward(totals, local_state):
    count = lax.axis_size("seq")
    heads, nstate, width = local_state.shape
    pieces = to_pieces(local_state, count)
    high = lax.reduce_precision(totals, exponent_bits=8, mantissa_bits=7)
    rest = totals - high
    middle = lax.reduce_precision(rest, exponent_bits=8, mantissa_bits=7)
    parts = jnp.stack([high, middle, rest - middle])
    tot_row = jnp.pad(parts, ((0, 13), (0, width - heads)))
    tot_row = jnp.broadcast_to(tot_row, (count, 16, width))
    sent = jnp.concatenate([pieces, tot_row], axis=1).astype(jnp.bfloat16)
    back, scales = scan_pieces(sent, "seq", heads, 0)
    return from_pieces(back, heads).astype(jnp.float32), scales


def scan_backward(scales, state_grad):
    count = lax.axis_size("seq")
    heads = state_grad.shape[0]
    pieces = to_pieces(state_grad, count).astype(jnp.bfloat16)
    back = scan_pieces(pieces, "seq", heads, 1, scales)
    return from_pieces(back, heads).astype(jnp.float32)


def shards(
    x_input,
    z_input,
    bc_input,
    dt_raw,
    dt_bias,
    a_log,
    d_skip,
    conv_x,
    convolution_bc_taps,
    rescale_factor,
    grad_out,
):
    length = x_input.shape[0]
    channels = x_input.shape[1]
    head_count = dt_raw.shape[0]
    width = channels // head_count
    f32 = jnp.float32
    bf16 = jnp.bfloat16
    decay_rate = -jnp.exp(a_log)
    step_size = jax.nn.softplus(dt_raw + dt_bias[:, None])
    causal = jnp.tril(jnp.ones((length, length), dtype=bool))
    nstate = bc_input.shape[2]
    rows_last = jnp.concatenate(
        [x_input[length - 3 :], jnp.moveaxis(bc_input[:, length - 3 :], 0, 1).reshape(3, 2 * nstate)],
        axis=1,
    )
    rows_prior = passed_along(rows_last, "seq", 1)
    x_ext = jnp.concatenate([rows_prior[:, :channels], x_input], axis=0)
    bc_prior = jnp.moveaxis(rows_prior[:, channels:].reshape(3, 2, nstate), 0, 1)
    bc_ext = jnp.concatenate([bc_prior, bc_input], axis=1)
    x_pre = conv_rows(x_ext.astype(f32), conv_x)
    bc_pre = conv_rows(bc_ext.astype(f32), convolution_bc_taps)
    x_rows = jax.nn.silu(x_pre).astype(bf16)
    bc_rows = jax.nn.silu(bc_pre).astype(bf16)
    b_rows = bc_rows[0]
    c_rows = bc_rows[1]
    gram = jnp.dot(c_rows, b_rows.T, preferred_element_type=f32)
    x_heads = x_rows.reshape(length, head_count, width)

    cumul = jnp.cumsum(decay_rate[:, None] * step_size, axis=1)
    totals = cumul[:, -1]
    trailing = jnp.exp(cumul[:, -1:] - cumul)
    tail_step = trailing * step_size
    weighted_b = (tail_step[:, :, None] * b_rows.astype(f32)[None]).astype(bf16)
    local_state = jnp.einsum("hsn,shp->hnp", weighted_b, x_heads, preferred_element_type=f32)

    state_exact, weight = scan_forward(totals, local_state)
    state_low = state_exact.astype(bf16)

    between = cumul[:, :, None] - cumul[:, None, :]
    decay = jnp.where(causal[None], jnp.exp(jnp.minimum(between, 0.0)), 0.0)
    mixer_low = (gram[None] * decay * step_size[:, None, :]).astype(bf16)
    intra = jnp.einsum("hts,shp->thp", mixer_low, x_heads, preferred_element_type=f32)
    handed = jnp.einsum("tn,hnp->thp", c_rows, state_low, preferred_element_type=f32)
    lifted = jnp.exp(cumul)
    mixed_heads = (
        intra + lifted.T[:, :, None] * handed + d_skip[None, :, None] * x_heads.astype(f32)
    )
    mixed_out = mixed_heads.reshape(length, channels)

    z_rows = z_input.astype(f32)
    gate_value = jax.nn.silu(z_rows)
    gated = mixed_out * gate_value
    scaled = grad_out.astype(f32) * rescale_factor
    hcount = lax.axis_size("head")
    own_sums = jnp.stack([jnp.sum(gated * gated, axis=1), jnp.sum(scaled * gated, axis=1)])
    own_sums = jnp.concatenate([own_sums, jnp.zeros((6, length), f32)], axis=0)
    sums = jnp.sum(exchange(jnp.broadcast_to(own_sums, (hcount,) + own_sums.shape), "head", 3), axis=0)
    inv_rms = lax.rsqrt(sums[0] / INNER + EPS)
    normed = gated * inv_rms[:, None]
    mean_dot = inv_rms * sums[1] / INNER
    grad_gated = inv_rms[:, None] * (scaled - normed * mean_dot[:, None])
    grad_z = (grad_gated * mixed_out * silu_grad(z_rows)).astype(bf16)
    grad_mixed = (grad_gated * gate_value).astype(bf16)
    grad_heads = grad_mixed.reshape(length, head_count, width)

    lifted_c = (lifted[:, :, None] * c_rows.astype(f32)[None]).astype(bf16)
    state_grad = jnp.einsum("htn,thp->hnp", lifted_c, grad_heads, preferred_element_type=f32)
    out_exact = scan_backward(weight, state_grad)
    out_low = out_exact.astype(bf16)

    grad_mix = jnp.einsum("thp,shp->hts", grad_heads, x_heads, preferred_element_type=f32)
    decayed = grad_mix * decay
    zterm = decayed * step_size[:, None, :]
    gram_grad = zterm * gram[None]
    reached = jnp.einsum("shp,hnp->hsn", x_heads, out_low, preferred_element_type=f32)
    inner_b = jnp.sum(b_rows.astype(f32)[None] * reached, axis=2)
    state_term = tail_step * inner_b
    grad_cumul = jnp.sum(gram_grad, axis=2) - jnp.sum(gram_grad, axis=1)
    carried_dot = jnp.sum(grad_heads.astype(f32) * handed, axis=2).T
    grad_cumul = grad_cumul + lifted * carried_dot - state_term
    end_grad = jnp.sum(state_term, axis=1) + jnp.exp(totals) * jnp.sum(
        out_exact * state_exact, axis=(1, 2)
    )
    grad_cumul = grad_cumul.at[:, -1].add(end_grad)
    grad_log = jnp.cumsum(grad_cumul[:, ::-1], axis=1)[:, ::-1]
    grad_steps = (
        jnp.sum(decayed * gram[None], axis=1)
        + trailing * inner_b
        + decay_rate[:, None] * grad_log
    )
    grad_x_heads = jnp.einsum("hts,thp->shp", mixer_low, grad_heads, preferred_element_type=f32)
    grad_x_heads = (
        grad_x_heads
        + d_skip[None, :, None] * grad_heads.astype(f32)
        + jnp.einsum("hsn,hnp->shp", weighted_b, out_low, preferred_element_type=f32)
    )
    grad_c_heads = lifted[:, :, None] * jnp.einsum(
        "thp,hnp->htn", grad_heads, state_low, preferred_element_type=f32
    )
    grad_b_heads = tail_step[:, :, None] * reached
    grad_sum = jnp.sum(zterm, axis=0)
    grad_c = jnp.sum(grad_c_heads, axis=0) + jnp.dot(grad_sum, b_rows.astype(f32), precision=HIGH)
    grad_b = jnp.sum(grad_b_heads, axis=0) + jnp.dot(
        grad_sum.T, c_rows.astype(f32), precision=HIGH
    )
    grad_bc_rows = jnp.stack([grad_b, grad_c])
    grad_x_rows = grad_x_heads.reshape(length, channels)

    grad_x_pre = grad_x_rows * silu_grad(x_pre)
    hcount = lax.axis_size("head")
    row_share = length // hcount
    hidx = lax.axis_index("head")
    first_row = hidx * row_share
    picks = []
    for h in range(hcount):
        own = [h * row_share + i for i in range(row_share + 3)]
        own = [r if r < length else length for r in own]
        picks.append(own + [length] * (16 - row_share - 3))
    picks = jnp.array(picks, jnp.int32)
    piece_rows = picks.shape[1]
    bc_rows_z = jnp.concatenate([grad_bc_rows, jnp.zeros((2, 1, nstate), f32)], axis=1)
    bc_pieces = jnp.moveaxis(jnp.take(bc_rows_z, picks.reshape(-1), axis=1).reshape(2, hcount, piece_rows, -1), 1, 0)
    top = (grad_bc_rows[:, :3] * silu_grad(bc_pre[:, :3])).reshape(6, nstate)
    rim_send = jnp.concatenate(
        [jnp.pad(grad_x_pre[:3], ((0, 5), (0, 0))), jnp.pad(top, ((0, 2), (0, 0)))], axis=1
    )
    summed, rim_got = tail_exchange(bc_pieces.reshape(hcount, 2 * piece_rows, -1), rim_send, 2)
    grad_bc_mine = summed.reshape(2, piece_rows, -1)[:, : row_share + 3]
    bc_pre_pad = jnp.concatenate([bc_pre, jnp.zeros((2, 3, nstate), f32)], axis=1)
    bc_pre_mine = lax.dynamic_slice_in_dim(bc_pre_pad, first_row, row_share + 3, 1)
    in_rim = (hidx == hcount - 1) & (jnp.arange(row_share + 3) >= row_share)
    grad_bc_ext = grad_bc_mine * jnp.where(in_rim[None, :, None], 1.0, silu_grad(bc_pre_mine))
    rim_x = rim_got[:3]
    grad_x = conv_back(jnp.concatenate([grad_x_pre, rim_x], axis=0), conv_x).astype(bf16)
    grad_bc = conv_back(grad_bc_ext, convolution_bc_taps).astype(bf16)
    grad_dt = grad_steps * jax.nn.sigmoid(dt_raw + dt_bias[:, None])
    return (grad_x, grad_z, grad_bc, grad_dt)


def solution(mesh):
    return jax.shard_map(
        shards,
        mesh=mesh,
        in_specs=(
            P("seq", "head"),
            P("seq", "head"),
            P(None, "seq", None),
            P("head", "seq"),
            P("head"),
            P("head"),
            P("head"),
            P(None, "head"),
            P(),
            P("head"),
            P("seq", "head"),
        ),
        out_specs=(
            P("seq", "head"),
            P("seq", "head"),
            P(None, ("seq", "head"), None),
            P("head", "seq"),
        ),
        check_vma=False,
    )
```

```python
import jax
import jax.numpy as jnp
from jax import lax
from jax.experimental import pallas as pl
from jax.experimental.pallas import tpu as pltpu
from jax.sharding import PartitionSpec as P
import functools

MESH = pl.DeviceIdType.MESH
AXES = ("seq", "head")


def exchange_kernel(axis, n, in_ref, out_ref, land, send_sem, recv_sem):
    me = lax.axis_index(axis)
    coords = {a: lax.axis_index(a) for a in AXES}

    def dev(k):
        return tuple(k if a == axis else coords[a] for a in AXES)

    barrier = pltpu.get_barrier_semaphore()
    for i in range(1, n):
        pl.semaphore_signal(barrier, inc=1, device_id=dev(lax.rem(me + i, n)), device_id_type=MESH)
    pl.semaphore_wait(barrier, n - 1)
    copies = []
    for i in range(1, n):
        peer = lax.rem(me + i, n)
        copy = pltpu.make_async_remote_copy(
            src_ref=in_ref.at[peer],
            dst_ref=land.at[me],
            send_sem=send_sem.at[i],
            recv_sem=recv_sem.at[i],
            device_id=dev(peer),
            device_id_type=MESH,
        )
        copy.start()
        copies.append(copy)
    land[me] = in_ref[me]
    for i in range(1, n):
        copies[i - 1].wait_send()
        src = lax.rem(me + (n - i), n)
        incoming = pltpu.make_async_remote_copy(
            src_ref=in_ref.at[src],
            dst_ref=land.at[src],
            send_sem=send_sem.at[i],
            recv_sem=recv_sem.at[i],
            device_id=dev(src),
            device_id_type=MESH,
        )
        incoming.wait_recv()
    out_ref[...] = land[...]


def exchange(x, axis, cid):
    n = lax.axis_size(axis)
    return pl.pallas_call(
        functools.partial(exchange_kernel, axis, n),
        out_shape=jax.ShapeDtypeStruct(x.shape, x.dtype),
        in_specs=[pl.BlockSpec(memory_space=pltpu.VMEM)],
        out_specs=pl.BlockSpec(memory_space=pltpu.VMEM),
        scratch_shapes=[
            pltpu.VMEM(x.shape, x.dtype),
            pltpu.SemaphoreType.DMA((n,)),
            pltpu.SemaphoreType.DMA((n,)),
        ],
        compiler_params=pltpu.CompilerParams(collective_id=cid, has_side_effects=True),
    )(x)

def _peer_copies(axis, n, src_of, dst, send_sem, recv_sem):
    me = lax.axis_index(axis)
    coords = {a: lax.axis_index(a) for a in AXES}

    def dev(k):
        return tuple(k if a == axis else coords[a] for a in AXES)

    copies = []
    for i in range(1, n):
        peer = lax.rem(me + i, n)
        copy = pltpu.make_async_remote_copy(
            src_ref=src_of(peer),
            dst_ref=dst.at[me],
            send_sem=send_sem.at[i],
            recv_sem=recv_sem.at[i],
            device_id=dev(peer),
            device_id_type=MESH,
        )
        copy.start()
        copies.append(copy)
    return copies


def _peer_waits(axis, n, copies, src_of, dst, send_sem, recv_sem):
    me = lax.axis_index(axis)
    coords = {a: lax.axis_index(a) for a in AXES}

    def dev(k):
        return tuple(k if a == axis else coords[a] for a in AXES)

    for i in range(1, n):
        copies[i - 1].wait_send()
        src = lax.rem(me + (n - i), n)
        incoming = pltpu.make_async_remote_copy(
            src_ref=src_of(src),
            dst_ref=dst.at[src],
            send_sem=send_sem.at[i],
            recv_sem=recv_sem.at[i],
            device_id=dev(src),
            device_id_type=MESH,
        )
        incoming.wait_recv()


def _barrier(axis, n):
    me = lax.axis_index(axis)
    coords = {a: lax.axis_index(a) for a in AXES}
    barrier = pltpu.get_barrier_semaphore()
    for i in range(1, n):
        peer = lax.rem(me + i, n)
        dev = tuple(peer if a == axis else coords[a] for a in AXES)
        pl.semaphore_signal(barrier, inc=1, device_id=dev, device_id_type=MESH)
    pl.semaphore_wait(barrier, n - 1)


def scan_kernel(forward, axis, n, heads, *refs):
    if forward:
        in_ref, out_ref, scale_out, land, res, land2, s1, r1, s2, r2 = refs
    else:
        in_ref, scale_in, out_ref, land, res, land2, s1, r1, s2, r2 = refs
    me = lax.axis_index(axis)
    rows = res.shape[1]
    _barrier(axis, n)
    copies = _peer_copies(axis, n, lambda p: in_ref.at[p], land, s1, r1)
    land[me] = in_ref[me]
    _peer_waits(axis, n, copies, lambda p: in_ref.at[p], land, s1, r1)
    if forward:
        lane = lax.broadcasted_iota(jnp.int32, (1, 128), 1)
        pick = lane == me // (n // heads)
        for k in range(n):
            parts = land[k, rows : rows + 3, :].astype(jnp.float32)
            grow = jnp.exp(parts[0:1] + parts[1:2] + parts[2:3])
            factor = jnp.sum(jnp.where(pick, grow, 0.0), axis=1, keepdims=True)
            scale_out[k] = jnp.broadcast_to(factor, (8, 128))
        acc = jnp.zeros((rows, 128), jnp.float32)
        for k in range(n):
            res[k] = acc.astype(res.dtype)
            acc = scale_out[k][0:1, 0:1] * acc + land[k, :rows, :].astype(jnp.float32)
    else:
        acc = jnp.zeros((rows, 128), jnp.float32)
        for k in reversed(range(n)):
            res[k] = acc.astype(res.dtype)
            acc = land[k].astype(jnp.float32) + scale_in[k][0:1, 0:1] * acc
    copies = _peer_copies(axis, n, lambda p: res.at[p], land2, s2, r2)
    land2[me] = res[me]
    _peer_waits(axis, n, copies, lambda p: res.at[p], land2, s2, r2)
    out_ref[...] = land2[...]


def scan_pieces(x, axis, heads, cid, scales=None):
    n = lax.axis_size(axis)
    forward = scales is None
    rows = x.shape[1] - 16 if forward else x.shape[1]
    piece = (n, rows, 128)
    low = x.dtype
    vm = pl.BlockSpec(memory_space=pltpu.VMEM)
    scratch = [
        pltpu.VMEM(x.shape, low),
        pltpu.VMEM(piece, low),
        pltpu.VMEM(piece, low),
        pltpu.SemaphoreType.DMA((n,)),
        pltpu.SemaphoreType.DMA((n,)),
        pltpu.SemaphoreType.DMA((n,)),
        pltpu.SemaphoreType.DMA((n,)),
    ]
    params = pltpu.CompilerParams(collective_id=cid, has_side_effects=True)
    kern = functools.partial(scan_kernel, forward, axis, n, heads)
    if forward:
        return pl.pallas_call(
            kern,
            out_shape=(jax.ShapeDtypeStruct(piece, low), jax.ShapeDtypeStruct((n, 8, 128), jnp.float32)),
            in_specs=[vm],
            out_specs=(vm, vm),
            scratch_shapes=scratch,
            compiler_params=params,
        )(x)
    return pl.pallas_call(
        kern,
        out_shape=jax.ShapeDtypeStruct(piece, low),
        in_specs=[vm, vm],
        out_specs=vm,
        scratch_shapes=scratch,
        compiler_params=params,
    )(x, scales)


def tail_kernel(n, hn, in_ref, rim_ref, out_ref, rim_out, land, send, rim_land, s1, r1, s2, r2):
    me = lax.axis_index("seq")
    hme = lax.axis_index("head")
    prev = lax.rem(me + n - 1, n)
    nxt = lax.rem(me + 1, n)
    barrier = pltpu.get_barrier_semaphore()
    for i in range(1, hn):
        pl.semaphore_signal(barrier, inc=1, device_id=(me, lax.rem(hme + i, hn)), device_id_type=MESH)
    pl.semaphore_signal(barrier, inc=1, device_id=(prev, hme), device_id_type=MESH)
    pl.semaphore_signal(barrier, inc=1, device_id=(nxt, hme), device_id_type=MESH)
    pl.semaphore_wait(barrier, hn + 1)
    rim_copy = pltpu.make_async_remote_copy(
        src_ref=rim_ref, dst_ref=rim_land, send_sem=s2.at[0], recv_sem=r2.at[0],
        device_id=(prev, hme), device_id_type=MESH,
    )
    rim_copy.start()
    send[...] = in_ref[...]
    rim_copy.wait_send()
    rim_copy.wait_recv()
    keep = (1 - me // (n - 1)).astype(jnp.float32)
    rows = in_ref.shape[1] // 2
    nst = in_ref.shape[2]
    width = rim_ref.shape[1] - nst
    rim_bc = rim_land[0:8, width:] * keep
    last = hn - 1
    send[last, 8:11, :] = send[last, 8:11, :] + rim_bc[0:3]
    send[last, rows + 8 : rows + 11, :] = send[last, rows + 8 : rows + 11, :] + rim_bc[3:6]
    rim_out[...] = rim_land[0:8, 0:width] * keep
    src_of = lambda p: send.at[p]
    copies = []
    for i in range(1, hn):
        peer = lax.rem(hme + i, hn)
        copy = pltpu.make_async_remote_copy(
            src_ref=send.at[peer], dst_ref=land.at[hme], send_sem=s1.at[i], recv_sem=r1.at[i],
            device_id=(me, peer), device_id_type=MESH,
        )
        copy.start()
        copies.append(copy)
    land[hme] = send[hme]
    for i in range(1, hn):
        copies[i - 1].wait_send()
        src = lax.rem(hme + (hn - i), hn)
        incoming = pltpu.make_async_remote_copy(
            src_ref=send.at[src], dst_ref=land.at[src], send_sem=s1.at[i], recv_sem=r1.at[i],
            device_id=(me, src), device_id_type=MESH,
        )
        incoming.wait_recv()
    total = land[0]
    for j in range(1, hn):
        total = total + land[j]
    out_ref[...] = total


def tail_exchange(pieces, rim, cid):
    n = lax.axis_size("seq")
    hn = lax.axis_size("head")
    vm = pl.BlockSpec(memory_space=pltpu.VMEM)
    width = rim.shape[1] - pieces.shape[2]
    return pl.pallas_call(
        functools.partial(tail_kernel, n, hn),
        out_shape=(
            jax.ShapeDtypeStruct(pieces.shape[1:], jnp.float32),
            jax.ShapeDtypeStruct((8, width), jnp.float32),
        ),
        in_specs=[vm, vm],
        out_specs=(vm, vm),
        scratch_shapes=[
            pltpu.VMEM(pieces.shape, jnp.float32),
            pltpu.VMEM(pieces.shape, jnp.float32),
            pltpu.VMEM(rim.shape, jnp.float32),
            pltpu.SemaphoreType.DMA((hn,)),
            pltpu.SemaphoreType.DMA((hn,)),
            pltpu.SemaphoreType.DMA((1,)),
            pltpu.SemaphoreType.DMA((1,)),
        ],
        compiler_params=pltpu.CompilerParams(collective_id=cid, has_side_effects=True),
    )(pieces, rim)


INNER = 16384


EPS = 1e-05
HIGH = lax.Precision.HIGHEST


def passed_along(block, axis, distance):
    devices = range(lax.axis_size(axis))
    route = [(i - distance, i) for i in devices if i - distance in devices]
    return lax.ppermute(block, axis, route)


def silu_grad(value):
    sigma = jax.nn.sigmoid(value)
    return sigma * (1.0 + value * (1.0 - sigma))


def conv_rows(extended, weight_matrix):
    length = extended.shape[-2] - 3
    summed = weight_matrix[..., 0, :][..., None, :] * extended[..., 0:length, :]
    for offset in range(1, 4):
        summed = (
            summed
            + weight_matrix[..., offset, :][..., None, :]
            * extended[..., offset : offset + length, :]
        )
    return summed


def conv_back(extended, weight_matrix):
    length = extended.shape[-2] - 3
    summed = weight_matrix[..., 0, :][..., None, :] * extended[..., 3 : 3 + length, :]
    for offset in range(1, 4):
        summed = (
            summed
            + weight_matrix[..., offset, :][..., None, :]
            * extended[..., 3 - offset : 3 - offset + length, :]
        )
    return summed


def to_pieces(state, count):
    heads, nstate, width = state.shape
    return state.reshape(count, heads * nstate // count, width)


def from_pieces(pieces, heads):
    count, rows, width = pieces.shape
    return pieces.reshape(heads, count * rows // heads, width)


def scan_forward(totals, local_state):
    count = lax.axis_size("seq")
    heads, nstate, width = local_state.shape
    pieces = to_pieces(local_state, count)
    high = lax.reduce_precision(totals, exponent_bits=8, mantissa_bits=7)
    rest = totals - high
    middle = lax.reduce_precision(rest, exponent_bits=8, mantissa_bits=7)
    parts = jnp.stack([high, middle, rest - middle])
    tot_row = jnp.pad(parts, ((0, 13), (0, width - heads)))
    tot_row = jnp.broadcast_to(tot_row, (count, 16, width))
    sent = jnp.concatenate([pieces, tot_row], axis=1).astype(jnp.bfloat16)
    back, scales = scan_pieces(sent, "seq", heads, 0)
    return from_pieces(back, heads).astype(jnp.float32), scales


def scan_backward(scales, state_grad):
    count = lax.axis_size("seq")
    heads = state_grad.shape[0]
    pieces = to_pieces(state_grad, count).astype(jnp.bfloat16)
    back = scan_pieces(pieces, "seq", heads, 1, scales)
    return from_pieces(back, heads).astype(jnp.float32)


def shards(
    x_input,
    z_input,
    bc_input,
    dt_raw,
    dt_bias,
    a_log,
    d_skip,
    conv_x,
    convolution_bc_taps,
    rescale_factor,
    grad_out,
):
    length = x_input.shape[0]
    channels = x_input.shape[1]
    head_count = dt_raw.shape[0]
    width = channels // head_count
    f32 = jnp.float32
    bf16 = jnp.bfloat16
    decay_rate = -jnp.exp(a_log)
    step_size = jax.nn.softplus(dt_raw + dt_bias[:, None])
    causal = jnp.tril(jnp.ones((length, length), dtype=bool))
    nstate = bc_input.shape[2]
    rows_last = jnp.concatenate(
        [x_input[length - 3 :], jnp.moveaxis(bc_input[:, length - 3 :], 0, 1).reshape(3, 2 * nstate)],
        axis=1,
    )
    rows_prior = passed_along(rows_last, "seq", 1)
    x_ext = jnp.concatenate([rows_prior[:, :channels], x_input], axis=0)
    bc_prior = jnp.moveaxis(rows_prior[:, channels:].reshape(3, 2, nstate), 0, 1)
    bc_ext = jnp.concatenate([bc_prior, bc_input], axis=1)
    x_pre = conv_rows(x_ext.astype(f32), conv_x)
    bc_pre = conv_rows(bc_ext.astype(f32), convolution_bc_taps)
    x_rows = jax.nn.silu(x_pre).astype(bf16)
    bc_rows = jax.nn.silu(bc_pre).astype(bf16)
    b_rows = bc_rows[0]
    c_rows = bc_rows[1]
    gram = jnp.dot(c_rows, b_rows.T, preferred_element_type=f32)
    x_heads = x_rows.reshape(length, head_count, width)

    cumul = jnp.cumsum(decay_rate[:, None] * step_size, axis=1)
    totals = cumul[:, -1]
    trailing = jnp.exp(cumul[:, -1:] - cumul)
    tail_step = trailing * step_size
    weighted_b = (tail_step[:, :, None] * b_rows.astype(f32)[None]).astype(bf16)
    local_state = jnp.einsum("hsn,shp->hnp", weighted_b, x_heads, preferred_element_type=f32)

    state_exact, weight = scan_forward(totals, local_state)
    state_low = state_exact.astype(bf16)

    between = cumul[:, :, None] - cumul[:, None, :]
    decay = jnp.where(causal[None], jnp.exp(jnp.minimum(between, 0.0)), 0.0)
    mixer_low = (gram[None] * decay * step_size[:, None, :]).astype(bf16)
    intra = jnp.einsum("hts,shp->thp", mixer_low, x_heads, preferred_element_type=f32)
    handed = jnp.einsum("tn,hnp->thp", c_rows, state_low, preferred_element_type=f32)
    lifted = jnp.exp(cumul)
    mixed_heads = (
        intra + lifted.T[:, :, None] * handed + d_skip[None, :, None] * x_heads.astype(f32)
    )
    mixed_out = mixed_heads.reshape(length, channels)

    z_rows = z_input.astype(f32)
    gate_value = jax.nn.silu(z_rows)
    gated = mixed_out * gate_value
    scaled = grad_out.astype(f32) * rescale_factor
    hcount = lax.axis_size("head")
    own_sums = jnp.stack([jnp.sum(gated * gated, axis=1), jnp.sum(scaled * gated, axis=1)])
    own_sums = jnp.concatenate([own_sums, jnp.zeros((6, length), f32)], axis=0)
    sums = jnp.sum(exchange(jnp.broadcast_to(own_sums, (hcount,) + own_sums.shape), "head", 3), axis=0)
    inv_rms = lax.rsqrt(sums[0] / INNER + EPS)
    normed = gated * inv_rms[:, None]
    mean_dot = inv_rms * sums[1] / INNER
    grad_gated = inv_rms[:, None] * (scaled - normed * mean_dot[:, None])
    grad_z = (grad_gated * mixed_out * silu_grad(z_rows)).astype(bf16)
    grad_mixed = (grad_gated * gate_value).astype(bf16)
    grad_heads = grad_mixed.reshape(length, head_count, width)

    lifted_c = (lifted[:, :, None] * c_rows.astype(f32)[None]).astype(bf16)
    state_grad = jnp.einsum("htn,thp->hnp", lifted_c, grad_heads, preferred_element_type=f32)
    out_exact = scan_backward(weight, state_grad)
    out_low = out_exact.astype(bf16)

    grad_mix = jnp.einsum("thp,shp->hts", grad_heads, x_heads, preferred_element_type=f32)
    decayed = grad_mix * decay
    zterm = decayed * step_size[:, None, :]
    gram_grad = zterm * gram[None]
    reached = jnp.einsum("shp,hnp->hsn", x_heads, out_low, preferred_element_type=f32)
    inner_b = jnp.sum(b_rows.astype(f32)[None] * reached, axis=2)
    state_term = tail_step * inner_b
    grad_cumul = jnp.sum(gram_grad, axis=2) - jnp.sum(gram_grad, axis=1)
    carried_dot = jnp.sum(grad_heads.astype(f32) * handed, axis=2).T
    grad_cumul = grad_cumul + lifted * carried_dot - state_term
    end_grad = jnp.sum(state_term, axis=1) + jnp.exp(totals) * jnp.sum(
        out_exact * state_exact, axis=(1, 2)
    )
    grad_cumul = grad_cumul.at[:, -1].add(end_grad)
    grad_log = jnp.cumsum(grad_cumul[:, ::-1], axis=1)[:, ::-1]
    grad_steps = (
        jnp.sum(decayed * gram[None], axis=1)
        + trailing * inner_b
        + decay_rate[:, None] * grad_log
    )
    grad_x_heads = jnp.einsum("hts,thp->shp", mixer_low, grad_heads, preferred_element_type=f32)
    grad_x_heads = (
        grad_x_heads
        + d_skip[None, :, None] * grad_heads.astype(f32)
        + jnp.einsum("hsn,hnp->shp", weighted_b, out_low, preferred_element_type=f32)
    )
    grad_c_heads = lifted[:, :, None] * jnp.einsum(
        "thp,hnp->htn", grad_heads, state_low, preferred_element_type=f32
    )
    grad_b_heads = tail_step[:, :, None] * reached
    grad_sum = jnp.sum(zterm, axis=0)
    grad_c = jnp.sum(grad_c_heads, axis=0) + jnp.dot(grad_sum, b_rows.astype(f32), precision=HIGH)
    grad_b = jnp.sum(grad_b_heads, axis=0) + jnp.dot(
        grad_sum.T, c_rows.astype(f32), precision=HIGH
    )
    grad_bc_rows = jnp.stack([grad_b, grad_c])
    grad_x_rows = grad_x_heads.reshape(length, channels)

    grad_x_pre = grad_x_rows * silu_grad(x_pre)
    hcount = lax.axis_size("head")
    row_share = length // hcount
    hidx = lax.axis_index("head")
    first_row = hidx * row_share
    picks = []
    for h in range(hcount):
        own = [h * row_share + i for i in range(row_share + 3)]
        own = [r if r < length else length for r in own]
        picks.append(own + [length] * (12 - row_share - 3))
    picks = jnp.array(picks, jnp.int32)
    piece_rows = picks.shape[1]
    bc_rows_z = jnp.concatenate([grad_bc_rows, jnp.zeros((2, 1, nstate), f32)], axis=1)
    bc_pieces = jnp.moveaxis(jnp.take(bc_rows_z, picks.reshape(-1), axis=1).reshape(2, hcount, piece_rows, -1), 1, 0)
    top = (grad_bc_rows[:, :3] * silu_grad(bc_pre[:, :3])).reshape(6, nstate)
    rim_send = jnp.concatenate(
        [jnp.pad(grad_x_pre[:3], ((0, 5), (0, 0))), jnp.pad(top, ((0, 2), (0, 0)))], axis=1
    )
    summed, rim_got = tail_exchange(bc_pieces.reshape(hcount, 2 * piece_rows, -1), rim_send, 2)
    grad_bc_mine = summed.reshape(2, piece_rows, -1)[:, : row_share + 3]
    bc_pre_pad = jnp.concatenate([bc_pre, jnp.zeros((2, 3, nstate), f32)], axis=1)
    bc_pre_mine = lax.dynamic_slice_in_dim(bc_pre_pad, first_row, row_share + 3, 1)
    in_rim = (hidx == hcount - 1) & (jnp.arange(row_share + 3) >= row_share)
    grad_bc_ext = grad_bc_mine * jnp.where(in_rim[None, :, None], 1.0, silu_grad(bc_pre_mine))
    rim_x = rim_got[:3]
    grad_x = conv_back(jnp.concatenate([grad_x_pre, rim_x], axis=0), conv_x).astype(bf16)
    grad_bc = conv_back(grad_bc_ext, convolution_bc_taps).astype(bf16)
    grad_dt = grad_steps * jax.nn.sigmoid(dt_raw + dt_bias[:, None])
    return (grad_x, grad_z, grad_bc, grad_dt)


def solution(mesh):
    return jax.shard_map(
        shards,
        mesh=mesh,
        in_specs=(
            P("seq", "head"),
            P("seq", "head"),
            P(None, "seq", None),
            P("head", "seq"),
            P("head"),
            P("head"),
            P("head"),
            P(None, "head"),
            P(),
            P("head"),
            P("seq", "head"),
        ),
        out_specs=(
            P("seq", "head"),
            P("seq", "head"),
            P(None, ("seq", "head"), None),
            P("head", "seq"),
        ),
        check_vma=False,
    )
```

```python
import jax
import jax.numpy as jnp
from jax import lax
from jax.experimental import pallas as pl
from jax.experimental.pallas import tpu as pltpu
from jax.sharding import PartitionSpec as P
import functools

MESH = pl.DeviceIdType.MESH
AXES = ("seq", "head")


def exchange_kernel(axis, n, in_ref, out_ref, land, send_sem, recv_sem):
    me = lax.axis_index(axis)
    coords = {a: lax.axis_index(a) for a in AXES}

    def dev(k):
        return tuple(k if a == axis else coords[a] for a in AXES)

    barrier = pltpu.get_barrier_semaphore()
    for i in range(1, n):
        pl.semaphore_signal(barrier, inc=1, device_id=dev(lax.rem(me + i, n)), device_id_type=MESH)
    pl.semaphore_wait(barrier, n - 1)
    copies = []
    for i in range(1, n):
        peer = lax.rem(me + i, n)
        copy = pltpu.make_async_remote_copy(
            src_ref=in_ref.at[peer],
            dst_ref=land.at[me],
            send_sem=send_sem.at[i],
            recv_sem=recv_sem.at[i],
            device_id=dev(peer),
            device_id_type=MESH,
        )
        copy.start()
        copies.append(copy)
    land[me] = in_ref[me]
    for i in range(1, n):
        copies[i - 1].wait_send()
        src = lax.rem(me + (n - i), n)
        incoming = pltpu.make_async_remote_copy(
            src_ref=in_ref.at[src],
            dst_ref=land.at[src],
            send_sem=send_sem.at[i],
            recv_sem=recv_sem.at[i],
            device_id=dev(src),
            device_id_type=MESH,
        )
        incoming.wait_recv()
    out_ref[...] = land[...]


def exchange(x, axis, cid):
    n = lax.axis_size(axis)
    return pl.pallas_call(
        functools.partial(exchange_kernel, axis, n),
        out_shape=jax.ShapeDtypeStruct(x.shape, x.dtype),
        in_specs=[pl.BlockSpec(memory_space=pltpu.VMEM)],
        out_specs=pl.BlockSpec(memory_space=pltpu.VMEM),
        scratch_shapes=[
            pltpu.VMEM(x.shape, x.dtype),
            pltpu.SemaphoreType.DMA((n,)),
            pltpu.SemaphoreType.DMA((n,)),
        ],
        compiler_params=pltpu.CompilerParams(collective_id=cid, has_side_effects=True),
    )(x)

def _peer_copies(axis, n, src_of, dst, send_sem, recv_sem):
    me = lax.axis_index(axis)
    coords = {a: lax.axis_index(a) for a in AXES}

    def dev(k):
        return tuple(k if a == axis else coords[a] for a in AXES)

    copies = []
    for i in range(1, n):
        peer = lax.rem(me + i, n)
        copy = pltpu.make_async_remote_copy(
            src_ref=src_of(peer),
            dst_ref=dst.at[me],
            send_sem=send_sem.at[i],
            recv_sem=recv_sem.at[i],
            device_id=dev(peer),
            device_id_type=MESH,
        )
        copy.start()
        copies.append(copy)
    return copies


def _peer_waits(axis, n, copies, src_of, dst, send_sem, recv_sem):
    me = lax.axis_index(axis)
    coords = {a: lax.axis_index(a) for a in AXES}

    def dev(k):
        return tuple(k if a == axis else coords[a] for a in AXES)

    for i in range(1, n):
        copies[i - 1].wait_send()
        src = lax.rem(me + (n - i), n)
        incoming = pltpu.make_async_remote_copy(
            src_ref=src_of(src),
            dst_ref=dst.at[src],
            send_sem=send_sem.at[i],
            recv_sem=recv_sem.at[i],
            device_id=dev(src),
            device_id_type=MESH,
        )
        incoming.wait_recv()


def _barrier(axis, n):
    me = lax.axis_index(axis)
    coords = {a: lax.axis_index(a) for a in AXES}
    barrier = pltpu.get_barrier_semaphore()
    for i in range(1, n):
        peer = lax.rem(me + i, n)
        dev = tuple(peer if a == axis else coords[a] for a in AXES)
        pl.semaphore_signal(barrier, inc=1, device_id=dev, device_id_type=MESH)
    pl.semaphore_wait(barrier, n - 1)


def scan_kernel(forward, axis, n, heads, *refs):
    if forward:
        in_ref, out_ref, scale_out, land, res, land2, s1, r1, s2, r2 = refs
    else:
        in_ref, scale_in, out_ref, land, res, land2, s1, r1, s2, r2 = refs
    me = lax.axis_index(axis)
    rows = res.shape[1]
    _barrier(axis, n)
    copies = _peer_copies(axis, n, lambda p: in_ref.at[p], land, s1, r1)
    land[me] = in_ref[me]
    _peer_waits(axis, n, copies, lambda p: in_ref.at[p], land, s1, r1)
    if forward:
        lane = lax.broadcasted_iota(jnp.int32, (1, 128), 1)
        pick = lane == me // (n // heads)
        for k in range(n):
            parts = land[k, rows : rows + 3, :].astype(jnp.float32)
            grow = jnp.exp(parts[0:1] + parts[1:2] + parts[2:3])
            factor = jnp.sum(jnp.where(pick, grow, 0.0), axis=1, keepdims=True)
            scale_out[k] = jnp.broadcast_to(factor, (8, 128))
        acc = jnp.zeros((rows, 128), jnp.float32)
        for k in range(n):
            res[k] = acc.astype(res.dtype)
            acc = scale_out[k][0:1, 0:1] * acc + land[k, :rows, :].astype(jnp.float32)
    else:
        acc = jnp.zeros((rows, 128), jnp.float32)
        for k in reversed(range(n)):
            res[k] = acc.astype(res.dtype)
            acc = land[k].astype(jnp.float32) + scale_in[k][0:1, 0:1] * acc
    copies = _peer_copies(axis, n, lambda p: res.at[p], land2, s2, r2)
    land2[me] = res[me]
    _peer_waits(axis, n, copies, lambda p: res.at[p], land2, s2, r2)
    out_ref[...] = land2[...]


def scan_pieces(x, axis, heads, cid, scales=None):
    n = lax.axis_size(axis)
    forward = scales is None
    rows = x.shape[1] - 16 if forward else x.shape[1]
    piece = (n, rows, 128)
    low = x.dtype
    vm = pl.BlockSpec(memory_space=pltpu.VMEM)
    scratch = [
        pltpu.VMEM(x.shape, low),
        pltpu.VMEM(piece, low),
        pltpu.VMEM(piece, low),
        pltpu.SemaphoreType.DMA((n,)),
        pltpu.SemaphoreType.DMA((n,)),
        pltpu.SemaphoreType.DMA((n,)),
        pltpu.SemaphoreType.DMA((n,)),
    ]
    params = pltpu.CompilerParams(collective_id=cid, has_side_effects=True)
    kern = functools.partial(scan_kernel, forward, axis, n, heads)
    if forward:
        return pl.pallas_call(
            kern,
            out_shape=(jax.ShapeDtypeStruct(piece, low), jax.ShapeDtypeStruct((n, 8, 128), jnp.float32)),
            in_specs=[vm],
            out_specs=(vm, vm),
            scratch_shapes=scratch,
            compiler_params=params,
        )(x)
    return pl.pallas_call(
        kern,
        out_shape=jax.ShapeDtypeStruct(piece, low),
        in_specs=[vm, vm],
        out_specs=vm,
        scratch_shapes=scratch,
        compiler_params=params,
    )(x, scales)


def tail_kernel(n, hn, in_ref, rim_ref, out_ref, rim_out, land, send, rim_land, s1, r1, s2, r2):
    me = lax.axis_index("seq")
    hme = lax.axis_index("head")
    prev = lax.rem(me + n - 1, n)
    nxt = lax.rem(me + 1, n)
    last = hn - 1
    barrier = pltpu.get_barrier_semaphore()
    for i in range(1, hn):
        pl.semaphore_signal(barrier, inc=1, device_id=(me, lax.rem(hme + i, hn)), device_id_type=MESH)
    pl.semaphore_signal(barrier, inc=1, device_id=(prev, hme), device_id_type=MESH)
    pl.semaphore_signal(barrier, inc=1, device_id=(nxt, hme), device_id_type=MESH)
    pl.semaphore_wait(barrier, hn + 1)
    rim_copy = pltpu.make_async_remote_copy(
        src_ref=rim_ref, dst_ref=rim_land, send_sem=s2.at[0], recv_sem=r2.at[0],
        device_id=(prev, hme), device_id_type=MESH,
    )
    rim_copy.start()

    def piece_copy(t, src):
        return pltpu.make_async_remote_copy(
            src_ref=src, dst_ref=land.at[hme], send_sem=s1.at[t], recv_sem=r1.at[hme],
            device_id=(me, t), device_id_type=MESH,
        )

    for t in range(last):
        @pl.when(hme != t)
        def _():
            piece_copy(t, in_ref.at[t]).start()

    land[hme] = in_ref[hme]
    send[...] = in_ref[last]
    rim_copy.wait_send()
    rim_copy.wait_recv()
    keep = (1 - me // (n - 1)).astype(jnp.float32)
    rows = in_ref.shape[1] // 2
    nst = in_ref.shape[2]
    width = rim_ref.shape[1] - nst
    rim_bc = rim_land[0:8, width:] * keep
    send[8:11, :] = send[8:11, :] + rim_bc[0:3]
    send[rows + 8 : rows + 11, :] = send[rows + 8 : rows + 11, :] + rim_bc[3:6]
    rim_out[...] = rim_land[0:8, 0:width] * keep

    @pl.when(hme != last)
    def _():
        piece_copy(last, send).start()

    @pl.when(hme == last)
    def _():
        land[last] = send[...]

    for t in range(hn):
        @pl.when(hme != t)
        def _():
            piece_copy(t, send).wait_send()

    for j in range(hn):
        @pl.when(hme != j)
        def _():
            pltpu.make_async_remote_copy(
                src_ref=send, dst_ref=land.at[j], send_sem=s1.at[j], recv_sem=r1.at[j],
                device_id=(me, j), device_id_type=MESH,
            ).wait_recv()

    total = land[0]
    for j in range(1, hn):
        total = total + land[j]
    out_ref[...] = total


def tail_exchange(pieces, rim, cid):
    n = lax.axis_size("seq")
    hn = lax.axis_size("head")
    vm = pl.BlockSpec(memory_space=pltpu.VMEM)
    width = rim.shape[1] - pieces.shape[2]
    return pl.pallas_call(
        functools.partial(tail_kernel, n, hn),
        out_shape=(
            jax.ShapeDtypeStruct(pieces.shape[1:], jnp.float32),
            jax.ShapeDtypeStruct((8, width), jnp.float32),
        ),
        in_specs=[vm, vm],
        out_specs=(vm, vm),
        scratch_shapes=[
            pltpu.VMEM(pieces.shape, jnp.float32),
            pltpu.VMEM(pieces.shape[1:], jnp.float32),
            pltpu.VMEM(rim.shape, jnp.float32),
            pltpu.SemaphoreType.DMA((hn,)),
            pltpu.SemaphoreType.DMA((hn,)),
            pltpu.SemaphoreType.DMA((1,)),
            pltpu.SemaphoreType.DMA((1,)),
        ],
        compiler_params=pltpu.CompilerParams(collective_id=cid, has_side_effects=True),
    )(pieces, rim)


INNER = 16384


EPS = 1e-05
HIGH = lax.Precision.HIGHEST


def passed_along(block, axis, distance):
    devices = range(lax.axis_size(axis))
    route = [(i - distance, i) for i in devices if i - distance in devices]
    return lax.ppermute(block, axis, route)


def silu_grad(value):
    sigma = jax.nn.sigmoid(value)
    return sigma * (1.0 + value * (1.0 - sigma))


def conv_rows(extended, weight_matrix):
    length = extended.shape[-2] - 3
    summed = weight_matrix[..., 0, :][..., None, :] * extended[..., 0:length, :]
    for offset in range(1, 4):
        summed = (
            summed
            + weight_matrix[..., offset, :][..., None, :]
            * extended[..., offset : offset + length, :]
        )
    return summed


def conv_back(extended, weight_matrix):
    length = extended.shape[-2] - 3
    summed = weight_matrix[..., 0, :][..., None, :] * extended[..., 3 : 3 + length, :]
    for offset in range(1, 4):
        summed = (
            summed
            + weight_matrix[..., offset, :][..., None, :]
            * extended[..., 3 - offset : 3 - offset + length, :]
        )
    return summed


def to_pieces(state, count):
    heads, nstate, width = state.shape
    return state.reshape(count, heads * nstate // count, width)


def from_pieces(pieces, heads):
    count, rows, width = pieces.shape
    return pieces.reshape(heads, count * rows // heads, width)


def scan_forward(totals, local_state):
    count = lax.axis_size("seq")
    heads, nstate, width = local_state.shape
    pieces = to_pieces(local_state, count)
    high = lax.reduce_precision(totals, exponent_bits=8, mantissa_bits=7)
    rest = totals - high
    middle = lax.reduce_precision(rest, exponent_bits=8, mantissa_bits=7)
    parts = jnp.stack([high, middle, rest - middle])
    tot_row = jnp.pad(parts, ((0, 13), (0, width - heads)))
    tot_row = jnp.broadcast_to(tot_row, (count, 16, width))
    sent = jnp.concatenate([pieces, tot_row], axis=1).astype(jnp.bfloat16)
    back, scales = scan_pieces(sent, "seq", heads, 0)
    return from_pieces(back, heads).astype(jnp.float32), scales


def scan_backward(scales, state_grad):
    count = lax.axis_size("seq")
    heads = state_grad.shape[0]
    pieces = to_pieces(state_grad, count).astype(jnp.bfloat16)
    back = scan_pieces(pieces, "seq", heads, 1, scales)
    return from_pieces(back, heads).astype(jnp.float32)


def shards(
    x_input,
    z_input,
    bc_input,
    dt_raw,
    dt_bias,
    a_log,
    d_skip,
    conv_x,
    convolution_bc_taps,
    rescale_factor,
    grad_out,
):
    length = x_input.shape[0]
    channels = x_input.shape[1]
    head_count = dt_raw.shape[0]
    width = channels // head_count
    f32 = jnp.float32
    bf16 = jnp.bfloat16
    decay_rate = -jnp.exp(a_log)
    step_size = jax.nn.softplus(dt_raw + dt_bias[:, None])
    causal = jnp.tril(jnp.ones((length, length), dtype=bool))
    nstate = bc_input.shape[2]
    rows_last = jnp.concatenate(
        [x_input[length - 3 :], jnp.moveaxis(bc_input[:, length - 3 :], 0, 1).reshape(3, 2 * nstate)],
        axis=1,
    )
    rows_prior = passed_along(rows_last, "seq", 1)
    x_ext = jnp.concatenate([rows_prior[:, :channels], x_input], axis=0)
    bc_prior = jnp.moveaxis(rows_prior[:, channels:].reshape(3, 2, nstate), 0, 1)
    bc_ext = jnp.concatenate([bc_prior, bc_input], axis=1)
    x_pre = conv_rows(x_ext.astype(f32), conv_x)
    bc_pre = conv_rows(bc_ext.astype(f32), convolution_bc_taps)
    x_rows = jax.nn.silu(x_pre).astype(bf16)
    bc_rows = jax.nn.silu(bc_pre).astype(bf16)
    b_rows = bc_rows[0]
    c_rows = bc_rows[1]
    gram = jnp.dot(c_rows, b_rows.T, preferred_element_type=f32)
    x_heads = x_rows.reshape(length, head_count, width)

    cumul = jnp.cumsum(decay_rate[:, None] * step_size, axis=1)
    totals = cumul[:, -1]
    trailing = jnp.exp(cumul[:, -1:] - cumul)
    tail_step = trailing * step_size
    weighted_b = (tail_step[:, :, None] * b_rows.astype(f32)[None]).astype(bf16)
    local_state = jnp.einsum("hsn,shp->hnp", weighted_b, x_heads, preferred_element_type=f32)

    state_exact, weight = scan_forward(totals, local_state)
    state_low = state_exact.astype(bf16)

    between = cumul[:, :, None] - cumul[:, None, :]
    decay = jnp.where(causal[None], jnp.exp(jnp.minimum(between, 0.0)), 0.0)
    mixer_low = (gram[None] * decay * step_size[:, None, :]).astype(bf16)
    intra = jnp.einsum("hts,shp->thp", mixer_low, x_heads, preferred_element_type=f32)
    handed = jnp.einsum("tn,hnp->thp", c_rows, state_low, preferred_element_type=f32)
    lifted = jnp.exp(cumul)
    mixed_heads = (
        intra + lifted.T[:, :, None] * handed + d_skip[None, :, None] * x_heads.astype(f32)
    )
    mixed_out = mixed_heads.reshape(length, channels)

    z_rows = z_input.astype(f32)
    gate_value = jax.nn.silu(z_rows)
    gated = mixed_out * gate_value
    scaled = grad_out.astype(f32) * rescale_factor
    hcount = lax.axis_size("head")
    own_sums = jnp.stack([jnp.sum(gated * gated, axis=1), jnp.sum(scaled * gated, axis=1)])
    own_sums = jnp.concatenate([own_sums, jnp.zeros((6, length), f32)], axis=0)
    sums = jnp.sum(exchange(jnp.broadcast_to(own_sums, (hcount,) + own_sums.shape), "head", 3), axis=0)
    inv_rms = lax.rsqrt(sums[0] / INNER + EPS)
    normed = gated * inv_rms[:, None]
    mean_dot = inv_rms * sums[1] / INNER
    grad_gated = inv_rms[:, None] * (scaled - normed * mean_dot[:, None])
    grad_z = (grad_gated * mixed_out * silu_grad(z_rows)).astype(bf16)
    grad_mixed = (grad_gated * gate_value).astype(bf16)
    grad_heads = grad_mixed.reshape(length, head_count, width)

    lifted_c = (lifted[:, :, None] * c_rows.astype(f32)[None]).astype(bf16)
    state_grad = jnp.einsum("htn,thp->hnp", lifted_c, grad_heads, preferred_element_type=f32)
    out_exact = scan_backward(weight, state_grad)
    out_low = out_exact.astype(bf16)

    grad_mix = jnp.einsum("thp,shp->hts", grad_heads, x_heads, preferred_element_type=f32)
    decayed = grad_mix * decay
    zterm = decayed * step_size[:, None, :]
    gram_grad = zterm * gram[None]
    reached = jnp.einsum("shp,hnp->hsn", x_heads, out_low, preferred_element_type=f32)
    inner_b = jnp.sum(b_rows.astype(f32)[None] * reached, axis=2)
    state_term = tail_step * inner_b
    grad_cumul = jnp.sum(gram_grad, axis=2) - jnp.sum(gram_grad, axis=1)
    carried_dot = jnp.sum(grad_heads.astype(f32) * handed, axis=2).T
    grad_cumul = grad_cumul + lifted * carried_dot - state_term
    end_grad = jnp.sum(state_term, axis=1) + jnp.exp(totals) * jnp.sum(
        out_exact * state_exact, axis=(1, 2)
    )
    grad_cumul = grad_cumul.at[:, -1].add(end_grad)
    grad_log = jnp.cumsum(grad_cumul[:, ::-1], axis=1)[:, ::-1]
    grad_steps = (
        jnp.sum(decayed * gram[None], axis=1)
        + trailing * inner_b
        + decay_rate[:, None] * grad_log
    )
    grad_x_heads = jnp.einsum("hts,thp->shp", mixer_low, grad_heads, preferred_element_type=f32)
    grad_x_heads = (
        grad_x_heads
        + d_skip[None, :, None] * grad_heads.astype(f32)
        + jnp.einsum("hsn,hnp->shp", weighted_b, out_low, preferred_element_type=f32)
    )
    grad_c_heads = lifted[:, :, None] * jnp.einsum(
        "thp,hnp->htn", grad_heads, state_low, preferred_element_type=f32
    )
    grad_b_heads = tail_step[:, :, None] * reached
    grad_sum = jnp.sum(zterm, axis=0)
    grad_c = jnp.sum(grad_c_heads, axis=0) + jnp.dot(grad_sum, b_rows.astype(f32), precision=HIGH)
    grad_b = jnp.sum(grad_b_heads, axis=0) + jnp.dot(
        grad_sum.T, c_rows.astype(f32), precision=HIGH
    )
    grad_bc_rows = jnp.stack([grad_b, grad_c])
    grad_x_rows = grad_x_heads.reshape(length, channels)

    grad_x_pre = grad_x_rows * silu_grad(x_pre)
    hcount = lax.axis_size("head")
    row_share = length // hcount
    hidx = lax.axis_index("head")
    first_row = hidx * row_share
    picks = []
    for h in range(hcount):
        own = [h * row_share + i for i in range(row_share + 3)]
        own = [r if r < length else length for r in own]
        picks.append(own + [length] * (12 - row_share - 3))
    picks = jnp.array(picks, jnp.int32)
    piece_rows = picks.shape[1]
    bc_rows_z = jnp.concatenate([grad_bc_rows, jnp.zeros((2, 1, nstate), f32)], axis=1)
    bc_pieces = jnp.moveaxis(jnp.take(bc_rows_z, picks.reshape(-1), axis=1).reshape(2, hcount, piece_rows, -1), 1, 0)
    top = (grad_bc_rows[:, :3] * silu_grad(bc_pre[:, :3])).reshape(6, nstate)
    rim_send = jnp.concatenate(
        [jnp.pad(grad_x_pre[:3], ((0, 5), (0, 0))), jnp.pad(top, ((0, 2), (0, 0)))], axis=1
    )
    summed, rim_got = tail_exchange(bc_pieces.reshape(hcount, 2 * piece_rows, -1), rim_send, 2)
    grad_bc_mine = summed.reshape(2, piece_rows, -1)[:, : row_share + 3]
    bc_pre_pad = jnp.concatenate([bc_pre, jnp.zeros((2, 3, nstate), f32)], axis=1)
    bc_pre_mine = lax.dynamic_slice_in_dim(bc_pre_pad, first_row, row_share + 3, 1)
    in_rim = (hidx == hcount - 1) & (jnp.arange(row_share + 3) >= row_share)
    grad_bc_ext = grad_bc_mine * jnp.where(in_rim[None, :, None], 1.0, silu_grad(bc_pre_mine))
    rim_x = rim_got[:3]
    grad_x = conv_back(jnp.concatenate([grad_x_pre, rim_x], axis=0), conv_x).astype(bf16)
    grad_bc = conv_back(grad_bc_ext, convolution_bc_taps).astype(bf16)
    grad_dt = grad_steps * jax.nn.sigmoid(dt_raw + dt_bias[:, None])
    return (grad_x, grad_z, grad_bc, grad_dt)


def solution(mesh):
    return jax.shard_map(
        shards,
        mesh=mesh,
        in_specs=(
            P("seq", "head"),
            P("seq", "head"),
            P(None, "seq", None),
            P("head", "seq"),
            P("head"),
            P("head"),
            P("head"),
            P(None, "head"),
            P(),
            P("head"),
            P("seq", "head"),
        ),
        out_specs=(
            P("seq", "head"),
            P("seq", "head"),
            P(None, ("seq", "head"), None),
            P("head", "seq"),
        ),
        check_vma=False,
    )
```

```python
import jax
import jax.numpy as jnp
from jax import lax
from jax.experimental import pallas as pl
from jax.experimental.pallas import tpu as pltpu
from jax.sharding import PartitionSpec as P
import functools

MESH = pl.DeviceIdType.MESH
AXES = ("seq", "head")


def exchange_kernel(axis, n, in_ref, out_ref, land, send_sem, recv_sem):
    me = lax.axis_index(axis)
    coords = {a: lax.axis_index(a) for a in AXES}

    def dev(k):
        return tuple(k if a == axis else coords[a] for a in AXES)

    barrier = pltpu.get_barrier_semaphore()
    for i in range(1, n):
        pl.semaphore_signal(barrier, inc=1, device_id=dev(lax.rem(me + i, n)), device_id_type=MESH)
    pl.semaphore_wait(barrier, n - 1)
    copies = []
    for i in range(1, n):
        peer = lax.rem(me + i, n)
        copy = pltpu.make_async_remote_copy(
            src_ref=in_ref.at[peer],
            dst_ref=land.at[me],
            send_sem=send_sem.at[i],
            recv_sem=recv_sem.at[i],
            device_id=dev(peer),
            device_id_type=MESH,
        )
        copy.start()
        copies.append(copy)
    land[me] = in_ref[me]
    for i in range(1, n):
        copies[i - 1].wait_send()
        src = lax.rem(me + (n - i), n)
        incoming = pltpu.make_async_remote_copy(
            src_ref=in_ref.at[src],
            dst_ref=land.at[src],
            send_sem=send_sem.at[i],
            recv_sem=recv_sem.at[i],
            device_id=dev(src),
            device_id_type=MESH,
        )
        incoming.wait_recv()
    out_ref[...] = land[...]


def exchange(x, axis, cid):
    n = lax.axis_size(axis)
    return pl.pallas_call(
        functools.partial(exchange_kernel, axis, n),
        out_shape=jax.ShapeDtypeStruct(x.shape, x.dtype),
        in_specs=[pl.BlockSpec(memory_space=pltpu.VMEM)],
        out_specs=pl.BlockSpec(memory_space=pltpu.VMEM),
        scratch_shapes=[
            pltpu.VMEM(x.shape, x.dtype),
            pltpu.SemaphoreType.DMA((n,)),
            pltpu.SemaphoreType.DMA((n,)),
        ],
        compiler_params=pltpu.CompilerParams(collective_id=cid, has_side_effects=True),
    )(x)

def _peer_copies(axis, n, src_of, dst, send_sem, recv_sem):
    me = lax.axis_index(axis)
    coords = {a: lax.axis_index(a) for a in AXES}

    def dev(k):
        return tuple(k if a == axis else coords[a] for a in AXES)

    copies = []
    for i in range(1, n):
        peer = lax.rem(me + i, n)
        copy = pltpu.make_async_remote_copy(
            src_ref=src_of(peer),
            dst_ref=dst.at[me],
            send_sem=send_sem.at[i],
            recv_sem=recv_sem.at[i],
            device_id=dev(peer),
            device_id_type=MESH,
        )
        copy.start()
        copies.append(copy)
    return copies


def _peer_waits(axis, n, copies, src_of, dst, send_sem, recv_sem):
    me = lax.axis_index(axis)
    coords = {a: lax.axis_index(a) for a in AXES}

    def dev(k):
        return tuple(k if a == axis else coords[a] for a in AXES)

    for i in range(1, n):
        copies[i - 1].wait_send()
        src = lax.rem(me + (n - i), n)
        incoming = pltpu.make_async_remote_copy(
            src_ref=src_of(src),
            dst_ref=dst.at[src],
            send_sem=send_sem.at[i],
            recv_sem=recv_sem.at[i],
            device_id=dev(src),
            device_id_type=MESH,
        )
        incoming.wait_recv()


def _barrier(axis, n):
    me = lax.axis_index(axis)
    coords = {a: lax.axis_index(a) for a in AXES}
    barrier = pltpu.get_barrier_semaphore()
    for i in range(1, n):
        peer = lax.rem(me + i, n)
        dev = tuple(peer if a == axis else coords[a] for a in AXES)
        pl.semaphore_signal(barrier, inc=1, device_id=dev, device_id_type=MESH)
    pl.semaphore_wait(barrier, n - 1)


def scan_kernel(forward, axis, n, heads, *refs):
    if forward:
        in_ref, out_ref, scale_out, land, res, land2, s1, r1, s2, r2 = refs
    else:
        in_ref, scale_in, out_ref, land, res, land2, s1, r1, s2, r2 = refs
    me = lax.axis_index(axis)
    rows = res.shape[1]
    _barrier(axis, n)
    copies = _peer_copies(axis, n, lambda p: in_ref.at[p], land, s1, r1)
    land[me] = in_ref[me]
    coords = {a: lax.axis_index(a) for a in AXES}

    def dev(k):
        return tuple(k if a == axis else coords[a] for a in AXES)

    def arrive(k):
        @pl.when(me != k)
        def _():
            pltpu.make_async_remote_copy(
                src_ref=in_ref.at[k], dst_ref=land.at[k], send_sem=s1.at[0],
                recv_sem=r1.at[lax.rem(me - k + n, n)], device_id=dev(k), device_id_type=MESH,
            ).wait_recv()

    def result_copy(k):
        return pltpu.make_async_remote_copy(
            src_ref=res.at[k], dst_ref=land2.at[me], send_sem=s2.at[k], recv_sem=r2.at[me],
            device_id=dev(k), device_id_type=MESH,
        )

    def give(k):
        @pl.when(me != k)
        def _():
            result_copy(k).start()

        @pl.when(me == k)
        def _():
            land2[k] = res[k]

    acc = jnp.zeros((rows, 128), jnp.float32)
    if forward:
        lane = lax.broadcasted_iota(jnp.int32, (1, 128), 1)
        pick = lane == me // (n // heads)
        for k in range(n):
            res[k] = acc.astype(res.dtype)
            give(k)
            arrive(k)
            parts = land[k, rows : rows + 3, :].astype(jnp.float32)
            grow = jnp.exp(parts[0:1] + parts[1:2] + parts[2:3])
            factor = jnp.sum(jnp.where(pick, grow, 0.0), axis=1, keepdims=True)
            scale_out[k] = jnp.broadcast_to(factor, (8, 128))
            acc = factor * acc + land[k, :rows, :].astype(jnp.float32)
    else:
        for k in reversed(range(n)):
            res[k] = acc.astype(res.dtype)
            give(k)
            arrive(k)
            acc = land[k].astype(jnp.float32) + scale_in[k][0:1, 0:1] * acc
    for c in copies:
        c.wait_send()
    for k in range(n):
        @pl.when(me != k)
        def _():
            result_copy(k).wait_send()

        @pl.when(me != k)
        def _():
            pltpu.make_async_remote_copy(
                src_ref=res.at[k], dst_ref=land2.at[k], send_sem=s2.at[k], recv_sem=r2.at[k],
                device_id=dev(k), device_id_type=MESH,
            ).wait_recv()
    out_ref[...] = land2[...]


def scan_pieces(x, axis, heads, cid, scales=None):
    n = lax.axis_size(axis)
    forward = scales is None
    rows = x.shape[1] - 16 if forward else x.shape[1]
    piece = (n, rows, 128)
    low = x.dtype
    vm = pl.BlockSpec(memory_space=pltpu.VMEM)
    scratch = [
        pltpu.VMEM(x.shape, low),
        pltpu.VMEM(piece, low),
        pltpu.VMEM(piece, low),
        pltpu.SemaphoreType.DMA((n,)),
        pltpu.SemaphoreType.DMA((n,)),
        pltpu.SemaphoreType.DMA((n,)),
        pltpu.SemaphoreType.DMA((n,)),
    ]
    params = pltpu.CompilerParams(collective_id=cid, has_side_effects=True)
    kern = functools.partial(scan_kernel, forward, axis, n, heads)
    if forward:
        return pl.pallas_call(
            kern,
            out_shape=(jax.ShapeDtypeStruct(piece, low), jax.ShapeDtypeStruct((n, 8, 128), jnp.float32)),
            in_specs=[vm],
            out_specs=(vm, vm),
            scratch_shapes=scratch,
            compiler_params=params,
        )(x)
    return pl.pallas_call(
        kern,
        out_shape=jax.ShapeDtypeStruct(piece, low),
        in_specs=[vm, vm],
        out_specs=vm,
        scratch_shapes=scratch,
        compiler_params=params,
    )(x, scales)


def tail_kernel(n, hn, in_ref, rim_ref, out_ref, rim_out, land, send, rim_land, s1, r1, s2, r2):
    me = lax.axis_index("seq")
    hme = lax.axis_index("head")
    prev = lax.rem(me + n - 1, n)
    nxt = lax.rem(me + 1, n)
    last = hn - 1
    barrier = pltpu.get_barrier_semaphore()
    for i in range(1, hn):
        pl.semaphore_signal(barrier, inc=1, device_id=(me, lax.rem(hme + i, hn)), device_id_type=MESH)
    pl.semaphore_signal(barrier, inc=1, device_id=(prev, hme), device_id_type=MESH)
    pl.semaphore_signal(barrier, inc=1, device_id=(nxt, hme), device_id_type=MESH)
    pl.semaphore_wait(barrier, hn + 1)
    rim_copy = pltpu.make_async_remote_copy(
        src_ref=rim_ref, dst_ref=rim_land, send_sem=s2.at[0], recv_sem=r2.at[0],
        device_id=(prev, hme), device_id_type=MESH,
    )
    rim_copy.start()

    def piece_copy(t, src):
        return pltpu.make_async_remote_copy(
            src_ref=src, dst_ref=land.at[hme], send_sem=s1.at[t], recv_sem=r1.at[hme],
            device_id=(me, t), device_id_type=MESH,
        )

    for t in range(last):
        @pl.when(hme != t)
        def _():
            piece_copy(t, in_ref.at[t]).start()

    land[hme] = in_ref[hme]
    send[...] = in_ref[last]
    rim_copy.wait_send()
    rim_copy.wait_recv()
    keep = (1 - me // (n - 1)).astype(jnp.float32)
    rows = in_ref.shape[1] // 2
    nst = in_ref.shape[2]
    width = rim_ref.shape[1] - nst
    rim_bc = rim_land[0:8, width:] * keep
    send[8:11, :] = send[8:11, :] + rim_bc[0:3]
    send[rows + 8 : rows + 11, :] = send[rows + 8 : rows + 11, :] + rim_bc[3:6]
    rim_out[...] = rim_land[0:8, 0:width] * keep

    @pl.when(hme != last)
    def _():
        piece_copy(last, send).start()

    @pl.when(hme == last)
    def _():
        land[last] = send[...]

    for t in range(hn):
        @pl.when(hme != t)
        def _():
            piece_copy(t, send).wait_send()

    for j in range(hn):
        @pl.when(hme != j)
        def _():
            pltpu.make_async_remote_copy(
                src_ref=send, dst_ref=land.at[j], send_sem=s1.at[j], recv_sem=r1.at[j],
                device_id=(me, j), device_id_type=MESH,
            ).wait_recv()

    total = land[0]
    for j in range(1, hn):
        total = total + land[j]
    out_ref[...] = total


def tail_exchange(pieces, rim, cid):
    n = lax.axis_size("seq")
    hn = lax.axis_size("head")
    vm = pl.BlockSpec(memory_space=pltpu.VMEM)
    width = rim.shape[1] - pieces.shape[2]
    return pl.pallas_call(
        functools.partial(tail_kernel, n, hn),
        out_shape=(
            jax.ShapeDtypeStruct(pieces.shape[1:], jnp.float32),
            jax.ShapeDtypeStruct((8, width), jnp.float32),
        ),
        in_specs=[vm, vm],
        out_specs=(vm, vm),
        scratch_shapes=[
            pltpu.VMEM(pieces.shape, jnp.float32),
            pltpu.VMEM(pieces.shape[1:], jnp.float32),
            pltpu.VMEM(rim.shape, jnp.float32),
            pltpu.SemaphoreType.DMA((hn,)),
            pltpu.SemaphoreType.DMA((hn,)),
            pltpu.SemaphoreType.DMA((1,)),
            pltpu.SemaphoreType.DMA((1,)),
        ],
        compiler_params=pltpu.CompilerParams(collective_id=cid, has_side_effects=True),
    )(pieces, rim)


INNER = 16384


EPS = 1e-05
HIGH = lax.Precision.HIGHEST


def passed_along(block, axis, distance):
    devices = range(lax.axis_size(axis))
    route = [(i - distance, i) for i in devices if i - distance in devices]
    return lax.ppermute(block, axis, route)


def silu_grad(value):
    sigma = jax.nn.sigmoid(value)
    return sigma * (1.0 + value * (1.0 - sigma))


def conv_rows(extended, weight_matrix):
    length = extended.shape[-2] - 3
    summed = weight_matrix[..., 0, :][..., None, :] * extended[..., 0:length, :]
    for offset in range(1, 4):
        summed = (
            summed
            + weight_matrix[..., offset, :][..., None, :]
            * extended[..., offset : offset + length, :]
        )
    return summed


def conv_back(extended, weight_matrix):
    length = extended.shape[-2] - 3
    summed = weight_matrix[..., 0, :][..., None, :] * extended[..., 3 : 3 + length, :]
    for offset in range(1, 4):
        summed = (
            summed
            + weight_matrix[..., offset, :][..., None, :]
            * extended[..., 3 - offset : 3 - offset + length, :]
        )
    return summed


def to_pieces(state, count):
    heads, nstate, width = state.shape
    return state.reshape(count, heads * nstate // count, width)


def from_pieces(pieces, heads):
    count, rows, width = pieces.shape
    return pieces.reshape(heads, count * rows // heads, width)


def scan_forward(totals, local_state):
    count = lax.axis_size("seq")
    heads, nstate, width = local_state.shape
    pieces = to_pieces(local_state, count)
    high = lax.reduce_precision(totals, exponent_bits=8, mantissa_bits=7)
    rest = totals - high
    middle = lax.reduce_precision(rest, exponent_bits=8, mantissa_bits=7)
    parts = jnp.stack([high, middle, rest - middle])
    tot_row = jnp.pad(parts, ((0, 13), (0, width - heads)))
    tot_row = jnp.broadcast_to(tot_row, (count, 16, width))
    sent = jnp.concatenate([pieces, tot_row], axis=1).astype(jnp.bfloat16)
    back, scales = scan_pieces(sent, "seq", heads, 0)
    return from_pieces(back, heads).astype(jnp.float32), scales


def scan_backward(scales, state_grad):
    count = lax.axis_size("seq")
    heads = state_grad.shape[0]
    pieces = to_pieces(state_grad, count).astype(jnp.bfloat16)
    back = scan_pieces(pieces, "seq", heads, 1, scales)
    return from_pieces(back, heads).astype(jnp.float32)


def shards(
    x_input,
    z_input,
    bc_input,
    dt_raw,
    dt_bias,
    a_log,
    d_skip,
    conv_x,
    convolution_bc_taps,
    rescale_factor,
    grad_out,
):
    length = x_input.shape[0]
    channels = x_input.shape[1]
    head_count = dt_raw.shape[0]
    width = channels // head_count
    f32 = jnp.float32
    bf16 = jnp.bfloat16
    decay_rate = -jnp.exp(a_log)
    step_size = jax.nn.softplus(dt_raw + dt_bias[:, None])
    causal = jnp.tril(jnp.ones((length, length), dtype=bool))
    nstate = bc_input.shape[2]
    rows_last = jnp.concatenate(
        [x_input[length - 3 :], jnp.moveaxis(bc_input[:, length - 3 :], 0, 1).reshape(3, 2 * nstate)],
        axis=1,
    )
    rows_prior = passed_along(rows_last, "seq", 1)
    x_ext = jnp.concatenate([rows_prior[:, :channels], x_input], axis=0)
    bc_prior = jnp.moveaxis(rows_prior[:, channels:].reshape(3, 2, nstate), 0, 1)
    bc_ext = jnp.concatenate([bc_prior, bc_input], axis=1)
    x_pre = conv_rows(x_ext.astype(f32), conv_x)
    bc_pre = conv_rows(bc_ext.astype(f32), convolution_bc_taps)
    x_rows = jax.nn.silu(x_pre).astype(bf16)
    bc_rows = jax.nn.silu(bc_pre).astype(bf16)
    b_rows = bc_rows[0]
    c_rows = bc_rows[1]
    gram = jnp.dot(c_rows, b_rows.T, preferred_element_type=f32)
    x_heads = x_rows.reshape(length, head_count, width)

    cumul = jnp.cumsum(decay_rate[:, None] * step_size, axis=1)
    totals = cumul[:, -1]
    trailing = jnp.exp(cumul[:, -1:] - cumul)
    tail_step = trailing * step_size
    weighted_b = (tail_step[:, :, None] * b_rows.astype(f32)[None]).astype(bf16)
    local_state = jnp.einsum("hsn,shp->hnp", weighted_b, x_heads, preferred_element_type=f32)

    state_exact, weight = scan_forward(totals, local_state)
    state_low = state_exact.astype(bf16)

    between = cumul[:, :, None] - cumul[:, None, :]
    decay = jnp.where(causal[None], jnp.exp(jnp.minimum(between, 0.0)), 0.0)
    mixer_low = (gram[None] * decay * step_size[:, None, :]).astype(bf16)
    intra = jnp.einsum("hts,shp->thp", mixer_low, x_heads, preferred_element_type=f32)
    handed = jnp.einsum("tn,hnp->thp", c_rows, state_low, preferred_element_type=f32)
    lifted = jnp.exp(cumul)
    mixed_heads = (
        intra + lifted.T[:, :, None] * handed + d_skip[None, :, None] * x_heads.astype(f32)
    )
    mixed_out = mixed_heads.reshape(length, channels)

    z_rows = z_input.astype(f32)
    gate_value = jax.nn.silu(z_rows)
    gated = mixed_out * gate_value
    scaled = grad_out.astype(f32) * rescale_factor
    hcount = lax.axis_size("head")
    own_sums = jnp.stack([jnp.sum(gated * gated, axis=1), jnp.sum(scaled * gated, axis=1)])
    own_sums = jnp.concatenate([own_sums, jnp.zeros((6, length), f32)], axis=0)
    sums = jnp.sum(exchange(jnp.broadcast_to(own_sums, (hcount,) + own_sums.shape), "head", 3), axis=0)
    inv_rms = lax.rsqrt(sums[0] / INNER + EPS)
    normed = gated * inv_rms[:, None]
    mean_dot = inv_rms * sums[1] / INNER
    grad_gated = inv_rms[:, None] * (scaled - normed * mean_dot[:, None])
    grad_z = (grad_gated * mixed_out * silu_grad(z_rows)).astype(bf16)
    grad_mixed = (grad_gated * gate_value).astype(bf16)
    grad_heads = grad_mixed.reshape(length, head_count, width)

    lifted_c = (lifted[:, :, None] * c_rows.astype(f32)[None]).astype(bf16)
    state_grad = jnp.einsum("htn,thp->hnp", lifted_c, grad_heads, preferred_element_type=f32)
    out_exact = scan_backward(weight, state_grad)
    out_low = out_exact.astype(bf16)

    grad_mix = jnp.einsum("thp,shp->hts", grad_heads, x_heads, preferred_element_type=f32)
    decayed = grad_mix * decay
    zterm = decayed * step_size[:, None, :]
    gram_grad = zterm * gram[None]
    reached = jnp.einsum("shp,hnp->hsn", x_heads, out_low, preferred_element_type=f32)
    inner_b = jnp.sum(b_rows.astype(f32)[None] * reached, axis=2)
    state_term = tail_step * inner_b
    grad_cumul = jnp.sum(gram_grad, axis=2) - jnp.sum(gram_grad, axis=1)
    carried_dot = jnp.sum(grad_heads.astype(f32) * handed, axis=2).T
    grad_cumul = grad_cumul + lifted * carried_dot - state_term
    end_grad = jnp.sum(state_term, axis=1) + jnp.exp(totals) * jnp.sum(
        out_exact * state_exact, axis=(1, 2)
    )
    grad_cumul = grad_cumul.at[:, -1].add(end_grad)
    grad_log = jnp.cumsum(grad_cumul[:, ::-1], axis=1)[:, ::-1]
    grad_steps = (
        jnp.sum(decayed * gram[None], axis=1)
        + trailing * inner_b
        + decay_rate[:, None] * grad_log
    )
    grad_x_heads = jnp.einsum("hts,thp->shp", mixer_low, grad_heads, preferred_element_type=f32)
    grad_x_heads = (
        grad_x_heads
        + d_skip[None, :, None] * grad_heads.astype(f32)
        + jnp.einsum("hsn,hnp->shp", weighted_b, out_low, preferred_element_type=f32)
    )
    grad_c_heads = lifted[:, :, None] * jnp.einsum(
        "thp,hnp->htn", grad_heads, state_low, preferred_element_type=f32
    )
    grad_b_heads = tail_step[:, :, None] * reached
    grad_sum = jnp.sum(zterm, axis=0)
    grad_c = jnp.sum(grad_c_heads, axis=0) + jnp.dot(grad_sum, b_rows.astype(f32), precision=HIGH)
    grad_b = jnp.sum(grad_b_heads, axis=0) + jnp.dot(
        grad_sum.T, c_rows.astype(f32), precision=HIGH
    )
    grad_bc_rows = jnp.stack([grad_b, grad_c])
    grad_x_rows = grad_x_heads.reshape(length, channels)

    grad_x_pre = grad_x_rows * silu_grad(x_pre)
    hcount = lax.axis_size("head")
    row_share = length // hcount
    hidx = lax.axis_index("head")
    first_row = hidx * row_share
    picks = []
    for h in range(hcount):
        own = [h * row_share + i for i in range(row_share + 3)]
        own = [r if r < length else length for r in own]
        picks.append(own + [length] * (12 - row_share - 3))
    picks = jnp.array(picks, jnp.int32)
    piece_rows = picks.shape[1]
    bc_rows_z = jnp.concatenate([grad_bc_rows, jnp.zeros((2, 1, nstate), f32)], axis=1)
    bc_pieces = jnp.moveaxis(jnp.take(bc_rows_z, picks.reshape(-1), axis=1).reshape(2, hcount, piece_rows, -1), 1, 0)
    top = (grad_bc_rows[:, :3] * silu_grad(bc_pre[:, :3])).reshape(6, nstate)
    rim_send = jnp.concatenate(
        [jnp.pad(grad_x_pre[:3], ((0, 5), (0, 0))), jnp.pad(top, ((0, 2), (0, 0)))], axis=1
    )
    summed, rim_got = tail_exchange(bc_pieces.reshape(hcount, 2 * piece_rows, -1), rim_send, 2)
    grad_bc_mine = summed.reshape(2, piece_rows, -1)[:, : row_share + 3]
    bc_pre_pad = jnp.concatenate([bc_pre, jnp.zeros((2, 3, nstate), f32)], axis=1)
    bc_pre_mine = lax.dynamic_slice_in_dim(bc_pre_pad, first_row, row_share + 3, 1)
    in_rim = (hidx == hcount - 1) & (jnp.arange(row_share + 3) >= row_share)
    grad_bc_ext = grad_bc_mine * jnp.where(in_rim[None, :, None], 1.0, silu_grad(bc_pre_mine))
    rim_x = rim_got[:3]
    grad_x = conv_back(jnp.concatenate([grad_x_pre, rim_x], axis=0), conv_x).astype(bf16)
    grad_bc = conv_back(grad_bc_ext, convolution_bc_taps).astype(bf16)
    grad_dt = grad_steps * jax.nn.sigmoid(dt_raw + dt_bias[:, None])
    return (grad_x, grad_z, grad_bc, grad_dt)


def solution(mesh):
    return jax.shard_map(
        shards,
        mesh=mesh,
        in_specs=(
            P("seq", "head"),
            P("seq", "head"),
            P(None, "seq", None),
            P("head", "seq"),
            P("head"),
            P("head"),
            P("head"),
            P(None, "head"),
            P(),
            P("head"),
            P("seq", "head"),
        ),
        out_specs=(
            P("seq", "head"),
            P("seq", "head"),
            P(None, ("seq", "head"), None),
            P("head", "seq"),
        ),
        check_vma=False,
    )
```

```python
import jax
import jax.numpy as jnp
from jax import lax
from jax.experimental import pallas as pl
from jax.experimental.pallas import tpu as pltpu
from jax.sharding import PartitionSpec as P
import functools

MESH = pl.DeviceIdType.MESH
AXES = ("seq", "head")


def exchange_kernel(axis, n, in_ref, out_ref, land, send_sem, recv_sem):
    me = lax.axis_index(axis)
    coords = {a: lax.axis_index(a) for a in AXES}

    def dev(k):
        return tuple(k if a == axis else coords[a] for a in AXES)

    barrier = pltpu.get_barrier_semaphore()
    for i in range(1, n):
        pl.semaphore_signal(barrier, inc=1, device_id=dev(lax.rem(me + i, n)), device_id_type=MESH)
    pl.semaphore_wait(barrier, n - 1)
    copies = []
    for i in range(1, n):
        peer = lax.rem(me + i, n)
        copy = pltpu.make_async_remote_copy(
            src_ref=in_ref.at[peer],
            dst_ref=land.at[me],
            send_sem=send_sem.at[i],
            recv_sem=recv_sem.at[i],
            device_id=dev(peer),
            device_id_type=MESH,
        )
        copy.start()
        copies.append(copy)
    land[me] = in_ref[me]
    for i in range(1, n):
        copies[i - 1].wait_send()
        src = lax.rem(me + (n - i), n)
        incoming = pltpu.make_async_remote_copy(
            src_ref=in_ref.at[src],
            dst_ref=land.at[src],
            send_sem=send_sem.at[i],
            recv_sem=recv_sem.at[i],
            device_id=dev(src),
            device_id_type=MESH,
        )
        incoming.wait_recv()
    out_ref[...] = land[...]


def exchange(x, axis, cid):
    n = lax.axis_size(axis)
    return pl.pallas_call(
        functools.partial(exchange_kernel, axis, n),
        out_shape=jax.ShapeDtypeStruct(x.shape, x.dtype),
        in_specs=[pl.BlockSpec(memory_space=pltpu.VMEM)],
        out_specs=pl.BlockSpec(memory_space=pltpu.VMEM),
        scratch_shapes=[
            pltpu.VMEM(x.shape, x.dtype),
            pltpu.SemaphoreType.DMA((n,)),
            pltpu.SemaphoreType.DMA((n,)),
        ],
        compiler_params=pltpu.CompilerParams(collective_id=cid, has_side_effects=True),
    )(x)

def _peer_copies(axis, n, src_of, dst, send_sem, recv_sem):
    me = lax.axis_index(axis)
    coords = {a: lax.axis_index(a) for a in AXES}

    def dev(k):
        return tuple(k if a == axis else coords[a] for a in AXES)

    copies = []
    for i in sorted(range(1, n), key=lambda i: -min(i, n - i)):
        peer = lax.rem(me + i, n)
        copy = pltpu.make_async_remote_copy(
            src_ref=src_of(peer),
            dst_ref=dst.at[me],
            send_sem=send_sem.at[i],
            recv_sem=recv_sem.at[i],
            device_id=dev(peer),
            device_id_type=MESH,
        )
        copy.start()
        copies.append(copy)
    return copies


def _peer_waits(axis, n, copies, src_of, dst, send_sem, recv_sem):
    me = lax.axis_index(axis)
    coords = {a: lax.axis_index(a) for a in AXES}

    def dev(k):
        return tuple(k if a == axis else coords[a] for a in AXES)

    for i in range(1, n):
        copies[i - 1].wait_send()
        src = lax.rem(me + (n - i), n)
        incoming = pltpu.make_async_remote_copy(
            src_ref=src_of(src),
            dst_ref=dst.at[src],
            send_sem=send_sem.at[i],
            recv_sem=recv_sem.at[i],
            device_id=dev(src),
            device_id_type=MESH,
        )
        incoming.wait_recv()


def _barrier(axis, n):
    me = lax.axis_index(axis)
    coords = {a: lax.axis_index(a) for a in AXES}
    barrier = pltpu.get_barrier_semaphore()
    for i in range(1, n):
        peer = lax.rem(me + i, n)
        dev = tuple(peer if a == axis else coords[a] for a in AXES)
        pl.semaphore_signal(barrier, inc=1, device_id=dev, device_id_type=MESH)
    pl.semaphore_wait(barrier, n - 1)


def scan_kernel(forward, axis, n, heads, *refs):
    if forward:
        in_ref, out_ref, scale_out, land, res, land2, s1, r1, s2, r2 = refs
    else:
        in_ref, scale_in, out_ref, land, res, land2, s1, r1, s2, r2 = refs
    me = lax.axis_index(axis)
    rows = res.shape[1]
    _barrier(axis, n)
    copies = _peer_copies(axis, n, lambda p: in_ref.at[p], land, s1, r1)
    land[me] = in_ref[me]
    coords = {a: lax.axis_index(a) for a in AXES}

    def dev(k):
        return tuple(k if a == axis else coords[a] for a in AXES)

    def arrive(k):
        @pl.when(me != k)
        def _():
            pltpu.make_async_remote_copy(
                src_ref=in_ref.at[k], dst_ref=land.at[k], send_sem=s1.at[0],
                recv_sem=r1.at[lax.rem(me - k + n, n)], device_id=dev(k), device_id_type=MESH,
            ).wait_recv()

    def result_copy(k):
        return pltpu.make_async_remote_copy(
            src_ref=res.at[k], dst_ref=land2.at[me], send_sem=s2.at[k], recv_sem=r2.at[me],
            device_id=dev(k), device_id_type=MESH,
        )

    def give(k):
        @pl.when(me != k)
        def _():
            result_copy(k).start()

        @pl.when(me == k)
        def _():
            land2[k] = res[k]

    acc = jnp.zeros((rows, 128), jnp.float32)
    if forward:
        lane = lax.broadcasted_iota(jnp.int32, (1, 128), 1)
        pick = lane == me // (n // heads)
        for k in range(n):
            res[k] = acc.astype(res.dtype)
            give(k)
            arrive(k)
            parts = land[k, rows : rows + 3, :].astype(jnp.float32)
            grow = jnp.exp(parts[0:1] + parts[1:2] + parts[2:3])
            factor = jnp.sum(jnp.where(pick, grow, 0.0), axis=1, keepdims=True)
            scale_out[k] = jnp.broadcast_to(factor, (8, 128))
            acc = factor * acc + land[k, :rows, :].astype(jnp.float32)
    else:
        for k in reversed(range(n)):
            res[k] = acc.astype(res.dtype)
            give(k)
            arrive(k)
            acc = land[k].astype(jnp.float32) + scale_in[k][0:1, 0:1] * acc
    for c in copies:
        c.wait_send()
    for k in range(n):
        @pl.when(me != k)
        def _():
            result_copy(k).wait_send()

        @pl.when(me != k)
        def _():
            pltpu.make_async_remote_copy(
                src_ref=res.at[k], dst_ref=land2.at[k], send_sem=s2.at[k], recv_sem=r2.at[k],
                device_id=dev(k), device_id_type=MESH,
            ).wait_recv()
    out_ref[...] = land2[...]


def scan_pieces(x, axis, heads, cid, scales=None):
    n = lax.axis_size(axis)
    forward = scales is None
    rows = x.shape[1] - 16 if forward else x.shape[1]
    piece = (n, rows, 128)
    low = x.dtype
    vm = pl.BlockSpec(memory_space=pltpu.VMEM)
    scratch = [
        pltpu.VMEM(x.shape, low),
        pltpu.VMEM(piece, low),
        pltpu.VMEM(piece, low),
        pltpu.SemaphoreType.DMA((n,)),
        pltpu.SemaphoreType.DMA((n,)),
        pltpu.SemaphoreType.DMA((n,)),
        pltpu.SemaphoreType.DMA((n,)),
    ]
    params = pltpu.CompilerParams(collective_id=cid, has_side_effects=True)
    kern = functools.partial(scan_kernel, forward, axis, n, heads)
    if forward:
        return pl.pallas_call(
            kern,
            out_shape=(jax.ShapeDtypeStruct(piece, low), jax.ShapeDtypeStruct((n, 8, 128), jnp.float32)),
            in_specs=[vm],
            out_specs=(vm, vm),
            scratch_shapes=scratch,
            compiler_params=params,
        )(x)
    return pl.pallas_call(
        kern,
        out_shape=jax.ShapeDtypeStruct(piece, low),
        in_specs=[vm, vm],
        out_specs=vm,
        scratch_shapes=scratch,
        compiler_params=params,
    )(x, scales)


def tail_kernel(n, hn, in_ref, rim_ref, out_ref, rim_out, land, send, rim_land, s1, r1, s2, r2):
    me = lax.axis_index("seq")
    hme = lax.axis_index("head")
    prev = lax.rem(me + n - 1, n)
    nxt = lax.rem(me + 1, n)
    last = hn - 1
    barrier = pltpu.get_barrier_semaphore()
    for i in range(1, hn):
        pl.semaphore_signal(barrier, inc=1, device_id=(me, lax.rem(hme + i, hn)), device_id_type=MESH)
    pl.semaphore_signal(barrier, inc=1, device_id=(prev, hme), device_id_type=MESH)
    pl.semaphore_signal(barrier, inc=1, device_id=(nxt, hme), device_id_type=MESH)
    pl.semaphore_wait(barrier, hn + 1)
    rim_copy = pltpu.make_async_remote_copy(
        src_ref=rim_ref, dst_ref=rim_land, send_sem=s2.at[0], recv_sem=r2.at[0],
        device_id=(prev, hme), device_id_type=MESH,
    )
    rim_copy.start()

    def piece_copy(t, src):
        return pltpu.make_async_remote_copy(
            src_ref=src, dst_ref=land.at[hme], send_sem=s1.at[t], recv_sem=r1.at[hme],
            device_id=(me, t), device_id_type=MESH,
        )

    for t in range(last):
        @pl.when(hme != t)
        def _():
            piece_copy(t, in_ref.at[t]).start()

    land[hme] = in_ref[hme]
    send[...] = in_ref[last]
    rim_copy.wait_send()
    rim_copy.wait_recv()
    keep = (1 - me // (n - 1)).astype(jnp.float32)
    rows = in_ref.shape[1] // 2
    nst = in_ref.shape[2]
    width = rim_ref.shape[1] - nst
    rim_bc = rim_land[0:8, width:] * keep
    send[8:11, :] = send[8:11, :] + rim_bc[0:3]
    send[rows + 8 : rows + 11, :] = send[rows + 8 : rows + 11, :] + rim_bc[3:6]
    rim_out[...] = rim_land[0:8, 0:width] * keep

    @pl.when(hme != last)
    def _():
        piece_copy(last, send).start()

    @pl.when(hme == last)
    def _():
        land[last] = send[...]

    for t in range(hn):
        @pl.when(hme != t)
        def _():
            piece_copy(t, send).wait_send()

    for j in range(hn):
        @pl.when(hme != j)
        def _():
            pltpu.make_async_remote_copy(
                src_ref=send, dst_ref=land.at[j], send_sem=s1.at[j], recv_sem=r1.at[j],
                device_id=(me, j), device_id_type=MESH,
            ).wait_recv()

    total = land[0]
    for j in range(1, hn):
        total = total + land[j]
    out_ref[...] = total


def tail_exchange(pieces, rim, cid):
    n = lax.axis_size("seq")
    hn = lax.axis_size("head")
    vm = pl.BlockSpec(memory_space=pltpu.VMEM)
    width = rim.shape[1] - pieces.shape[2]
    return pl.pallas_call(
        functools.partial(tail_kernel, n, hn),
        out_shape=(
            jax.ShapeDtypeStruct(pieces.shape[1:], jnp.float32),
            jax.ShapeDtypeStruct((8, width), jnp.float32),
        ),
        in_specs=[vm, vm],
        out_specs=(vm, vm),
        scratch_shapes=[
            pltpu.VMEM(pieces.shape, jnp.float32),
            pltpu.VMEM(pieces.shape[1:], jnp.float32),
            pltpu.VMEM(rim.shape, jnp.float32),
            pltpu.SemaphoreType.DMA((hn,)),
            pltpu.SemaphoreType.DMA((hn,)),
            pltpu.SemaphoreType.DMA((1,)),
            pltpu.SemaphoreType.DMA((1,)),
        ],
        compiler_params=pltpu.CompilerParams(collective_id=cid, has_side_effects=True),
    )(pieces, rim)


INNER = 16384


EPS = 1e-05
HIGH = lax.Precision.HIGHEST


def passed_along(block, axis, distance):
    devices = range(lax.axis_size(axis))
    route = [(i - distance, i) for i in devices if i - distance in devices]
    return lax.ppermute(block, axis, route)


def silu_grad(value):
    sigma = jax.nn.sigmoid(value)
    return sigma * (1.0 + value * (1.0 - sigma))


def conv_rows(extended, weight_matrix):
    length = extended.shape[-2] - 3
    summed = weight_matrix[..., 0, :][..., None, :] * extended[..., 0:length, :]
    for offset in range(1, 4):
        summed = (
            summed
            + weight_matrix[..., offset, :][..., None, :]
            * extended[..., offset : offset + length, :]
        )
    return summed


def conv_back(extended, weight_matrix):
    length = extended.shape[-2] - 3
    summed = weight_matrix[..., 0, :][..., None, :] * extended[..., 3 : 3 + length, :]
    for offset in range(1, 4):
        summed = (
            summed
            + weight_matrix[..., offset, :][..., None, :]
            * extended[..., 3 - offset : 3 - offset + length, :]
        )
    return summed


def to_pieces(state, count):
    heads, nstate, width = state.shape
    return state.reshape(count, heads * nstate // count, width)


def from_pieces(pieces, heads):
    count, rows, width = pieces.shape
    return pieces.reshape(heads, count * rows // heads, width)


def scan_forward(totals, local_state):
    count = lax.axis_size("seq")
    heads, nstate, width = local_state.shape
    pieces = to_pieces(local_state, count)
    high = lax.reduce_precision(totals, exponent_bits=8, mantissa_bits=7)
    rest = totals - high
    middle = lax.reduce_precision(rest, exponent_bits=8, mantissa_bits=7)
    parts = jnp.stack([high, middle, rest - middle])
    tot_row = jnp.pad(parts, ((0, 13), (0, width - heads)))
    tot_row = jnp.broadcast_to(tot_row, (count, 16, width))
    sent = jnp.concatenate([pieces, tot_row], axis=1).astype(jnp.bfloat16)
    back, scales = scan_pieces(sent, "seq", heads, 0)
    return from_pieces(back, heads).astype(jnp.float32), scales


def scan_backward(scales, state_grad):
    count = lax.axis_size("seq")
    heads = state_grad.shape[0]
    pieces = to_pieces(state_grad, count).astype(jnp.bfloat16)
    back = scan_pieces(pieces, "seq", heads, 1, scales)
    return from_pieces(back, heads).astype(jnp.float32)


def shards(
    x_input,
    z_input,
    bc_input,
    dt_raw,
    dt_bias,
    a_log,
    d_skip,
    conv_x,
    convolution_bc_taps,
    rescale_factor,
    grad_out,
):
    length = x_input.shape[0]
    channels = x_input.shape[1]
    head_count = dt_raw.shape[0]
    width = channels // head_count
    f32 = jnp.float32
    bf16 = jnp.bfloat16
    decay_rate = -jnp.exp(a_log)
    step_size = jax.nn.softplus(dt_raw + dt_bias[:, None])
    causal = jnp.tril(jnp.ones((length, length), dtype=bool))
    nstate = bc_input.shape[2]
    rows_last = jnp.concatenate(
        [x_input[length - 3 :], jnp.moveaxis(bc_input[:, length - 3 :], 0, 1).reshape(3, 2 * nstate)],
        axis=1,
    )
    rows_prior = passed_along(rows_last, "seq", 1)
    x_ext = jnp.concatenate([rows_prior[:, :channels], x_input], axis=0)
    bc_prior = jnp.moveaxis(rows_prior[:, channels:].reshape(3, 2, nstate), 0, 1)
    bc_ext = jnp.concatenate([bc_prior, bc_input], axis=1)
    x_pre = conv_rows(x_ext.astype(f32), conv_x)
    bc_pre = conv_rows(bc_ext.astype(f32), convolution_bc_taps)
    x_rows = jax.nn.silu(x_pre).astype(bf16)
    bc_rows = jax.nn.silu(bc_pre).astype(bf16)
    b_rows = bc_rows[0]
    c_rows = bc_rows[1]
    gram = jnp.dot(c_rows, b_rows.T, preferred_element_type=f32)
    x_heads = x_rows.reshape(length, head_count, width)

    cumul = jnp.cumsum(decay_rate[:, None] * step_size, axis=1)
    totals = cumul[:, -1]
    trailing = jnp.exp(cumul[:, -1:] - cumul)
    tail_step = trailing * step_size
    weighted_b = (tail_step[:, :, None] * b_rows.astype(f32)[None]).astype(bf16)
    local_state = jnp.einsum("hsn,shp->hnp", weighted_b, x_heads, preferred_element_type=f32)

    state_exact, weight = scan_forward(totals, local_state)
    state_low = state_exact.astype(bf16)

    between = cumul[:, :, None] - cumul[:, None, :]
    decay = jnp.where(causal[None], jnp.exp(jnp.minimum(between, 0.0)), 0.0)
    mixer_low = (gram[None] * decay * step_size[:, None, :]).astype(bf16)
    intra = jnp.einsum("hts,shp->thp", mixer_low, x_heads, preferred_element_type=f32)
    handed = jnp.einsum("tn,hnp->thp", c_rows, state_low, preferred_element_type=f32)
    lifted = jnp.exp(cumul)
    mixed_heads = (
        intra + lifted.T[:, :, None] * handed + d_skip[None, :, None] * x_heads.astype(f32)
    )
    mixed_out = mixed_heads.reshape(length, channels)

    z_rows = z_input.astype(f32)
    gate_value = jax.nn.silu(z_rows)
    gated = mixed_out * gate_value
    scaled = grad_out.astype(f32) * rescale_factor
    hcount = lax.axis_size("head")
    own_sums = jnp.stack([jnp.sum(gated * gated, axis=1), jnp.sum(scaled * gated, axis=1)])
    own_sums = jnp.concatenate([own_sums, jnp.zeros((6, length), f32)], axis=0)
    sums = jnp.sum(exchange(jnp.broadcast_to(own_sums, (hcount,) + own_sums.shape), "head", 3), axis=0)
    inv_rms = lax.rsqrt(sums[0] / INNER + EPS)
    normed = gated * inv_rms[:, None]
    mean_dot = inv_rms * sums[1] / INNER
    grad_gated = inv_rms[:, None] * (scaled - normed * mean_dot[:, None])
    grad_z = (grad_gated * mixed_out * silu_grad(z_rows)).astype(bf16)
    grad_mixed = (grad_gated * gate_value).astype(bf16)
    grad_heads = grad_mixed.reshape(length, head_count, width)

    lifted_c = (lifted[:, :, None] * c_rows.astype(f32)[None]).astype(bf16)
    state_grad = jnp.einsum("htn,thp->hnp", lifted_c, grad_heads, preferred_element_type=f32)
    out_exact = scan_backward(weight, state_grad)
    out_low = out_exact.astype(bf16)

    grad_mix = jnp.einsum("thp,shp->hts", grad_heads, x_heads, preferred_element_type=f32)
    decayed = grad_mix * decay
    zterm = decayed * step_size[:, None, :]
    gram_grad = zterm * gram[None]
    reached = jnp.einsum("shp,hnp->hsn", x_heads, out_low, preferred_element_type=f32)
    inner_b = jnp.sum(b_rows.astype(f32)[None] * reached, axis=2)
    state_term = tail_step * inner_b
    grad_cumul = jnp.sum(gram_grad, axis=2) - jnp.sum(gram_grad, axis=1)
    carried_dot = jnp.sum(grad_heads.astype(f32) * handed, axis=2).T
    grad_cumul = grad_cumul + lifted * carried_dot - state_term
    end_grad = jnp.sum(state_term, axis=1) + jnp.exp(totals) * jnp.sum(
        out_exact * state_exact, axis=(1, 2)
    )
    grad_cumul = grad_cumul.at[:, -1].add(end_grad)
    grad_log = jnp.cumsum(grad_cumul[:, ::-1], axis=1)[:, ::-1]
    grad_steps = (
        jnp.sum(decayed * gram[None], axis=1)
        + trailing * inner_b
        + decay_rate[:, None] * grad_log
    )
    grad_x_heads = jnp.einsum("hts,thp->shp", mixer_low, grad_heads, preferred_element_type=f32)
    grad_x_heads = (
        grad_x_heads
        + d_skip[None, :, None] * grad_heads.astype(f32)
        + jnp.einsum("hsn,hnp->shp", weighted_b, out_low, preferred_element_type=f32)
    )
    grad_c_heads = lifted[:, :, None] * jnp.einsum(
        "thp,hnp->htn", grad_heads, state_low, preferred_element_type=f32
    )
    grad_b_heads = tail_step[:, :, None] * reached
    grad_sum = jnp.sum(zterm, axis=0)
    grad_c = jnp.sum(grad_c_heads, axis=0) + jnp.dot(grad_sum, b_rows.astype(f32), precision=HIGH)
    grad_b = jnp.sum(grad_b_heads, axis=0) + jnp.dot(
        grad_sum.T, c_rows.astype(f32), precision=HIGH
    )
    grad_bc_rows = jnp.stack([grad_b, grad_c])
    grad_x_rows = grad_x_heads.reshape(length, channels)

    grad_x_pre = grad_x_rows * silu_grad(x_pre)
    hcount = lax.axis_size("head")
    row_share = length // hcount
    hidx = lax.axis_index("head")
    first_row = hidx * row_share
    picks = []
    for h in range(hcount):
        own = [h * row_share + i for i in range(row_share + 3)]
        own = [r if r < length else length for r in own]
        picks.append(own + [length] * (12 - row_share - 3))
    picks = jnp.array(picks, jnp.int32)
    piece_rows = picks.shape[1]
    bc_rows_z = jnp.concatenate([grad_bc_rows, jnp.zeros((2, 1, nstate), f32)], axis=1)
    bc_pieces = jnp.moveaxis(jnp.take(bc_rows_z, picks.reshape(-1), axis=1).reshape(2, hcount, piece_rows, -1), 1, 0)
    top = (grad_bc_rows[:, :3] * silu_grad(bc_pre[:, :3])).reshape(6, nstate)
    rim_send = jnp.concatenate(
        [jnp.pad(grad_x_pre[:3], ((0, 5), (0, 0))), jnp.pad(top, ((0, 2), (0, 0)))], axis=1
    )
    summed, rim_got = tail_exchange(bc_pieces.reshape(hcount, 2 * piece_rows, -1), rim_send, 2)
    grad_bc_mine = summed.reshape(2, piece_rows, -1)[:, : row_share + 3]
    bc_pre_pad = jnp.concatenate([bc_pre, jnp.zeros((2, 3, nstate), f32)], axis=1)
    bc_pre_mine = lax.dynamic_slice_in_dim(bc_pre_pad, first_row, row_share + 3, 1)
    in_rim = (hidx == hcount - 1) & (jnp.arange(row_share + 3) >= row_share)
    grad_bc_ext = grad_bc_mine * jnp.where(in_rim[None, :, None], 1.0, silu_grad(bc_pre_mine))
    rim_x = rim_got[:3]
    grad_x = conv_back(jnp.concatenate([grad_x_pre, rim_x], axis=0), conv_x).astype(bf16)
    grad_bc = conv_back(grad_bc_ext, convolution_bc_taps).astype(bf16)
    grad_dt = grad_steps * jax.nn.sigmoid(dt_raw + dt_bias[:, None])
    return (grad_x, grad_z, grad_bc, grad_dt)


def solution(mesh):
    return jax.shard_map(
        shards,
        mesh=mesh,
        in_specs=(
            P("seq", "head"),
            P("seq", "head"),
            P(None, "seq", None),
            P("head", "seq"),
            P("head"),
            P("head"),
            P("head"),
            P(None, "head"),
            P(),
            P("head"),
            P("seq", "head"),
        ),
        out_specs=(
            P("seq", "head"),
            P("seq", "head"),
            P(None, ("seq", "head"), None),
            P("head", "seq"),
        ),
        check_vma=False,
    )
```

```python
import jax
import jax.numpy as jnp
from jax import lax
from jax.experimental import pallas as pl
from jax.experimental.pallas import tpu as pltpu
from jax.sharding import PartitionSpec as P
import functools

MESH = pl.DeviceIdType.MESH
AXES = ("seq", "head")


def exchange_kernel(axis, n, in_ref, out_ref, land, send_sem, recv_sem):
    me = lax.axis_index(axis)
    coords = {a: lax.axis_index(a) for a in AXES}

    def dev(k):
        return tuple(k if a == axis else coords[a] for a in AXES)

    barrier = pltpu.get_barrier_semaphore()
    for i in range(1, n):
        pl.semaphore_signal(barrier, inc=1, device_id=dev(lax.rem(me + i, n)), device_id_type=MESH)
    pl.semaphore_wait(barrier, n - 1)
    copies = []
    order = sorted(range(1, n), key=lambda i: -min(i, n - i))
    for i in order:
        peer = lax.rem(me + i, n)
        copy = pltpu.make_async_remote_copy(
            src_ref=in_ref.at[peer],
            dst_ref=land.at[me],
            send_sem=send_sem.at[i],
            recv_sem=recv_sem.at[i],
            device_id=dev(peer),
            device_id_type=MESH,
        )
        copy.start()
        copies.append(copy)
    land[me] = in_ref[me]
    for c in copies:
        c.wait_send()
    for i in range(1, n):
        src = lax.rem(me + (n - i), n)
        incoming = pltpu.make_async_remote_copy(
            src_ref=in_ref.at[src],
            dst_ref=land.at[src],
            send_sem=send_sem.at[i],
            recv_sem=recv_sem.at[i],
            device_id=dev(src),
            device_id_type=MESH,
        )
        incoming.wait_recv()
    out_ref[...] = land[...]


def exchange(x, axis, cid):
    n = lax.axis_size(axis)
    return pl.pallas_call(
        functools.partial(exchange_kernel, axis, n),
        out_shape=jax.ShapeDtypeStruct(x.shape, x.dtype),
        in_specs=[pl.BlockSpec(memory_space=pltpu.VMEM)],
        out_specs=pl.BlockSpec(memory_space=pltpu.VMEM),
        scratch_shapes=[
            pltpu.VMEM(x.shape, x.dtype),
            pltpu.SemaphoreType.DMA((n,)),
            pltpu.SemaphoreType.DMA((n,)),
        ],
        compiler_params=pltpu.CompilerParams(collective_id=cid, has_side_effects=True),
    )(x)

def _peer_copies(axis, n, src_of, dst, send_sem, recv_sem):
    me = lax.axis_index(axis)
    coords = {a: lax.axis_index(a) for a in AXES}

    def dev(k):
        return tuple(k if a == axis else coords[a] for a in AXES)

    copies = []
    for i in sorted(range(1, n), key=lambda i: -min(i, n - i)):
        peer = lax.rem(me + i, n)
        copy = pltpu.make_async_remote_copy(
            src_ref=src_of(peer),
            dst_ref=dst.at[me],
            send_sem=send_sem.at[i],
            recv_sem=recv_sem.at[i],
            device_id=dev(peer),
            device_id_type=MESH,
        )
        copy.start()
        copies.append(copy)
    return copies


def _peer_waits(axis, n, copies, src_of, dst, send_sem, recv_sem):
    me = lax.axis_index(axis)
    coords = {a: lax.axis_index(a) for a in AXES}

    def dev(k):
        return tuple(k if a == axis else coords[a] for a in AXES)

    for i in range(1, n):
        copies[i - 1].wait_send()
        src = lax.rem(me + (n - i), n)
        incoming = pltpu.make_async_remote_copy(
            src_ref=src_of(src),
            dst_ref=dst.at[src],
            send_sem=send_sem.at[i],
            recv_sem=recv_sem.at[i],
            device_id=dev(src),
            device_id_type=MESH,
        )
        incoming.wait_recv()


def _barrier(axis, n):
    me = lax.axis_index(axis)
    coords = {a: lax.axis_index(a) for a in AXES}
    barrier = pltpu.get_barrier_semaphore()
    for i in range(1, n):
        peer = lax.rem(me + i, n)
        dev = tuple(peer if a == axis else coords[a] for a in AXES)
        pl.semaphore_signal(barrier, inc=1, device_id=dev, device_id_type=MESH)
    pl.semaphore_wait(barrier, n - 1)


def scan_kernel(forward, axis, n, heads, *refs):
    if forward:
        in_ref, out_ref, scale_out, land, res, land2, s1, r1, s2, r2 = refs
    else:
        in_ref, scale_in, out_ref, land, res, land2, s1, r1, s2, r2 = refs
    me = lax.axis_index(axis)
    rows = res.shape[1]
    _barrier(axis, n)
    copies = _peer_copies(axis, n, lambda p: in_ref.at[p], land, s1, r1)
    land[me] = in_ref[me]
    coords = {a: lax.axis_index(a) for a in AXES}

    def dev(k):
        return tuple(k if a == axis else coords[a] for a in AXES)

    def arrive(k):
        @pl.when(me != k)
        def _():
            pltpu.make_async_remote_copy(
                src_ref=in_ref.at[k], dst_ref=land.at[k], send_sem=s1.at[0],
                recv_sem=r1.at[lax.rem(me - k + n, n)], device_id=dev(k), device_id_type=MESH,
            ).wait_recv()

    def result_copy(k):
        return pltpu.make_async_remote_copy(
            src_ref=res.at[k], dst_ref=land2.at[me], send_sem=s2.at[k], recv_sem=r2.at[me],
            device_id=dev(k), device_id_type=MESH,
        )

    def give(k):
        @pl.when(me != k)
        def _():
            result_copy(k).start()

        @pl.when(me == k)
        def _():
            land2[k] = res[k]

    acc = jnp.zeros((rows, 128), jnp.float32)
    if forward:
        lane = lax.broadcasted_iota(jnp.int32, (1, 128), 1)
        pick = lane == me // (n // heads)
        for k in range(n):
            res[k] = acc.astype(res.dtype)
            give(k)
            arrive(k)
            parts = land[k, rows : rows + 3, :].astype(jnp.float32)
            grow = jnp.exp(parts[0:1] + parts[1:2] + parts[2:3])
            factor = jnp.sum(jnp.where(pick, grow, 0.0), axis=1, keepdims=True)
            scale_out[k] = jnp.broadcast_to(factor, (8, 128))
            acc = factor * acc + land[k, :rows, :].astype(jnp.float32)
    else:
        for k in reversed(range(n)):
            res[k] = acc.astype(res.dtype)
            give(k)
            arrive(k)
            acc = land[k].astype(jnp.float32) + scale_in[k][0:1, 0:1] * acc
    for c in copies:
        c.wait_send()
    for k in range(n):
        @pl.when(me != k)
        def _():
            result_copy(k).wait_send()

        @pl.when(me != k)
        def _():
            pltpu.make_async_remote_copy(
                src_ref=res.at[k], dst_ref=land2.at[k], send_sem=s2.at[k], recv_sem=r2.at[k],
                device_id=dev(k), device_id_type=MESH,
            ).wait_recv()
    out_ref[...] = land2[...]


def scan_pieces(x, axis, heads, cid, scales=None):
    n = lax.axis_size(axis)
    forward = scales is None
    rows = x.shape[1] - 16 if forward else x.shape[1]
    piece = (n, rows, 128)
    low = x.dtype
    vm = pl.BlockSpec(memory_space=pltpu.VMEM)
    scratch = [
        pltpu.VMEM(x.shape, low),
        pltpu.VMEM(piece, low),
        pltpu.VMEM(piece, low),
        pltpu.SemaphoreType.DMA((n,)),
        pltpu.SemaphoreType.DMA((n,)),
        pltpu.SemaphoreType.DMA((n,)),
        pltpu.SemaphoreType.DMA((n,)),
    ]
    params = pltpu.CompilerParams(collective_id=cid, has_side_effects=True)
    kern = functools.partial(scan_kernel, forward, axis, n, heads)
    if forward:
        return pl.pallas_call(
            kern,
            out_shape=(jax.ShapeDtypeStruct(piece, low), jax.ShapeDtypeStruct((n, 8, 128), jnp.float32)),
            in_specs=[vm],
            out_specs=(vm, vm),
            scratch_shapes=scratch,
            compiler_params=params,
        )(x)
    return pl.pallas_call(
        kern,
        out_shape=jax.ShapeDtypeStruct(piece, low),
        in_specs=[vm, vm],
        out_specs=vm,
        scratch_shapes=scratch,
        compiler_params=params,
    )(x, scales)


def tail_kernel(n, hn, in_ref, rim_ref, out_ref, rim_out, land, send, rim_land, s1, r1, s2, r2):
    me = lax.axis_index("seq")
    hme = lax.axis_index("head")
    prev = lax.rem(me + n - 1, n)
    nxt = lax.rem(me + 1, n)
    last = hn - 1
    barrier = pltpu.get_barrier_semaphore()
    for i in range(1, hn):
        pl.semaphore_signal(barrier, inc=1, device_id=(me, lax.rem(hme + i, hn)), device_id_type=MESH)
    pl.semaphore_signal(barrier, inc=1, device_id=(prev, hme), device_id_type=MESH)
    pl.semaphore_signal(barrier, inc=1, device_id=(nxt, hme), device_id_type=MESH)
    pl.semaphore_wait(barrier, hn + 1)
    rim_copy = pltpu.make_async_remote_copy(
        src_ref=rim_ref, dst_ref=rim_land, send_sem=s2.at[0], recv_sem=r2.at[0],
        device_id=(prev, hme), device_id_type=MESH,
    )
    rim_copy.start()

    def piece_copy(t, src):
        return pltpu.make_async_remote_copy(
            src_ref=src, dst_ref=land.at[hme], send_sem=s1.at[t], recv_sem=r1.at[hme],
            device_id=(me, t), device_id_type=MESH,
        )

    for t in range(last):
        @pl.when(hme != t)
        def _():
            piece_copy(t, in_ref.at[t]).start()

    land[hme] = in_ref[hme]
    send[...] = in_ref[last]
    rim_copy.wait_send()
    rim_copy.wait_recv()
    keep = (1 - me // (n - 1)).astype(jnp.float32)
    rows = in_ref.shape[1] // 2
    nst = in_ref.shape[2]
    width = rim_ref.shape[1] - nst
    rim_bc = rim_land[0:8, width:] * keep
    send[8:11, :] = send[8:11, :] + rim_bc[0:3]
    send[rows + 8 : rows + 11, :] = send[rows + 8 : rows + 11, :] + rim_bc[3:6]
    rim_out[...] = rim_land[0:8, 0:width] * keep

    @pl.when(hme != last)
    def _():
        piece_copy(last, send).start()

    @pl.when(hme == last)
    def _():
        land[last] = send[...]

    for t in range(hn):
        @pl.when(hme != t)
        def _():
            piece_copy(t, send).wait_send()

    for j in range(hn):
        @pl.when(hme != j)
        def _():
            pltpu.make_async_remote_copy(
                src_ref=send, dst_ref=land.at[j], send_sem=s1.at[j], recv_sem=r1.at[j],
                device_id=(me, j), device_id_type=MESH,
            ).wait_recv()

    total = land[0]
    for j in range(1, hn):
        total = total + land[j]
    out_ref[...] = total


def tail_exchange(pieces, rim, cid):
    n = lax.axis_size("seq")
    hn = lax.axis_size("head")
    vm = pl.BlockSpec(memory_space=pltpu.VMEM)
    width = rim.shape[1] - pieces.shape[2]
    return pl.pallas_call(
        functools.partial(tail_kernel, n, hn),
        out_shape=(
            jax.ShapeDtypeStruct(pieces.shape[1:], jnp.float32),
            jax.ShapeDtypeStruct((8, width), jnp.float32),
        ),
        in_specs=[vm, vm],
        out_specs=(vm, vm),
        scratch_shapes=[
            pltpu.VMEM(pieces.shape, jnp.float32),
            pltpu.VMEM(pieces.shape[1:], jnp.float32),
            pltpu.VMEM(rim.shape, jnp.float32),
            pltpu.SemaphoreType.DMA((hn,)),
            pltpu.SemaphoreType.DMA((hn,)),
            pltpu.SemaphoreType.DMA((1,)),
            pltpu.SemaphoreType.DMA((1,)),
        ],
        compiler_params=pltpu.CompilerParams(collective_id=cid, has_side_effects=True),
    )(pieces, rim)


INNER = 16384


EPS = 1e-05
HIGH = lax.Precision.HIGHEST


def passed_along(block, axis, distance):
    devices = range(lax.axis_size(axis))
    route = [(i - distance, i) for i in devices if i - distance in devices]
    return lax.ppermute(block, axis, route)


def silu_grad(value):
    sigma = jax.nn.sigmoid(value)
    return sigma * (1.0 + value * (1.0 - sigma))


def conv_rows(extended, weight_matrix):
    length = extended.shape[-2] - 3
    summed = weight_matrix[..., 0, :][..., None, :] * extended[..., 0:length, :]
    for offset in range(1, 4):
        summed = (
            summed
            + weight_matrix[..., offset, :][..., None, :]
            * extended[..., offset : offset + length, :]
        )
    return summed


def conv_back(extended, weight_matrix):
    length = extended.shape[-2] - 3
    summed = weight_matrix[..., 0, :][..., None, :] * extended[..., 3 : 3 + length, :]
    for offset in range(1, 4):
        summed = (
            summed
            + weight_matrix[..., offset, :][..., None, :]
            * extended[..., 3 - offset : 3 - offset + length, :]
        )
    return summed


def to_pieces(state, count):
    heads, nstate, width = state.shape
    return state.reshape(count, heads * nstate // count, width)


def from_pieces(pieces, heads):
    count, rows, width = pieces.shape
    return pieces.reshape(heads, count * rows // heads, width)


def scan_forward(totals, local_state):
    count = lax.axis_size("seq")
    heads, nstate, width = local_state.shape
    pieces = to_pieces(local_state, count)
    high = lax.reduce_precision(totals, exponent_bits=8, mantissa_bits=7)
    rest = totals - high
    middle = lax.reduce_precision(rest, exponent_bits=8, mantissa_bits=7)
    parts = jnp.stack([high, middle, rest - middle])
    tot_row = jnp.pad(parts, ((0, 13), (0, width - heads)))
    tot_row = jnp.broadcast_to(tot_row, (count, 16, width))
    sent = jnp.concatenate([pieces, tot_row], axis=1).astype(jnp.bfloat16)
    back, scales = scan_pieces(sent, "seq", heads, 0)
    return from_pieces(back, heads).astype(jnp.float32), scales


def scan_backward(scales, state_grad):
    count = lax.axis_size("seq")
    heads = state_grad.shape[0]
    pieces = to_pieces(state_grad, count).astype(jnp.bfloat16)
    back = scan_pieces(pieces, "seq", heads, 1, scales)
    return from_pieces(back, heads).astype(jnp.float32)


def shards(
    x_input,
    z_input,
    bc_input,
    dt_raw,
    dt_bias,
    a_log,
    d_skip,
    conv_x,
    convolution_bc_taps,
    rescale_factor,
    grad_out,
):
    length = x_input.shape[0]
    channels = x_input.shape[1]
    head_count = dt_raw.shape[0]
    width = channels // head_count
    f32 = jnp.float32
    bf16 = jnp.bfloat16
    decay_rate = -jnp.exp(a_log)
    step_size = jax.nn.softplus(dt_raw + dt_bias[:, None])
    causal = jnp.tril(jnp.ones((length, length), dtype=bool))
    nstate = bc_input.shape[2]
    rows_last = jnp.concatenate(
        [x_input[length - 3 :], jnp.moveaxis(bc_input[:, length - 3 :], 0, 1).reshape(3, 2 * nstate)],
        axis=1,
    )
    rows_prior = passed_along(rows_last, "seq", 1)
    x_ext = jnp.concatenate([rows_prior[:, :channels], x_input], axis=0)
    bc_prior = jnp.moveaxis(rows_prior[:, channels:].reshape(3, 2, nstate), 0, 1)
    bc_ext = jnp.concatenate([bc_prior, bc_input], axis=1)
    x_pre = conv_rows(x_ext.astype(f32), conv_x)
    bc_pre = conv_rows(bc_ext.astype(f32), convolution_bc_taps)
    x_rows = jax.nn.silu(x_pre).astype(bf16)
    bc_rows = jax.nn.silu(bc_pre).astype(bf16)
    b_rows = bc_rows[0]
    c_rows = bc_rows[1]
    gram = jnp.dot(c_rows, b_rows.T, preferred_element_type=f32)
    x_heads = x_rows.reshape(length, head_count, width)

    cumul = jnp.cumsum(decay_rate[:, None] * step_size, axis=1)
    totals = cumul[:, -1]
    trailing = jnp.exp(cumul[:, -1:] - cumul)
    tail_step = trailing * step_size
    weighted_b = (tail_step[:, :, None] * b_rows.astype(f32)[None]).astype(bf16)
    local_state = jnp.einsum("hsn,shp->hnp", weighted_b, x_heads, preferred_element_type=f32)

    state_exact, weight = scan_forward(totals, local_state)
    state_low = state_exact.astype(bf16)

    between = cumul[:, :, None] - cumul[:, None, :]
    decay = jnp.where(causal[None], jnp.exp(jnp.minimum(between, 0.0)), 0.0)
    mixer_low = (gram[None] * decay * step_size[:, None, :]).astype(bf16)
    intra = jnp.einsum("hts,shp->thp", mixer_low, x_heads, preferred_element_type=f32)
    handed = jnp.einsum("tn,hnp->thp", c_rows, state_low, preferred_element_type=f32)
    lifted = jnp.exp(cumul)
    mixed_heads = (
        intra + lifted.T[:, :, None] * handed + d_skip[None, :, None] * x_heads.astype(f32)
    )
    mixed_out = mixed_heads.reshape(length, channels)

    z_rows = z_input.astype(f32)
    gate_value = jax.nn.silu(z_rows)
    gated = mixed_out * gate_value
    scaled = grad_out.astype(f32) * rescale_factor
    hcount = lax.axis_size("head")
    own_sums = jnp.stack([jnp.sum(gated * gated, axis=1), jnp.sum(scaled * gated, axis=1)])
    own_sums = jnp.concatenate([own_sums, jnp.zeros((6, length), f32)], axis=0)
    sums = jnp.sum(exchange(jnp.broadcast_to(own_sums, (hcount,) + own_sums.shape), "head", 3), axis=0)
    inv_rms = lax.rsqrt(sums[0] / INNER + EPS)
    normed = gated * inv_rms[:, None]
    mean_dot = inv_rms * sums[1] / INNER
    grad_gated = inv_rms[:, None] * (scaled - normed * mean_dot[:, None])
    grad_z = (grad_gated * mixed_out * silu_grad(z_rows)).astype(bf16)
    grad_mixed = (grad_gated * gate_value).astype(bf16)
    grad_heads = grad_mixed.reshape(length, head_count, width)

    lifted_c = (lifted[:, :, None] * c_rows.astype(f32)[None]).astype(bf16)
    state_grad = jnp.einsum("htn,thp->hnp", lifted_c, grad_heads, preferred_element_type=f32)
    out_exact = scan_backward(weight, state_grad)
    out_low = out_exact.astype(bf16)

    grad_mix = jnp.einsum("thp,shp->hts", grad_heads, x_heads, preferred_element_type=f32)
    decayed = grad_mix * decay
    zterm = decayed * step_size[:, None, :]
    gram_grad = zterm * gram[None]
    reached = jnp.einsum("shp,hnp->hsn", x_heads, out_low, preferred_element_type=f32)
    inner_b = jnp.sum(b_rows.astype(f32)[None] * reached, axis=2)
    state_term = tail_step * inner_b
    grad_cumul = jnp.sum(gram_grad, axis=2) - jnp.sum(gram_grad, axis=1)
    carried_dot = jnp.sum(grad_heads.astype(f32) * handed, axis=2).T
    grad_cumul = grad_cumul + lifted * carried_dot - state_term
    end_grad = jnp.sum(state_term, axis=1) + jnp.exp(totals) * jnp.sum(
        out_exact * state_exact, axis=(1, 2)
    )
    grad_cumul = grad_cumul.at[:, -1].add(end_grad)
    grad_log = jnp.cumsum(grad_cumul[:, ::-1], axis=1)[:, ::-1]
    grad_steps = (
        jnp.sum(decayed * gram[None], axis=1)
        + trailing * inner_b
        + decay_rate[:, None] * grad_log
    )
    grad_x_heads = jnp.einsum("hts,thp->shp", mixer_low, grad_heads, preferred_element_type=f32)
    grad_x_heads = (
        grad_x_heads
        + d_skip[None, :, None] * grad_heads.astype(f32)
        + jnp.einsum("hsn,hnp->shp", weighted_b, out_low, preferred_element_type=f32)
    )
    grad_c_heads = lifted[:, :, None] * jnp.einsum(
        "thp,hnp->htn", grad_heads, state_low, preferred_element_type=f32
    )
    grad_b_heads = tail_step[:, :, None] * reached
    grad_sum = jnp.sum(zterm, axis=0)
    grad_c = jnp.sum(grad_c_heads, axis=0) + jnp.dot(grad_sum, b_rows.astype(f32), precision=HIGH)
    grad_b = jnp.sum(grad_b_heads, axis=0) + jnp.dot(
        grad_sum.T, c_rows.astype(f32), precision=HIGH
    )
    grad_bc_rows = jnp.stack([grad_b, grad_c])
    grad_x_rows = grad_x_heads.reshape(length, channels)

    grad_x_pre = grad_x_rows * silu_grad(x_pre)
    hcount = lax.axis_size("head")
    row_share = length // hcount
    hidx = lax.axis_index("head")
    first_row = hidx * row_share
    picks = []
    for h in range(hcount):
        own = [h * row_share + i for i in range(row_share + 3)]
        own = [r if r < length else length for r in own]
        picks.append(own + [length] * (12 - row_share - 3))
    picks = jnp.array(picks, jnp.int32)
    piece_rows = picks.shape[1]
    bc_rows_z = jnp.concatenate([grad_bc_rows, jnp.zeros((2, 1, nstate), f32)], axis=1)
    bc_pieces = jnp.moveaxis(jnp.take(bc_rows_z, picks.reshape(-1), axis=1).reshape(2, hcount, piece_rows, -1), 1, 0)
    top = (grad_bc_rows[:, :3] * silu_grad(bc_pre[:, :3])).reshape(6, nstate)
    rim_send = jnp.concatenate(
        [jnp.pad(grad_x_pre[:3], ((0, 5), (0, 0))), jnp.pad(top, ((0, 2), (0, 0)))], axis=1
    )
    summed, rim_got = tail_exchange(bc_pieces.reshape(hcount, 2 * piece_rows, -1), rim_send, 2)
    grad_bc_mine = summed.reshape(2, piece_rows, -1)[:, : row_share + 3]
    bc_pre_pad = jnp.concatenate([bc_pre, jnp.zeros((2, 3, nstate), f32)], axis=1)
    bc_pre_mine = lax.dynamic_slice_in_dim(bc_pre_pad, first_row, row_share + 3, 1)
    in_rim = (hidx == hcount - 1) & (jnp.arange(row_share + 3) >= row_share)
    grad_bc_ext = grad_bc_mine * jnp.where(in_rim[None, :, None], 1.0, silu_grad(bc_pre_mine))
    rim_x = rim_got[:3]
    grad_x = conv_back(jnp.concatenate([grad_x_pre, rim_x], axis=0), conv_x).astype(bf16)
    grad_bc = conv_back(grad_bc_ext, convolution_bc_taps).astype(bf16)
    grad_dt = grad_steps * jax.nn.sigmoid(dt_raw + dt_bias[:, None])
    return (grad_x, grad_z, grad_bc, grad_dt)


def solution(mesh):
    return jax.shard_map(
        shards,
        mesh=mesh,
        in_specs=(
            P("seq", "head"),
            P("seq", "head"),
            P(None, "seq", None),
            P("head", "seq"),
            P("head"),
            P("head"),
            P("head"),
            P(None, "head"),
            P(),
            P("head"),
            P("seq", "head"),
        ),
        out_specs=(
            P("seq", "head"),
            P("seq", "head"),
            P(None, ("seq", "head"), None),
            P("head", "seq"),
        ),
        check_vma=False,
    )
```

```python
import jax
import jax.numpy as jnp
from jax import lax
from jax.experimental import pallas as pl
from jax.experimental.pallas import tpu as pltpu
from jax.sharding import PartitionSpec as P
import functools

MESH = pl.DeviceIdType.MESH
AXES = ("seq", "head")


def gather_sum_kernel(axis, n, in_ref, out_ref, land, send_sem, recv_sem):
    me = lax.axis_index(axis)
    coords = {a: lax.axis_index(a) for a in AXES}

    def dev(k):
        return tuple(k if a == axis else coords[a] for a in AXES)

    barrier = pltpu.get_barrier_semaphore()
    for i in range(1, n):
        pl.semaphore_signal(barrier, inc=1, device_id=dev(lax.rem(me + i, n)), device_id_type=MESH)
    pl.semaphore_wait(barrier, n - 1)
    copies = []
    order = sorted(range(1, n), key=lambda i: -min(i, n - i))
    for i in order:
        peer = lax.rem(me + i, n)
        copy = pltpu.make_async_remote_copy(
            src_ref=in_ref,
            dst_ref=land.at[me],
            send_sem=send_sem.at[i],
            recv_sem=recv_sem.at[i],
            device_id=dev(peer),
            device_id_type=MESH,
        )
        copy.start()
        copies.append(copy)
    land[me] = in_ref[...]
    for c in copies:
        c.wait_send()
    for i in range(1, n):
        src = lax.rem(me + (n - i), n)
        incoming = pltpu.make_async_remote_copy(
            src_ref=in_ref,
            dst_ref=land.at[src],
            send_sem=send_sem.at[i],
            recv_sem=recv_sem.at[i],
            device_id=dev(src),
            device_id_type=MESH,
        )
        incoming.wait_recv()
    total = land[0]
    for j in range(1, n):
        total = total + land[j]
    out_ref[...] = total


def gather_sum(x, axis, cid):
    n = lax.axis_size(axis)
    return pl.pallas_call(
        functools.partial(gather_sum_kernel, axis, n),
        out_shape=jax.ShapeDtypeStruct(x.shape, x.dtype),
        in_specs=[pl.BlockSpec(memory_space=pltpu.VMEM)],
        out_specs=pl.BlockSpec(memory_space=pltpu.VMEM),
        scratch_shapes=[
            pltpu.VMEM((n,) + x.shape, x.dtype),
            pltpu.SemaphoreType.DMA((n,)),
            pltpu.SemaphoreType.DMA((n,)),
        ],
        compiler_params=pltpu.CompilerParams(collective_id=cid, has_side_effects=True),
    )(x)

def _peer_copies(axis, n, src_of, dst, send_sem, recv_sem):
    me = lax.axis_index(axis)
    coords = {a: lax.axis_index(a) for a in AXES}

    def dev(k):
        return tuple(k if a == axis else coords[a] for a in AXES)

    copies = []
    for i in sorted(range(1, n), key=lambda i: -min(i, n - i)):
        peer = lax.rem(me + i, n)
        copy = pltpu.make_async_remote_copy(
            src_ref=src_of(peer),
            dst_ref=dst.at[me],
            send_sem=send_sem.at[i],
            recv_sem=recv_sem.at[i],
            device_id=dev(peer),
            device_id_type=MESH,
        )
        copy.start()
        copies.append(copy)
    return copies


def _peer_waits(axis, n, copies, src_of, dst, send_sem, recv_sem):
    me = lax.axis_index(axis)
    coords = {a: lax.axis_index(a) for a in AXES}

    def dev(k):
        return tuple(k if a == axis else coords[a] for a in AXES)

    for i in range(1, n):
        copies[i - 1].wait_send()
        src = lax.rem(me + (n - i), n)
        incoming = pltpu.make_async_remote_copy(
            src_ref=src_of(src),
            dst_ref=dst.at[src],
            send_sem=send_sem.at[i],
            recv_sem=recv_sem.at[i],
            device_id=dev(src),
            device_id_type=MESH,
        )
        incoming.wait_recv()


def _barrier(axis, n):
    me = lax.axis_index(axis)
    coords = {a: lax.axis_index(a) for a in AXES}
    barrier = pltpu.get_barrier_semaphore()
    for i in range(1, n):
        peer = lax.rem(me + i, n)
        dev = tuple(peer if a == axis else coords[a] for a in AXES)
        pl.semaphore_signal(barrier, inc=1, device_id=dev, device_id_type=MESH)
    pl.semaphore_wait(barrier, n - 1)


def scan_kernel(forward, axis, n, heads, *refs):
    if forward:
        in_ref, out_ref, scale_out, land, res, land2, s1, r1, s2, r2 = refs
    else:
        in_ref, scale_in, out_ref, land, res, land2, s1, r1, s2, r2 = refs
    me = lax.axis_index(axis)
    rows = res.shape[1]
    _barrier(axis, n)
    copies = _peer_copies(axis, n, lambda p: in_ref.at[p], land, s1, r1)
    land[me] = in_ref[me]
    coords = {a: lax.axis_index(a) for a in AXES}

    def dev(k):
        return tuple(k if a == axis else coords[a] for a in AXES)

    def arrive(k):
        @pl.when(me != k)
        def _():
            pltpu.make_async_remote_copy(
                src_ref=in_ref.at[k], dst_ref=land.at[k], send_sem=s1.at[0],
                recv_sem=r1.at[lax.rem(me - k + n, n)], device_id=dev(k), device_id_type=MESH,
            ).wait_recv()

    def result_copy(k):
        return pltpu.make_async_remote_copy(
            src_ref=res.at[k], dst_ref=land2.at[me], send_sem=s2.at[k], recv_sem=r2.at[me],
            device_id=dev(k), device_id_type=MESH,
        )

    def give(k):
        @pl.when(me != k)
        def _():
            result_copy(k).start()

        @pl.when(me == k)
        def _():
            land2[k] = res[k]

    acc = jnp.zeros((rows, 128), jnp.float32)
    if forward:
        lane = lax.broadcasted_iota(jnp.int32, (1, 128), 1)
        pick = lane == me // (n // heads)
        for k in range(n):
            res[k] = acc.astype(res.dtype)
            give(k)
            arrive(k)
            parts = land[k, rows : rows + 3, :].astype(jnp.float32)
            grow = jnp.exp(parts[0:1] + parts[1:2] + parts[2:3])
            factor = jnp.sum(jnp.where(pick, grow, 0.0), axis=1, keepdims=True)
            scale_out[k] = jnp.broadcast_to(factor, (8, 128))
            acc = factor * acc + land[k, :rows, :].astype(jnp.float32)
    else:
        for k in reversed(range(n)):
            res[k] = acc.astype(res.dtype)
            give(k)
            arrive(k)
            acc = land[k].astype(jnp.float32) + scale_in[k][0:1, 0:1] * acc
    for c in copies:
        c.wait_send()
    for k in range(n):
        @pl.when(me != k)
        def _():
            result_copy(k).wait_send()

        @pl.when(me != k)
        def _():
            pltpu.make_async_remote_copy(
                src_ref=res.at[k], dst_ref=land2.at[k], send_sem=s2.at[k], recv_sem=r2.at[k],
                device_id=dev(k), device_id_type=MESH,
            ).wait_recv()
    out_ref[...] = land2[...]


def scan_pieces(x, axis, heads, cid, scales=None):
    n = lax.axis_size(axis)
    forward = scales is None
    rows = x.shape[1] - 16 if forward else x.shape[1]
    piece = (n, rows, 128)
    low = x.dtype
    vm = pl.BlockSpec(memory_space=pltpu.VMEM)
    scratch = [
        pltpu.VMEM(x.shape, low),
        pltpu.VMEM(piece, low),
        pltpu.VMEM(piece, low),
        pltpu.SemaphoreType.DMA((n,)),
        pltpu.SemaphoreType.DMA((n,)),
        pltpu.SemaphoreType.DMA((n,)),
        pltpu.SemaphoreType.DMA((n,)),
    ]
    params = pltpu.CompilerParams(collective_id=cid, has_side_effects=True)
    kern = functools.partial(scan_kernel, forward, axis, n, heads)
    if forward:
        return pl.pallas_call(
            kern,
            out_shape=(jax.ShapeDtypeStruct(piece, low), jax.ShapeDtypeStruct((n, 8, 128), jnp.float32)),
            in_specs=[vm],
            out_specs=(vm, vm),
            scratch_shapes=scratch,
            compiler_params=params,
        )(x)
    return pl.pallas_call(
        kern,
        out_shape=jax.ShapeDtypeStruct(piece, low),
        in_specs=[vm, vm],
        out_specs=vm,
        scratch_shapes=scratch,
        compiler_params=params,
    )(x, scales)


def tail_kernel(n, hn, in_ref, rim_ref, out_ref, rim_out, land, send, rim_land, s1, r1, s2, r2):
    me = lax.axis_index("seq")
    hme = lax.axis_index("head")
    prev = lax.rem(me + n - 1, n)
    nxt = lax.rem(me + 1, n)
    last = hn - 1
    barrier = pltpu.get_barrier_semaphore()
    for i in range(1, hn):
        pl.semaphore_signal(barrier, inc=1, device_id=(me, lax.rem(hme + i, hn)), device_id_type=MESH)
    pl.semaphore_signal(barrier, inc=1, device_id=(prev, hme), device_id_type=MESH)
    pl.semaphore_signal(barrier, inc=1, device_id=(nxt, hme), device_id_type=MESH)
    pl.semaphore_wait(barrier, hn + 1)
    rim_copy = pltpu.make_async_remote_copy(
        src_ref=rim_ref, dst_ref=rim_land, send_sem=s2.at[0], recv_sem=r2.at[0],
        device_id=(prev, hme), device_id_type=MESH,
    )
    rim_copy.start()

    def piece_copy(t, src):
        return pltpu.make_async_remote_copy(
            src_ref=src, dst_ref=land.at[hme], send_sem=s1.at[t], recv_sem=r1.at[hme],
            device_id=(me, t), device_id_type=MESH,
        )

    for t in range(last):
        @pl.when(hme != t)
        def _():
            piece_copy(t, in_ref.at[t]).start()

    land[hme] = in_ref[hme]
    send[...] = in_ref[last]
    rim_copy.wait_send()
    rim_copy.wait_recv()
    keep = (1 - me // (n - 1)).astype(jnp.float32)
    rows = in_ref.shape[1] // 2
    nst = in_ref.shape[2]
    width = rim_ref.shape[1] - nst
    rim_bc = rim_land[0:8, width:] * keep
    send[8:11, :] = send[8:11, :] + rim_bc[0:3]
    send[rows + 8 : rows + 11, :] = send[rows + 8 : rows + 11, :] + rim_bc[3:6]
    rim_out[...] = rim_land[0:8, 0:width] * keep

    @pl.when(hme != last)
    def _():
        piece_copy(last, send).start()

    @pl.when(hme == last)
    def _():
        land[last] = send[...]

    for t in range(hn):
        @pl.when(hme != t)
        def _():
            piece_copy(t, send).wait_send()

    for j in range(hn):
        @pl.when(hme != j)
        def _():
            pltpu.make_async_remote_copy(
                src_ref=send, dst_ref=land.at[j], send_sem=s1.at[j], recv_sem=r1.at[j],
                device_id=(me, j), device_id_type=MESH,
            ).wait_recv()

    total = land[0]
    for j in range(1, hn):
        total = total + land[j]
    out_ref[...] = total


def tail_exchange(pieces, rim, cid):
    n = lax.axis_size("seq")
    hn = lax.axis_size("head")
    vm = pl.BlockSpec(memory_space=pltpu.VMEM)
    width = rim.shape[1] - pieces.shape[2]
    return pl.pallas_call(
        functools.partial(tail_kernel, n, hn),
        out_shape=(
            jax.ShapeDtypeStruct(pieces.shape[1:], jnp.float32),
            jax.ShapeDtypeStruct((8, width), jnp.float32),
        ),
        in_specs=[vm, vm],
        out_specs=(vm, vm),
        scratch_shapes=[
            pltpu.VMEM(pieces.shape, jnp.float32),
            pltpu.VMEM(pieces.shape[1:], jnp.float32),
            pltpu.VMEM(rim.shape, jnp.float32),
            pltpu.SemaphoreType.DMA((hn,)),
            pltpu.SemaphoreType.DMA((hn,)),
            pltpu.SemaphoreType.DMA((1,)),
            pltpu.SemaphoreType.DMA((1,)),
        ],
        compiler_params=pltpu.CompilerParams(collective_id=cid, has_side_effects=True),
    )(pieces, rim)


INNER = 16384


EPS = 1e-05
HIGH = lax.Precision.HIGHEST


def passed_along(block, axis, distance):
    devices = range(lax.axis_size(axis))
    route = [(i - distance, i) for i in devices if i - distance in devices]
    return lax.ppermute(block, axis, route)


def silu_grad(value):
    sigma = jax.nn.sigmoid(value)
    return sigma * (1.0 + value * (1.0 - sigma))


def conv_rows(extended, weight_matrix):
    length = extended.shape[-2] - 3
    summed = weight_matrix[..., 0, :][..., None, :] * extended[..., 0:length, :]
    for offset in range(1, 4):
        summed = (
            summed
            + weight_matrix[..., offset, :][..., None, :]
            * extended[..., offset : offset + length, :]
        )
    return summed


def conv_back(extended, weight_matrix):
    length = extended.shape[-2] - 3
    summed = weight_matrix[..., 0, :][..., None, :] * extended[..., 3 : 3 + length, :]
    for offset in range(1, 4):
        summed = (
            summed
            + weight_matrix[..., offset, :][..., None, :]
            * extended[..., 3 - offset : 3 - offset + length, :]
        )
    return summed


def to_pieces(state, count):
    heads, nstate, width = state.shape
    return state.reshape(count, heads * nstate // count, width)


def from_pieces(pieces, heads):
    count, rows, width = pieces.shape
    return pieces.reshape(heads, count * rows // heads, width)


def scan_forward(totals, local_state):
    count = lax.axis_size("seq")
    heads, nstate, width = local_state.shape
    pieces = to_pieces(local_state, count)
    high = lax.reduce_precision(totals, exponent_bits=8, mantissa_bits=7)
    rest = totals - high
    middle = lax.reduce_precision(rest, exponent_bits=8, mantissa_bits=7)
    parts = jnp.stack([high, middle, rest - middle])
    tot_row = jnp.pad(parts, ((0, 13), (0, width - heads)))
    tot_row = jnp.broadcast_to(tot_row, (count, 16, width))
    sent = jnp.concatenate([pieces, tot_row], axis=1).astype(jnp.bfloat16)
    back, scales = scan_pieces(sent, "seq", heads, 0)
    return from_pieces(back, heads).astype(jnp.float32), scales


def scan_backward(scales, state_grad):
    count = lax.axis_size("seq")
    heads = state_grad.shape[0]
    pieces = to_pieces(state_grad, count).astype(jnp.bfloat16)
    back = scan_pieces(pieces, "seq", heads, 1, scales)
    return from_pieces(back, heads).astype(jnp.float32)


def shards(
    x_input,
    z_input,
    bc_input,
    dt_raw,
    dt_bias,
    a_log,
    d_skip,
    conv_x,
    convolution_bc_taps,
    rescale_factor,
    grad_out,
):
    length = x_input.shape[0]
    channels = x_input.shape[1]
    head_count = dt_raw.shape[0]
    width = channels // head_count
    f32 = jnp.float32
    bf16 = jnp.bfloat16
    decay_rate = -jnp.exp(a_log)
    step_size = jax.nn.softplus(dt_raw + dt_bias[:, None])
    causal = jnp.tril(jnp.ones((length, length), dtype=bool))
    nstate = bc_input.shape[2]
    rows_last = jnp.concatenate(
        [x_input[length - 3 :], jnp.moveaxis(bc_input[:, length - 3 :], 0, 1).reshape(3, 2 * nstate)],
        axis=1,
    )
    rows_prior = passed_along(rows_last, "seq", 1)
    x_ext = jnp.concatenate([rows_prior[:, :channels], x_input], axis=0)
    bc_prior = jnp.moveaxis(rows_prior[:, channels:].reshape(3, 2, nstate), 0, 1)
    bc_ext = jnp.concatenate([bc_prior, bc_input], axis=1)
    x_pre = conv_rows(x_ext.astype(f32), conv_x)
    bc_pre = conv_rows(bc_ext.astype(f32), convolution_bc_taps)
    x_rows = jax.nn.silu(x_pre).astype(bf16)
    bc_rows = jax.nn.silu(bc_pre).astype(bf16)
    b_rows = bc_rows[0]
    c_rows = bc_rows[1]
    gram = jnp.dot(c_rows, b_rows.T, preferred_element_type=f32)
    x_heads = x_rows.reshape(length, head_count, width)

    cumul = jnp.cumsum(decay_rate[:, None] * step_size, axis=1)
    totals = cumul[:, -1]
    trailing = jnp.exp(cumul[:, -1:] - cumul)
    tail_step = trailing * step_size
    weighted_b = (tail_step[:, :, None] * b_rows.astype(f32)[None]).astype(bf16)
    local_state = jnp.einsum("hsn,shp->hnp", weighted_b, x_heads, preferred_element_type=f32)

    state_exact, weight = scan_forward(totals, local_state)
    state_low = state_exact.astype(bf16)

    between = cumul[:, :, None] - cumul[:, None, :]
    decay = jnp.where(causal[None], jnp.exp(jnp.minimum(between, 0.0)), 0.0)
    mixer_low = (gram[None] * decay * step_size[:, None, :]).astype(bf16)
    intra = jnp.einsum("hts,shp->thp", mixer_low, x_heads, preferred_element_type=f32)
    handed = jnp.einsum("tn,hnp->thp", c_rows, state_low, preferred_element_type=f32)
    lifted = jnp.exp(cumul)
    mixed_heads = (
        intra + lifted.T[:, :, None] * handed + d_skip[None, :, None] * x_heads.astype(f32)
    )
    mixed_out = mixed_heads.reshape(length, channels)

    z_rows = z_input.astype(f32)
    gate_value = jax.nn.silu(z_rows)
    gated = mixed_out * gate_value
    scaled = grad_out.astype(f32) * rescale_factor
    hcount = lax.axis_size("head")
    own_sums = jnp.stack([jnp.sum(gated * gated, axis=1), jnp.sum(scaled * gated, axis=1)])
    own_sums = jnp.concatenate([own_sums, jnp.zeros((6, length), f32)], axis=0)
    sums = gather_sum(own_sums, "head", 3)
    inv_rms = lax.rsqrt(sums[0] / INNER + EPS)
    normed = gated * inv_rms[:, None]
    mean_dot = inv_rms * sums[1] / INNER
    grad_gated = inv_rms[:, None] * (scaled - normed * mean_dot[:, None])
    grad_z = (grad_gated * mixed_out * silu_grad(z_rows)).astype(bf16)
    grad_mixed = (grad_gated * gate_value).astype(bf16)
    grad_heads = grad_mixed.reshape(length, head_count, width)

    lifted_c = (lifted[:, :, None] * c_rows.astype(f32)[None]).astype(bf16)
    state_grad = jnp.einsum("htn,thp->hnp", lifted_c, grad_heads, preferred_element_type=f32)
    out_exact = scan_backward(weight, state_grad)
    out_low = out_exact.astype(bf16)

    grad_mix = jnp.einsum("thp,shp->hts", grad_heads, x_heads, preferred_element_type=f32)
    decayed = grad_mix * decay
    zterm = decayed * step_size[:, None, :]
    gram_grad = zterm * gram[None]
    reached = jnp.einsum("shp,hnp->hsn", x_heads, out_low, preferred_element_type=f32)
    inner_b = jnp.sum(b_rows.astype(f32)[None] * reached, axis=2)
    state_term = tail_step * inner_b
    grad_cumul = jnp.sum(gram_grad, axis=2) - jnp.sum(gram_grad, axis=1)
    carried_dot = jnp.sum(grad_heads.astype(f32) * handed, axis=2).T
    grad_cumul = grad_cumul + lifted * carried_dot - state_term
    end_grad = jnp.sum(state_term, axis=1) + jnp.exp(totals) * jnp.sum(
        out_exact * state_exact, axis=(1, 2)
    )
    grad_cumul = grad_cumul.at[:, -1].add(end_grad)
    grad_log = jnp.cumsum(grad_cumul[:, ::-1], axis=1)[:, ::-1]
    grad_steps = (
        jnp.sum(decayed * gram[None], axis=1)
        + trailing * inner_b
        + decay_rate[:, None] * grad_log
    )
    grad_x_heads = jnp.einsum("hts,thp->shp", mixer_low, grad_heads, preferred_element_type=f32)
    grad_x_heads = (
        grad_x_heads
        + d_skip[None, :, None] * grad_heads.astype(f32)
        + jnp.einsum("hsn,hnp->shp", weighted_b, out_low, preferred_element_type=f32)
    )
    grad_c_heads = lifted[:, :, None] * jnp.einsum(
        "thp,hnp->htn", grad_heads, state_low, preferred_element_type=f32
    )
    grad_b_heads = tail_step[:, :, None] * reached
    grad_sum = jnp.sum(zterm, axis=0)
    grad_c = jnp.sum(grad_c_heads, axis=0) + jnp.dot(grad_sum, b_rows.astype(f32), precision=HIGH)
    grad_b = jnp.sum(grad_b_heads, axis=0) + jnp.dot(
        grad_sum.T, c_rows.astype(f32), precision=HIGH
    )
    grad_bc_rows = jnp.stack([grad_b, grad_c])
    grad_x_rows = grad_x_heads.reshape(length, channels)

    grad_x_pre = grad_x_rows * silu_grad(x_pre)
    hcount = lax.axis_size("head")
    row_share = length // hcount
    hidx = lax.axis_index("head")
    first_row = hidx * row_share
    picks = []
    for h in range(hcount):
        own = [h * row_share + i for i in range(row_share + 3)]
        own = [r if r < length else length for r in own]
        picks.append(own + [length] * (12 - row_share - 3))
    picks = jnp.array(picks, jnp.int32)
    piece_rows = picks.shape[1]
    bc_rows_z = jnp.concatenate([grad_bc_rows, jnp.zeros((2, 1, nstate), f32)], axis=1)
    bc_pieces = jnp.moveaxis(jnp.take(bc_rows_z, picks.reshape(-1), axis=1).reshape(2, hcount, piece_rows, -1), 1, 0)
    top = (grad_bc_rows[:, :3] * silu_grad(bc_pre[:, :3])).reshape(6, nstate)
    rim_send = jnp.concatenate(
        [jnp.pad(grad_x_pre[:3], ((0, 5), (0, 0))), jnp.pad(top, ((0, 2), (0, 0)))], axis=1
    )
    summed, rim_got = tail_exchange(bc_pieces.reshape(hcount, 2 * piece_rows, -1), rim_send, 2)
    grad_bc_mine = summed.reshape(2, piece_rows, -1)[:, : row_share + 3]
    bc_pre_pad = jnp.concatenate([bc_pre, jnp.zeros((2, 3, nstate), f32)], axis=1)
    bc_pre_mine = lax.dynamic_slice_in_dim(bc_pre_pad, first_row, row_share + 3, 1)
    in_rim = (hidx == hcount - 1) & (jnp.arange(row_share + 3) >= row_share)
    grad_bc_ext = grad_bc_mine * jnp.where(in_rim[None, :, None], 1.0, silu_grad(bc_pre_mine))
    rim_x = rim_got[:3]
    grad_x = conv_back(jnp.concatenate([grad_x_pre, rim_x], axis=0), conv_x).astype(bf16)
    grad_bc = conv_back(grad_bc_ext, convolution_bc_taps).astype(bf16)
    grad_dt = grad_steps * jax.nn.sigmoid(dt_raw + dt_bias[:, None])
    return (grad_x, grad_z, grad_bc, grad_dt)


def solution(mesh):
    return jax.shard_map(
        shards,
        mesh=mesh,
        in_specs=(
            P("seq", "head"),
            P("seq", "head"),
            P(None, "seq", None),
            P("head", "seq"),
            P("head"),
            P("head"),
            P("head"),
            P(None, "head"),
            P(),
            P("head"),
            P("seq", "head"),
        ),
        out_specs=(
            P("seq", "head"),
            P("seq", "head"),
            P(None, ("seq", "head"), None),
            P("head", "seq"),
        ),
        check_vma=False,
    )
```

```python
import jax
import jax.numpy as jnp
from jax import lax
from jax.experimental import pallas as pl
from jax.experimental.pallas import tpu as pltpu
from jax.sharding import PartitionSpec as P
import functools

MESH = pl.DeviceIdType.MESH
AXES = ("seq", "head")


def exchange_kernel(axis, n, in_ref, out_ref, land, send_sem, recv_sem):
    me = lax.axis_index(axis)
    coords = {a: lax.axis_index(a) for a in AXES}

    def dev(k):
        return tuple(k if a == axis else coords[a] for a in AXES)

    barrier = pltpu.get_barrier_semaphore()
    for i in range(1, n):
        pl.semaphore_signal(barrier, inc=1, device_id=dev(lax.rem(me + i, n)), device_id_type=MESH)
    pl.semaphore_wait(barrier, n - 1)
    copies = []
    order = sorted(range(1, n), key=lambda i: -min(i, n - i))
    for i in order:
        peer = lax.rem(me + i, n)
        copy = pltpu.make_async_remote_copy(
            src_ref=in_ref.at[peer],
            dst_ref=land.at[me],
            send_sem=send_sem.at[i],
            recv_sem=recv_sem.at[i],
            device_id=dev(peer),
            device_id_type=MESH,
        )
        copy.start()
        copies.append(copy)
    land[me] = in_ref[me]
    for c in copies:
        c.wait_send()
    for i in range(1, n):
        src = lax.rem(me + (n - i), n)
        incoming = pltpu.make_async_remote_copy(
            src_ref=in_ref.at[src],
            dst_ref=land.at[src],
            send_sem=send_sem.at[i],
            recv_sem=recv_sem.at[i],
            device_id=dev(src),
            device_id_type=MESH,
        )
        incoming.wait_recv()
    out_ref[...] = land[...]


def exchange(x, axis, cid):
    n = lax.axis_size(axis)
    return pl.pallas_call(
        functools.partial(exchange_kernel, axis, n),
        out_shape=jax.ShapeDtypeStruct(x.shape, x.dtype),
        in_specs=[pl.BlockSpec(memory_space=pltpu.VMEM)],
        out_specs=pl.BlockSpec(memory_space=pltpu.VMEM),
        scratch_shapes=[
            pltpu.VMEM(x.shape, x.dtype),
            pltpu.SemaphoreType.DMA((n,)),
            pltpu.SemaphoreType.DMA((n,)),
        ],
        compiler_params=pltpu.CompilerParams(collective_id=cid, has_side_effects=True),
    )(x)

def _peer_copies(axis, n, src_of, dst, send_sem, recv_sem):
    me = lax.axis_index(axis)
    coords = {a: lax.axis_index(a) for a in AXES}

    def dev(k):
        return tuple(k if a == axis else coords[a] for a in AXES)

    copies = []
    for i in sorted(range(1, n), key=lambda i: -min(i, n - i)):
        peer = lax.rem(me + i, n)
        copy = pltpu.make_async_remote_copy(
            src_ref=src_of(peer),
            dst_ref=dst.at[me],
            send_sem=send_sem.at[i],
            recv_sem=recv_sem.at[i],
            device_id=dev(peer),
            device_id_type=MESH,
        )
        copy.start()
        copies.append(copy)
    return copies


def _peer_waits(axis, n, copies, src_of, dst, send_sem, recv_sem):
    me = lax.axis_index(axis)
    coords = {a: lax.axis_index(a) for a in AXES}

    def dev(k):
        return tuple(k if a == axis else coords[a] for a in AXES)

    for i in range(1, n):
        copies[i - 1].wait_send()
        src = lax.rem(me + (n - i), n)
        incoming = pltpu.make_async_remote_copy(
            src_ref=src_of(src),
            dst_ref=dst.at[src],
            send_sem=send_sem.at[i],
            recv_sem=recv_sem.at[i],
            device_id=dev(src),
            device_id_type=MESH,
        )
        incoming.wait_recv()


def _barrier(axis, n):
    me = lax.axis_index(axis)
    coords = {a: lax.axis_index(a) for a in AXES}
    barrier = pltpu.get_barrier_semaphore()
    for i in range(1, n):
        peer = lax.rem(me + i, n)
        dev = tuple(peer if a == axis else coords[a] for a in AXES)
        pl.semaphore_signal(barrier, inc=1, device_id=dev, device_id_type=MESH)
    pl.semaphore_wait(barrier, n - 1)


def scan_kernel(forward, axis, n, heads, *refs):
    if forward:
        in_ref, out_ref, scale_out, land, res, land2, s1, r1, s2, r2 = refs
    else:
        in_ref, scale_in, out_ref, land, res, land2, s1, r1, s2, r2 = refs
    me = lax.axis_index(axis)
    rows = res.shape[1]
    _barrier(axis, n)
    copies = _peer_copies(axis, n, lambda p: in_ref.at[p], land, s1, r1)
    land[me] = in_ref[me]
    coords = {a: lax.axis_index(a) for a in AXES}

    def dev(k):
        return tuple(k if a == axis else coords[a] for a in AXES)

    def arrive(k):
        @pl.when(me != k)
        def _():
            pltpu.make_async_remote_copy(
                src_ref=in_ref.at[k], dst_ref=land.at[k], send_sem=s1.at[0],
                recv_sem=r1.at[lax.rem(me - k + n, n)], device_id=dev(k), device_id_type=MESH,
            ).wait_recv()

    def result_copy(k):
        return pltpu.make_async_remote_copy(
            src_ref=res.at[k], dst_ref=land2.at[me], send_sem=s2.at[k], recv_sem=r2.at[me],
            device_id=dev(k), device_id_type=MESH,
        )

    def give(k):
        @pl.when(me != k)
        def _():
            result_copy(k).start()

        @pl.when(me == k)
        def _():
            land2[k] = res[k]

    acc = jnp.zeros((rows, 128), jnp.float32)
    if forward:
        lane = lax.broadcasted_iota(jnp.int32, (1, 128), 1)
        pick = lane == me // (n // heads)
        for k in range(n):
            res[k] = acc.astype(res.dtype)
            give(k)
            arrive(k)
            parts = land[k, rows : rows + 3, :].astype(jnp.float32)
            grow = jnp.exp(parts[0:1] + parts[1:2] + parts[2:3])
            factor = jnp.sum(jnp.where(pick, grow, 0.0), axis=1, keepdims=True)
            scale_out[k] = jnp.broadcast_to(factor, (8, 128))
            acc = factor * acc + land[k, :rows, :].astype(jnp.float32)
    else:
        for k in reversed(range(n)):
            res[k] = acc.astype(res.dtype)
            give(k)
            arrive(k)
            acc = land[k].astype(jnp.float32) + scale_in[k][0:1, 0:1] * acc
    for c in copies:
        c.wait_send()
    for k in range(n):
        @pl.when(me != k)
        def _():
            result_copy(k).wait_send()

        @pl.when(me != k)
        def _():
            pltpu.make_async_remote_copy(
                src_ref=res.at[k], dst_ref=land2.at[k], send_sem=s2.at[k], recv_sem=r2.at[k],
                device_id=dev(k), device_id_type=MESH,
            ).wait_recv()
    out_ref[...] = land2[...]


def scan_pieces(x, axis, heads, cid, scales=None):
    n = lax.axis_size(axis)
    forward = scales is None
    rows = x.shape[1] - 16 if forward else x.shape[1]
    piece = (n, rows, 128)
    low = x.dtype
    vm = pl.BlockSpec(memory_space=pltpu.VMEM)
    scratch = [
        pltpu.VMEM(x.shape, low),
        pltpu.VMEM(piece, low),
        pltpu.VMEM(piece, low),
        pltpu.SemaphoreType.DMA((n,)),
        pltpu.SemaphoreType.DMA((n,)),
        pltpu.SemaphoreType.DMA((n,)),
        pltpu.SemaphoreType.DMA((n,)),
    ]
    params = pltpu.CompilerParams(collective_id=cid, has_side_effects=True)
    kern = functools.partial(scan_kernel, forward, axis, n, heads)
    if forward:
        return pl.pallas_call(
            kern,
            out_shape=(jax.ShapeDtypeStruct(piece, low), jax.ShapeDtypeStruct((n, 8, 128), jnp.float32)),
            in_specs=[vm],
            out_specs=(vm, vm),
            scratch_shapes=scratch,
            compiler_params=params,
        )(x)
    return pl.pallas_call(
        kern,
        out_shape=jax.ShapeDtypeStruct(piece, low),
        in_specs=[vm, vm],
        out_specs=vm,
        scratch_shapes=scratch,
        compiler_params=params,
    )(x, scales)


def tail_kernel(n, hn, in_ref, rim_ref, out_ref, rim_out, land, send, rim_land, s1, r1, s2, r2):
    me = lax.axis_index("seq")
    hme = lax.axis_index("head")
    prev = lax.rem(me + n - 1, n)
    nxt = lax.rem(me + 1, n)
    last = hn - 1
    barrier = pltpu.get_barrier_semaphore()
    for i in range(1, hn):
        pl.semaphore_signal(barrier, inc=1, device_id=(me, lax.rem(hme + i, hn)), device_id_type=MESH)
    pl.semaphore_signal(barrier, inc=1, device_id=(prev, hme), device_id_type=MESH)
    pl.semaphore_signal(barrier, inc=1, device_id=(nxt, hme), device_id_type=MESH)
    pl.semaphore_wait(barrier, hn + 1)
    rim_copy = pltpu.make_async_remote_copy(
        src_ref=rim_ref, dst_ref=rim_land, send_sem=s2.at[0], recv_sem=r2.at[0],
        device_id=(prev, hme), device_id_type=MESH,
    )
    rim_copy.start()

    def piece_copy(t, src):
        return pltpu.make_async_remote_copy(
            src_ref=src, dst_ref=land.at[hme], send_sem=s1.at[t], recv_sem=r1.at[hme],
            device_id=(me, t), device_id_type=MESH,
        )

    for t in range(last):
        @pl.when(hme != t)
        def _():
            piece_copy(t, in_ref.at[t]).start()

    land[hme] = in_ref[hme]
    send[...] = in_ref[last]
    rim_copy.wait_send()
    rim_copy.wait_recv()
    keep = (1 - me // (n - 1)).astype(jnp.float32)
    rows = in_ref.shape[1] // 2
    nst = in_ref.shape[2]
    width = rim_ref.shape[1] - nst
    rim_bc = rim_land[0:8, width:] * keep
    send[8:11, :] = send[8:11, :] + rim_bc[0:3]
    send[rows + 8 : rows + 11, :] = send[rows + 8 : rows + 11, :] + rim_bc[3:6]
    rim_out[...] = rim_land[0:8, 0:width] * keep

    @pl.when(hme != last)
    def _():
        piece_copy(last, send).start()

    @pl.when(hme == last)
    def _():
        land[last] = send[...]

    for t in range(hn):
        @pl.when(hme != t)
        def _():
            piece_copy(t, send).wait_send()

    for j in range(hn):
        @pl.when(hme != j)
        def _():
            pltpu.make_async_remote_copy(
                src_ref=send, dst_ref=land.at[j], send_sem=s1.at[j], recv_sem=r1.at[j],
                device_id=(me, j), device_id_type=MESH,
            ).wait_recv()

    total = land[0]
    for j in range(1, hn):
        total = total + land[j]
    out_ref[...] = total


def tail_exchange(pieces, rim, cid):
    n = lax.axis_size("seq")
    hn = lax.axis_size("head")
    vm = pl.BlockSpec(memory_space=pltpu.VMEM)
    width = rim.shape[1] - pieces.shape[2]
    return pl.pallas_call(
        functools.partial(tail_kernel, n, hn),
        out_shape=(
            jax.ShapeDtypeStruct(pieces.shape[1:], jnp.float32),
            jax.ShapeDtypeStruct((8, width), jnp.float32),
        ),
        in_specs=[vm, vm],
        out_specs=(vm, vm),
        scratch_shapes=[
            pltpu.VMEM(pieces.shape, jnp.float32),
            pltpu.VMEM(pieces.shape[1:], jnp.float32),
            pltpu.VMEM(rim.shape, jnp.float32),
            pltpu.SemaphoreType.DMA((hn,)),
            pltpu.SemaphoreType.DMA((hn,)),
            pltpu.SemaphoreType.DMA((1,)),
            pltpu.SemaphoreType.DMA((1,)),
        ],
        compiler_params=pltpu.CompilerParams(collective_id=cid, has_side_effects=True),
    )(pieces, rim)


INNER = 16384


EPS = 1e-05
HIGH = lax.Precision.HIGHEST


def passed_along(block, axis, distance):
    devices = range(lax.axis_size(axis))
    route = [(i - distance, i) for i in devices if i - distance in devices]
    return lax.ppermute(block, axis, route)


def silu_grad(value):
    sigma = jax.nn.sigmoid(value)
    return sigma * (1.0 + value * (1.0 - sigma))


def conv_rows(extended, weight_matrix):
    length = extended.shape[-2] - 3
    summed = weight_matrix[..., 0, :][..., None, :] * extended[..., 0:length, :]
    for offset in range(1, 4):
        summed = (
            summed
            + weight_matrix[..., offset, :][..., None, :]
            * extended[..., offset : offset + length, :]
        )
    return summed


def conv_back(extended, weight_matrix):
    length = extended.shape[-2] - 3
    summed = weight_matrix[..., 0, :][..., None, :] * extended[..., 3 : 3 + length, :]
    for offset in range(1, 4):
        summed = (
            summed
            + weight_matrix[..., offset, :][..., None, :]
            * extended[..., 3 - offset : 3 - offset + length, :]
        )
    return summed


def to_pieces(state, count):
    heads, nstate, width = state.shape
    return state.reshape(count, heads * nstate // count, width)


def from_pieces(pieces, heads):
    count, rows, width = pieces.shape
    return pieces.reshape(heads, count * rows // heads, width)


def scan_forward(totals, local_state):
    count = lax.axis_size("seq")
    heads, nstate, width = local_state.shape
    pieces = to_pieces(local_state, count)
    high = lax.reduce_precision(totals, exponent_bits=8, mantissa_bits=7)
    rest = totals - high
    middle = lax.reduce_precision(rest, exponent_bits=8, mantissa_bits=7)
    parts = jnp.stack([high, middle, rest - middle])
    tot_row = jnp.pad(parts, ((0, 13), (0, width - heads)))
    tot_row = jnp.broadcast_to(tot_row, (count, 16, width))
    sent = jnp.concatenate([pieces, tot_row], axis=1).astype(jnp.bfloat16)
    back, scales = scan_pieces(sent, "seq", heads, 0)
    return from_pieces(back, heads).astype(jnp.float32), scales


def scan_backward(scales, state_grad):
    count = lax.axis_size("seq")
    heads = state_grad.shape[0]
    pieces = to_pieces(state_grad, count).astype(jnp.bfloat16)
    back = scan_pieces(pieces, "seq", heads, 1, scales)
    return from_pieces(back, heads).astype(jnp.float32)


def shards(
    x_input,
    z_input,
    bc_input,
    dt_raw,
    dt_bias,
    a_log,
    d_skip,
    conv_x,
    convolution_bc_taps,
    rescale_factor,
    grad_out,
):
    length = x_input.shape[0]
    channels = x_input.shape[1]
    head_count = dt_raw.shape[0]
    width = channels // head_count
    f32 = jnp.float32
    bf16 = jnp.bfloat16
    decay_rate = -jnp.exp(a_log)
    step_size = jax.nn.softplus(dt_raw + dt_bias[:, None])
    causal = jnp.tril(jnp.ones((length, length), dtype=bool))
    nstate = bc_input.shape[2]
    rows_last = jnp.concatenate(
        [x_input[length - 3 :], jnp.moveaxis(bc_input[:, length - 3 :], 0, 1).reshape(3, 2 * nstate)],
        axis=1,
    )
    rows_prior = passed_along(rows_last, "seq", 1)
    x_ext = jnp.concatenate([rows_prior[:, :channels], x_input], axis=0)
    bc_prior = jnp.moveaxis(rows_prior[:, channels:].reshape(3, 2, nstate), 0, 1)
    bc_ext = jnp.concatenate([bc_prior, bc_input], axis=1)
    x_pre = conv_rows(x_ext.astype(f32), conv_x)
    bc_pre = conv_rows(bc_ext.astype(f32), convolution_bc_taps)
    x_rows = jax.nn.silu(x_pre).astype(bf16)
    bc_rows = jax.nn.silu(bc_pre).astype(bf16)
    b_rows = bc_rows[0]
    c_rows = bc_rows[1]
    gram = jnp.dot(c_rows, b_rows.T, preferred_element_type=f32)
    x_heads = x_rows.reshape(length, head_count, width)

    cumul = jnp.cumsum(decay_rate[:, None] * step_size, axis=1)
    totals = cumul[:, -1]
    trailing = jnp.exp(cumul[:, -1:] - cumul)
    tail_step = trailing * step_size
    weighted_b = (tail_step[:, :, None] * b_rows.astype(f32)[None]).astype(bf16)
    local_state = jnp.einsum("hsn,shp->hnp", weighted_b, x_heads, preferred_element_type=f32)

    state_exact, weight = scan_forward(totals, local_state)
    state_low = state_exact.astype(bf16)

    between = cumul[:, :, None] - cumul[:, None, :]
    decay = jnp.where(causal[None], jnp.exp(jnp.minimum(between, 0.0)), 0.0)
    mixer_low = (gram[None] * decay * step_size[:, None, :]).astype(bf16)
    intra = jnp.einsum("hts,shp->thp", mixer_low, x_heads, preferred_element_type=f32)
    handed = jnp.einsum("tn,hnp->thp", c_rows, state_low, preferred_element_type=f32)
    lifted = jnp.exp(cumul)
    mixed_heads = (
        intra + lifted.T[:, :, None] * handed + d_skip[None, :, None] * x_heads.astype(f32)
    )
    mixed_out = mixed_heads.reshape(length, channels)

    z_rows = z_input.astype(f32)
    gate_value = jax.nn.silu(z_rows)
    gated = mixed_out * gate_value
    scaled = grad_out.astype(f32) * rescale_factor
    hcount = lax.axis_size("head")
    own_sums = jnp.stack([jnp.sum(gated * gated, axis=1), jnp.sum(scaled * gated, axis=1)])
    own_sums = jnp.concatenate([own_sums, jnp.zeros((6, length), f32)], axis=0)
    sums = jnp.sum(exchange(jnp.broadcast_to(own_sums, (hcount,) + own_sums.shape), "head", 3), axis=0)
    inv_rms = lax.rsqrt(sums[0] / INNER + EPS)
    normed = gated * inv_rms[:, None]
    mean_dot = inv_rms * sums[1] / INNER
    grad_gated = inv_rms[:, None] * (scaled - normed * mean_dot[:, None])
    grad_z = (grad_gated * mixed_out * silu_grad(z_rows)).astype(bf16)
    grad_mixed = (grad_gated * gate_value).astype(bf16)
    grad_heads = grad_mixed.reshape(length, head_count, width)

    lifted_c = (lifted[:, :, None] * c_rows.astype(f32)[None]).astype(bf16)
    state_grad = jnp.einsum("htn,thp->hnp", lifted_c, grad_heads, preferred_element_type=f32)
    out_exact = scan_backward(weight, state_grad)
    out_low = out_exact.astype(bf16)

    grad_mix = jnp.einsum("thp,shp->hts", grad_heads, x_heads, preferred_element_type=f32)
    decayed = grad_mix * decay
    zterm = decayed * step_size[:, None, :]
    gram_grad = zterm * gram[None]
    reached = jnp.einsum("shp,hnp->hsn", x_heads, out_low, preferred_element_type=f32)
    inner_b = jnp.sum(b_rows.astype(f32)[None] * reached, axis=2)
    state_term = tail_step * inner_b
    grad_cumul = jnp.sum(gram_grad, axis=2) - jnp.sum(gram_grad, axis=1)
    carried_dot = jnp.sum(grad_heads.astype(f32) * handed, axis=2).T
    grad_cumul = grad_cumul + lifted * carried_dot - state_term
    end_grad = jnp.sum(state_term, axis=1) + jnp.exp(totals) * jnp.sum(
        out_exact * state_exact, axis=(1, 2)
    )
    grad_cumul = grad_cumul.at[:, -1].add(end_grad)
    grad_log = jnp.cumsum(grad_cumul[:, ::-1], axis=1)[:, ::-1]
    grad_steps = (
        jnp.sum(decayed * gram[None], axis=1)
        + trailing * inner_b
        + decay_rate[:, None] * grad_log
    )
    grad_x_heads = jnp.einsum("hts,thp->shp", mixer_low, grad_heads, preferred_element_type=f32)
    grad_x_heads = (
        grad_x_heads
        + d_skip[None, :, None] * grad_heads.astype(f32)
        + jnp.einsum("hsn,hnp->shp", weighted_b, out_low, preferred_element_type=f32)
    )
    grad_c_heads = lifted[:, :, None] * jnp.einsum(
        "thp,hnp->htn", grad_heads, state_low, preferred_element_type=f32
    )
    grad_b_heads = tail_step[:, :, None] * reached
    grad_sum = jnp.sum(zterm, axis=0)
    grad_c = jnp.sum(grad_c_heads, axis=0) + jnp.dot(grad_sum, b_rows.astype(f32), precision=HIGH)
    grad_b = jnp.sum(grad_b_heads, axis=0) + jnp.dot(
        grad_sum.T, c_rows.astype(f32), precision=HIGH
    )
    grad_bc_rows = jnp.stack([grad_b, grad_c])
    grad_x_rows = grad_x_heads.reshape(length, channels)

    grad_x_pre = grad_x_rows * silu_grad(x_pre)
    hcount = lax.axis_size("head")
    row_share = length // hcount
    hidx = lax.axis_index("head")
    first_row = hidx * row_share
    picks = []
    for h in range(hcount):
        own = [h * row_share + i for i in range(row_share + 3)]
        own = [r if r < length else length for r in own]
        picks.append(own + [length] * (12 - row_share - 3))
    picks = jnp.array(picks, jnp.int32)
    piece_rows = picks.shape[1]
    bc_rows_z = jnp.concatenate([grad_bc_rows, jnp.zeros((2, 1, nstate), f32)], axis=1)
    both = jnp.concatenate([picks, picks + (length + 1)], axis=1)
    bc_pieces = jnp.take(bc_rows_z.reshape(2 * (length + 1), nstate), both.reshape(-1), axis=0)
    top = (grad_bc_rows[:, :3] * silu_grad(bc_pre[:, :3])).reshape(6, nstate)
    rim_send = jnp.concatenate(
        [jnp.pad(grad_x_pre[:3], ((0, 5), (0, 0))), jnp.pad(top, ((0, 2), (0, 0)))], axis=1
    )
    summed, rim_got = tail_exchange(bc_pieces.reshape(hcount, 2 * piece_rows, -1), rim_send, 2)
    grad_bc_mine = summed.reshape(2, piece_rows, -1)[:, : row_share + 3]
    bc_pre_pad = jnp.concatenate([bc_pre, jnp.zeros((2, 3, nstate), f32)], axis=1)
    bc_pre_mine = lax.dynamic_slice_in_dim(bc_pre_pad, first_row, row_share + 3, 1)
    in_rim = (hidx == hcount - 1) & (jnp.arange(row_share + 3) >= row_share)
    grad_bc_ext = grad_bc_mine * jnp.where(in_rim[None, :, None], 1.0, silu_grad(bc_pre_mine))
    rim_x = rim_got[:3]
    grad_x = conv_back(jnp.concatenate([grad_x_pre, rim_x], axis=0), conv_x).astype(bf16)
    grad_bc = conv_back(grad_bc_ext, convolution_bc_taps).astype(bf16)
    grad_dt = grad_steps * jax.nn.sigmoid(dt_raw + dt_bias[:, None])
    return (grad_x, grad_z, grad_bc, grad_dt)


def solution(mesh):
    return jax.shard_map(
        shards,
        mesh=mesh,
        in_specs=(
            P("seq", "head"),
            P("seq", "head"),
            P(None, "seq", None),
            P("head", "seq"),
            P("head"),
            P("head"),
            P("head"),
            P(None, "head"),
            P(),
            P("head"),
            P("seq", "head"),
        ),
        out_specs=(
            P("seq", "head"),
            P("seq", "head"),
            P(None, ("seq", "head"), None),
            P("head", "seq"),
        ),
        check_vma=False,
    )
```

```python
import jax
import jax.numpy as jnp
from jax import lax
from jax.experimental import pallas as pl
from jax.experimental.pallas import tpu as pltpu
from jax.sharding import PartitionSpec as P
import functools

MESH = pl.DeviceIdType.MESH
AXES = ("seq", "head")


def exchange_kernel(axis, n, in_ref, out_ref, land, send_sem, recv_sem):
    me = lax.axis_index(axis)
    coords = {a: lax.axis_index(a) for a in AXES}

    def dev(k):
        return tuple(k if a == axis else coords[a] for a in AXES)

    barrier = pltpu.get_barrier_semaphore()
    for i in range(1, n):
        pl.semaphore_signal(barrier, inc=1, device_id=dev(lax.rem(me + i, n)), device_id_type=MESH)
    pl.semaphore_wait(barrier, n - 1)
    copies = []
    order = sorted(range(1, n), key=lambda i: -min(i, n - i))
    for i in order:
        peer = lax.rem(me + i, n)
        copy = pltpu.make_async_remote_copy(
            src_ref=in_ref.at[peer],
            dst_ref=land.at[me],
            send_sem=send_sem.at[i],
            recv_sem=recv_sem.at[i],
            device_id=dev(peer),
            device_id_type=MESH,
        )
        copy.start()
        copies.append(copy)
    land[me] = in_ref[me]
    for c in copies:
        c.wait_send()
    for i in range(1, n):
        src = lax.rem(me + (n - i), n)
        incoming = pltpu.make_async_remote_copy(
            src_ref=in_ref.at[src],
            dst_ref=land.at[src],
            send_sem=send_sem.at[i],
            recv_sem=recv_sem.at[i],
            device_id=dev(src),
            device_id_type=MESH,
        )
        incoming.wait_recv()
    out_ref[...] = land[...]


def exchange(x, axis, cid):
    n = lax.axis_size(axis)
    return pl.pallas_call(
        functools.partial(exchange_kernel, axis, n),
        out_shape=jax.ShapeDtypeStruct(x.shape, x.dtype),
        in_specs=[pl.BlockSpec(memory_space=pltpu.VMEM)],
        out_specs=pl.BlockSpec(memory_space=pltpu.VMEM),
        scratch_shapes=[
            pltpu.VMEM(x.shape, x.dtype),
            pltpu.SemaphoreType.DMA((n,)),
            pltpu.SemaphoreType.DMA((n,)),
        ],
        compiler_params=pltpu.CompilerParams(collective_id=cid, has_side_effects=True),
    )(x)

def _peer_copies(axis, n, src_of, dst, send_sem, recv_sem):
    me = lax.axis_index(axis)
    coords = {a: lax.axis_index(a) for a in AXES}

    def dev(k):
        return tuple(k if a == axis else coords[a] for a in AXES)

    copies = []
    for i in sorted(range(1, n), key=lambda i: -min(i, n - i)):
        peer = lax.rem(me + i, n)
        copy = pltpu.make_async_remote_copy(
            src_ref=src_of(peer),
            dst_ref=dst.at[me],
            send_sem=send_sem.at[i],
            recv_sem=recv_sem.at[i],
            device_id=dev(peer),
            device_id_type=MESH,
        )
        copy.start()
        copies.append(copy)
    return copies


def _peer_waits(axis, n, copies, src_of, dst, send_sem, recv_sem):
    me = lax.axis_index(axis)
    coords = {a: lax.axis_index(a) for a in AXES}

    def dev(k):
        return tuple(k if a == axis else coords[a] for a in AXES)

    for i in range(1, n):
        copies[i - 1].wait_send()
        src = lax.rem(me + (n - i), n)
        incoming = pltpu.make_async_remote_copy(
            src_ref=src_of(src),
            dst_ref=dst.at[src],
            send_sem=send_sem.at[i],
            recv_sem=recv_sem.at[i],
            device_id=dev(src),
            device_id_type=MESH,
        )
        incoming.wait_recv()


def _barrier(axis, n):
    me = lax.axis_index(axis)
    coords = {a: lax.axis_index(a) for a in AXES}
    barrier = pltpu.get_barrier_semaphore()
    for i in range(1, n):
        peer = lax.rem(me + i, n)
        dev = tuple(peer if a == axis else coords[a] for a in AXES)
        pl.semaphore_signal(barrier, inc=1, device_id=dev, device_id_type=MESH)
    pl.semaphore_wait(barrier, n - 1)


def scan_kernel(forward, axis, n, heads, *refs):
    if forward:
        in_ref, out_ref, scale_out, land, res, land2, s1, r1, s2, r2 = refs
    else:
        in_ref, scale_in, out_ref, land, res, land2, s1, r1, s2, r2 = refs
    me = lax.axis_index(axis)
    rows = res.shape[1]
    _barrier(axis, n)
    copies = _peer_copies(axis, n, lambda p: in_ref.at[p], land, s1, r1)
    land[me] = in_ref[me]
    coords = {a: lax.axis_index(a) for a in AXES}

    def dev(k):
        return tuple(k if a == axis else coords[a] for a in AXES)

    def arrive(k):
        @pl.when(me != k)
        def _():
            pltpu.make_async_remote_copy(
                src_ref=in_ref.at[k], dst_ref=land.at[k], send_sem=s1.at[0],
                recv_sem=r1.at[lax.rem(me - k + n, n)], device_id=dev(k), device_id_type=MESH,
            ).wait_recv()

    def result_copy(k):
        return pltpu.make_async_remote_copy(
            src_ref=res.at[k], dst_ref=land2.at[me], send_sem=s2.at[k], recv_sem=r2.at[me],
            device_id=dev(k), device_id_type=MESH,
        )

    def give(k):
        @pl.when(me != k)
        def _():
            result_copy(k).start()

        @pl.when(me == k)
        def _():
            land2[k] = res[k]

    acc = jnp.zeros((rows, 128), jnp.float32)
    if forward:
        lane = lax.broadcasted_iota(jnp.int32, (1, 128), 1)
        pick = lane == me // (n // heads)
        for k in range(n):
            res[k] = acc.astype(res.dtype)
            give(k)
            arrive(k)
            parts = land[k, rows : rows + 3, :].astype(jnp.float32)
            grow = jnp.exp(parts[0:1] + parts[1:2] + parts[2:3])
            factor = jnp.sum(jnp.where(pick, grow, 0.0), axis=1, keepdims=True)
            scale_out[k] = jnp.broadcast_to(factor, (8, 128))
            acc = factor * acc + land[k, :rows, :].astype(jnp.float32)
    else:
        for k in reversed(range(n)):
            res[k] = acc.astype(res.dtype)
            give(k)
            arrive(k)
            acc = land[k].astype(jnp.float32) + scale_in[k][0:1, 0:1] * acc
    for c in copies:
        c.wait_send()
    for k in range(n):
        @pl.when(me != k)
        def _():
            result_copy(k).wait_send()

        @pl.when(me != k)
        def _():
            pltpu.make_async_remote_copy(
                src_ref=res.at[k], dst_ref=land2.at[k], send_sem=s2.at[k], recv_sem=r2.at[k],
                device_id=dev(k), device_id_type=MESH,
            ).wait_recv()
    out_ref[...] = land2[...]


def scan_pieces(x, axis, heads, cid, scales=None):
    n = lax.axis_size(axis)
    forward = scales is None
    rows = x.shape[1] - 16 if forward else x.shape[1]
    piece = (n, rows, 128)
    low = x.dtype
    vm = pl.BlockSpec(memory_space=pltpu.VMEM)
    scratch = [
        pltpu.VMEM(x.shape, low),
        pltpu.VMEM(piece, low),
        pltpu.VMEM(piece, low),
        pltpu.SemaphoreType.DMA((n,)),
        pltpu.SemaphoreType.DMA((n,)),
        pltpu.SemaphoreType.DMA((n,)),
        pltpu.SemaphoreType.DMA((n,)),
    ]
    params = pltpu.CompilerParams(collective_id=cid, has_side_effects=True)
    kern = functools.partial(scan_kernel, forward, axis, n, heads)
    if forward:
        return pl.pallas_call(
            kern,
            out_shape=(jax.ShapeDtypeStruct(piece, low), jax.ShapeDtypeStruct((n, 8, 128), jnp.float32)),
            in_specs=[vm],
            out_specs=(vm, vm),
            scratch_shapes=scratch,
            compiler_params=params,
        )(x)
    return pl.pallas_call(
        kern,
        out_shape=jax.ShapeDtypeStruct(piece, low),
        in_specs=[vm, vm],
        out_specs=vm,
        scratch_shapes=scratch,
        compiler_params=params,
    )(x, scales)


def tail_kernel(n, hn, in_ref, rim_ref, out_ref, rim_out, land, send, rim_land, s1, r1, s2, r2):
    me = lax.axis_index("seq")
    hme = lax.axis_index("head")
    prev = lax.rem(me + n - 1, n)
    nxt = lax.rem(me + 1, n)
    last = hn - 1
    barrier = pltpu.get_barrier_semaphore()
    for i in range(1, hn):
        pl.semaphore_signal(barrier, inc=1, device_id=(me, lax.rem(hme + i, hn)), device_id_type=MESH)
    pl.semaphore_signal(barrier, inc=1, device_id=(prev, hme), device_id_type=MESH)
    pl.semaphore_signal(barrier, inc=1, device_id=(nxt, hme), device_id_type=MESH)
    pl.semaphore_wait(barrier, hn + 1)
    rim_copy = pltpu.make_async_remote_copy(
        src_ref=rim_ref, dst_ref=rim_land, send_sem=s2.at[0], recv_sem=r2.at[0],
        device_id=(prev, hme), device_id_type=MESH,
    )
    rim_copy.start()

    def piece_copy(t, src):
        return pltpu.make_async_remote_copy(
            src_ref=src, dst_ref=land.at[hme], send_sem=s1.at[t], recv_sem=r1.at[hme],
            device_id=(me, t), device_id_type=MESH,
        )

    for i in sorted(range(1, hn), key=lambda i: -min(i, hn - i)):
        t = lax.rem(hme + i, hn)

        @pl.when(t != last)
        def _():
            piece_copy(t, in_ref.at[t]).start()

    land[hme] = in_ref[hme]
    send[...] = in_ref[last]
    rim_copy.wait_send()
    rim_copy.wait_recv()
    keep = (1 - me // (n - 1)).astype(jnp.float32)
    rows = in_ref.shape[1] // 2
    nst = in_ref.shape[2]
    width = rim_ref.shape[1] - nst
    rim_bc = rim_land[0:8, width:] * keep
    send[8:11, :] = send[8:11, :] + rim_bc[0:3]
    send[rows + 8 : rows + 11, :] = send[rows + 8 : rows + 11, :] + rim_bc[3:6]
    rim_out[...] = rim_land[0:8, 0:width] * keep

    @pl.when(hme != last)
    def _():
        piece_copy(last, send).start()

    @pl.when(hme == last)
    def _():
        land[last] = send[...]

    for t in range(hn):
        @pl.when(hme != t)
        def _():
            piece_copy(t, send).wait_send()

    for j in range(hn):
        @pl.when(hme != j)
        def _():
            pltpu.make_async_remote_copy(
                src_ref=send, dst_ref=land.at[j], send_sem=s1.at[j], recv_sem=r1.at[j],
                device_id=(me, j), device_id_type=MESH,
            ).wait_recv()

    total = land[0]
    for j in range(1, hn):
        total = total + land[j]
    out_ref[...] = total


def tail_exchange(pieces, rim, cid):
    n = lax.axis_size("seq")
    hn = lax.axis_size("head")
    vm = pl.BlockSpec(memory_space=pltpu.VMEM)
    width = rim.shape[1] - pieces.shape[2]
    return pl.pallas_call(
        functools.partial(tail_kernel, n, hn),
        out_shape=(
            jax.ShapeDtypeStruct(pieces.shape[1:], jnp.float32),
            jax.ShapeDtypeStruct((8, width), jnp.float32),
        ),
        in_specs=[vm, vm],
        out_specs=(vm, vm),
        scratch_shapes=[
            pltpu.VMEM(pieces.shape, jnp.float32),
            pltpu.VMEM(pieces.shape[1:], jnp.float32),
            pltpu.VMEM(rim.shape, jnp.float32),
            pltpu.SemaphoreType.DMA((hn,)),
            pltpu.SemaphoreType.DMA((hn,)),
            pltpu.SemaphoreType.DMA((1,)),
            pltpu.SemaphoreType.DMA((1,)),
        ],
        compiler_params=pltpu.CompilerParams(collective_id=cid, has_side_effects=True),
    )(pieces, rim)


INNER = 16384


EPS = 1e-05
HIGH = lax.Precision.HIGHEST


def passed_along(block, axis, distance):
    devices = range(lax.axis_size(axis))
    route = [(i - distance, i) for i in devices if i - distance in devices]
    return lax.ppermute(block, axis, route)


def silu_grad(value):
    sigma = jax.nn.sigmoid(value)
    return sigma * (1.0 + value * (1.0 - sigma))


def conv_rows(extended, weight_matrix):
    length = extended.shape[-2] - 3
    summed = weight_matrix[..., 0, :][..., None, :] * extended[..., 0:length, :]
    for offset in range(1, 4):
        summed = (
            summed
            + weight_matrix[..., offset, :][..., None, :]
            * extended[..., offset : offset + length, :]
        )
    return summed


def conv_back(extended, weight_matrix):
    length = extended.shape[-2] - 3
    summed = weight_matrix[..., 0, :][..., None, :] * extended[..., 3 : 3 + length, :]
    for offset in range(1, 4):
        summed = (
            summed
            + weight_matrix[..., offset, :][..., None, :]
            * extended[..., 3 - offset : 3 - offset + length, :]
        )
    return summed


def to_pieces(state, count):
    heads, nstate, width = state.shape
    return state.reshape(count, heads * nstate // count, width)


def from_pieces(pieces, heads):
    count, rows, width = pieces.shape
    return pieces.reshape(heads, count * rows // heads, width)


def scan_forward(totals, local_state):
    count = lax.axis_size("seq")
    heads, nstate, width = local_state.shape
    pieces = to_pieces(local_state, count)
    high = lax.reduce_precision(totals, exponent_bits=8, mantissa_bits=7)
    rest = totals - high
    middle = lax.reduce_precision(rest, exponent_bits=8, mantissa_bits=7)
    parts = jnp.stack([high, middle, rest - middle])
    tot_row = jnp.pad(parts, ((0, 13), (0, width - heads)))
    tot_row = jnp.broadcast_to(tot_row, (count, 16, width))
    sent = jnp.concatenate([pieces, tot_row], axis=1).astype(jnp.bfloat16)
    back, scales = scan_pieces(sent, "seq", heads, 0)
    return from_pieces(back, heads).astype(jnp.float32), scales


def scan_backward(scales, state_grad):
    count = lax.axis_size("seq")
    heads = state_grad.shape[0]
    pieces = to_pieces(state_grad, count).astype(jnp.bfloat16)
    back = scan_pieces(pieces, "seq", heads, 1, scales)
    return from_pieces(back, heads).astype(jnp.float32)


def shards(
    x_input,
    z_input,
    bc_input,
    dt_raw,
    dt_bias,
    a_log,
    d_skip,
    conv_x,
    convolution_bc_taps,
    rescale_factor,
    grad_out,
):
    length = x_input.shape[0]
    channels = x_input.shape[1]
    head_count = dt_raw.shape[0]
    width = channels // head_count
    f32 = jnp.float32
    bf16 = jnp.bfloat16
    decay_rate = -jnp.exp(a_log)
    step_size = jax.nn.softplus(dt_raw + dt_bias[:, None])
    causal = jnp.tril(jnp.ones((length, length), dtype=bool))
    nstate = bc_input.shape[2]
    rows_last = jnp.concatenate(
        [x_input[length - 3 :], jnp.moveaxis(bc_input[:, length - 3 :], 0, 1).reshape(3, 2 * nstate)],
        axis=1,
    )
    rows_prior = passed_along(rows_last, "seq", 1)
    x_ext = jnp.concatenate([rows_prior[:, :channels], x_input], axis=0)
    bc_prior = jnp.moveaxis(rows_prior[:, channels:].reshape(3, 2, nstate), 0, 1)
    bc_ext = jnp.concatenate([bc_prior, bc_input], axis=1)
    x_pre = conv_rows(x_ext.astype(f32), conv_x)
    bc_pre = conv_rows(bc_ext.astype(f32), convolution_bc_taps)
    x_rows = jax.nn.silu(x_pre).astype(bf16)
    bc_rows = jax.nn.silu(bc_pre).astype(bf16)
    b_rows = bc_rows[0]
    c_rows = bc_rows[1]
    gram = jnp.dot(c_rows, b_rows.T, preferred_element_type=f32)
    x_heads = x_rows.reshape(length, head_count, width)

    cumul = jnp.cumsum(decay_rate[:, None] * step_size, axis=1)
    totals = cumul[:, -1]
    trailing = jnp.exp(cumul[:, -1:] - cumul)
    tail_step = trailing * step_size
    weighted_b = (tail_step[:, :, None] * b_rows.astype(f32)[None]).astype(bf16)
    local_state = jnp.einsum("hsn,shp->hnp", weighted_b, x_heads, preferred_element_type=f32)

    state_exact, weight = scan_forward(totals, local_state)
    state_low = state_exact.astype(bf16)

    between = cumul[:, :, None] - cumul[:, None, :]
    decay = jnp.where(causal[None], jnp.exp(jnp.minimum(between, 0.0)), 0.0)
    mixer_low = (gram[None] * decay * step_size[:, None, :]).astype(bf16)
    intra = jnp.einsum("hts,shp->thp", mixer_low, x_heads, preferred_element_type=f32)
    handed = jnp.einsum("tn,hnp->thp", c_rows, state_low, preferred_element_type=f32)
    lifted = jnp.exp(cumul)
    mixed_heads = (
        intra + lifted.T[:, :, None] * handed + d_skip[None, :, None] * x_heads.astype(f32)
    )
    mixed_out = mixed_heads.reshape(length, channels)

    z_rows = z_input.astype(f32)
    gate_value = jax.nn.silu(z_rows)
    gated = mixed_out * gate_value
    scaled = grad_out.astype(f32) * rescale_factor
    hcount = lax.axis_size("head")
    own_sums = jnp.stack([jnp.sum(gated * gated, axis=1), jnp.sum(scaled * gated, axis=1)])
    own_sums = jnp.concatenate([own_sums, jnp.zeros((6, length), f32)], axis=0)
    sums = jnp.sum(exchange(jnp.broadcast_to(own_sums, (hcount,) + own_sums.shape), "head", 3), axis=0)
    inv_rms = lax.rsqrt(sums[0] / INNER + EPS)
    normed = gated * inv_rms[:, None]
    mean_dot = inv_rms * sums[1] / INNER
    grad_gated = inv_rms[:, None] * (scaled - normed * mean_dot[:, None])
    grad_z = (grad_gated * mixed_out * silu_grad(z_rows)).astype(bf16)
    grad_mixed = (grad_gated * gate_value).astype(bf16)
    grad_heads = grad_mixed.reshape(length, head_count, width)

    lifted_c = (lifted[:, :, None] * c_rows.astype(f32)[None]).astype(bf16)
    state_grad = jnp.einsum("htn,thp->hnp", lifted_c, grad_heads, preferred_element_type=f32)
    out_exact = scan_backward(weight, state_grad)
    out_low = out_exact.astype(bf16)

    grad_mix = jnp.einsum("thp,shp->hts", grad_heads, x_heads, preferred_element_type=f32)
    decayed = grad_mix * decay
    zterm = decayed * step_size[:, None, :]
    gram_grad = zterm * gram[None]
    reached = jnp.einsum("shp,hnp->hsn", x_heads, out_low, preferred_element_type=f32)
    inner_b = jnp.sum(b_rows.astype(f32)[None] * reached, axis=2)
    state_term = tail_step * inner_b
    grad_cumul = jnp.sum(gram_grad, axis=2) - jnp.sum(gram_grad, axis=1)
    carried_dot = jnp.sum(grad_heads.astype(f32) * handed, axis=2).T
    grad_cumul = grad_cumul + lifted * carried_dot - state_term
    end_grad = jnp.sum(state_term, axis=1) + jnp.exp(totals) * jnp.sum(
        out_exact * state_exact, axis=(1, 2)
    )
    grad_cumul = grad_cumul.at[:, -1].add(end_grad)
    grad_log = jnp.cumsum(grad_cumul[:, ::-1], axis=1)[:, ::-1]
    grad_steps = (
        jnp.sum(decayed * gram[None], axis=1)
        + trailing * inner_b
        + decay_rate[:, None] * grad_log
    )
    grad_x_heads = jnp.einsum("hts,thp->shp", mixer_low, grad_heads, preferred_element_type=f32)
    grad_x_heads = (
        grad_x_heads
        + d_skip[None, :, None] * grad_heads.astype(f32)
        + jnp.einsum("hsn,hnp->shp", weighted_b, out_low, preferred_element_type=f32)
    )
    grad_c_heads = lifted[:, :, None] * jnp.einsum(
        "thp,hnp->htn", grad_heads, state_low, preferred_element_type=f32
    )
    grad_b_heads = tail_step[:, :, None] * reached
    grad_sum = jnp.sum(zterm, axis=0)
    grad_c = jnp.sum(grad_c_heads, axis=0) + jnp.dot(grad_sum, b_rows.astype(f32), precision=HIGH)
    grad_b = jnp.sum(grad_b_heads, axis=0) + jnp.dot(
        grad_sum.T, c_rows.astype(f32), precision=HIGH
    )
    grad_bc_rows = jnp.stack([grad_b, grad_c])
    grad_x_rows = grad_x_heads.reshape(length, channels)

    grad_x_pre = grad_x_rows * silu_grad(x_pre)
    hcount = lax.axis_size("head")
    row_share = length // hcount
    hidx = lax.axis_index("head")
    first_row = hidx * row_share
    picks = []
    for h in range(hcount):
        own = [h * row_share + i for i in range(row_share + 3)]
        own = [r if r < length else length for r in own]
        picks.append(own + [length] * (12 - row_share - 3))
    picks = jnp.array(picks, jnp.int32)
    piece_rows = picks.shape[1]
    bc_rows_z = jnp.concatenate([grad_bc_rows, jnp.zeros((2, 1, nstate), f32)], axis=1)
    both = jnp.concatenate([picks, picks + (length + 1)], axis=1)
    bc_pieces = jnp.take(bc_rows_z.reshape(2 * (length + 1), nstate), both.reshape(-1), axis=0)
    top = (grad_bc_rows[:, :3] * silu_grad(bc_pre[:, :3])).reshape(6, nstate)
    rim_send = jnp.concatenate(
        [jnp.pad(grad_x_pre[:3], ((0, 5), (0, 0))), jnp.pad(top, ((0, 2), (0, 0)))], axis=1
    )
    summed, rim_got = tail_exchange(bc_pieces.reshape(hcount, 2 * piece_rows, -1), rim_send, 2)
    grad_bc_mine = summed.reshape(2, piece_rows, -1)[:, : row_share + 3]
    bc_pre_pad = jnp.concatenate([bc_pre, jnp.zeros((2, 3, nstate), f32)], axis=1)
    bc_pre_mine = lax.dynamic_slice_in_dim(bc_pre_pad, first_row, row_share + 3, 1)
    in_rim = (hidx == hcount - 1) & (jnp.arange(row_share + 3) >= row_share)
    grad_bc_ext = grad_bc_mine * jnp.where(in_rim[None, :, None], 1.0, silu_grad(bc_pre_mine))
    rim_x = rim_got[:3]
    grad_x = conv_back(jnp.concatenate([grad_x_pre, rim_x], axis=0), conv_x).astype(bf16)
    grad_bc = conv_back(grad_bc_ext, convolution_bc_taps).astype(bf16)
    grad_dt = grad_steps * jax.nn.sigmoid(dt_raw + dt_bias[:, None])
    return (grad_x, grad_z, grad_bc, grad_dt)


def solution(mesh):
    return jax.shard_map(
        shards,
        mesh=mesh,
        in_specs=(
            P("seq", "head"),
            P("seq", "head"),
            P(None, "seq", None),
            P("head", "seq"),
            P("head"),
            P("head"),
            P("head"),
            P(None, "head"),
            P(),
            P("head"),
            P("seq", "head"),
        ),
        out_specs=(
            P("seq", "head"),
            P("seq", "head"),
            P(None, ("seq", "head"), None),
            P("head", "seq"),
        ),
        check_vma=False,
    )
```
